32 devices in a mesh: dp: 8 (over y, x, core), fsdp: 4 (over z).
Axes of the slice: x: 2, y: 2, z: 4, core: 2. Of those that a mesh axis runs over, the one named last changes fastest.
Arguments:
- x_prompt: bfloat16 [8, 1024, 1024], P('dp', 'fsdp'), may hold values from -6 to 6
- x_cont: bfloat16 [8, 1024, 1024], P('dp', 'fsdp'), may hold values from -6 to 6
- cot_prompt: bfloat16 [8, 1024, 1024], P('dp', 'fsdp'), may hold values from -6 to 6
- cot_cont: bfloat16 [8, 1024, 1024], P('dp', 'fsdp'), may hold values from -6 to 6
- gain_attn: float32 [1024], replicated, may hold values from 0.25 to 1.75
- gain_mem: float32 [1024], replicated, may hold values from 0.25 to 1.75
- w_qkv: bfloat16 [3, 1024, 1024], P(None, 'fsdp'), may hold values from -0.1875 to 0.1875
- w_attn_out: bfloat16 [1024, 1024], P('fsdp'), may hold values from -2 to 2
- w_mem_query: bfloat16 [1024, 4096], P('fsdp'), may hold values from -0.1875 to 0.1875
- sub_keys: bfloat16 [2048, 512], P('fsdp'), may hold values from -0.25 to 0.25
- w_gate: bfloat16 [1024, 1024], P('fsdp'), may hold values from -0.1875 to 0.1875
- w_mem_out: bfloat16 [1024, 1024], P('fsdp'), may hold values from -0.1875 to 0.1875
- value_rows: bfloat16 [65536, 1024], P(('dp', 'fsdp')), may hold values from -9 to 9
- request: int32 [2, 32, 32, 16], P(None, ('dp', 'fsdp')), may hold values from -1 to 2047, as said below
- slot_prompt: int32 [8, 1024, 4, 32], P('dp', 'fsdp'), may hold values from 0 to 511, as said below
- slot_cont: int32 [8, 1024, 4, 32], P('dp', 'fsdp'), may hold values from 0 to 511, as said below
Outputs:
- out_prompt: bfloat16 [8, 1024, 1024], P('dp', 'fsdp')
- out_cont: bfloat16 [8, 1024, 1024], P('dp', 'fsdp')
- grad_prompt: float32 [8, 1024, 1024], P('dp', 'fsdp')
- grad_cont: float32 [8, 1024, 1024], P('dp', 'fsdp')
- grad_gain_attn: float32 [1024], P(('dp', 'fsdp'))
- grad_gain_mem: float32 [1024], P(('dp', 'fsdp'))
- grad_qkv: float32 [3, 1024, 1024], P(None, ('dp', 'fsdp'))
- grad_attn_out: float32 [1024, 1024], P(('dp', 'fsdp'))
- grad_mem_query: float32 [1024, 4096], P(('dp', 'fsdp'))
- grad_sub_keys: float32 [2048, 512], P(('dp', 'fsdp'))
- grad_gate: float32 [1024, 1024], P(('dp', 'fsdp'))
- grad_mem_out: float32 [1024, 1024], P(('dp', 'fsdp'))
- grad_values: float32 [65536, 1024], P(('dp', 'fsdp'))
The draws below stay inside these ranges and needn't reach their ends.
Inputs may be any that keep to these rules, and one draw needn't show every extreme that they name: request[u, s, o, j] is an offset into owner o's 2048 value rows, or -1 for an empty slot. In each list the offsets come first, are distinct, and number 1 to 16. In each micro-batch 32 // 4 owners receive a full list from every device. `slot_prompt`: A slot o * 16 + j names entry j of the list from the token's own device to owner o in micro-batch 0; that entry is not -1. Every non-empty entry of a device's lists is named by some pick of that device. `slot_cont`: as slot_prompt, for micro-batch 1.
All inputs are finite; a program needn't handle non-finite values.
Results may differ from the reference program's by a relative error of at most 0.015.
The reference program's roundings to bfloat16 on the way count: a program that leaves them out, or rounds other values in their place, can miss the bound.
Values may be sent and summed in bfloat16 or wider, within the bound.
A program may use at most 192 MiB of HBM per device.

```python
import jax
import jax.numpy as jnp
from jax import lax

D = 1024
HEADS = 16
HDIM = 64
MH = 4
HALF = 512
SUB = 256
PICKS = 32
PL = 1024
CL = 256
MICRO = 2
SLOTS_DEV = 512
VROWS = 65536
GROUPS = 8
CONTS = 4
OWNERS = 32
ROWS_DEV = 2048
PR = 256
N_DP = 8
N_FSDP = 4


def route_tables(key, micro_index):
    base_key = jax.random.fold_in(jax.random.fold_in(key, 7001), micro_index)
    rank_key, light_key, start_key = jax.random.split(base_key, 3)
    capacity = SLOTS_DEV // OWNERS
    ranking = jax.random.permutation(rank_key, OWNERS)
    heavy_owner = ranking < OWNERS // 4
    light_count = jax.random.randint(light_key, (OWNERS, OWNERS), 1, capacity // 2 + 1)
    counts = jnp.where(heavy_owner[None, :], capacity, light_count).astype(jnp.int32)
    counts = counts.at[0, OWNERS - 1].set(capacity)
    starts = jax.random.randint(start_key, (OWNERS, OWNERS, 1), 0, ROWS_DEV)
    places = jnp.arange(capacity, dtype=jnp.int32)[None, None, :]
    offsets = (starts + places * (ROWS_DEV // capacity)) % ROWS_DEV
    asked = jnp.where(places < counts[..., None], offsets, -1).astype(jnp.int32)
    return (counts, asked)


def pick_slots(key, micro_index, tokens_dev):
    counts, asked = route_tables(key, micro_index)
    filled = (asked >= 0).reshape(OWNERS, SLOTS_DEV)
    filled_first = jnp.argsort(jnp.where(filled, 0, 1).astype(jnp.int32), axis=1, stable=True).astype(jnp.int32)
    totals = jnp.sum(counts, axis=1).astype(jnp.int32)[:, None]
    pick_count = tokens_dev * MH * PICKS
    extra_key, shuffle_key = jax.random.split(jax.random.fold_in(jax.random.fold_in(key, 9001), micro_index))
    places = jnp.arange(pick_count, dtype=jnp.int32)[None, :]
    extra_pick = jax.random.randint(extra_key, (OWNERS, pick_count), 0, totals)
    chosen = jnp.where(places < totals, places, extra_pick).astype(jnp.int32)
    noise_keys = jax.random.randint(shuffle_key, (OWNERS, pick_count), 0, 2 ** 31 // pick_count)
    shuffle = jnp.argsort(noise_keys * pick_count + places, axis=1)
    chosen = jnp.take_along_axis(chosen, shuffle, axis=1)
    slot_ids = jnp.take_along_axis(filled_first, chosen, axis=1).astype(jnp.int32)
    return slot_ids.reshape(GROUPS, N_FSDP * tokens_dev, MH, PICKS)


def draw_request(key, part):
    return jnp.stack([route_tables(key, number)[1] for number in range(MICRO)], axis=0)


def draw_slot_prompt(key, part):
    return pick_slots(key, 0, PR)


def draw_slot_cont(key, part):
    return pick_slots(key, 1, CL)


def block_levels(key, shape, shards, low, high):
    def one(position, shards_of):
        draws = jax.random.uniform(jax.random.fold_in(jax.random.fold_in(key, 6), position), (shards_of,), jnp.float32, low / len(shards), high / len(shards))
        return jnp.repeat(jnp.exp(draws), shape[position] // shards_of).reshape((-1,) + (1,) * (len(shape) - position - 1))

    loudness = one(*shards[0])
    for cut in shards[1:]:
        loudness = loudness * one(*cut)
    return loudness


def centred(key, shape, spread, limit, cuts=(), held_as=jnp.bfloat16):
    values = jax.random.normal(key, shape, jnp.float32) * spread
    if len(cuts) > 0:
        values = block_levels(key, shape, cuts, -0.22, 0.18) * values
    return jnp.clip(values, min=-limit, max=limit).astype(held_as)


def setup_inputs(seed: int = 0) -> dict:
    key_list = jax.random.split(jax.random.key(seed), 17)
    return {
        "x_prompt": centred(key_list[0], (GROUPS, PL, D), 1.0, 6.0, ((0, 8), (1, 4))),
        "x_cont": centred(key_list[1], (GROUPS, CONTS * CL, D), 1.0, 6.0, ((0, 8), (1, 4))),
        "cot_prompt": centred(key_list[2], (GROUPS, PL, D), 1.0, 6.0, ((0, 8), (1, 4))),
        "cot_cont": centred(key_list[3], (GROUPS, CONTS * CL, D), 1.0, 6.0, ((0, 8), (1, 4))),
        "gain_attn": jnp.clip(1.0 + 0.15 * jax.random.normal(key_list[4], (D,), jnp.float32), 0.25, 1.75),
        "gain_mem": jnp.clip(1.0 + 0.15 * jax.random.normal(key_list[5], (D,), jnp.float32), 0.25, 1.75),
        "w_qkv": centred(key_list[6], (3, D, D), D ** -0.5, 0.1875, ((1, 4),)),
        "w_attn_out": centred(key_list[7], (D, D), 8 ** -0.5, 2.0, ((0, 4),)),
        "w_mem_query": centred(key_list[8], (D, MH * 2 * HALF), D ** -0.5, 0.1875, ((0, 4),)),
        "sub_keys": centred(key_list[9], (MH * 2 * SUB, HALF), HALF ** -0.5, 0.25, ((0, 4),)),
        "w_gate": centred(key_list[10], (D, D), D ** -0.5, 0.1875, ((0, 4),)),
        "w_mem_out": centred(key_list[11], (D, D), D ** -0.5, 0.1875, ((0, 4),)),
        "value_rows": centred(key_list[12], (VROWS, D), 1.5, 9.0, ((0, 32),)),
        "request": draw_request(jax.random.fold_in(key_list[16], 71), 0),
        "slot_prompt": draw_slot_prompt(jax.random.fold_in(key_list[16], 71), 0),
        "slot_cont": draw_slot_cont(jax.random.fold_in(key_list[16], 71), 0),
    }


highest = lax.Precision.HIGHEST

@jax.custom_vjp
def low(v):
    return lax.optimization_barrier(v.astype(jnp.bfloat16)).astype(jnp.float32)

@jax.custom_vjp
def low_back(v):
    return v

def low_keep(v):
    return (low(v), None)

def low_pass(kept, grad):
    return (grad,)

def back_keep(v):
    return (v, None)

def back_low(kept, grad):
    return (low(grad),)
low.defvjp(low_keep, low_pass)
low_back.defvjp(back_keep, back_low)

def matmul(left, right):
    return jnp.dot(left, right, precision=highest)

def normalize(matrix, gain_vec):
    return matrix * lax.rsqrt(lax.optimization_barrier(jnp.mean(matrix * matrix, axis=-1, keepdims=True)) + 1e-05) * gain_vec

def attend(queries, key_rows, val_rows, visible):
    row_count = queries.shape[0]
    key_count = key_rows.shape[0]
    q_heads = queries.reshape(row_count, HEADS, HDIM)
    k_heads = key_rows.reshape(key_count, HEADS, HDIM)
    v_heads = val_rows.reshape(key_count, HEADS, HDIM)
    scores = low_back(jnp.einsum('qhd,khd->hqk', q_heads, k_heads, precision=highest) * 0.125)
    scores = jnp.where(visible[None], scores, -1e+30)
    weights = low(jax.nn.softmax(scores, axis=-1))
    blended = jnp.einsum('hqk,khd->qhd', weights, v_heads, precision=highest)
    return low_back(low(blended.reshape(row_count, HEADS * HDIM)))

def memory(normed, asked_rows, slot_ids, w_mem_query, sub_keys, w_gate, w_mem_out, value_table):
    row_count = normed.shape[0]
    owners = asked_rows.shape[0]
    capacity = asked_rows.shape[1]
    shard_rows = VROWS // owners
    query_all = low_back(low(matmul(normed, w_mem_query))).reshape(row_count, MH, 2, HALF)
    key_heads = sub_keys.reshape(MH, 2, SUB, HALF)
    sub_scores = low_back(jnp.einsum('rmah,mash->rmas', query_all, key_heads, precision=highest))
    owner_of = slot_ids // capacity
    picked = owner_of * shard_rows + asked_rows[owner_of, slot_ids % capacity]
    first_part = jnp.take_along_axis(sub_scores[:, :, 0], picked // SUB, axis=2)
    second_part = jnp.take_along_axis(sub_scores[:, :, 1], picked % SUB, axis=2)
    pick_weight = jax.nn.softmax(first_part + second_part, axis=-1)
    mixing = jnp.zeros((row_count, owners * capacity), pick_weight.dtype)
    mixing = low(mixing.at[jnp.arange(row_count)[:, None, None], slot_ids].add(pick_weight))
    slot_rows = jnp.arange(owners * capacity) // capacity * shard_rows + jnp.maximum(asked_rows.reshape(-1), 0)
    memory_out = low_back(matmul(mixing, value_table[slot_rows]))
    gate_pre = low_back(matmul(normed, w_gate))
    blended = low(memory_out * jax.nn.silu(gate_pre))
    return low_back(matmul(blended, w_mem_out))

def group_layer(params, value_table, inputs):
    gain_attn, gain_mem, w_qkv, w_attn_out, w_mem_query, sub_keys, w_gate, w_mem_out = params
    x_prompt, x_cont, request_group, slot_prompt, slot_cont = inputs

    def project(tokens):
        normed = low(normalize(tokens, gain_attn))
        return [low_back(low(matmul(normed, w_qkv[number]))) for number in range(3)]
    prompt_q, prompt_k, prompt_v = project(x_prompt)
    cont_q, cont_k, cont_v = project(x_cont)
    prompt_mask = jnp.arange(PL)[:, None] >= jnp.arange(PL)[None, :]
    cont_mask = jnp.concatenate([jnp.ones((CL, PL), jnp.bool_), jnp.arange(CL)[:, None] >= jnp.arange(CL)[None, :]], axis=1)
    prompt_pieces = [attend(prompt_q, prompt_k, prompt_v, prompt_mask)]
    cont_pieces = []
    for number in range(N_FSDP):
        section = slice(number * CL, (number + 1) * CL)
        joined_k = jnp.concatenate([prompt_k, cont_k[section]], axis=0)
        joined_v = jnp.concatenate([prompt_v, cont_v[section]], axis=0)
        cont_pieces.append(attend(cont_q[section], joined_k, joined_v, cont_mask))

    def finish(tokens, pieces, micro_index, slot_ids, block_rows):
        hidden = tokens + low_back(matmul(jnp.concatenate(pieces, axis=0), w_attn_out))
        normed = low(normalize(hidden, gain_mem))
        branches = [memory(normed[number * block_rows:(number + 1) * block_rows], request_group[micro_index, number], slot_ids[number * block_rows:(number + 1) * block_rows], w_mem_query, sub_keys, w_gate, w_mem_out, value_table) for number in range(N_FSDP)]
        return hidden + jnp.concatenate(branches, axis=0)
    return (finish(x_prompt, prompt_pieces, 0, slot_prompt, PL // N_FSDP), finish(x_cont, cont_pieces, 1, slot_cont, CL))

def reference(x_prompt, x_cont, cot_prompt, cot_cont, gain_attn, gain_mem, w_qkv, w_attn_out, w_mem_query, sub_keys, w_gate, w_mem_out, value_rows, request, slot_prompt, slot_cont):
    params = (gain_attn, gain_mem, w_qkv.astype(jnp.float32), w_attn_out.astype(jnp.float32), w_mem_query.astype(jnp.float32), sub_keys.astype(jnp.float32), w_gate.astype(jnp.float32), w_mem_out.astype(jnp.float32))
    requests = jnp.transpose(request.reshape(MICRO, N_DP, N_FSDP, N_DP * N_FSDP, -1), (1, 0, 2, 3, 4))

    def forward(weights, value_table, prompt_in, cont_in):

        def one_group(inputs):
            return group_layer(weights, value_table, inputs)
        return lax.map(jax.checkpoint(one_group), (prompt_in, cont_in, requests, slot_prompt, slot_cont))
    outputs, pullback = jax.vjp(forward, params, value_rows.astype(jnp.float32), x_prompt.astype(jnp.float32), x_cont.astype(jnp.float32))
    grads, grad_values, grad_prompt, grad_cont = pullback((cot_prompt.astype(jnp.float32), cot_cont.astype(jnp.float32)))
    return (outputs[0].astype(jnp.bfloat16), outputs[1].astype(jnp.bfloat16), grad_prompt, grad_cont, grads[0], grads[1], grads[2], grads[3], grads[4], grads[5], grads[6], grads[7], grad_values)
```

```python
import jax
import jax.numpy as jnp
from jax import lax
from jax.sharding import PartitionSpec as P

HEADS = 16
HDIM = 64
MH = 4
HALF = 512
SUB = 256
PL = 1024


BF = jnp.bfloat16
F32 = jnp.float32
ALL = ("dp", "fsdp")


def mm(left, right):
    return jnp.dot(left, right, preferred_element_type=F32)


def mm_t(left, right):
    return lax.dot_general(left, right, (((1,), (1,)), ((), ())), preferred_element_type=F32)


def mm_l(left, right):
    return lax.dot_general(left, right, (((0,), (0,)), ((), ())), preferred_element_type=F32)


def normalize(matrix, gain_vec):
    inverse = lax.rsqrt(jnp.mean(matrix * matrix, axis=-1, keepdims=True) + 1e-05)
    return (matrix * inverse * gain_vec, inverse)


def norm_backward(matrix, inverse, gain_vec, grad_normed):
    scaled = gain_vec * grad_normed
    cubed = inverse * inverse * inverse
    grad_matrix = inverse * scaled - matrix * cubed * jnp.mean(
        matrix * scaled, axis=-1, keepdims=True
    )
    return (grad_matrix, jnp.sum(grad_normed * matrix * inverse, axis=0))


def head_pairs(matrix):
    row_count = matrix.shape[0]
    return matrix.reshape(row_count, HEADS // 2, 2, HDIM).transpose(1, 0, 2, 3)


def merge_pairs(matrix):
    row_count = matrix.shape[1]
    return matrix.transpose(1, 0, 2, 3).reshape(row_count, HEADS * HDIM)


def attend_forward(queries, key_rows, val_rows, visible):

    def one_pair(pieces):
        q_pair, k_pair, v_pair = pieces
        scores = (
            jnp.einsum("qhd,khd->hqk", q_pair, k_pair, preferred_element_type=jnp.float32) * 0.125
        )
        scores = jnp.where(visible[None], scores, -1e30)
        row_max = jnp.max(scores, axis=-1, keepdims=True)
        expo_rows = jnp.exp(scores - row_max)
        row_total = jnp.sum(expo_rows, axis=-1, keepdims=True)
        weights = (expo_rows / row_total).astype(jnp.bfloat16)
        blended = jnp.einsum("hqk,khd->qhd", weights, v_pair, preferred_element_type=jnp.float32)
        return (blended.astype(jnp.bfloat16), (row_max + jnp.log(row_total))[..., 0])

    blended, logsum = lax.map(
        one_pair, (head_pairs(queries), head_pairs(key_rows), head_pairs(val_rows))
    )
    return (merge_pairs(blended), logsum)


def attend_backward(queries, key_rows, val_rows, visible, logsum, grad_out):

    def one_pair(pieces):
        q_pair, k_pair, v_pair, lse_pair, g_pair = pieces
        scores = (
            jnp.einsum("qhd,khd->hqk", q_pair, k_pair, preferred_element_type=jnp.float32) * 0.125
        )
        scores = jnp.where(visible[None], scores, -1e30)
        weights = jnp.exp(scores - lse_pair[..., None])
        grad_weights = jnp.einsum(
            "qhd,khd->hqk", g_pair, v_pair, preferred_element_type=jnp.float32
        )
        row_dot = jnp.sum(weights * grad_weights, axis=-1, keepdims=True)
        grad_scores = (weights * (grad_weights - row_dot)).astype(jnp.bfloat16)
        grad_q = (
            jnp.einsum("hqk,khd->qhd", grad_scores, k_pair, preferred_element_type=jnp.float32)
            * 0.125
        )
        grad_k = (
            jnp.einsum("hqk,qhd->khd", grad_scores, q_pair, preferred_element_type=jnp.float32)
            * 0.125
        )
        grad_v = jnp.einsum(
            "hqk,qhd->khd", weights.astype(jnp.bfloat16), g_pair, preferred_element_type=jnp.float32
        )
        return (grad_q, grad_k, grad_v)

    results = lax.map(
        one_pair,
        (
            head_pairs(queries),
            head_pairs(key_rows),
            head_pairs(val_rows),
            logsum,
            head_pairs(grad_out),
        ),
    )
    return (merge_pairs(results[0]), merge_pairs(results[1]), merge_pairs(results[2]))


def one_hot(ids, count):
    return (ids[:, None] == jnp.arange(count, dtype=jnp.int32)[None, :]).astype(BF)


def split_low(value):
    high = value.astype(BF)
    return (high, (value - high.astype(F32)).astype(BF))


def pick_weights(slot_ids, scores):
    slots = scores.shape[-1]
    count = jnp.sum(
        (slot_ids[..., None] == jnp.arange(slots, dtype=jnp.int32)).astype(F32), axis=2
    )
    named = count > 0.0
    top = jnp.max(jnp.where(named, scores, -jnp.inf), axis=-1, keepdims=True)
    raised = jnp.where(named, count * jnp.exp(scores - top), 0.0)
    return raised / jnp.sum(raised, axis=-1, keepdims=True)


def per_device(
    x_prompt,
    x_cont,
    cot_prompt,
    cot_cont,
    gain_attn,
    gain_mem,
    w_qkv,
    w_attn_out,
    w_mem_query,
    sub_keys,
    w_gate,
    w_mem_out,
    value_rows,
    request,
    slot_prompt,
    slot_cont,
):
    shard_rows, width = value_rows.shape
    owners, capacity = request.shape[2:]
    slots = owners * capacity
    rows = x_prompt.shape[1]
    cols = w_qkv.shape[2]
    asked = lax.all_to_all(request[:, 0], ALL, split_axis=1, concat_axis=1, tiled=True)
    serve_pick = one_hot(asked.transpose(1, 0, 2).reshape(-1), shard_rows)
    served = mm(serve_pick, value_rows).astype(BF).reshape(owners, 2 * capacity, width)
    table = lax.all_to_all(served, ALL, split_axis=0, concat_axis=0, tiled=True)
    table = table.reshape(owners, 2, capacity, width).transpose(1, 0, 2, 3).reshape(2, slots, width)

    qkv_full = lax.all_gather(w_qkv, "fsdp", axis=1, tiled=True)
    attn_out_full = lax.all_gather(w_attn_out, "fsdp", axis=0, tiled=True)
    query_full = lax.all_gather(w_mem_query, "fsdp", axis=0, tiled=True)
    keys_full = lax.all_gather(sub_keys, "fsdp", axis=0, tiled=True)
    gate_full = lax.all_gather(w_gate, "fsdp", axis=0, tiled=True)
    mem_out_full = lax.all_gather(w_mem_out, "fsdp", axis=0, tiled=True)

    x_rows = jnp.concatenate([x_prompt[0], x_cont[0]], axis=0).astype(F32)
    dy_low = jnp.concatenate([cot_prompt[0], cot_cont[0]], axis=0)
    normed, inverse = normalize(x_rows, gain_attn)
    normed = normed.astype(BF)
    queries = mm(normed, qkv_full[0]).astype(BF)
    keys = mm(normed, qkv_full[1]).astype(BF)
    vals = mm(normed, qkv_full[2]).astype(BF)
    all_keys = lax.all_gather(keys[:rows], "fsdp", axis=0, tiled=True)
    all_vals = lax.all_gather(vals[:rows], "fsdp", axis=0, tiled=True)
    start_row = lax.axis_index("fsdp") * rows
    visible_p = jnp.arange(PL)[None, :] <= start_row + jnp.arange(rows)[:, None]
    att_p, logsum_p = attend_forward(queries[:rows], all_keys, all_vals, visible_p)
    key_join = jnp.concatenate([all_keys, keys[rows:]], axis=0)
    val_join = jnp.concatenate([all_vals, vals[rows:]], axis=0)
    visible_c = jnp.concatenate(
        [
            jnp.ones((rows, PL), jnp.bool_),
            jnp.arange(rows)[None, :] <= jnp.arange(rows)[:, None],
        ],
        axis=1,
    )
    att_c, logsum_c = attend_forward(queries[rows:], key_join, val_join, visible_c)
    att = jnp.concatenate([att_p, att_c], axis=0)
    hidden = x_rows + mm(att, attn_out_full)
    normed2, inverse2 = normalize(hidden, gain_mem)
    normed2 = normed2.astype(BF)

    mquery = mm(normed2, query_full).astype(BF)
    gate_pre = mm(normed2, gate_full)
    key_heads = keys_full.reshape(MH, 2, SUB, HALF)
    offsets = jnp.maximum(request[:, 0].reshape(2, slots), 0)
    picked = (jnp.arange(slots, dtype=jnp.int32) // capacity)[None] * shard_rows + offsets
    slot_ids = (slot_prompt[0], slot_cont[0])
    first, second, weights, mixing, memory_out = [], [], [], [], []
    for part in range(2):
        first.append(one_hot(picked[part] // SUB, SUB))
        second.append(one_hot(picked[part] % SUB, SUB))
        section = slice(part * rows, (part + 1) * rows)
        heads = []
        for head in range(MH):
            slot_keys = jnp.concatenate(
                [
                    mm(first[part], key_heads[head, 0]).astype(BF),
                    mm(second[part], key_heads[head, 1]).astype(BF),
                ],
                axis=1,
            )
            span = slice(head * 2 * HALF, (head + 1) * 2 * HALF)
            heads.append(mm_t(mquery[section, span], slot_keys))
        weights.append(pick_weights(slot_ids[part], jnp.stack(heads, axis=1)))
        mixing.append(jnp.sum(weights[part], axis=1).astype(BF))
        memory_out.append(mm(mixing[part], table[part]))
    memory_out = jnp.concatenate(memory_out, axis=0)
    sigmoid_gate = jax.nn.sigmoid(gate_pre)
    blended = (memory_out * (gate_pre * sigmoid_gate)).astype(BF)
    out = (hidden + mm(blended, mem_out_full)).astype(BF)

    grad_blend = mm_t(dy_low, mem_out_full)
    grad_mem_out = mm_l(blended, dy_low)
    grad_memory = (grad_blend * gate_pre * sigmoid_gate).astype(BF)
    grad_gate = (
        grad_blend * memory_out * sigmoid_gate * (1.0 + gate_pre * (1.0 - sigmoid_gate))
    ).astype(BF)
    slot_grads, grad_query, sub_grads = [], [], []
    for part in range(2):
        section = slice(part * rows, (part + 1) * rows)
        slot_grads.append(mm_l(mixing[part], grad_memory[section]).astype(BF))
        grad_mixing = mm_t(grad_memory[section], table[part])[:, None, :]
        pulled = weights[part] * grad_mixing
        grad_scores = pulled - weights[part] * jnp.sum(pulled, axis=-1, keepdims=True)
        high, low = split_low(grad_scores.reshape(rows * MH, slots))
        halves = [
            (mm(high, picker) + mm(low, picker)).astype(BF).reshape(rows, MH, SUB)
            for picker in (first[part], second[part])
        ]
        sub_grads.append(jnp.stack(halves, axis=2))
    sub_grads = jnp.concatenate(sub_grads, axis=0)
    grad_query = jnp.concatenate(
        [
            mm(sub_grads[:, head, half], key_heads[head, half]).astype(BF)
            for head in range(MH)
            for half in range(2)
        ],
        axis=1,
    )
    grad_keys = jnp.concatenate(
        [
            mm_l(
                sub_grads[:, head, half],
                mquery[:, (2 * head + half) * HALF : (2 * head + half + 1) * HALF],
            )
            for head in range(MH)
            for half in range(2)
        ],
        axis=0,
    )
    arrived = lax.all_to_all(
        jnp.stack([piece.reshape(owners, capacity, width) for piece in slot_grads], axis=1),
        ALL,
        split_axis=0,
        concat_axis=0,
        tiled=True,
    )
    grad_rows = mm_l(serve_pick, arrived.reshape(owners * 2 * capacity, width))
    grad_normed2 = mm_t(grad_query, query_full) + mm_t(grad_gate, gate_full)
    grad_query_w = mm_l(normed2, grad_query)
    grad_gate_w = mm_l(normed2, grad_gate)
    back, gain_mem_part = norm_backward(hidden, inverse2, gain_mem, grad_normed2)
    grad_hidden = dy_low.astype(F32) + back
    hidden_low = grad_hidden.astype(BF)
    grad_attn_out = mm_l(att, hidden_low)
    grad_att = mm_t(hidden_low, attn_out_full).astype(BF)
    grad_q_p, grad_k_p, grad_v_p = attend_backward(
        queries[:rows], all_keys, all_vals, visible_p, logsum_p, grad_att[:rows]
    )
    grad_q_c, grad_k_c, grad_v_c = attend_backward(
        queries[rows:], key_join, val_join, visible_c, logsum_c, grad_att[rows:]
    )
    own_keys = lax.psum_scatter(
        (grad_k_c[:PL] + grad_k_p).astype(BF), "fsdp", scatter_dimension=0, tiled=True
    )
    own_vals = lax.psum_scatter(
        (grad_v_c[:PL] + grad_v_p).astype(BF), "fsdp", scatter_dimension=0, tiled=True
    )
    grad_q = jnp.concatenate([grad_q_p, grad_q_c], axis=0).astype(BF)
    grad_k = jnp.concatenate([own_keys, grad_k_c[PL:].astype(BF)], axis=0)
    grad_v = jnp.concatenate([own_vals, grad_v_c[PL:].astype(BF)], axis=0)
    grad_normed = (
        mm_t(grad_q, qkv_full[0]) + mm_t(grad_k, qkv_full[1]) + mm_t(grad_v, qkv_full[2])
    )
    grad_x, gain_attn_part = norm_backward(x_rows, inverse, gain_attn, grad_normed)
    grad_x = grad_hidden + grad_x
    grad_qkv = jnp.stack([mm_l(normed, piece) for piece in (grad_q, grad_k, grad_v)])

    def scatter(value, axis):
        return lax.psum_scatter(value, ALL, scatter_dimension=axis, tiled=True)

    return (
        out[None, :rows],
        out[None, rows:],
        grad_x[None, :rows],
        grad_x[None, rows:],
        scatter(gain_attn_part, 0),
        scatter(gain_mem_part, 0),
        scatter(grad_qkv.astype(BF), 1).astype(F32),
        scatter(grad_attn_out.astype(BF), 0).astype(F32),
        scatter(grad_query_w.astype(BF), 0).astype(F32),
        scatter(grad_keys.astype(BF), 0).astype(F32),
        scatter(grad_gate_w.astype(BF), 0).astype(F32),
        scatter(grad_mem_out.astype(BF), 0).astype(F32),
        grad_rows,
    )


def solution(mesh):
    in_specs = (
        P("dp", "fsdp", None),
        P("dp", "fsdp", None),
        P("dp", "fsdp", None),
        P("dp", "fsdp", None),
        P(),
        P(),
        P(None, "fsdp", None),
        P("fsdp", None),
        P("fsdp", None),
        P("fsdp", None),
        P("fsdp", None),
        P("fsdp", None),
        P(("dp", "fsdp"), None),
        P(None, ("dp", "fsdp"), None, None),
        P("dp", "fsdp", None, None),
        P("dp", "fsdp", None, None),
    )
    out_specs = (
        P("dp", "fsdp", None),
        P("dp", "fsdp", None),
        P("dp", "fsdp", None),
        P("dp", "fsdp", None),
        P(("dp", "fsdp")),
        P(("dp", "fsdp")),
        P(None, ("dp", "fsdp"), None),
        P(("dp", "fsdp"), None),
        P(("dp", "fsdp"), None),
        P(("dp", "fsdp"), None),
        P(("dp", "fsdp"), None),
        P(("dp", "fsdp"), None),
        P(("dp", "fsdp"), None),
    )
    return jax.shard_map(
        per_device, mesh=mesh, in_specs=in_specs, out_specs=out_specs, check_vma=False
    )
```

```python
import functools
import jax
import jax.numpy as jnp
from jax import lax
from jax.experimental import pallas as pl
from jax.experimental.pallas import tpu as pltpu
from jax.sharding import PartitionSpec as P
BF = jnp.bfloat16
F32 = jnp.float32
ALL = ("dp", "fsdp")
MESH = pl.DeviceIdType.MESH
LAG = 2
GATHER_LAG = 2
PIECE = 1024
HEADS = 16
HDIM = 64
MH = 4
HALF = 512
SUB = 256
PL = 1024


def mm(left, right):
    return jnp.dot(left, right, preferred_element_type=F32)


def mm_t(left, right):
    return lax.dot_general(left, right, (((1,), (1,)), ((), ())), preferred_element_type=F32)


def mm_l(left, right):
    return lax.dot_general(left, right, (((0,), (0,)), ((), ())), preferred_element_type=F32)


def normalize(matrix, gain_vec):
    inverse = lax.rsqrt(jnp.mean(matrix * matrix, axis=-1, keepdims=True) + 1e-05)
    return (matrix * inverse * gain_vec, inverse)


def norm_backward(matrix, inverse, gain_vec, grad_normed):
    scaled = gain_vec * grad_normed
    cubed = inverse * inverse * inverse
    grad_matrix = inverse * scaled - matrix * cubed * jnp.mean(
        matrix * scaled, axis=-1, keepdims=True
    )
    return (grad_matrix, jnp.sum(grad_normed * matrix * inverse, axis=0))


def grid_of(plane, depth):
    side = 1
    while 2 * side * side < plane:
        side += 1
    return side, depth


def place(side):
    dp = lax.axis_index("dp")
    return (dp // (2 * side), (dp // 2) % side, dp % 2, lax.axis_index("fsdp"))


def device_at(side, y, x, core, z):
    return ((y * side + x) * 2 + core, z)


def greet(side, depth):
    y, x, core, z = place(side)
    barrier = pltpu.get_barrier_semaphore()
    peers = [device_at(side, y, x, 1 - core, z)]
    for hop in range(1, side):
        peers.append(device_at(side, y, (x + hop) % side, core, z))
        peers.append(device_at(side, (y + hop) % side, x, core, z))
    for hop in range(1, depth):
        peers.append(device_at(side, y, x, core, (z + hop) % depth))
    for peer in peers:
        pl.semaphore_signal(barrier, inc=1, device_id=peer, device_id_type=MESH)
    pl.semaphore_wait(barrier, len(peers))


def remote(source, target, send_sem, recv_sem, peer):
    return pltpu.make_async_remote_copy(
        src_ref=source,
        dst_ref=target,
        send_sem=send_sem,
        recv_sem=recv_sem,
        device_id=peer,
        device_id_type=MESH,
    )


def reduce_kernel(side, depth, layout, *refs):
    count = sum(len(columns) for columns in layout)
    n_in = len(layout)
    sources = refs[:n_in]
    gains = refs[n_in]
    outs = refs[n_in + 1 : 2 * n_in + 1]
    gains_out = refs[2 * n_in + 1]
    (mine, got_core, got_one, got_two, got_deep, total, gain_sum, gain_got, local_sem, core_send,
     core_recv, one_send, one_recv, two_send, two_recv, deep_send, deep_recv, gain_send,
     gain_recv) = refs[2 * n_in + 2 :]
    y, x, core, z = place(side)
    block = total.shape[1:]
    pieces = []
    for number, columns in enumerate(layout):
        for lead, start in columns:
            def cut(half, number=number, lead=lead, start=start):
                ref = sources[number] if lead is None else sources[number].at[lead]
                return ref.at[:, :, half, :, :, pl.ds(start, block[1])]
            pieces.append((cut, number, lead, start))
    greet(side, depth)
    partner = device_at(side, y, x, 1 - core, z)
    for k, piece in enumerate(pieces):
        remote(piece[0](1 - core), got_core.at[k], core_send.at[k], core_recv.at[k], partner).start()
        pltpu.make_async_copy(piece[0](core), mine.at[k], local_sem.at[k]).start()

    def one_copy(k, hop, x_first):
        peer = device_at(side, y, (x + hop) % side, core, z) if x_first else device_at(
            side, (y + hop) % side, x, core, z)
        source = mine.at[k, :, (x + hop) % side] if x_first else mine.at[k, (y + hop) % side]
        return remote(source, got_one.at[k, hop - 1], one_send.at[k, hop - 1],
                      one_recv.at[k, hop - 1], peer)

    def two_copy(k, hop, x_first):
        peer = device_at(side, (y + hop) % side, x, core, z) if x_first else device_at(
            side, y, (x + hop) % side, core, z)
        source = mine.at[k, (y + hop) % side, x] if x_first else mine.at[k, y, (x + hop) % side]
        return remote(source, got_two.at[k, hop - 1], two_send.at[k, hop - 1],
                      two_recv.at[k, hop - 1], peer)

    def deep_copy(k, hop):
        there = (z + hop) % depth
        return remote(mine.at[k, y, x, there], got_deep.at[k, hop - 1], deep_send.at[k, hop - 1],
                      deep_recv.at[k, hop - 1], device_at(side, y, x, core, there))

    def both_orders(k, action):
        @pl.when(k % 2 == 0)
        def _():
            action(True)

        @pl.when(k % 2 == 1)
        def _():
            action(False)

    def added(base, others):
        if len(others) == 1:
            return base + others[0]
        value = base.astype(F32)
        for other in others:
            value = value + other.astype(F32)
        return value.astype(base.dtype)

    def after_core(k):
        remote(got_core.at[k], got_core.at[k], core_send.at[k], core_recv.at[k], partner).wait_recv()
        pltpu.make_async_copy(got_core.at[k], mine.at[k], local_sem.at[k]).wait()

        def add(index, carry):
            a, b, c = index // (side * depth), (index // depth) % side, index % depth
            mine[k, a, b, c] = mine[k, a, b, c] + got_core[k, a, b, c]
            return carry

        lax.fori_loop(0, side * side * depth, add, 0)

        def send(x_first):
            for hop in range(1, side):
                one_copy(k, hop, x_first).start()

        both_orders(k, send)

    def after_one(k):
        def finish(x_first):
            for hop in range(1, side):
                one_copy(k, hop, x_first).wait_recv()

            def add(index, carry):
                a, c = index // depth, index % depth
                spot = (k, a, x, c) if x_first else (k, y, a, c)
                mine[spot] = added(mine[spot], [got_one[k, hop, a, c] for hop in range(side - 1)])
                return carry

            lax.fori_loop(0, side * depth, add, 0)
            for hop in range(1, side):
                two_copy(k, hop, x_first).start()

        both_orders(k, finish)

    def after_two(k):
        def finish(x_first):
            for hop in range(1, side):
                two_copy(k, hop, x_first).wait_recv()

        both_orders(k, finish)

        def add(c, carry):
            mine[k, y, x, c] = added(mine[k, y, x, c], [got_two[k, hop, c] for hop in range(side - 1)])
            return carry

        lax.fori_loop(0, depth, add, 0)
        for hop in range(1, depth):
            deep_copy(k, hop).start()

    def after_deep(k):
        for hop in range(1, depth):
            deep_copy(k, hop).wait_recv()
        value = mine[k, y, x, z].astype(F32)
        for hop in range(depth - 1):
            value = value + got_deep[k, hop].astype(F32)
        total[k] = value

    gain_peers = [
        [partner],
        [device_at(side, y, (x + hop) % side, core, z) for hop in range(1, side)],
        [device_at(side, (y + hop) % side, x, core, z) for hop in range(1, side)],
        [device_at(side, y, x, core, (z + hop) % depth) for hop in range(1, depth)],
    ]

    def gain_copy(stage, number):
        source = gains if stage == 0 else gain_sum.at[stage - 1]
        return remote(source, gain_got.at[stage, number], gain_send.at[stage, number],
                      gain_recv.at[stage, number], gain_peers[stage][number])

    for number in range(len(gain_peers[0])):
        gain_copy(0, number).start()

    def run(i, carry):
        for lag, action in ((0, after_core), (LAG, after_one), (2 * LAG, after_two), (3 * LAG, after_deep)):
            @pl.when(jnp.logical_and(i >= lag, i < count + lag))
            def _(lag=lag, action=action):
                action(i - lag)

        for stage in range(4):
            @pl.when(i == stage + 1)
            def _(stage=stage):
                value = gains[...] if stage == 0 else gain_sum[stage - 1]
                for number in range(len(gain_peers[stage])):
                    gain_copy(stage, number).wait_recv()
                    value = value + gain_got[stage, number]
                gain_sum[stage] = value
                if stage < 3:
                    for number in range(len(gain_peers[stage + 1])):
                        gain_copy(stage + 1, number).start()

        return carry

    lax.fori_loop(0, count + 3 * LAG, run, 0)
    gains_out[...] = gain_sum[3]
    for k, (cut, number, lead, start) in enumerate(pieces):
        spot = (slice(None), pl.ds(start, block[1]))
        if lead is None:
            outs[number][spot] = total[k]
        else:
            outs[number][(lead,) + spot] = total[k]

    def drain(k, carry):
        remote(got_core.at[k], got_core.at[k], core_send.at[k], core_recv.at[k], partner).wait_send()

        def finish(x_first):
            for hop in range(1, side):
                one_copy(k, hop, x_first).wait_send()
                two_copy(k, hop, x_first).wait_send()

        both_orders(k, finish)
        for hop in range(1, depth):
            deep_copy(k, hop).wait_send()
        return carry

    lax.fori_loop(0, count, drain, 0)
    for stage in range(4):
        for number in range(len(gain_peers[stage])):
            gain_copy(stage, number).wait_send()


def reduce_grads(side, depth, grads, gains, call_id):
    devices = 2 * side * side * depth
    layout, views, outs = [], [], []
    width = 1024
    for grad in grads:
        rows, cols = grad.shape[-2:]
        block = rows // devices
        lead = grad.shape[:-2]
        views.append(grad.reshape(lead + (side, side, 2, depth, block, cols)))
        leads = range(lead[0]) if lead else (None,)
        layout.append([(number, start) for number in leads for start in range(0, cols, width)])
        outs.append(jax.ShapeDtypeStruct(lead + (block, cols), F32))
    count = sum(len(columns) for columns in layout)
    most = max(side, depth) - 1
    dma = pltpu.SemaphoreType.DMA
    return pl.pallas_call(
        functools.partial(reduce_kernel, side, depth, layout),
        out_shape=tuple(outs) + (jax.ShapeDtypeStruct(gains.shape, F32),),
        in_specs=[pl.BlockSpec(memory_space=pl.ANY)] * len(views)
        + [pl.BlockSpec(memory_space=pltpu.VMEM)],
        out_specs=(pl.BlockSpec(memory_space=pltpu.VMEM),) * (len(views) + 1),
        scratch_shapes=[
            pltpu.VMEM((count, side, side, depth, block, width), BF),
            pltpu.VMEM((count, side, side, depth, block, width), BF),
            pltpu.VMEM((count, side - 1, side, depth, block, width), BF),
            pltpu.VMEM((count, side - 1, depth, block, width), BF),
            pltpu.VMEM((count, depth - 1, block, width), BF),
            pltpu.VMEM((count, block, width), F32),
            pltpu.VMEM((4,) + gains.shape, F32),
            pltpu.VMEM((4, most) + gains.shape, F32),
            dma((count,)),
            dma((count,)),
            dma((count,)),
            dma((count, side - 1)),
            dma((count, side - 1)),
            dma((count, side - 1)),
            dma((count, side - 1)),
            dma((count, depth - 1)),
            dma((count, depth - 1)),
            dma((4, most)),
            dma((4, most)),
        ],
        compiler_params=pltpu.CompilerParams(
            collective_id=call_id, has_side_effects=True, vmem_limit_bytes=60 * 1024 * 1024
        ),
    )(*views, gains)


def gather_kernel(side, depth, layout, *refs):
    n_in = len(layout)
    sources, outs = refs[:n_in], refs[n_in : 2 * n_in]
    held = refs[2 * n_in : 3 * n_in]
    (in_sem, out_sem, right_send, left_send, deep_recv, one_send, one_recv, two_send, two_recv,
     core_send, core_recv) = refs[3 * n_in :]
    y, x, core, z = place(side)
    pieces = []
    for number, columns in enumerate(layout):
        for place_in, (lead, start) in enumerate(columns):
            width = held[number].shape[-1]
            width = width if sources[number].shape[-1] > width else None
            pieces.append((number, lead, start, width, place_in))
    count = len(pieces)

    def cut(refs, k, *spot):
        number, lead, start, width = pieces[k][:4]
        ref = refs[number] if lead is None else refs[number].at[lead]
        ref = ref.at[spot] if spot else ref
        if width is None:
            return ref
        return ref.at[(slice(None),) * (len(ref.shape) - 1) + (pl.ds(start, width),)]

    greet(side, depth)
    partner = device_at(side, y, x, 1 - core, z)

    def to_right(k, zp):
        return remote(cut(outs, k, zp, y, x, core), cut(outs, k, zp, y, x, core),
                      right_send.at[k, zp], deep_recv.at[k, zp],
                      device_at(side, y, x, core, z + 1))

    def to_left(k, zp):
        return remote(cut(outs, k, zp, y, x, core), cut(outs, k, zp, y, x, core),
                      left_send.at[k, zp], deep_recv.at[k, zp],
                      device_at(side, y, x, core, z - 1))

    def one_copy(k, zp, hop):
        x_first = k % 2 == 0
        peer = device_at(side, y, (x + hop) % side, core, z) if x_first else device_at(
            side, (y + hop) % side, x, core, z)
        ref = cut(outs, k, zp, y, x, core)
        return remote(ref, ref, one_send.at[k, zp, hop - 1], one_recv.at[k, zp, hop - 1], peer)

    def two_copy(k, zp, hop):
        x_first = k % 2 == 0
        peer = device_at(side, (y + hop) % side, x, core, z) if x_first else device_at(
            side, y, (x + hop) % side, core, z)
        ref = (cut(outs, k, zp, y, slice(None), core) if x_first
               else cut(outs, k, zp, slice(None), x, core))
        return remote(ref, ref, two_send.at[k, zp, hop - 1], two_recv.at[k, zp, hop - 1], peer)

    def core_copy(k, zp):
        ref = cut(outs, k, zp, slice(None), slice(None), core)
        return remote(ref, ref, core_send.at[k, zp], core_recv.at[k, zp], partner)

    def holder(k):
        return held[pieces[k][0]].at[pieces[k][4]]

    def take(k):
        return pltpu.make_async_copy(cut(sources, k), holder(k), in_sem.at[k])

    def put(k):
        return pltpu.make_async_copy(holder(k), cut(outs, k, z), out_sem.at[k])

    for k in range(count):
        take(k).start()

        @pl.when(z < depth - 1)
        def _():
            remote(cut(sources, k, y, x, core), cut(outs, k, z, y, x, core), right_send.at[k, z],
                   deep_recv.at[k, z], device_at(side, y, x, core, z + 1)).start()

        @pl.when(z > 0)
        def _():
            remote(cut(sources, k, y, x, core), cut(outs, k, z, y, x, core), left_send.at[k, z],
                   deep_recv.at[k, z], device_at(side, y, x, core, z - 1)).start()

    def arrivals(first):
        for distance in range(1, depth):
            for sign in (1, -1):
                yield first + distance - 1, sign, distance

    for i in range(count + depth - 2 + 3 * GATHER_LAG):
        if i < count:
            take(i).wait()
            put(i).start()
        for stage in range(4):
            for lag, sign, distance in arrivals(stage * GATHER_LAG):
                k = i - lag
                if not 0 <= k < count:
                    continue
                zp = z + sign * distance

                @pl.when(jnp.logical_and(zp >= 0, zp < depth))
                def _(k=k, zp=zp, sign=sign, stage=stage):
                    if stage == 0:
                        to_right(k, zp).wait_recv()
                        if sign < 0:
                            @pl.when(z < depth - 1)
                            def _():
                                to_right(k, zp).start()
                        else:
                            @pl.when(z > 0)
                            def _():
                                to_left(k, zp).start()
                        for hop in range(1, side):
                            one_copy(k, zp, hop).start()
                    elif stage == 1:
                        for hop in range(1, side):
                            one_copy(k, zp, hop).wait_recv()
                        for hop in range(1, side):
                            two_copy(k, zp, hop).start()
                    elif stage == 2:
                        for hop in range(1, side):
                            two_copy(k, zp, hop).wait_recv()
                        core_copy(k, zp).start()
                    else:
                        core_copy(k, zp).wait_recv()

    for k in range(count):
        put(k).wait()

        @pl.when(z < depth - 1)
        def _(k=k):
            to_right(k, z).wait_send()

        @pl.when(z > 0)
        def _(k=k):
            to_left(k, z).wait_send()

        for zp in range(depth):
            @pl.when(zp != z)
            def _(k=k, zp=zp):
                @pl.when(jnp.logical_and(zp < z, z < depth - 1))
                def _():
                    to_right(k, zp).wait_send()

                @pl.when(jnp.logical_and(zp > z, z > 0))
                def _():
                    to_left(k, zp).wait_send()

                for hop in range(1, side):
                    one_copy(k, zp, hop).wait_send()
                    two_copy(k, zp, hop).wait_send()
                core_copy(k, zp).wait_send()


def gather_weights(side, depth, shards, call_id):
    plane = 2 * side * side
    layout, views, outs, shapes, held = [], [], [], [], []
    for shard in shards:
        rows, cols = shard.shape[-2:]
        block, width = rows // plane, min(cols, PIECE)
        lead = shard.shape[:-2]
        views.append(shard.reshape(lead + (side, side, 2, block, cols)))
        leads = range(lead[0]) if lead else (None,)
        layout.append([(number, start) for number in leads for start in range(0, cols, width)])
        outs.append(jax.ShapeDtypeStruct(lead + (depth, side, side, 2, block, cols), BF))
        shapes.append(lead + (depth * rows, cols))
        held.append(pltpu.VMEM((len(layout[-1]), side, side, 2, block, width), BF))
    count = sum(len(columns) for columns in layout)
    dma = pltpu.SemaphoreType.DMA
    full = pl.pallas_call(
        functools.partial(gather_kernel, side, depth, layout),
        out_shape=tuple(outs),
        in_specs=[pl.BlockSpec(memory_space=pl.ANY)] * len(views),
        out_specs=(pl.BlockSpec(memory_space=pl.ANY),) * len(views),
        scratch_shapes=held
        + [
            dma((count,)),
            dma((count,)),
            dma((count, depth)),
            dma((count, depth)),
            dma((count, depth)),
            dma((count, depth, side - 1)),
            dma((count, depth, side - 1)),
            dma((count, depth, side - 1)),
            dma((count, depth, side - 1)),
            dma((count, depth)),
            dma((count, depth)),
        ],
        compiler_params=pltpu.CompilerParams(
            collective_id=call_id, has_side_effects=True, vmem_limit_bytes=32 * 1024 * 1024
        ),
    )(*views)
    return [one.reshape(shape) for one, shape in zip(full, shapes)]


def head_pairs(matrix):
    row_count = matrix.shape[0]
    return matrix.reshape(row_count, HEADS // 2, 2, HDIM).transpose(1, 0, 2, 3)


def merge_pairs(matrix):
    row_count = matrix.shape[1]
    return matrix.transpose(1, 0, 2, 3).reshape(row_count, HEADS * HDIM)


def attend_forward(queries, key_rows, val_rows, visible):

    def one_pair(pieces):
        q_pair, k_pair, v_pair = pieces
        scores = (
            jnp.einsum("qhd,khd->hqk", q_pair, k_pair, preferred_element_type=jnp.float32) * 0.125
        )
        scores = jnp.where(visible[None], scores, -1e30)
        row_max = jnp.max(scores, axis=-1, keepdims=True)
        expo_rows = jnp.exp(scores - row_max)
        row_total = jnp.sum(expo_rows, axis=-1, keepdims=True)
        weights = (expo_rows / row_total).astype(jnp.bfloat16)
        blended = jnp.einsum("hqk,khd->qhd", weights, v_pair, preferred_element_type=jnp.float32)
        return (blended.astype(jnp.bfloat16), (row_max + jnp.log(row_total))[..., 0])

    blended, logsum = lax.map(
        one_pair, (head_pairs(queries), head_pairs(key_rows), head_pairs(val_rows))
    )
    return (merge_pairs(blended), logsum)


def attend_backward(queries, key_rows, val_rows, visible, logsum, grad_out):

    def one_pair(pieces):
        q_pair, k_pair, v_pair, lse_pair, g_pair = pieces
        scores = (
            jnp.einsum("qhd,khd->hqk", q_pair, k_pair, preferred_element_type=jnp.float32) * 0.125
        )
        scores = jnp.where(visible[None], scores, -1e30)
        weights = jnp.exp(scores - lse_pair[..., None])
        grad_weights = jnp.einsum(
            "qhd,khd->hqk", g_pair, v_pair, preferred_element_type=jnp.float32
        )
        row_dot = jnp.sum(weights * grad_weights, axis=-1, keepdims=True)
        grad_scores = (weights * (grad_weights - row_dot)).astype(jnp.bfloat16)
        grad_q = (
            jnp.einsum("hqk,khd->qhd", grad_scores, k_pair, preferred_element_type=jnp.float32)
            * 0.125
        )
        grad_k = (
            jnp.einsum("hqk,qhd->khd", grad_scores, q_pair, preferred_element_type=jnp.float32)
            * 0.125
        )
        grad_v = jnp.einsum(
            "hqk,qhd->khd", weights.astype(jnp.bfloat16), g_pair, preferred_element_type=jnp.float32
        )
        return (grad_q, grad_k, grad_v)

    results = lax.map(
        one_pair,
        (
            head_pairs(queries),
            head_pairs(key_rows),
            head_pairs(val_rows),
            logsum,
            head_pairs(grad_out),
        ),
    )
    return (merge_pairs(results[0]), merge_pairs(results[1]), merge_pairs(results[2]))


def one_hot(ids, count):
    return (ids[:, None] == jnp.arange(count, dtype=jnp.int32)[None, :]).astype(BF)


def split_low(value):
    high = value.astype(BF)
    return (high, (value - high.astype(F32)).astype(BF))


def pick_weights(slot_ids, scores):
    slots = scores.shape[-1]
    count = jnp.sum(
        (slot_ids[..., None] == jnp.arange(slots, dtype=jnp.int32)).astype(F32), axis=2
    )
    named = count > 0.0
    top = jnp.max(jnp.where(named, scores, -jnp.inf), axis=-1, keepdims=True)
    raised = jnp.where(named, count * jnp.exp(scores - top), 0.0)
    return raised / jnp.sum(raised, axis=-1, keepdims=True)


def per_device(
    x_prompt,
    x_cont,
    cot_prompt,
    cot_cont,
    gain_attn,
    gain_mem,
    w_qkv,
    w_attn_out,
    w_mem_query,
    sub_keys,
    w_gate,
    w_mem_out,
    value_rows,
    request,
    slot_prompt,
    slot_cont,
):
    shard_rows, width = value_rows.shape
    owners, capacity = request.shape[2:]
    slots = owners * capacity
    rows = x_prompt.shape[1]
    cols = w_qkv.shape[2]
    asked = lax.all_to_all(request[:, 0], ALL, split_axis=1, concat_axis=1, tiled=True)
    serve_pick = one_hot(asked.transpose(1, 0, 2).reshape(-1), shard_rows)
    served = mm(serve_pick, value_rows).astype(BF).reshape(owners, 2 * capacity, width)
    table = lax.all_to_all(served, ALL, split_axis=0, concat_axis=0, tiled=True)
    table = table.reshape(owners, 2, capacity, width).transpose(1, 0, 2, 3).reshape(2, slots, width)

    side, depth = grid_of(lax.axis_size("dp"), lax.axis_size("fsdp"))
    qkv_full, attn_out_full, query_full, keys_full, gate_full, mem_out_full = gather_weights(
        side,
        depth,
        (w_qkv, w_attn_out, w_mem_query, sub_keys, w_gate, w_mem_out),
        0,
    )

    x_rows = jnp.concatenate([x_prompt[0], x_cont[0]], axis=0).astype(F32)
    dy_low = jnp.concatenate([cot_prompt[0], cot_cont[0]], axis=0)
    normed, inverse = normalize(x_rows, gain_attn)
    normed = normed.astype(BF)
    queries = mm(normed, qkv_full[0]).astype(BF)
    keys = mm(normed, qkv_full[1]).astype(BF)
    vals = mm(normed, qkv_full[2]).astype(BF)
    all_keys = lax.all_gather(keys[:rows], "fsdp", axis=0, tiled=True)
    all_vals = lax.all_gather(vals[:rows], "fsdp", axis=0, tiled=True)
    start_row = lax.axis_index("fsdp") * rows
    visible_p = jnp.arange(PL)[None, :] <= start_row + jnp.arange(rows)[:, None]
    att_p, logsum_p = attend_forward(queries[:rows], all_keys, all_vals, visible_p)
    key_join = jnp.concatenate([all_keys, keys[rows:]], axis=0)
    val_join = jnp.concatenate([all_vals, vals[rows:]], axis=0)
    visible_c = jnp.concatenate(
        [
            jnp.ones((rows, PL), jnp.bool_),
            jnp.arange(rows)[None, :] <= jnp.arange(rows)[:, None],
        ],
        axis=1,
    )
    att_c, logsum_c = attend_forward(queries[rows:], key_join, val_join, visible_c)
    att = jnp.concatenate([att_p, att_c], axis=0)
    hidden = x_rows + mm(att, attn_out_full)
    normed2, inverse2 = normalize(hidden, gain_mem)
    normed2 = normed2.astype(BF)

    mquery = mm(normed2, query_full).astype(BF)
    gate_pre = mm(normed2, gate_full)
    key_heads = keys_full.reshape(MH, 2, SUB, HALF)
    offsets = jnp.maximum(request[:, 0].reshape(2, slots), 0)
    picked = (jnp.arange(slots, dtype=jnp.int32) // capacity)[None] * shard_rows + offsets
    slot_ids = (slot_prompt[0], slot_cont[0])
    first, second, weights, mixing, memory_out = [], [], [], [], []
    for part in range(2):
        first.append(one_hot(picked[part] // SUB, SUB))
        second.append(one_hot(picked[part] % SUB, SUB))
        section = slice(part * rows, (part + 1) * rows)
        heads = []
        for head in range(MH):
            slot_keys = jnp.concatenate(
                [
                    mm(first[part], key_heads[head, 0]).astype(BF),
                    mm(second[part], key_heads[head, 1]).astype(BF),
                ],
                axis=1,
            )
            span = slice(head * 2 * HALF, (head + 1) * 2 * HALF)
            heads.append(mm_t(mquery[section, span], slot_keys))
        weights.append(pick_weights(slot_ids[part], jnp.stack(heads, axis=1)))
        mixing.append(jnp.sum(weights[part], axis=1).astype(BF))
        memory_out.append(mm(mixing[part], table[part]))
    memory_out = jnp.concatenate(memory_out, axis=0)
    sigmoid_gate = jax.nn.sigmoid(gate_pre)
    blended = (memory_out * (gate_pre * sigmoid_gate)).astype(BF)
    out = (hidden + mm(blended, mem_out_full)).astype(BF)

    grad_blend = mm_t(dy_low, mem_out_full)
    grad_mem_out = mm_l(blended, dy_low)
    grad_memory = (grad_blend * gate_pre * sigmoid_gate).astype(BF)
    grad_gate = (
        grad_blend * memory_out * sigmoid_gate * (1.0 + gate_pre * (1.0 - sigmoid_gate))
    ).astype(BF)
    slot_grads, grad_query, sub_grads = [], [], []
    for part in range(2):
        section = slice(part * rows, (part + 1) * rows)
        slot_grads.append(mm_l(mixing[part], grad_memory[section]).astype(BF))
        grad_mixing = mm_t(grad_memory[section], table[part])[:, None, :]
        pulled = weights[part] * grad_mixing
        grad_scores = pulled - weights[part] * jnp.sum(pulled, axis=-1, keepdims=True)
        high, low = split_low(grad_scores.reshape(rows * MH, slots))
        halves = [
            (mm(high, picker) + mm(low, picker)).astype(BF).reshape(rows, MH, SUB)
            for picker in (first[part], second[part])
        ]
        sub_grads.append(jnp.stack(halves, axis=2))
    sub_grads = jnp.concatenate(sub_grads, axis=0)
    grad_query = jnp.concatenate(
        [
            mm(sub_grads[:, head, half], key_heads[head, half]).astype(BF)
            for head in range(MH)
            for half in range(2)
        ],
        axis=1,
    )
    grad_keys = jnp.concatenate(
        [
            mm_l(
                sub_grads[:, head, half],
                mquery[:, (2 * head + half) * HALF : (2 * head + half + 1) * HALF],
            )
            for head in range(MH)
            for half in range(2)
        ],
        axis=0,
    )
    arrived = lax.all_to_all(
        jnp.stack([piece.reshape(owners, capacity, width) for piece in slot_grads], axis=1),
        ALL,
        split_axis=0,
        concat_axis=0,
        tiled=True,
    )
    grad_rows = mm_l(serve_pick, arrived.reshape(owners * 2 * capacity, width))
    grad_normed2 = mm_t(grad_query, query_full) + mm_t(grad_gate, gate_full)
    grad_query_w = mm_l(normed2, grad_query)
    grad_gate_w = mm_l(normed2, grad_gate)
    back, gain_mem_part = norm_backward(hidden, inverse2, gain_mem, grad_normed2)
    grad_hidden = dy_low.astype(F32) + back
    hidden_low = grad_hidden.astype(BF)
    grad_attn_out = mm_l(att, hidden_low)
    grad_att = mm_t(hidden_low, attn_out_full).astype(BF)
    grad_q_p, grad_k_p, grad_v_p = attend_backward(
        queries[:rows], all_keys, all_vals, visible_p, logsum_p, grad_att[:rows]
    )
    grad_q_c, grad_k_c, grad_v_c = attend_backward(
        queries[rows:], key_join, val_join, visible_c, logsum_c, grad_att[rows:]
    )
    own_keys = lax.psum_scatter(
        (grad_k_c[:PL] + grad_k_p).astype(BF), "fsdp", scatter_dimension=0, tiled=True
    )
    own_vals = lax.psum_scatter(
        (grad_v_c[:PL] + grad_v_p).astype(BF), "fsdp", scatter_dimension=0, tiled=True
    )
    grad_q = jnp.concatenate([grad_q_p, grad_q_c], axis=0).astype(BF)
    grad_k = jnp.concatenate([own_keys, grad_k_c[PL:].astype(BF)], axis=0)
    grad_v = jnp.concatenate([own_vals, grad_v_c[PL:].astype(BF)], axis=0)
    grad_normed = (
        mm_t(grad_q, qkv_full[0]) + mm_t(grad_k, qkv_full[1]) + mm_t(grad_v, qkv_full[2])
    )
    grad_x, gain_attn_part = norm_backward(x_rows, inverse, gain_attn, grad_normed)
    grad_x = grad_hidden + grad_x
    grad_qkv = jnp.stack([mm_l(normed, piece) for piece in (grad_q, grad_k, grad_v)])

    devices = owners
    block = cols // devices
    keys_low = grad_keys.astype(BF).reshape(devices, 2, block, HALF).transpose(0, 2, 1, 3)
    gains = jnp.concatenate([gain_attn_part, gain_mem_part]).reshape(2 * cols // 128, 128)
    sums = reduce_grads(
        side,
        depth,
        (
            grad_qkv.astype(BF),
            grad_attn_out.astype(BF),
            grad_query_w.astype(BF),
            keys_low.reshape(cols, 2 * HALF),
            grad_gate_w.astype(BF),
            grad_mem_out.astype(BF),
        ),
        gains,
        1,
    )
    own = lax.axis_index("dp") * depth + lax.axis_index("fsdp")
    gain_shards = lax.dynamic_index_in_dim(
        sums[6].reshape(2, devices, block), own, axis=1, keepdims=False
    )
    sub_shard = sums[3].reshape(block, 2, HALF).transpose(1, 0, 2).reshape(2 * block, HALF)
    return (
        out[None, :rows],
        out[None, rows:],
        grad_x[None, :rows],
        grad_x[None, rows:],
        gain_shards[0],
        gain_shards[1],
        sums[0],
        sums[1],
        sums[2],
        sub_shard,
        sums[4],
        sums[5],
        grad_rows,
    )


def solution(mesh):
    in_specs = (
        P("dp", "fsdp", None),
        P("dp", "fsdp", None),
        P("dp", "fsdp", None),
        P("dp", "fsdp", None),
        P(),
        P(),
        P(None, "fsdp", None),
        P("fsdp", None),
        P("fsdp", None),
        P("fsdp", None),
        P("fsdp", None),
        P("fsdp", None),
        P(("dp", "fsdp"), None),
        P(None, ("dp", "fsdp"), None, None),
        P("dp", "fsdp", None, None),
        P("dp", "fsdp", None, None),
    )
    out_specs = (
        P("dp", "fsdp", None),
        P("dp", "fsdp", None),
        P("dp", "fsdp", None),
        P("dp", "fsdp", None),
        P(("dp", "fsdp")),
        P(("dp", "fsdp")),
        P(None, ("dp", "fsdp"), None),
        P(("dp", "fsdp"), None),
        P(("dp", "fsdp"), None),
        P(("dp", "fsdp"), None),
        P(("dp", "fsdp"), None),
        P(("dp", "fsdp"), None),
        P(("dp", "fsdp"), None),
    )
    return jax.shard_map(
        per_device, mesh=mesh, in_specs=in_specs, out_specs=out_specs, check_vma=False
    )
```

```python
import functools
import jax
import jax.numpy as jnp
from jax import lax
from jax.experimental import pallas as pl
from jax.experimental.pallas import tpu as pltpu
from jax.sharding import PartitionSpec as P
BF = jnp.bfloat16
F32 = jnp.float32
ALL = ("dp", "fsdp")
MESH = pl.DeviceIdType.MESH
LAG = 2
GATHER_LAG = 2
COLLECT_LAG = 2
AHEAD = 3
PIECE = 1024
PAIR = 128
HDIM = 64
MH = 4
HALF = 512
SUB = 256
NEVER = -1e30


def mm(left, right):
    return jnp.dot(left, right, preferred_element_type=F32)


def mm_t(left, right):
    return lax.dot_general(left, right, (((1,), (1,)), ((), ())), preferred_element_type=F32)


def mm_l(left, right):
    return lax.dot_general(left, right, (((0,), (0,)), ((), ())), preferred_element_type=F32)


def normalize(matrix, gain_vec):
    inverse = lax.rsqrt(jnp.mean(matrix * matrix, axis=-1, keepdims=True) + 1e-05)
    return (matrix * inverse * gain_vec, inverse)


def norm_backward(matrix, inverse, gain_vec, grad_normed):
    scaled = gain_vec * grad_normed
    cubed = inverse * inverse * inverse
    grad_matrix = inverse * scaled - matrix * cubed * jnp.mean(
        matrix * scaled, axis=-1, keepdims=True
    )
    return (grad_matrix, jnp.sum(grad_normed * matrix * inverse, axis=0))


def grid_of(plane, depth):
    side = 1
    while 2 * side * side < plane:
        side += 1
    return side, depth


def place(side):
    dp = lax.axis_index("dp")
    return (dp // (2 * side), (dp // 2) % side, dp % 2, lax.axis_index("fsdp"))


def device_at(side, y, x, core, z):
    return ((y * side + x) * 2 + core, z)


def greet(side, depth):
    y, x, core, z = place(side)
    barrier = pltpu.get_barrier_semaphore()
    peers = [device_at(side, y, x, 1 - core, z)]
    for hop in range(1, side):
        peers.append(device_at(side, y, (x + hop) % side, core, z))
        peers.append(device_at(side, (y + hop) % side, x, core, z))
    for hop in range(1, depth):
        peers.append(device_at(side, y, x, core, (z + hop) % depth))
    for peer in peers:
        pl.semaphore_signal(barrier, inc=1, device_id=peer, device_id_type=MESH)
    pl.semaphore_wait(barrier, len(peers))


def remote(source, target, send_sem, recv_sem, peer):
    return pltpu.make_async_remote_copy(
        src_ref=source,
        dst_ref=target,
        send_sem=send_sem,
        recv_sem=recv_sem,
        device_id=peer,
        device_id_type=MESH,
    )


class Gather:
    def __init__(self, side, depth, shards):
        self.side, self.depth = side, depth
        self.views, self.outs, self.shapes, self.held, self.layout = [], [], [], [], []
        plane = 2 * side * side
        for shard in shards:
            rows, cols = shard.shape[-2:]
            block, width = rows // plane, min(cols, PIECE)
            lead = shard.shape[:-2]
            self.views.append(shard.reshape(lead + (side, side, 2, block, cols)))
            leads = range(lead[0]) if lead else (None,)
            self.layout.append(
                [(number, start) for number in leads for start in range(0, cols, width)]
            )
            self.outs.append(
                jax.ShapeDtypeStruct(lead + (depth, side, side, 2, block, cols), BF)
            )
            self.shapes.append(lead + (depth * rows, cols))
            self.held.append(
                pltpu.VMEM((len(self.layout[-1]), side, side, 2, block, width), BF)
            )
        self.count = count = sum(len(columns) for columns in self.layout)
        self.steps = count + depth - 2 + 3 * GATHER_LAG
        dma = pltpu.SemaphoreType.DMA
        self.scratch = self.held + [
            dma((count,)),
            dma((count,)),
            dma((count, depth)),
            dma((count, depth)),
            dma((count, depth)),
            dma((count, depth, side - 1)),
            dma((count, depth, side - 1)),
            dma((count, depth, side - 1)),
            dma((count, depth, side - 1)),
            dma((count, depth)),
            dma((count, depth)),
        ]

    def restore(self, full):
        return [one.reshape(shape) for one, shape in zip(full, self.shapes)]

    def bind(self, sources, outs, scratch):
        self.sources, self.results = sources, outs
        n_in = len(self.layout)
        self.holders = scratch[:n_in]
        (self.in_sem, self.out_sem, self.right_send, self.left_send, self.deep_recv,
         self.one_send, self.one_recv, self.two_send, self.two_recv, self.core_send,
         self.core_recv) = scratch[n_in:]
        self.pieces = []
        for number, columns in enumerate(self.layout):
            width = self.holders[number].shape[-1]
            width = width if sources[number].shape[-1] > width else None
            for inner, (lead, start) in enumerate(columns):
                self.pieces.append((number, lead, start, width, inner))

    def cut(self, refs, k, *spot):
        number, lead, start, width = self.pieces[k][:4]
        ref = refs[number] if lead is None else refs[number].at[lead]
        ref = ref.at[spot] if spot else ref
        if width is None:
            return ref
        return ref.at[(slice(None),) * (len(ref.shape) - 1) + (pl.ds(start, width),)]

    def along_z(self, k, zp, move, source=None):
        y, x, core, z = place(self.side)
        target = self.cut(self.results, k, zp, y, x, core)
        send = self.right_send if move > 0 else self.left_send
        return remote(target if source is None else source, target, send.at[k, zp],
                      self.deep_recv.at[k, zp], device_at(self.side, y, x, core, z + move))

    def one_copy(self, k, zp, hop):
        side = self.side
        y, x, core, z = place(side)
        peer = device_at(side, y, (x + hop) % side, core, z) if k % 2 == 0 else device_at(
            side, (y + hop) % side, x, core, z)
        ref = self.cut(self.results, k, zp, y, x, core)
        return remote(ref, ref, self.one_send.at[k, zp, hop - 1],
                      self.one_recv.at[k, zp, hop - 1], peer)

    def two_copy(self, k, zp, hop):
        side = self.side
        y, x, core, z = place(side)
        x_first = k % 2 == 0
        peer = device_at(side, (y + hop) % side, x, core, z) if x_first else device_at(
            side, y, (x + hop) % side, core, z)
        ref = (self.cut(self.results, k, zp, y, slice(None), core) if x_first
               else self.cut(self.results, k, zp, slice(None), x, core))
        return remote(ref, ref, self.two_send.at[k, zp, hop - 1],
                      self.two_recv.at[k, zp, hop - 1], peer)

    def core_copy(self, k, zp):
        y, x, core, z = place(self.side)
        ref = self.cut(self.results, k, zp, slice(None), slice(None), core)
        return remote(ref, ref, self.core_send.at[k, zp], self.core_recv.at[k, zp],
                      device_at(self.side, y, x, 1 - core, z))

    def take(self, k):
        number, inner = self.pieces[k][0], self.pieces[k][4]
        return pltpu.make_async_copy(self.cut(self.sources, k), self.holders[number].at[inner],
                                     self.in_sem.at[k])

    def put(self, k):
        z = place(self.side)[3]
        number, inner = self.pieces[k][0], self.pieces[k][4]
        return pltpu.make_async_copy(self.holders[number].at[inner],
                                     self.cut(self.results, k, z), self.out_sem.at[k])

    def start(self):
        y, x, core, z = place(self.side)
        for k in range(self.count):
            self.take(k).start()
            own = self.cut(self.sources, k, y, x, core)

            @pl.when(z < self.depth - 1)
            def _(k=k, own=own):
                self.along_z(k, z, 1, own).start()

            @pl.when(z > 0)
            def _(k=k, own=own):
                self.along_z(k, z, -1, own).start()

    def step(self, i):
        side, depth = self.side, self.depth
        z = place(side)[3]
        if i < self.count:
            self.take(i).wait()
            self.put(i).start()
        for stage in range(4):
            for distance in range(1, depth):
                k = i - stage * GATHER_LAG - (distance - 1)
                if not 0 <= k < self.count:
                    continue
                for sign in (1, -1):
                    zp = z + sign * distance

                    @pl.when(jnp.logical_and(zp >= 0, zp < depth))
                    def _(k=k, zp=zp, sign=sign, stage=stage):
                        self.arrival(stage, k, zp, sign)

    def arrival(self, stage, k, zp, sign):
        side, depth = self.side, self.depth
        z = place(side)[3]
        if stage == 0:
            self.along_z(k, zp, 1).wait_recv()

            @pl.when(z < depth - 1 if sign < 0 else z > 0)
            def _():
                self.along_z(k, zp, -sign).start()

            for hop in range(1, side):
                self.one_copy(k, zp, hop).start()
        elif stage == 1:
            for hop in range(1, side):
                self.one_copy(k, zp, hop).wait_recv()
            for hop in range(1, side):
                self.two_copy(k, zp, hop).start()
        elif stage == 2:
            for hop in range(1, side):
                self.two_copy(k, zp, hop).wait_recv()
            self.core_copy(k, zp).start()
        else:
            self.core_copy(k, zp).wait_recv()

    def finish(self):
        side, depth = self.side, self.depth
        z = place(side)[3]
        for k in range(self.count):
            self.put(k).wait()
            for zp in range(depth):
                @pl.when(jnp.logical_and(zp <= z, z < depth - 1))
                def _(k=k, zp=zp):
                    self.along_z(k, zp, 1).wait_send()

                @pl.when(jnp.logical_and(zp >= z, z > 0))
                def _(k=k, zp=zp):
                    self.along_z(k, zp, -1).wait_send()

                @pl.when(zp != z)
                def _(k=k, zp=zp):
                    for hop in range(1, side):
                        self.one_copy(k, zp, hop).wait_send()
                        self.two_copy(k, zp, hop).wait_send()
                    self.core_copy(k, zp).wait_send()


class Reduce:
    def __init__(self, side, depth, grads, gains=None):
        self.side, self.depth = side, depth
        self.layout, self.views, self.outs = [], [], []
        self.width = width = 1024
        devices = 2 * side * side * depth
        for grad in grads:
            rows, cols = grad.shape[-2:]
            self.block = block = rows // devices
            lead = grad.shape[:-2]
            self.views.append(grad.reshape(lead + (side, side, 2, depth, block, cols)))
            leads = range(lead[0]) if lead else (None,)
            self.layout.append(
                [(number, start) for number in leads for start in range(0, cols, width)]
            )
            self.outs.append(jax.ShapeDtypeStruct(lead + (block, cols), F32))
        self.count = count = sum(len(columns) for columns in self.layout)
        self.steps = count + 3 * LAG
        self.gains = gains is not None
        most = max(side, depth) - 1
        dma = pltpu.SemaphoreType.DMA
        self.scratch = [
            pltpu.VMEM((count, side, side, depth, block, width), BF),
            pltpu.VMEM((count, side, side, depth, block, width), BF),
            pltpu.VMEM((count, side - 1, side, depth, block, width), BF),
            pltpu.VMEM((count, side - 1, depth, block, width), BF),
            pltpu.VMEM((count, depth - 1, block, width), BF),
            pltpu.VMEM((count, block, width), F32),
            dma((count,)),
            dma((count,)),
            dma((count,)),
            dma((count, side - 1)),
            dma((count, side - 1)),
            dma((count, side - 1)),
            dma((count, side - 1)),
            dma((count, depth - 1)),
            dma((count, depth - 1)),
        ]
        if self.gains:
            self.views.append(gains)
            self.outs.append(jax.ShapeDtypeStruct(gains.shape, F32))
            self.scratch += [
                pltpu.VMEM((4,) + gains.shape, F32),
                pltpu.VMEM((4, most) + gains.shape, F32),
                dma((4, most)),
                dma((4, most)),
            ]
        any_space, vmem = pl.BlockSpec(memory_space=pl.ANY), pl.BlockSpec(memory_space=pltpu.VMEM)
        self.in_specs = [any_space] * len(self.layout) + [vmem] * self.gains
        self.out_specs = [vmem] * len(self.views)

    def bind(self, sources, outs, scratch):
        (self.mine, self.got_core, self.got_one, self.got_two, self.got_deep, self.total,
         self.local_sem, self.core_send, self.core_recv, self.one_send, self.one_recv,
         self.two_send, self.two_recv, self.deep_send, self.deep_recv) = scratch[:15]
        self.results = outs
        if self.gains:
            self.gain_in, self.gain_out = sources[-1], outs[-1]
            self.gain_sum, self.gain_got, self.gain_send, self.gain_recv = scratch[15:]
        self.pieces = []
        for number, columns in enumerate(self.layout):
            for lead, start in columns:
                ref = sources[number] if lead is None else sources[number].at[lead]
                self.pieces.append((ref, number, lead, start))

    def core_wait(self, k):
        y, x, core, z = place(self.side)
        return remote(self.got_core.at[k], self.got_core.at[k], self.core_send.at[k],
                      self.core_recv.at[k], device_at(self.side, y, x, 1 - core, z))

    def start(self):
        y, x, core, z = place(self.side)
        for k, (ref, _, _, start) in enumerate(self.pieces):
            spot = pl.ds(start, self.width)
            remote(ref.at[:, :, 1 - core, :, :, spot], self.got_core.at[k], self.core_send.at[k],
                   self.core_recv.at[k], device_at(self.side, y, x, 1 - core, z)).start()
            pltpu.make_async_copy(ref.at[:, :, core, :, :, spot], self.mine.at[k],
                                  self.local_sem.at[k]).start()
        if self.gains:
            self.gain_copy(0, 0).start()

    def one_copy(self, k, hop, x_first):
        side = self.side
        y, x, core, z = place(side)
        peer = device_at(side, y, (x + hop) % side, core, z) if x_first else device_at(
            side, (y + hop) % side, x, core, z)
        source = (self.mine.at[k, :, (x + hop) % side] if x_first
                  else self.mine.at[k, (y + hop) % side])
        return remote(source, self.got_one.at[k, hop - 1], self.one_send.at[k, hop - 1],
                      self.one_recv.at[k, hop - 1], peer)

    def two_copy(self, k, hop, x_first):
        side = self.side
        y, x, core, z = place(side)
        peer = device_at(side, (y + hop) % side, x, core, z) if x_first else device_at(
            side, y, (x + hop) % side, core, z)
        source = (self.mine.at[k, (y + hop) % side, x] if x_first
                  else self.mine.at[k, y, (x + hop) % side])
        return remote(source, self.got_two.at[k, hop - 1], self.two_send.at[k, hop - 1],
                      self.two_recv.at[k, hop - 1], peer)

    def deep_copy(self, k, hop):
        y, x, core, z = place(self.side)
        there = (z + hop) % self.depth
        return remote(self.mine.at[k, y, x, there], self.got_deep.at[k, hop - 1],
                      self.deep_send.at[k, hop - 1], self.deep_recv.at[k, hop - 1],
                      device_at(self.side, y, x, core, there))

    def gain_count(self, stage):
        return (1, self.side - 1, self.side - 1, self.depth - 1)[stage]

    def gain_copy(self, stage, number):
        side, depth, hop = self.side, self.depth, number + 1
        y, x, core, z = place(side)
        peer = (
            device_at(side, y, x, 1 - core, z),
            device_at(side, y, (x + hop) % side, core, z),
            device_at(side, (y + hop) % side, x, core, z),
            device_at(side, y, x, core, (z + hop) % depth),
        )[stage]
        source = self.gain_in if stage == 0 else self.gain_sum.at[stage - 1]
        return remote(source, self.gain_got.at[stage, number], self.gain_send.at[stage, number],
                      self.gain_recv.at[stage, number], peer)

    def both_orders(self, k, action):
        @pl.when(k % 2 == 0)
        def _():
            action(True)

        @pl.when(k % 2 == 1)
        def _():
            action(False)

    def added(self, base, others):
        if len(others) == 1:
            return base + others[0]
        value = base.astype(F32)
        for other in others:
            value = value + other.astype(F32)
        return value.astype(base.dtype)

    def after_core(self, k):
        side, depth, mine, got = self.side, self.depth, self.mine, self.got_core
        self.core_wait(k).wait_recv()
        pltpu.make_async_copy(got.at[k], mine.at[k], self.local_sem.at[k]).wait()

        def add(index, carry):
            spot = (k, index // (side * depth), (index // depth) % side, index % depth)
            mine[spot] = mine[spot] + got[spot]
            return carry

        lax.fori_loop(0, side * side * depth, add, 0)

        def send(x_first):
            for hop in range(1, side):
                self.one_copy(k, hop, x_first).start()

        self.both_orders(k, send)

    def after_one(self, k):
        side, depth, mine = self.side, self.depth, self.mine
        y, x, core, z = place(side)

        def finish(x_first):
            for hop in range(1, side):
                self.one_copy(k, hop, x_first).wait_recv()

            def add(index, carry):
                a, c = index // depth, index % depth
                spot = (k, a, x, c) if x_first else (k, y, a, c)
                mine[spot] = self.added(
                    mine[spot], [self.got_one[k, hop, a, c] for hop in range(side - 1)]
                )
                return carry

            lax.fori_loop(0, side * depth, add, 0)
            for hop in range(1, side):
                self.two_copy(k, hop, x_first).start()

        self.both_orders(k, finish)

    def after_two(self, k):
        side, depth, mine = self.side, self.depth, self.mine
        y, x, core, z = place(side)

        def finish(x_first):
            for hop in range(1, side):
                self.two_copy(k, hop, x_first).wait_recv()

        self.both_orders(k, finish)

        def add(c, carry):
            mine[k, y, x, c] = self.added(
                mine[k, y, x, c], [self.got_two[k, hop, c] for hop in range(side - 1)]
            )
            return carry

        lax.fori_loop(0, depth, add, 0)
        for hop in range(1, depth):
            self.deep_copy(k, hop).start()

    def after_deep(self, k):
        y, x, core, z = place(self.side)
        for hop in range(1, self.depth):
            self.deep_copy(k, hop).wait_recv()
        value = self.mine[k, y, x, z].astype(F32)
        for hop in range(self.depth - 1):
            value = value + self.got_deep[k, hop].astype(F32)
        self.total[k] = value

    def step(self, i):
        stages = (self.after_core, self.after_one, self.after_two, self.after_deep)
        for number, action in enumerate(stages):
            lag = number * LAG

            @pl.when(jnp.logical_and(i >= lag, i < self.count + lag))
            def _(lag=lag, action=action):
                action(i - lag)

        for stage in range(4 if self.gains else 0):
            @pl.when(i == stage + 1)
            def _(stage=stage):
                value = self.gain_in[...] if stage == 0 else self.gain_sum[stage - 1]
                for number in range(self.gain_count(stage)):
                    self.gain_copy(stage, number).wait_recv()
                    value = value + self.gain_got[stage, number]
                self.gain_sum[stage] = value
                if stage < 3:
                    for number in range(self.gain_count(stage + 1)):
                        self.gain_copy(stage + 1, number).start()

    def finish(self):
        if self.gains:
            self.gain_out[...] = self.gain_sum[3]
        for k, (_, number, lead, start) in enumerate(self.pieces):
            spot = (slice(None), pl.ds(start, self.width))
            if lead is None:
                self.results[number][spot] = self.total[k]
            else:
                self.results[number][(lead,) + spot] = self.total[k]

        def drain(k, carry):
            self.core_wait(k).wait_send()

            def sent(x_first):
                for hop in range(1, self.side):
                    self.one_copy(k, hop, x_first).wait_send()
                    self.two_copy(k, hop, x_first).wait_send()

            self.both_orders(k, sent)
            for hop in range(1, self.depth):
                self.deep_copy(k, hop).wait_send()
            return carry

        lax.fori_loop(0, self.count, drain, 0)
        for stage in range(4 if self.gains else 0):
            for number in range(self.gain_count(stage)):
                self.gain_copy(stage, number).wait_send()


def split_refs(refs, *counts):
    groups, at = [], 0
    for count in counts:
        groups.append(refs[at : at + count])
        at += count
    return groups + [refs[at:]]


def params(call_id, mib):
    return pltpu.CompilerParams(
        collective_id=call_id, has_side_effects=True, vmem_limit_bytes=mib * 1024 * 1024
    )


def gather_kernel(plan, *refs):
    n = len(plan.views)
    sources, outs, scratch = split_refs(refs, n, n)
    plan.bind(sources, outs, scratch)
    greet(plan.side, plan.depth)
    plan.start()
    for i in range(plan.steps):
        plan.step(i)
    plan.finish()


def gather_weights(side, depth, shards, call_id):
    plan = Gather(side, depth, shards)
    any_space = pl.BlockSpec(memory_space=pl.ANY)
    full = pl.pallas_call(
        functools.partial(gather_kernel, plan),
        out_shape=tuple(plan.outs),
        in_specs=[any_space] * len(plan.views),
        out_specs=(any_space,) * len(plan.views),
        scratch_shapes=plan.scratch,
        compiler_params=params(call_id, 32),
    )(*plan.views)
    return plan.restore(full)


def reduce_kernel(plan, *refs):
    n = len(plan.views)
    sources, outs, scratch = split_refs(refs, n, n)
    plan.bind(sources, outs, scratch)
    greet(plan.side, plan.depth)
    plan.start()

    def run(i, carry):
        plan.step(i)
        return carry

    lax.fori_loop(0, max(plan.steps, 5), run, 0)
    plan.finish()


def reduce_grads(side, depth, grads, gains, call_id):
    plan = Reduce(side, depth, grads, gains)
    return pl.pallas_call(
        functools.partial(reduce_kernel, plan),
        out_shape=tuple(plan.outs),
        in_specs=plan.in_specs,
        out_specs=tuple(plan.out_specs),
        scratch_shapes=plan.scratch,
        compiler_params=params(call_id, 60),
    )(*plan.views)


def half_masks(width):
    lane = lax.broadcasted_iota(jnp.int32, (1, width), 1)
    return (lane < width // 2, lane >= width // 2)


def dot_rows(left, right):
    return lax.dot_general(left, right, (((1,), (1,)), ((), ())), preferred_element_type=F32)


def dot_first(left, right):
    return lax.dot_general(left, right, (((0,), (0,)), ((), ())), preferred_element_type=F32)


def dot_plain(left, right):
    return lax.dot_general(left, right, (((1,), (0,)), ((), ())), preferred_element_type=F32)


def prompt_mask(scores, chunk, z, rows):
    key = lax.broadcasted_iota(jnp.int32, scores.shape, 0) + chunk * rows
    query = lax.broadcasted_iota(jnp.int32, scores.shape, 1)
    seen = jnp.logical_or(query >= rows, key <= query + z * rows)
    return jnp.where(seen, scores, NEVER)


def own_mask(scores):
    key = lax.broadcasted_iota(jnp.int32, scores.shape, 0)
    query = lax.broadcasted_iota(jnp.int32, scores.shape, 1)
    return jnp.where(key <= query, scores, NEVER)


def forward_pair(p, z, rows, depth, q_ref, k_ref, v_ref, keys, vals, att_ref, lse_ref):
    cols = pl.ds(pl.multiple_of(p * PAIR, PAIR), PAIR)
    q_pair = q_ref[:, cols] * jnp.asarray(0.125, BF)
    k_own, v_own = k_ref[pl.ds(rows, rows), cols], v_ref[pl.ds(rows, rows), cols]
    outs = []
    for head, mask in enumerate(half_masks(PAIR)):
        q_head = jnp.where(mask, q_pair, jnp.zeros_like(q_pair))
        scores = [
            prompt_mask(dot_rows(keys[p, chunk], q_head), chunk, z, rows) for chunk in range(depth)
        ]
        own = own_mask(dot_rows(k_own, q_head[rows:]))
        top = jnp.max(scores[0], axis=0, keepdims=True)
        for piece in scores[1:]:
            top = jnp.maximum(top, jnp.max(piece, axis=0, keepdims=True))
        top_c = jnp.maximum(top[:, rows:], jnp.max(own, axis=0, keepdims=True))
        top = jnp.concatenate([top[:, :rows], top_c], axis=1)
        total = jnp.zeros_like(top)
        out = jnp.zeros((PAIR, 2 * rows), F32)
        for chunk in range(depth):
            expo = jnp.exp(scores[chunk] - top)
            total = total + jnp.sum(expo, axis=0, keepdims=True)
            out = out + dot_first(vals[p, chunk], expo.astype(BF))
        expo = jnp.exp(own - top_c)
        total_c = total[:, rows:] + jnp.sum(expo, axis=0, keepdims=True)
        out_c = out[:, rows:] + dot_first(v_own, expo.astype(BF))
        total = jnp.concatenate([total[:, :rows], total_c], axis=1)
        out = jnp.concatenate([out[:, :rows], out_c], axis=1) / total
        lse_ref[pl.ds(2 * p + head, 1), :] = top + jnp.log(total)
        outs.append(out[head * HDIM : (head + 1) * HDIM])
    att_ref[:, cols] = jnp.concatenate(outs, axis=0).T.astype(BF)


def backward_pair(p, z, rows, depth, q_ref, k_ref, v_ref, keys, vals, lse_ref, att_ref, g_ref,
                  dq_ref, dk_ref, dv_ref, part):
    cols = pl.ds(pl.multiple_of(p * PAIR, PAIR), PAIR)
    own_rows = pl.ds(rows, rows)
    q_pair = q_ref[:, cols] * jnp.asarray(0.125, BF)
    g_pair = g_ref[:, cols]
    k_own, v_own = k_ref[own_rows, cols], v_ref[own_rows, cols]
    pulled = (g_pair.astype(F32) * att_ref[:, cols].astype(F32)).T
    masks = half_masks(PAIR)
    q_heads = [jnp.where(mask, q_pair, jnp.zeros_like(q_pair)) for mask in masks]
    g_heads = [jnp.where(mask, g_pair, jnp.zeros_like(g_pair)) for mask in masks]
    lses = [lse_ref[pl.ds(2 * p + head, 1), :] for head in range(2)]
    deltas = [
        jnp.sum(pulled[head * HDIM : (head + 1) * HDIM], axis=0, keepdims=True)
        for head in range(2)
    ]
    dq = [jnp.zeros((PAIR, 2 * rows), F32) for _ in range(2)]
    for chunk in range(depth):
        dk = jnp.zeros((rows, PAIR), F32)
        dv = jnp.zeros((rows, PAIR), F32)
        k_chunk, v_chunk = keys[p, chunk], vals[p, chunk]
        for head in range(2):
            scores = prompt_mask(dot_rows(k_chunk, q_heads[head]), chunk, z, rows)
            prob = jnp.exp(scores - lses[head])
            d_prob = dot_rows(v_chunk, g_heads[head])
            d_score = (prob * (d_prob - deltas[head])).astype(BF)
            dv = dv + dot_plain(prob.astype(BF), g_heads[head])
            dk = dk + dot_plain(d_score, q_heads[head])
            dq[head] = dq[head] + dot_first(k_chunk, d_score)
        part[p, chunk, 0] = dk.astype(BF)
        part[p, chunk, 1] = dv.astype(BF)
    dk = jnp.zeros((rows, PAIR), F32)
    dv = jnp.zeros((rows, PAIR), F32)
    for head in range(2):
        q_head, g_head = q_heads[head][rows:], g_heads[head][rows:]
        scores = own_mask(dot_rows(k_own, q_head))
        prob = jnp.exp(scores - lses[head][:, rows:])
        d_prob = dot_rows(v_own, g_head)
        d_score = (prob * (d_prob - deltas[head][:, rows:])).astype(BF)
        dv = dv + dot_plain(prob.astype(BF), g_head)
        dk = dk + dot_plain(d_score, q_head)
        more = dot_first(k_own, d_score)
        dq[head] = jnp.concatenate([dq[head][:, :rows], dq[head][:, rows:] + more], axis=1)
    dk_ref[own_rows, cols] = dk.astype(BF)
    dv_ref[own_rows, cols] = dv.astype(BF)
    both = jnp.concatenate([dq[0][:HDIM], dq[1][HDIM:]], axis=0) * 0.125
    dq_ref[:, cols] = both.T.astype(BF)


class Exchange:
    def __init__(self, depth, rows, pairs):
        self.depth, self.rows, self.pairs = depth, rows, pairs
        dma = pltpu.SemaphoreType.DMA
        self.scratch = [dma((2, 2, pairs, depth)), dma((2, pairs, depth))]

    def bind(self, owned, gathered, scratch):
        self.owned, self.gathered = owned, gathered
        self.send_sem, self.recv_sem = scratch

    def hop(self, kind, p, zp, move, own=False):
        target = self.gathered[kind].at[p, zp]
        cols = pl.ds(pl.multiple_of(p * PAIR, PAIR), PAIR)
        source = self.owned[kind].at[pl.ds(0, self.rows), cols] if own else target
        z = lax.axis_index("fsdp")
        return remote(source, target, self.send_sem.at[kind, (move + 1) // 2, p, zp],
                      self.recv_sem.at[kind, p, zp], (lax.axis_index("dp"), z + move))

    def offer(self, p):
        z = lax.axis_index("fsdp")
        for move in (1, -1):
            @pl.when(z < self.depth - 1 if move > 0 else z > 0)
            def _(move=move):
                for kind in range(2):
                    self.hop(kind, p, z, move, own=True).start()
        cols = pl.ds(pl.multiple_of(p * PAIR, PAIR), PAIR)
        for kind in range(2):
            self.gathered[kind][p, z] = self.owned[kind][pl.ds(0, self.rows), cols]

    def step(self, i):
        z = lax.axis_index("fsdp")
        for distance in range(1, self.depth):
            p = i - (distance - 1)
            for sign in (1, -1):
                zp = z + sign * distance
                seen = jnp.logical_and(zp >= 0, zp < self.depth)

                @pl.when(jnp.logical_and(seen, jnp.logical_and(p >= 0, p < self.pairs)))
                def _(p=p, zp=zp, sign=sign):
                    for kind in range(2):
                        self.hop(kind, p, zp, 1).wait_recv()

                    @pl.when(z < self.depth - 1 if sign < 0 else z > 0)
                    def _():
                        for kind in range(2):
                            self.hop(kind, p, zp, -sign).start()

    def finish(self):
        z = lax.axis_index("fsdp")

        def drain(p, carry):
            for zp in range(self.depth):
                for move in (1, -1):
                    far = zp <= z if move > 0 else zp >= z
                    inner = z < self.depth - 1 if move > 0 else z > 0

                    @pl.when(jnp.logical_and(far, inner))
                    def _(zp=zp, move=move):
                        for kind in range(2):
                            self.hop(kind, p, zp, move).wait_send()
            return carry

        lax.fori_loop(0, self.pairs, drain, 0)


def forward_kernel(gather, exchange, *refs):
    depth, rows, pairs = exchange.depth, exchange.rows, exchange.pairs
    n = len(gather.views)
    (q_ref, k_ref, v_ref), shards, (att_ref, lse_ref, keys, vals), full, swap, rest = split_refs(
        refs, 3, n, 4, n, len(exchange.scratch))
    gather.bind(shards, full, rest)
    exchange.bind((k_ref, v_ref), (keys, vals), swap)
    z = lax.axis_index("fsdp")
    greet(gather.side, depth)
    ahead = min(AHEAD, pairs)
    for p in range(ahead):
        exchange.offer(p)
    gather.start()
    turns = pairs + depth - 1

    def run(i, carry):
        @pl.when(i + ahead < pairs)
        def _():
            exchange.offer(i + ahead)

        exchange.step(i)
        for number in range(min(turns, gather.steps)):
            @pl.when(i == number)
            def _(number=number):
                gather.step(number)

        @pl.when(i >= depth - 1)
        def _():
            forward_pair(i - (depth - 1), z, rows, depth, q_ref, k_ref, v_ref, keys, vals, att_ref,
                         lse_ref)

        return carry

    lax.fori_loop(0, turns, run, 0)
    for number in range(turns, gather.steps):
        gather.step(number)
    exchange.finish()
    gather.finish()


def attention_forward(side, depth, q, k, v, shards, call_id):
    rows, width = q.shape[0] // 2, q.shape[1]
    pairs = width // PAIR
    gather, exchange = Gather(side, depth, shards), Exchange(depth, rows, pairs)
    any_space, vmem = pl.BlockSpec(memory_space=pl.ANY), pl.BlockSpec(memory_space=pltpu.VMEM)
    spread = jax.ShapeDtypeStruct((pairs, depth, rows, PAIR), BF)
    results = pl.pallas_call(
        functools.partial(forward_kernel, gather, exchange),
        out_shape=(
            jax.ShapeDtypeStruct(q.shape, BF),
            jax.ShapeDtypeStruct((2 * pairs, 2 * rows), F32),
            spread,
            spread,
        )
        + tuple(gather.outs),
        in_specs=[vmem] * 3 + [any_space] * len(gather.views),
        out_specs=(vmem,) * 4 + (any_space,) * len(gather.views),
        scratch_shapes=exchange.scratch + gather.scratch,
        compiler_params=params(call_id, 56),
    )(q, k, v, *gather.views)
    return results[:4], gather.restore(results[4:])


class Collect:
    def __init__(self, depth, rows, pairs):
        self.depth, self.rows, self.pairs = depth, rows, pairs
        dma = pltpu.SemaphoreType.DMA
        shape = (pairs, depth, 2, rows, PAIR)
        self.scratch = [
            pltpu.VMEM(shape, BF),
            pltpu.VMEM(shape, BF),
            pltpu.VMEM(shape, BF),
            pltpu.VMEM((2, rows, PAIR), F32),
            dma((2, pairs, depth)),
            dma((2, pairs, depth)),
        ]
        self.steps = pairs + (depth - 1) * COLLECT_LAG + 1

    def bind(self, scratch):
        (self.part, self.from_left, self.from_right, self.whole, self.send_sem,
         self.recv_sem) = scratch

    def hop(self, p, zd, move):
        z = lax.axis_index("fsdp")
        target = self.from_left if move > 0 else self.from_right
        way = (move + 1) // 2
        return remote(self.part.at[p, zd], target.at[p, zd], self.send_sem.at[way, p, zd],
                      self.recv_sem.at[way, p, zd], (lax.axis_index("dp"), z + move))

    def flow(self, p, move):
        depth = self.depth
        z = lax.axis_index("fsdp")
        first = z == 0 if move > 0 else z == depth - 1
        arrived = self.from_left if move > 0 else self.from_right
        for zd in range(depth - 1, -1, -1) if move > 0 else range(depth):
            beyond = zd > z if move > 0 else zd < z

            @pl.when(jnp.logical_and(jnp.logical_not(first), jnp.logical_or(beyond, zd == z)))
            def _(zd=zd):
                self.hop(p, zd, move).wait_recv()

                def add(part, carry):
                    self.part[p, zd, part] = self.part[p, zd, part] + arrived[p, zd, part]
                    return carry

                @pl.when(zd != z)
                def _():
                    lax.fori_loop(0, 2, add, 0)

            @pl.when(beyond)
            def _(zd=zd):
                self.hop(p, zd, move).start()

    def step(self, i):
        depth = self.depth
        z = lax.axis_index("fsdp")
        for move in (1, -1):
            stage = z if move > 0 else depth - 1 - z
            p = i - stage * COLLECT_LAG

            @pl.when(jnp.logical_and(p >= 0, p < self.pairs))
            def _(p=p, move=move):
                self.flow(p, move)

    def result(self, p):
        z = lax.axis_index("fsdp")
        depth = self.depth
        whole = self.whole
        whole[...] = self.part[p, z].astype(F32)

        @pl.when(z > 0)
        def _():
            whole[...] = whole[...] + self.from_left[p, z].astype(F32)

        @pl.when(z < depth - 1)
        def _():
            whole[...] = whole[...] + self.from_right[p, z].astype(F32)

        return whole[...]

    def finish(self):
        depth = self.depth
        z = lax.axis_index("fsdp")

        def drain(p, carry):
            for zd in range(depth):
                for move in (1, -1):
                    @pl.when(zd > z if move > 0 else zd < z)
                    def _(zd=zd, move=move):
                        self.hop(p, zd, move).wait_send()
            return carry

        lax.fori_loop(0, self.pairs, drain, 0)


def backward_kernel(plan, collect, *refs):
    depth, rows, pairs = collect.depth, collect.rows, collect.pairs
    n = len(plan.views)
    ins, sources, (dq_ref, dk_ref, dv_ref), sums, swap, rest = split_refs(
        refs, 8, n, 3, n, len(collect.scratch))
    q_ref, k_ref, v_ref, keys, vals, lse_ref, att_ref, g_ref = ins
    plan.bind(sources, sums, rest)
    collect.bind(swap)
    z = lax.axis_index("fsdp")
    greet(plan.side, depth)
    plan.start()
    last = (depth - 1) * COLLECT_LAG

    def run(i, carry):
        @pl.when(i < pairs)
        def _():
            backward_pair(i, z, rows, depth, q_ref, k_ref, v_ref, keys, vals, lse_ref, att_ref,
                          g_ref, dq_ref, dk_ref, dv_ref, collect.part)

        collect.step(i)
        plan.step(i)

        @pl.when(jnp.logical_and(i >= last, i < last + pairs))
        def _():
            p = i - last
            cols = pl.ds(pl.multiple_of(p * PAIR, PAIR), PAIR)
            value = collect.result(p)
            dk_ref[pl.ds(0, rows), cols] = value[0].astype(BF)
            dv_ref[pl.ds(0, rows), cols] = value[1].astype(BF)

        return carry

    lax.fori_loop(0, max(pairs + last, plan.steps), run, 0)
    collect.finish()
    plan.finish()


def attention_backward(side, depth, q, k, v, keys, vals, lse, att, grad_att, grads, call_id):
    rows, width = q.shape[0] // 2, q.shape[1]
    plan, collect = Reduce(side, depth, grads), Collect(depth, rows, width // PAIR)
    vmem = pl.BlockSpec(memory_space=pltpu.VMEM)
    results = pl.pallas_call(
        functools.partial(backward_kernel, plan, collect),
        out_shape=(jax.ShapeDtypeStruct(q.shape, BF),) * 3 + tuple(plan.outs),
        in_specs=[vmem] * 8 + plan.in_specs,
        out_specs=(vmem,) * 3 + tuple(plan.out_specs),
        scratch_shapes=collect.scratch + plan.scratch,
        compiler_params=params(call_id, 62),
    )(q, k, v, keys, vals, lse, att, grad_att, *plan.views)
    return results[:3], results[3:]


def one_hot(ids, count):
    return (ids[:, None] == jnp.arange(count, dtype=jnp.int32)[None, :]).astype(BF)


def split_low(value):
    high = value.astype(BF)
    return (high, (value - high.astype(F32)).astype(BF))


def pick_weights(slot_ids, scores):
    slots = scores.shape[-1]
    count = jnp.sum(
        (slot_ids[..., None] == jnp.arange(slots, dtype=jnp.int32)).astype(F32), axis=2
    )
    named = count > 0.0
    top = jnp.max(jnp.where(named, scores, -jnp.inf), axis=-1, keepdims=True)
    raised = jnp.where(named, count * jnp.exp(scores - top), 0.0)
    return raised / jnp.sum(raised, axis=-1, keepdims=True)


def per_device(
    x_prompt,
    x_cont,
    cot_prompt,
    cot_cont,
    gain_attn,
    gain_mem,
    w_qkv,
    w_attn_out,
    w_mem_query,
    sub_keys,
    w_gate,
    w_mem_out,
    value_rows,
    request,
    slot_prompt,
    slot_cont,
):
    shard_rows, width = value_rows.shape
    owners, capacity = request.shape[2:]
    slots = owners * capacity
    rows = x_prompt.shape[1]
    cols = w_qkv.shape[2]
    asked = lax.all_to_all(request[:, 0], ALL, split_axis=1, concat_axis=1, tiled=True)
    serve_pick = one_hot(asked.transpose(1, 0, 2).reshape(-1), shard_rows)
    served = mm(serve_pick, value_rows).astype(BF).reshape(owners, 2 * capacity, width)
    table = lax.all_to_all(served, ALL, split_axis=0, concat_axis=0, tiled=True)
    table = table.reshape(owners, 2, capacity, width).transpose(1, 0, 2, 3).reshape(2, slots, width)

    side, depth = grid_of(lax.axis_size("dp"), lax.axis_size("fsdp"))
    (qkv_full,) = gather_weights(side, depth, (w_qkv,), 0)

    x_rows = jnp.concatenate([x_prompt[0], x_cont[0]], axis=0).astype(F32)
    dy_low = jnp.concatenate([cot_prompt[0], cot_cont[0]], axis=0)
    normed, inverse = normalize(x_rows, gain_attn)
    normed = normed.astype(BF)
    queries = mm(normed, qkv_full[0]).astype(BF)
    keys = mm(normed, qkv_full[1]).astype(BF)
    vals = mm(normed, qkv_full[2]).astype(BF)
    (att, lse, all_keys, all_vals), full = attention_forward(
        side,
        depth,
        queries,
        keys,
        vals,
        (w_attn_out, w_mem_query, sub_keys, w_gate, w_mem_out),
        1,
    )
    attn_out_full, query_full, keys_full, gate_full, mem_out_full = full
    hidden = x_rows + mm(att, attn_out_full)
    normed2, inverse2 = normalize(hidden, gain_mem)
    normed2 = normed2.astype(BF)

    mquery = mm(normed2, query_full).astype(BF)
    gate_pre = mm(normed2, gate_full)
    key_heads = keys_full.reshape(MH, 2, SUB, HALF)
    offsets = jnp.maximum(request[:, 0].reshape(2, slots), 0)
    picked = (jnp.arange(slots, dtype=jnp.int32) // capacity)[None] * shard_rows + offsets
    slot_ids = (slot_prompt[0], slot_cont[0])
    first, second, weights, mixing, memory_out = [], [], [], [], []
    for part in range(2):
        first.append(one_hot(picked[part] // SUB, SUB))
        second.append(one_hot(picked[part] % SUB, SUB))
        section = slice(part * rows, (part + 1) * rows)
        heads = []
        for head in range(MH):
            slot_keys = jnp.concatenate(
                [
                    mm(first[part], key_heads[head, 0]).astype(BF),
                    mm(second[part], key_heads[head, 1]).astype(BF),
                ],
                axis=1,
            )
            span = slice(head * 2 * HALF, (head + 1) * 2 * HALF)
            heads.append(mm_t(mquery[section, span], slot_keys))
        weights.append(pick_weights(slot_ids[part], jnp.stack(heads, axis=1)))
        mixing.append(jnp.sum(weights[part], axis=1).astype(BF))
        memory_out.append(mm(mixing[part], table[part]))
    memory_out = jnp.concatenate(memory_out, axis=0)
    sigmoid_gate = jax.nn.sigmoid(gate_pre)
    blended = (memory_out * (gate_pre * sigmoid_gate)).astype(BF)
    out = (hidden + mm(blended, mem_out_full)).astype(BF)

    grad_blend = mm_t(dy_low, mem_out_full)
    grad_mem_out = mm_l(blended, dy_low)
    grad_memory = (grad_blend * gate_pre * sigmoid_gate).astype(BF)
    grad_gate = (
        grad_blend * memory_out * sigmoid_gate * (1.0 + gate_pre * (1.0 - sigmoid_gate))
    ).astype(BF)
    slot_grads, grad_query, sub_grads = [], [], []
    for part in range(2):
        section = slice(part * rows, (part + 1) * rows)
        slot_grads.append(mm_l(mixing[part], grad_memory[section]).astype(BF))
        grad_mixing = mm_t(grad_memory[section], table[part])[:, None, :]
        pulled = weights[part] * grad_mixing
        grad_scores = pulled - weights[part] * jnp.sum(pulled, axis=-1, keepdims=True)
        high, low = split_low(grad_scores.reshape(rows * MH, slots))
        halves = [
            (mm(high, picker) + mm(low, picker)).astype(BF).reshape(rows, MH, SUB)
            for picker in (first[part], second[part])
        ]
        sub_grads.append(jnp.stack(halves, axis=2))
    sub_grads = jnp.concatenate(sub_grads, axis=0)
    grad_query = jnp.concatenate(
        [
            mm(sub_grads[:, head, half], key_heads[head, half]).astype(BF)
            for head in range(MH)
            for half in range(2)
        ],
        axis=1,
    )
    grad_keys = jnp.concatenate(
        [
            mm_l(
                sub_grads[:, head, half],
                mquery[:, (2 * head + half) * HALF : (2 * head + half + 1) * HALF],
            )
            for head in range(MH)
            for half in range(2)
        ],
        axis=0,
    )
    arrived = lax.all_to_all(
        jnp.stack([piece.reshape(owners, capacity, width) for piece in slot_grads], axis=1),
        ALL,
        split_axis=0,
        concat_axis=0,
        tiled=True,
    )
    grad_rows = mm_l(serve_pick, arrived.reshape(owners * 2 * capacity, width))
    grad_normed2 = mm_t(grad_query, query_full) + mm_t(grad_gate, gate_full)
    grad_query_w = mm_l(normed2, grad_query)
    grad_gate_w = mm_l(normed2, grad_gate)
    back, gain_mem_part = norm_backward(hidden, inverse2, gain_mem, grad_normed2)
    grad_hidden = dy_low.astype(F32) + back
    hidden_low = grad_hidden.astype(BF)
    grad_attn_out = mm_l(att, hidden_low)
    grad_att = mm_t(hidden_low, attn_out_full).astype(BF)
    block = cols // owners
    keys_low = grad_keys.astype(BF).reshape(owners, 2, block, HALF).transpose(0, 2, 1, 3)
    (grad_q, grad_k, grad_v), early = attention_backward(
        side,
        depth,
        queries,
        keys,
        vals,
        all_keys,
        all_vals,
        lse,
        att,
        grad_att,
        (
            grad_query_w.astype(BF),
            keys_low.reshape(cols, 2 * HALF),
            grad_gate_w.astype(BF),
            grad_mem_out.astype(BF),
            grad_attn_out.astype(BF),
        ),
        2,
    )
    grad_normed = (
        mm_t(grad_q, qkv_full[0]) + mm_t(grad_k, qkv_full[1]) + mm_t(grad_v, qkv_full[2])
    )
    grad_x, gain_attn_part = norm_backward(x_rows, inverse, gain_attn, grad_normed)
    grad_x = grad_hidden + grad_x
    grad_qkv = jnp.stack([mm_l(normed, piece) for piece in (grad_q, grad_k, grad_v)])

    gains = jnp.concatenate([gain_attn_part, gain_mem_part]).reshape(2 * cols // 128, 128)
    qkv_shard, gain_sums = reduce_grads(side, depth, (grad_qkv.astype(BF),), gains, 3)
    own = lax.axis_index("dp") * depth + lax.axis_index("fsdp")
    gain_shards = lax.dynamic_index_in_dim(
        gain_sums.reshape(2, owners, block), own, axis=1, keepdims=False
    )
    sub_shard = early[1].reshape(block, 2, HALF).transpose(1, 0, 2).reshape(2 * block, HALF)
    return (
        out[None, :rows],
        out[None, rows:],
        grad_x[None, :rows],
        grad_x[None, rows:],
        gain_shards[0],
        gain_shards[1],
        qkv_shard,
        early[4],
        early[0],
        sub_shard,
        early[2],
        early[3],
        grad_rows,
    )


def solution(mesh):
    in_specs = (
        P("dp", "fsdp", None),
        P("dp", "fsdp", None),
        P("dp", "fsdp", None),
        P("dp", "fsdp", None),
        P(),
        P(),
        P(None, "fsdp", None),
        P("fsdp", None),
        P("fsdp", None),
        P("fsdp", None),
        P("fsdp", None),
        P("fsdp", None),
        P(("dp", "fsdp"), None),
        P(None, ("dp", "fsdp"), None, None),
        P("dp", "fsdp", None, None),
        P("dp", "fsdp", None, None),
    )
    out_specs = (
        P("dp", "fsdp", None),
        P("dp", "fsdp", None),
        P("dp", "fsdp", None),
        P("dp", "fsdp", None),
        P(("dp", "fsdp")),
        P(("dp", "fsdp")),
        P(None, ("dp", "fsdp"), None),
        P(("dp", "fsdp"), None),
        P(("dp", "fsdp"), None),
        P(("dp", "fsdp"), None),
        P(("dp", "fsdp"), None),
        P(("dp", "fsdp"), None),
        P(("dp", "fsdp"), None),
    )
    return jax.shard_map(
        per_device, mesh=mesh, in_specs=in_specs, out_specs=out_specs, check_vma=False
    )
```

```python
import functools
import jax
import jax.numpy as jnp
from jax import lax
from jax.experimental import pallas as pl
from jax.experimental.pallas import tpu as pltpu
from jax.sharding import PartitionSpec as P
BF = jnp.bfloat16
F32 = jnp.float32
ALL = ("dp", "fsdp")
MESH = pl.DeviceIdType.MESH
LAG = 2
GATHER_LAG = 2
GATHER_RATE = 1
COLLECT_LAG = 2
AHEAD = 3
HOP_LAG = 1
PIECE = 1024
PAIR = 128
HDIM = 64
MH = 4
HALF = 512
SUB = 256
NEVER = -1e30


def mm(left, right):
    return jnp.dot(left, right, preferred_element_type=F32)


def mm_t(left, right):
    return lax.dot_general(left, right, (((1,), (1,)), ((), ())), preferred_element_type=F32)


def mm_l(left, right):
    return lax.dot_general(left, right, (((0,), (0,)), ((), ())), preferred_element_type=F32)


def normalize(matrix, gain_vec):
    inverse = lax.rsqrt(jnp.mean(matrix * matrix, axis=-1, keepdims=True) + 1e-05)
    return (matrix * inverse * gain_vec, inverse)


def norm_backward(matrix, inverse, gain_vec, grad_normed):
    scaled = gain_vec * grad_normed
    cubed = inverse * inverse * inverse
    grad_matrix = inverse * scaled - matrix * cubed * jnp.mean(
        matrix * scaled, axis=-1, keepdims=True
    )
    return (grad_matrix, jnp.sum(grad_normed * matrix * inverse, axis=0))


def grid_of(plane, depth):
    side = 1
    while 2 * side * side < plane:
        side += 1
    return side, depth


def place(side):
    dp = lax.axis_index("dp")
    return (dp // (2 * side), (dp // 2) % side, dp % 2, lax.axis_index("fsdp"))


def device_at(side, y, x, core, z):
    return ((y * side + x) * 2 + core, z)


def greet(side, depth):
    y, x, core, z = place(side)
    barrier = pltpu.get_barrier_semaphore()
    peers = [device_at(side, y, x, 1 - core, z)]
    for hop in range(1, side):
        peers.append(device_at(side, y, (x + hop) % side, core, z))
        peers.append(device_at(side, (y + hop) % side, x, core, z))
    for hop in range(1, depth):
        peers.append(device_at(side, y, x, core, (z + hop) % depth))
    for peer in peers:
        pl.semaphore_signal(barrier, inc=1, device_id=peer, device_id_type=MESH)
    pl.semaphore_wait(barrier, len(peers))


def remote(source, target, send_sem, recv_sem, peer):
    return pltpu.make_async_remote_copy(
        src_ref=source,
        dst_ref=target,
        send_sem=send_sem,
        recv_sem=recv_sem,
        device_id=peer,
        device_id_type=MESH,
    )


class Gather:
    def __init__(self, side, depth, shards):
        self.side, self.depth = side, depth
        self.views, self.outs, self.shapes, self.held, self.layout = [], [], [], [], []
        plane = 2 * side * side
        for shard in shards:
            rows, cols = shard.shape[-2:]
            block, width = rows // plane, min(cols, PIECE)
            lead = shard.shape[:-2]
            self.views.append(shard.reshape(lead + (side, side, 2, block, cols)))
            leads = range(lead[0]) if lead else (None,)
            self.layout.append(
                [(number, start) for number in leads for start in range(0, cols, width)]
            )
            self.outs.append(
                jax.ShapeDtypeStruct(lead + (depth, side, side, 2, block, cols), BF)
            )
            self.shapes.append(lead + (depth * rows, cols))
            self.held.append(
                pltpu.VMEM((len(self.layout[-1]), side, side, 2, block, width), BF)
            )
        self.count = count = sum(len(columns) for columns in self.layout)
        self.steps = count + depth - 2 + 3 * GATHER_LAG
        dma = pltpu.SemaphoreType.DMA
        self.scratch = self.held + [
            dma((count,)),
            dma((count,)),
            dma((count, depth)),
            dma((count, depth)),
            dma((count, depth)),
            dma((count, depth, side - 1)),
            dma((count, depth, side - 1)),
            dma((count, depth, side - 1)),
            dma((count, depth, side - 1)),
            dma((count, depth)),
            dma((count, depth)),
        ]

    def restore(self, full):
        return [one.reshape(shape) for one, shape in zip(full, self.shapes)]

    def bind(self, sources, outs, scratch):
        self.sources, self.results = sources, outs
        n_in = len(self.layout)
        self.holders = scratch[:n_in]
        (self.in_sem, self.out_sem, self.right_send, self.left_send, self.deep_recv,
         self.one_send, self.one_recv, self.two_send, self.two_recv, self.core_send,
         self.core_recv) = scratch[n_in:]
        self.pieces = []
        for number, columns in enumerate(self.layout):
            width = self.holders[number].shape[-1]
            width = width if sources[number].shape[-1] > width else None
            for inner, (lead, start) in enumerate(columns):
                self.pieces.append((number, lead, start, width, inner))

    def cut(self, refs, k, *spot):
        number, lead, start, width = self.pieces[k][:4]
        ref = refs[number] if lead is None else refs[number].at[lead]
        ref = ref.at[spot] if spot else ref
        if width is None:
            return ref
        return ref.at[(slice(None),) * (len(ref.shape) - 1) + (pl.ds(start, width),)]

    def along_z(self, k, zp, move, source=None):
        y, x, core, z = place(self.side)
        target = self.cut(self.results, k, zp, y, x, core)
        send = self.right_send if move > 0 else self.left_send
        return remote(target if source is None else source, target, send.at[k, zp],
                      self.deep_recv.at[k, zp], device_at(self.side, y, x, core, z + move))

    def one_copy(self, k, zp, hop):
        side = self.side
        y, x, core, z = place(side)
        peer = device_at(side, y, (x + hop) % side, core, z) if k % 2 == 0 else device_at(
            side, (y + hop) % side, x, core, z)
        ref = self.cut(self.results, k, zp, y, x, core)
        return remote(ref, ref, self.one_send.at[k, zp, hop - 1],
                      self.one_recv.at[k, zp, hop - 1], peer)

    def two_copy(self, k, zp, hop):
        side = self.side
        y, x, core, z = place(side)
        x_first = k % 2 == 0
        peer = device_at(side, (y + hop) % side, x, core, z) if x_first else device_at(
            side, y, (x + hop) % side, core, z)
        ref = (self.cut(self.results, k, zp, y, slice(None), core) if x_first
               else self.cut(self.results, k, zp, slice(None), x, core))
        return remote(ref, ref, self.two_send.at[k, zp, hop - 1],
                      self.two_recv.at[k, zp, hop - 1], peer)

    def core_copy(self, k, zp):
        y, x, core, z = place(self.side)
        ref = self.cut(self.results, k, zp, slice(None), slice(None), core)
        return remote(ref, ref, self.core_send.at[k, zp], self.core_recv.at[k, zp],
                      device_at(self.side, y, x, 1 - core, z))

    def take(self, k):
        number, inner = self.pieces[k][0], self.pieces[k][4]
        return pltpu.make_async_copy(self.cut(self.sources, k), self.holders[number].at[inner],
                                     self.in_sem.at[k])

    def put(self, k):
        z = place(self.side)[3]
        number, inner = self.pieces[k][0], self.pieces[k][4]
        return pltpu.make_async_copy(self.holders[number].at[inner],
                                     self.cut(self.results, k, z), self.out_sem.at[k])

    def start(self):
        y, x, core, z = place(self.side)
        for k in range(self.count):
            self.take(k).start()
            own = self.cut(self.sources, k, y, x, core)

            @pl.when(z < self.depth - 1)
            def _(k=k, own=own):
                self.along_z(k, z, 1, own).start()

            @pl.when(z > 0)
            def _(k=k, own=own):
                self.along_z(k, z, -1, own).start()

    def step(self, i):
        side, depth = self.side, self.depth
        z = place(side)[3]
        if i < self.count:
            self.take(i).wait()
            self.put(i).start()
        for stage in range(4):
            for distance in range(1, depth):
                k = i - stage * GATHER_LAG - (distance - 1)
                if not 0 <= k < self.count:
                    continue
                for sign in (1, -1):
                    zp = z + sign * distance

                    @pl.when(jnp.logical_and(zp >= 0, zp < depth))
                    def _(k=k, zp=zp, sign=sign, stage=stage):
                        self.arrival(stage, k, zp, sign)

    def arrival(self, stage, k, zp, sign):
        side, depth = self.side, self.depth
        z = place(side)[3]
        if stage == 0:
            self.along_z(k, zp, 1).wait_recv()

            @pl.when(z < depth - 1 if sign < 0 else z > 0)
            def _():
                self.along_z(k, zp, -sign).start()

            for hop in range(1, side):
                self.one_copy(k, zp, hop).start()
        elif stage == 1:
            for hop in range(1, side):
                self.one_copy(k, zp, hop).wait_recv()
            for hop in range(1, side):
                self.two_copy(k, zp, hop).start()
        elif stage == 2:
            for hop in range(1, side):
                self.two_copy(k, zp, hop).wait_recv()
            self.core_copy(k, zp).start()
        else:
            self.core_copy(k, zp).wait_recv()

    def finish(self):
        side, depth = self.side, self.depth
        z = place(side)[3]
        for k in range(self.count):
            self.put(k).wait()
            for zp in range(depth):
                @pl.when(jnp.logical_and(zp <= z, z < depth - 1))
                def _(k=k, zp=zp):
                    self.along_z(k, zp, 1).wait_send()

                @pl.when(jnp.logical_and(zp >= z, z > 0))
                def _(k=k, zp=zp):
                    self.along_z(k, zp, -1).wait_send()

                @pl.when(zp != z)
                def _(k=k, zp=zp):
                    for hop in range(1, side):
                        self.one_copy(k, zp, hop).wait_send()
                        self.two_copy(k, zp, hop).wait_send()
                    self.core_copy(k, zp).wait_send()


class Reduce:
    def __init__(self, side, depth, grads, gains=None):
        self.side, self.depth = side, depth
        self.layout, self.views, self.outs = [], [], []
        self.width = width = 1024
        devices = 2 * side * side * depth
        for grad in grads:
            rows, cols = grad.shape[-2:]
            self.block = block = rows // devices
            lead = grad.shape[:-2]
            self.views.append(grad.reshape(lead + (side, side, 2, depth, block, cols)))
            leads = range(lead[0]) if lead else (None,)
            self.layout.append(
                [(number, start) for number in leads for start in range(0, cols, width)]
            )
            self.outs.append(jax.ShapeDtypeStruct(lead + (block, cols), F32))
        self.count = count = sum(len(columns) for columns in self.layout)
        self.steps = count + 3 * LAG
        self.gains = gains is not None
        most = max(side, depth) - 1
        dma = pltpu.SemaphoreType.DMA
        self.scratch = [
            pltpu.VMEM((count, side, side, depth, block, width), BF),
            pltpu.VMEM((count, side, side, depth, block, width), BF),
            pltpu.VMEM((count, side - 1, side, depth, block, width), BF),
            pltpu.VMEM((count, side - 1, depth, block, width), BF),
            pltpu.VMEM((count, depth - 1, block, width), BF),
            pltpu.VMEM((count, block, width), F32),
            dma((count,)),
            dma((count,)),
            dma((count,)),
            dma((count, side - 1)),
            dma((count, side - 1)),
            dma((count, side - 1)),
            dma((count, side - 1)),
            dma((count, depth - 1)),
            dma((count, depth - 1)),
        ]
        if self.gains:
            self.views.append(gains)
            self.outs.append(jax.ShapeDtypeStruct(gains.shape, F32))
            self.scratch += [
                pltpu.VMEM((4,) + gains.shape, F32),
                pltpu.VMEM((4, most) + gains.shape, F32),
                dma((4, most)),
                dma((4, most)),
            ]
        any_space, vmem = pl.BlockSpec(memory_space=pl.ANY), pl.BlockSpec(memory_space=pltpu.VMEM)
        self.in_specs = [any_space] * len(self.layout) + [vmem] * self.gains
        self.out_specs = [vmem] * len(self.views)

    def bind(self, sources, outs, scratch):
        (self.mine, self.got_core, self.got_one, self.got_two, self.got_deep, self.total,
         self.local_sem, self.core_send, self.core_recv, self.one_send, self.one_recv,
         self.two_send, self.two_recv, self.deep_send, self.deep_recv) = scratch[:15]
        self.results = outs
        if self.gains:
            self.gain_in, self.gain_out = sources[-1], outs[-1]
            self.gain_sum, self.gain_got, self.gain_send, self.gain_recv = scratch[15:]
        self.pieces = []
        for number, columns in enumerate(self.layout):
            for lead, start in columns:
                ref = sources[number] if lead is None else sources[number].at[lead]
                self.pieces.append((ref, number, lead, start))

    def core_wait(self, k):
        y, x, core, z = place(self.side)
        return remote(self.got_core.at[k], self.got_core.at[k], self.core_send.at[k],
                      self.core_recv.at[k], device_at(self.side, y, x, 1 - core, z))

    def start(self):
        y, x, core, z = place(self.side)
        for k, (ref, _, _, start) in enumerate(self.pieces):
            spot = pl.ds(start, self.width)
            remote(ref.at[:, :, 1 - core, :, :, spot], self.got_core.at[k], self.core_send.at[k],
                   self.core_recv.at[k], device_at(self.side, y, x, 1 - core, z)).start()
            pltpu.make_async_copy(ref.at[:, :, core, :, :, spot], self.mine.at[k],
                                  self.local_sem.at[k]).start()
        if self.gains:
            self.gain_copy(0, 0).start()

    def one_copy(self, k, hop, x_first):
        side = self.side
        y, x, core, z = place(side)
        peer = device_at(side, y, (x + hop) % side, core, z) if x_first else device_at(
            side, (y + hop) % side, x, core, z)
        source = (self.mine.at[k, :, (x + hop) % side] if x_first
                  else self.mine.at[k, (y + hop) % side])
        return remote(source, self.got_one.at[k, hop - 1], self.one_send.at[k, hop - 1],
                      self.one_recv.at[k, hop - 1], peer)

    def two_copy(self, k, hop, x_first):
        side = self.side
        y, x, core, z = place(side)
        peer = device_at(side, (y + hop) % side, x, core, z) if x_first else device_at(
            side, y, (x + hop) % side, core, z)
        source = (self.mine.at[k, (y + hop) % side, x] if x_first
                  else self.mine.at[k, y, (x + hop) % side])
        return remote(source, self.got_two.at[k, hop - 1], self.two_send.at[k, hop - 1],
                      self.two_recv.at[k, hop - 1], peer)

    def deep_copy(self, k, hop):
        y, x, core, z = place(self.side)
        there = (z + hop) % self.depth
        return remote(self.mine.at[k, y, x, there], self.got_deep.at[k, hop - 1],
                      self.deep_send.at[k, hop - 1], self.deep_recv.at[k, hop - 1],
                      device_at(self.side, y, x, core, there))

    def gain_count(self, stage):
        return (1, self.side - 1, self.side - 1, self.depth - 1)[stage]

    def gain_copy(self, stage, number):
        side, depth, hop = self.side, self.depth, number + 1
        y, x, core, z = place(side)
        peer = (
            device_at(side, y, x, 1 - core, z),
            device_at(side, y, (x + hop) % side, core, z),
            device_at(side, (y + hop) % side, x, core, z),
            device_at(side, y, x, core, (z + hop) % depth),
        )[stage]
        source = self.gain_in if stage == 0 else self.gain_sum.at[stage - 1]
        return remote(source, self.gain_got.at[stage, number], self.gain_send.at[stage, number],
                      self.gain_recv.at[stage, number], peer)

    def both_orders(self, k, action):
        @pl.when(k % 2 == 0)
        def _():
            action(True)

        @pl.when(k % 2 == 1)
        def _():
            action(False)

    def added(self, base, others):
        if len(others) == 1:
            return base + others[0]
        value = base.astype(F32)
        for other in others:
            value = value + other.astype(F32)
        return value.astype(base.dtype)

    def after_core(self, k):
        side, depth, mine, got = self.side, self.depth, self.mine, self.got_core
        self.core_wait(k).wait_recv()
        pltpu.make_async_copy(got.at[k], mine.at[k], self.local_sem.at[k]).wait()

        def add(index, carry):
            spot = (k, index // (side * depth), (index // depth) % side, index % depth)
            mine[spot] = mine[spot] + got[spot]
            return carry

        lax.fori_loop(0, side * side * depth, add, 0)

        def send(x_first):
            for hop in range(1, side):
                self.one_copy(k, hop, x_first).start()

        self.both_orders(k, send)

    def after_one(self, k):
        side, depth, mine = self.side, self.depth, self.mine
        y, x, core, z = place(side)

        def finish(x_first):
            for hop in range(1, side):
                self.one_copy(k, hop, x_first).wait_recv()

            def add(index, carry):
                a, c = index // depth, index % depth
                spot = (k, a, x, c) if x_first else (k, y, a, c)
                mine[spot] = self.added(
                    mine[spot], [self.got_one[k, hop, a, c] for hop in range(side - 1)]
                )
                return carry

            lax.fori_loop(0, side * depth, add, 0)
            for hop in range(1, side):
                self.two_copy(k, hop, x_first).start()

        self.both_orders(k, finish)

    def after_two(self, k):
        side, depth, mine = self.side, self.depth, self.mine
        y, x, core, z = place(side)

        def finish(x_first):
            for hop in range(1, side):
                self.two_copy(k, hop, x_first).wait_recv()

        self.both_orders(k, finish)

        def add(c, carry):
            mine[k, y, x, c] = self.added(
                mine[k, y, x, c], [self.got_two[k, hop, c] for hop in range(side - 1)]
            )
            return carry

        lax.fori_loop(0, depth, add, 0)
        for hop in range(1, depth):
            self.deep_copy(k, hop).start()

    def after_deep(self, k):
        y, x, core, z = place(self.side)
        for hop in range(1, self.depth):
            self.deep_copy(k, hop).wait_recv()
        value = self.mine[k, y, x, z].astype(F32)
        for hop in range(self.depth - 1):
            value = value + self.got_deep[k, hop].astype(F32)
        self.total[k] = value

    def step(self, i):
        stages = (self.after_core, self.after_one, self.after_two, self.after_deep)
        for number, action in enumerate(stages):
            lag = number * LAG

            @pl.when(jnp.logical_and(i >= lag, i < self.count + lag))
            def _(lag=lag, action=action):
                action(i - lag)

        for stage in range(4 if self.gains else 0):
            @pl.when(i == stage + 1)
            def _(stage=stage):
                value = self.gain_in[...] if stage == 0 else self.gain_sum[stage - 1]
                for number in range(self.gain_count(stage)):
                    self.gain_copy(stage, number).wait_recv()
                    value = value + self.gain_got[stage, number]
                self.gain_sum[stage] = value
                if stage < 3:
                    for number in range(self.gain_count(stage + 1)):
                        self.gain_copy(stage + 1, number).start()

    def finish(self):
        if self.gains:
            self.gain_out[...] = self.gain_sum[3]
        for k, (_, number, lead, start) in enumerate(self.pieces):
            spot = (slice(None), pl.ds(start, self.width))
            if lead is None:
                self.results[number][spot] = self.total[k]
            else:
                self.results[number][(lead,) + spot] = self.total[k]

        def drain(k, carry):
            self.core_wait(k).wait_send()

            def sent(x_first):
                for hop in range(1, self.side):
                    self.one_copy(k, hop, x_first).wait_send()
                    self.two_copy(k, hop, x_first).wait_send()

            self.both_orders(k, sent)
            for hop in range(1, self.depth):
                self.deep_copy(k, hop).wait_send()
            return carry

        lax.fori_loop(0, self.count, drain, 0)
        for stage in range(4 if self.gains else 0):
            for number in range(self.gain_count(stage)):
                self.gain_copy(stage, number).wait_send()


def split_refs(refs, *counts):
    groups, at = [], 0
    for count in counts:
        groups.append(refs[at : at + count])
        at += count
    return groups + [refs[at:]]


def params(call_id, mib):
    return pltpu.CompilerParams(
        collective_id=call_id, has_side_effects=True, vmem_limit_bytes=mib * 1024 * 1024
    )


def gather_kernel(plan, slots, rows, *refs):
    n = len(plan.views)
    (picks_ref,), sources, (counts_ref,), outs, scratch = split_refs(refs, 1, n, 1, n)
    plan.bind(sources, outs, scratch)
    blocks = picks_ref.shape[1] // 128
    turns = max(plan.steps, blocks)
    greet(plan.side, plan.depth)
    plan.start()

    def run(i, carry):
        for number in range(plan.steps):
            @pl.when(i == number)
            def _(number=number):
                plan.step(number)

        @pl.when(i < blocks)
        def _():
            count_block(i, rows, slots, picks_ref, counts_ref)

        return carry

    lax.fori_loop(0, turns, run, 0)
    plan.finish()


def gather_and_count(side, depth, shards, picks, slots, rows, call_id):
    plan = Gather(side, depth, shards)
    any_space, vmem = pl.BlockSpec(memory_space=pl.ANY), pl.BlockSpec(memory_space=pltpu.VMEM)
    results = pl.pallas_call(
        functools.partial(gather_kernel, plan, slots, rows),
        out_shape=(jax.ShapeDtypeStruct((2, MH, slots, rows), BF),) + tuple(plan.outs),
        in_specs=[vmem] + [any_space] * len(plan.views),
        out_specs=(vmem,) + (any_space,) * len(plan.views),
        scratch_shapes=plan.scratch,
        compiler_params=params(call_id, 32),
    )(picks, *plan.views)
    return results[0], plan.restore(results[1:])


def reduce_kernel(plan, *refs):
    n = len(plan.views)
    sources, outs, scratch = split_refs(refs, n, n)
    plan.bind(sources, outs, scratch)
    greet(plan.side, plan.depth)
    plan.start()

    def run(i, carry):
        plan.step(i)
        return carry

    lax.fori_loop(0, max(plan.steps, 5), run, 0)
    plan.finish()


def reduce_grads(side, depth, grads, gains, call_id):
    plan = Reduce(side, depth, grads, gains)
    return pl.pallas_call(
        functools.partial(reduce_kernel, plan),
        out_shape=tuple(plan.outs),
        in_specs=plan.in_specs,
        out_specs=tuple(plan.out_specs),
        scratch_shapes=plan.scratch,
        compiler_params=params(call_id, 60),
    )(*plan.views)


def half_masks(width):
    lane = lax.broadcasted_iota(jnp.int32, (1, width), 1)
    return (lane < width // 2, lane >= width // 2)


def dot_rows(left, right):
    return lax.dot_general(left, right, (((1,), (1,)), ((), ())), preferred_element_type=F32)


def dot_first(left, right):
    return lax.dot_general(left, right, (((0,), (0,)), ((), ())), preferred_element_type=F32)


def dot_plain(left, right):
    return lax.dot_general(left, right, (((1,), (0,)), ((), ())), preferred_element_type=F32)


def prompt_mask(scores, chunk, z, rows):
    key = lax.broadcasted_iota(jnp.int32, scores.shape, 0) + chunk * rows
    query = lax.broadcasted_iota(jnp.int32, scores.shape, 1)
    seen = jnp.logical_or(query >= rows, key <= query + z * rows)
    return jnp.where(seen, scores, NEVER)


def own_mask(scores):
    key = lax.broadcasted_iota(jnp.int32, scores.shape, 0)
    query = lax.broadcasted_iota(jnp.int32, scores.shape, 1)
    return jnp.where(key <= query, scores, NEVER)


def forward_pair(p, z, rows, depth, q_ref, k_ref, v_ref, keys, vals, att_ref, lse_ref):
    cols = pl.ds(pl.multiple_of(p * PAIR, PAIR), PAIR)
    q_pair = q_ref[:, cols] * jnp.asarray(0.125, BF)
    k_own, v_own = k_ref[pl.ds(rows, rows), cols], v_ref[pl.ds(rows, rows), cols]
    outs = []
    for head, mask in enumerate(half_masks(PAIR)):
        q_head = jnp.where(mask, q_pair, jnp.zeros_like(q_pair))
        scores = [
            prompt_mask(dot_rows(keys[p, chunk], q_head), chunk, z, rows) for chunk in range(depth)
        ]
        own = own_mask(dot_rows(k_own, q_head[rows:]))
        top = jnp.max(scores[0], axis=0, keepdims=True)
        for piece in scores[1:]:
            top = jnp.maximum(top, jnp.max(piece, axis=0, keepdims=True))
        top_c = jnp.maximum(top[:, rows:], jnp.max(own, axis=0, keepdims=True))
        top = jnp.concatenate([top[:, :rows], top_c], axis=1)
        total = jnp.zeros_like(top)
        out = jnp.zeros((PAIR, 2 * rows), F32)
        for chunk in range(depth):
            expo = jnp.exp(scores[chunk] - top)
            total = total + jnp.sum(expo, axis=0, keepdims=True)
            out = out + dot_first(vals[p, chunk], expo.astype(BF))
        expo = jnp.exp(own - top_c)
        total_c = total[:, rows:] + jnp.sum(expo, axis=0, keepdims=True)
        out_c = out[:, rows:] + dot_first(v_own, expo.astype(BF))
        total = jnp.concatenate([total[:, :rows], total_c], axis=1)
        out = jnp.concatenate([out[:, :rows], out_c], axis=1) / total
        lse_ref[pl.ds(2 * p + head, 1), :] = top + jnp.log(total)
        outs.append(out[head * HDIM : (head + 1) * HDIM])
    att_ref[:, cols] = jnp.concatenate(outs, axis=0).T.astype(BF)


def backward_pair(p, z, rows, depth, q_ref, k_ref, v_ref, keys, vals, lse_ref, att_ref, g_ref,
                  dq_ref, dk_ref, dv_ref, part):
    cols = pl.ds(pl.multiple_of(p * PAIR, PAIR), PAIR)
    own_rows = pl.ds(rows, rows)
    q_pair = q_ref[:, cols] * jnp.asarray(0.125, BF)
    g_pair = g_ref[:, cols]
    k_own, v_own = k_ref[own_rows, cols], v_ref[own_rows, cols]
    pulled = (g_pair.astype(F32) * att_ref[:, cols].astype(F32)).T
    masks = half_masks(PAIR)
    q_heads = [jnp.where(mask, q_pair, jnp.zeros_like(q_pair)) for mask in masks]
    g_heads = [jnp.where(mask, g_pair, jnp.zeros_like(g_pair)) for mask in masks]
    lses = [lse_ref[pl.ds(2 * p + head, 1), :] for head in range(2)]
    deltas = [
        jnp.sum(pulled[head * HDIM : (head + 1) * HDIM], axis=0, keepdims=True)
        for head in range(2)
    ]
    dq = [jnp.zeros((PAIR, 2 * rows), F32) for _ in range(2)]
    for chunk in range(depth):
        dk = jnp.zeros((rows, PAIR), F32)
        dv = jnp.zeros((rows, PAIR), F32)
        k_chunk, v_chunk = keys[p, chunk], vals[p, chunk]
        for head in range(2):
            scores = prompt_mask(dot_rows(k_chunk, q_heads[head]), chunk, z, rows)
            prob = jnp.exp(scores - lses[head])
            d_prob = dot_rows(v_chunk, g_heads[head])
            d_score = (prob * (d_prob - deltas[head])).astype(BF)
            dv = dv + dot_plain(prob.astype(BF), g_heads[head])
            dk = dk + dot_plain(d_score, q_heads[head])
            dq[head] = dq[head] + dot_first(k_chunk, d_score)
        part[p, chunk, 0] = dk.astype(BF)
        part[p, chunk, 1] = dv.astype(BF)
    dk = jnp.zeros((rows, PAIR), F32)
    dv = jnp.zeros((rows, PAIR), F32)
    for head in range(2):
        q_head, g_head = q_heads[head][rows:], g_heads[head][rows:]
        scores = own_mask(dot_rows(k_own, q_head))
        prob = jnp.exp(scores - lses[head][:, rows:])
        d_prob = dot_rows(v_own, g_head)
        d_score = (prob * (d_prob - deltas[head][:, rows:])).astype(BF)
        dv = dv + dot_plain(prob.astype(BF), g_head)
        dk = dk + dot_plain(d_score, q_head)
        more = dot_first(k_own, d_score)
        dq[head] = jnp.concatenate([dq[head][:, :rows], dq[head][:, rows:] + more], axis=1)
    dk_ref[own_rows, cols] = dk.astype(BF)
    dv_ref[own_rows, cols] = dv.astype(BF)
    both = jnp.concatenate([dq[0][:HDIM], dq[1][HDIM:]], axis=0) * 0.125
    dq_ref[:, cols] = both.T.astype(BF)


class Exchange:
    def __init__(self, depth, rows, pairs):
        self.depth, self.rows, self.pairs = depth, rows, pairs
        dma = pltpu.SemaphoreType.DMA
        self.scratch = [dma((2, 2, pairs, depth)), dma((2, pairs, depth))]

    def bind(self, owned, gathered, scratch):
        self.owned, self.gathered = owned, gathered
        self.send_sem, self.recv_sem = scratch

    def hop(self, kind, p, zp, move, own=False):
        target = self.gathered[kind].at[p, zp]
        cols = pl.ds(pl.multiple_of(p * PAIR, PAIR), PAIR)
        source = self.owned[kind].at[pl.ds(0, self.rows), cols] if own else target
        z = lax.axis_index("fsdp")
        return remote(source, target, self.send_sem.at[kind, (move + 1) // 2, p, zp],
                      self.recv_sem.at[kind, p, zp], (lax.axis_index("dp"), z + move))

    def offer(self, p):
        z = lax.axis_index("fsdp")
        for move in (1, -1):
            @pl.when(z < self.depth - 1 if move > 0 else z > 0)
            def _(move=move):
                for kind in range(2):
                    self.hop(kind, p, z, move, own=True).start()
        cols = pl.ds(pl.multiple_of(p * PAIR, PAIR), PAIR)
        for kind in range(2):
            self.gathered[kind][p, z] = self.owned[kind][pl.ds(0, self.rows), cols]

    def step(self, i):
        z = lax.axis_index("fsdp")
        for distance in range(1, self.depth):
            p = i - (distance - 1) * HOP_LAG
            for sign in (1, -1):
                zp = z + sign * distance
                seen = jnp.logical_and(zp >= 0, zp < self.depth)

                @pl.when(jnp.logical_and(seen, jnp.logical_and(p >= 0, p < self.pairs)))
                def _(p=p, zp=zp, sign=sign):
                    for kind in range(2):
                        self.hop(kind, p, zp, 1).wait_recv()

                    @pl.when(z < self.depth - 1 if sign < 0 else z > 0)
                    def _():
                        for kind in range(2):
                            self.hop(kind, p, zp, -sign).start()

    def finish(self):
        z = lax.axis_index("fsdp")

        def drain(p, carry):
            for zp in range(self.depth):
                for move in (1, -1):
                    far = zp <= z if move > 0 else zp >= z
                    inner = z < self.depth - 1 if move > 0 else z > 0

                    @pl.when(jnp.logical_and(far, inner))
                    def _(zp=zp, move=move):
                        for kind in range(2):
                            self.hop(kind, p, zp, move).wait_send()
            return carry

        lax.fori_loop(0, self.pairs, drain, 0)


def forward_kernel(gather, exchange, *refs):
    depth, rows, pairs = exchange.depth, exchange.rows, exchange.pairs
    n = len(gather.views)
    (q_ref, k_ref, v_ref), shards, (att_ref, lse_ref, keys, vals), full, swap, rest = split_refs(
        refs, 3, n, 4, n, len(exchange.scratch))
    gather.bind(shards, full, rest)
    exchange.bind((k_ref, v_ref), (keys, vals), swap)
    z = lax.axis_index("fsdp")
    greet(gather.side, depth)
    ahead = min(AHEAD, pairs)
    for p in range(ahead):
        exchange.offer(p)
    gather.start()
    delay = (depth - 2) * HOP_LAG + 1
    turns = pairs + delay

    def run(i, carry):
        @pl.when(i + ahead < pairs)
        def _():
            exchange.offer(i + ahead)

        exchange.step(i)
        for turn in range(turns):
            @pl.when(i == turn)
            def _(turn=turn):
                for number in range(turn * GATHER_RATE, min((turn + 1) * GATHER_RATE, gather.steps)):
                    gather.step(number)

        @pl.when(i >= delay)
        def _():
            forward_pair(i - delay, z, rows, depth, q_ref, k_ref, v_ref, keys, vals, att_ref,
                         lse_ref)

        return carry

    lax.fori_loop(0, turns, run, 0)
    for number in range(turns * GATHER_RATE, gather.steps):
        gather.step(number)
    exchange.finish()
    gather.finish()


def attention_forward(side, depth, q, k, v, shards, call_id):
    rows, width = q.shape[0] // 2, q.shape[1]
    pairs = width // PAIR
    gather, exchange = Gather(side, depth, shards), Exchange(depth, rows, pairs)
    any_space, vmem = pl.BlockSpec(memory_space=pl.ANY), pl.BlockSpec(memory_space=pltpu.VMEM)
    spread = jax.ShapeDtypeStruct((pairs, depth, rows, PAIR), BF)
    results = pl.pallas_call(
        functools.partial(forward_kernel, gather, exchange),
        out_shape=(
            jax.ShapeDtypeStruct(q.shape, BF),
            jax.ShapeDtypeStruct((2 * pairs, 2 * rows), F32),
            spread,
            spread,
        )
        + tuple(gather.outs),
        in_specs=[vmem] * 3 + [any_space] * len(gather.views),
        out_specs=(vmem,) * 4 + (any_space,) * len(gather.views),
        scratch_shapes=exchange.scratch + gather.scratch,
        compiler_params=params(call_id, 56),
    )(q, k, v, *gather.views)
    return results[:4], gather.restore(results[4:])


class Collect:
    def __init__(self, depth, rows, pairs):
        self.depth, self.rows, self.pairs = depth, rows, pairs
        dma = pltpu.SemaphoreType.DMA
        shape = (pairs, depth, 2, rows, PAIR)
        self.scratch = [
            pltpu.VMEM(shape, BF),
            pltpu.VMEM(shape, BF),
            pltpu.VMEM(shape, BF),
            pltpu.VMEM((2, rows, PAIR), F32),
            dma((2, pairs, depth)),
            dma((2, pairs, depth)),
        ]
        self.steps = pairs + (depth - 1) * COLLECT_LAG + 1

    def bind(self, scratch):
        (self.part, self.from_left, self.from_right, self.whole, self.send_sem,
         self.recv_sem) = scratch

    def hop(self, p, zd, move):
        z = lax.axis_index("fsdp")
        target = self.from_left if move > 0 else self.from_right
        way = (move + 1) // 2
        return remote(self.part.at[p, zd], target.at[p, zd], self.send_sem.at[way, p, zd],
                      self.recv_sem.at[way, p, zd], (lax.axis_index("dp"), z + move))

    def flow(self, p, move):
        depth = self.depth
        z = lax.axis_index("fsdp")
        first = z == 0 if move > 0 else z == depth - 1
        arrived = self.from_left if move > 0 else self.from_right
        for zd in range(depth - 1, -1, -1) if move > 0 else range(depth):
            beyond = zd > z if move > 0 else zd < z

            @pl.when(jnp.logical_and(jnp.logical_not(first), jnp.logical_or(beyond, zd == z)))
            def _(zd=zd):
                self.hop(p, zd, move).wait_recv()

                def add(part, carry):
                    self.part[p, zd, part] = self.part[p, zd, part] + arrived[p, zd, part]
                    return carry

                @pl.when(zd != z)
                def _():
                    lax.fori_loop(0, 2, add, 0)

            @pl.when(beyond)
            def _(zd=zd):
                self.hop(p, zd, move).start()

    def step(self, i):
        depth = self.depth
        z = lax.axis_index("fsdp")
        for move in (1, -1):
            stage = z if move > 0 else depth - 1 - z
            p = i - stage * COLLECT_LAG

            @pl.when(jnp.logical_and(p >= 0, p < self.pairs))
            def _(p=p, move=move):
                self.flow(p, move)

    def result(self, p):
        z = lax.axis_index("fsdp")
        depth = self.depth
        whole = self.whole
        whole[...] = self.part[p, z].astype(F32)

        @pl.when(z > 0)
        def _():
            whole[...] = whole[...] + self.from_left[p, z].astype(F32)

        @pl.when(z < depth - 1)
        def _():
            whole[...] = whole[...] + self.from_right[p, z].astype(F32)

        return whole[...]

    def finish(self):
        depth = self.depth
        z = lax.axis_index("fsdp")

        def drain(p, carry):
            for zd in range(depth):
                for move in (1, -1):
                    @pl.when(zd > z if move > 0 else zd < z)
                    def _(zd=zd, move=move):
                        self.hop(p, zd, move).wait_send()
            return carry

        lax.fori_loop(0, self.pairs, drain, 0)


def backward_kernel(plan, collect, *refs):
    depth, rows, pairs = collect.depth, collect.rows, collect.pairs
    n = len(plan.views)
    ins, sources, (dq_ref, dk_ref, dv_ref), sums, swap, rest = split_refs(
        refs, 8, n, 3, n, len(collect.scratch))
    q_ref, k_ref, v_ref, keys, vals, lse_ref, att_ref, g_ref = ins
    plan.bind(sources, sums, rest)
    collect.bind(swap)
    z = lax.axis_index("fsdp")
    greet(plan.side, depth)
    plan.start()
    last = (depth - 1) * COLLECT_LAG

    def run(i, carry):
        @pl.when(i < pairs)
        def _():
            backward_pair(i, z, rows, depth, q_ref, k_ref, v_ref, keys, vals, lse_ref, att_ref,
                          g_ref, dq_ref, dk_ref, dv_ref, collect.part)

        collect.step(i)
        plan.step(i)

        @pl.when(jnp.logical_and(i >= last, i < last + pairs))
        def _():
            p = i - last
            cols = pl.ds(pl.multiple_of(p * PAIR, PAIR), PAIR)
            value = collect.result(p)
            dk_ref[pl.ds(0, rows), cols] = value[0].astype(BF)
            dv_ref[pl.ds(0, rows), cols] = value[1].astype(BF)

        return carry

    lax.fori_loop(0, max(pairs + last, plan.steps), run, 0)
    collect.finish()
    plan.finish()


def attention_backward(side, depth, q, k, v, keys, vals, lse, att, grad_att, grads, call_id):
    rows, width = q.shape[0] // 2, q.shape[1]
    plan, collect = Reduce(side, depth, grads), Collect(depth, rows, width // PAIR)
    vmem = pl.BlockSpec(memory_space=pltpu.VMEM)
    results = pl.pallas_call(
        functools.partial(backward_kernel, plan, collect),
        out_shape=(jax.ShapeDtypeStruct(q.shape, BF),) * 3 + tuple(plan.outs),
        in_specs=[vmem] * 8 + plan.in_specs,
        out_specs=(vmem,) * 3 + tuple(plan.out_specs),
        scratch_shapes=collect.scratch + plan.scratch,
        compiler_params=params(call_id, 62),
    )(q, k, v, keys, vals, lse, att, grad_att, *plan.views)
    return results[:3], results[3:]


def count_block(b, rows, slots, picks_ref, counts_ref):
    low, per_word, bits = 16, 5, 6
    groups = -(-(slots // low) // per_word)
    per_head = rows // 128
    cols = pl.ds(pl.multiple_of(b * 128, 128), 128)
    picks = picks_ref[:, cols]
    high = jnp.right_shift(picks, 4)
    group = jnp.right_shift(high * 13, 6)
    word = group * low + jnp.bitwise_and(picks, low - 1)
    unit = jnp.left_shift(jnp.ones_like(picks), bits * (high - per_word * group))
    spot = lax.broadcasted_iota(jnp.int32, (groups * low, 128), 0)
    words = jnp.zeros((groups * low, 128), jnp.int32)
    for pick in range(picks.shape[0]):
        words = words + jnp.where(spot == word[pick : pick + 1], unit[pick : pick + 1], 0)
    part, head = b // (per_head * MH), (b // per_head) % MH
    lanes = pl.ds(pl.multiple_of((b % per_head) * 128, 128), 128)
    for tile in range(slots // low):
        piece = words[(tile // per_word) * low : (tile // per_word + 1) * low]
        count = jnp.bitwise_and(jnp.right_shift(piece, bits * (tile % per_word)), 2**bits - 1)
        counts_ref[part, head, pl.ds(tile * low, low), lanes] = count.astype(F32).astype(BF)


def selector(ids_ref, index, count):
    ids = ids_ref[pl.ds(index, 1), :]
    spot = lax.broadcasted_iota(jnp.int32, (count, ids.shape[1]), 0)
    return jnp.where(spot == ids, 1.0, 0.0).astype(BF)


def picks_kernel(ids_ref, counts_ref, query_ref, keys_ref, weight_ref, mixing_ref, total):
    part, head = pl.program_id(0), pl.program_id(1)
    scores = None
    for half in range(2):
        pick = selector(ids_ref, 2 * part + half, SUB)
        slot_keys = dot_first(pick, keys_ref[half * SUB : (half + 1) * SUB]).astype(BF)
        piece = dot_rows(slot_keys, query_ref[:, half * HALF : (half + 1) * HALF])
        scores = piece if scores is None else scores + piece
    count = counts_ref[0, 0].astype(F32)
    named = count > 0.0
    top = jnp.max(jnp.where(named, scores, -jnp.inf), axis=0, keepdims=True)
    raised = jnp.where(named, count * jnp.exp(scores - top), 0.0)
    weight = raised / jnp.sum(raised, axis=0, keepdims=True)
    weight_ref[0, 0] = weight

    @pl.when(head == 0)
    def _():
        total[...] = weight

    @pl.when(head > 0)
    def _():
        total[...] = total[...] + weight

    @pl.when(head == MH - 1)
    def _():
        mixing_ref[0] = total[...].astype(BF)


def slot_weights(ids, counts, mquery, keys_full):
    slots, rows = counts.shape[2:]
    return pl.pallas_call(
        picks_kernel,
        grid=(2, MH),
        out_shape=(
            jax.ShapeDtypeStruct(counts.shape, F32),
            jax.ShapeDtypeStruct((2, slots, rows), BF),
        ),
        in_specs=[
            pl.BlockSpec(ids.shape, lambda u, m: (0, 0)),
            pl.BlockSpec((1, 1, slots, rows), lambda u, m: (u, m, 0, 0)),
            pl.BlockSpec((rows, 2 * HALF), lambda u, m: (u, m)),
            pl.BlockSpec((2 * SUB, HALF), lambda u, m: (m, 0)),
        ],
        out_specs=(
            pl.BlockSpec((1, 1, slots, rows), lambda u, m: (u, m, 0, 0)),
            pl.BlockSpec((1, slots, rows), lambda u, m: (u, 0, 0)),
        ),
        scratch_shapes=[pltpu.VMEM((slots, rows), F32)],
        cost_estimate=pl.CostEstimate(
            flops=2 * 2 * MH * slots * 2 * HALF * (SUB + rows),
            bytes_accessed=24 * 2**20,
            transcendentals=2 * MH * slots * rows,
        ),
    )(ids, counts, mquery, keys_full)


def picks_back_kernel(block, ids_ref, weight_ref, table_ref, memory_ref, query_ref, keys_ref,
                      grad_query_ref, grad_keys_ref, grad_mixing, total):
    head, part = pl.program_id(0), pl.program_id(1)

    @pl.when(head == 0)
    def _():
        grad_mixing[part] = dot_rows(table_ref[0], memory_ref[...])

    weight = weight_ref[0, 0]
    pulled = weight * grad_mixing[part]
    grad = pulled - weight * jnp.sum(pulled, axis=0, keepdims=True)
    high = grad.astype(BF)
    low = (grad - high.astype(F32)).astype(BF)
    for half in range(2):
        pick = selector(ids_ref, 2 * part + half, SUB)
        sub = (dot_plain(pick, high) + dot_plain(pick, low)).astype(BF)
        span = slice(half * HALF, (half + 1) * HALF)
        keys = keys_ref[half * SUB : (half + 1) * SUB]
        grad_query_ref[:, span] = dot_first(sub, keys).astype(BF)
        piece = dot_plain(sub, query_ref[:, span])
        rows = slice(half * SUB, (half + 1) * SUB)

        @pl.when(part == 0)
        def _(piece=piece, rows=rows):
            total[rows] = piece

        @pl.when(part == 1)
        def _(piece=piece, rows=rows):
            total[rows] = total[rows] + piece

    @pl.when(part == 1)
    def _():
        for shard in range(SUB // block):
            for side in range(2):
                start = (2 * shard + side) * block
                grad_keys_ref[shard * block : (shard + 1) * block, side * HALF : (side + 1) * HALF] = (
                    total[start : start + block].astype(BF))


def slot_weights_back(ids, weights, table, grad_memory, mquery, keys_full, block):
    slots, rows = weights.shape[2:]
    width = table.shape[2]
    return pl.pallas_call(
        functools.partial(picks_back_kernel, block),
        grid=(MH, 2),
        out_shape=(
            jax.ShapeDtypeStruct(mquery.shape, BF),
            jax.ShapeDtypeStruct((MH * SUB, 2 * HALF), BF),
        ),
        in_specs=[
            pl.BlockSpec(ids.shape, lambda m, u: (0, 0)),
            pl.BlockSpec((1, 1, slots, rows), lambda m, u: (u, m, 0, 0)),
            pl.BlockSpec((1, slots, width), lambda m, u: (jnp.where(m == 0, u, 1), 0, 0)),
            pl.BlockSpec((rows, width), lambda m, u: (jnp.where(m == 0, u, 1), 0)),
            pl.BlockSpec((rows, 2 * HALF), lambda m, u: (u, m)),
            pl.BlockSpec((2 * SUB, HALF), lambda m, u: (m, 0)),
        ],
        out_specs=(
            pl.BlockSpec((rows, 2 * HALF), lambda m, u: (u, m)),
            pl.BlockSpec((SUB, 2 * HALF), lambda m, u: (m, 0)),
        ),
        scratch_shapes=[pltpu.VMEM((2, slots, rows), F32), pltpu.VMEM((2 * SUB, HALF), F32)],
        cost_estimate=pl.CostEstimate(
            flops=2 * 2 * MH * slots * rows * (4 * SUB + 4 * HALF),
            bytes_accessed=24 * 2**20,
            transcendentals=0,
        ),
    )(ids, weights, table, grad_memory, mquery, keys_full)


def one_hot(ids, count):
    return (ids[:, None] == jnp.arange(count, dtype=jnp.int32)[None, :]).astype(BF)


def per_device(
    x_prompt,
    x_cont,
    cot_prompt,
    cot_cont,
    gain_attn,
    gain_mem,
    w_qkv,
    w_attn_out,
    w_mem_query,
    sub_keys,
    w_gate,
    w_mem_out,
    value_rows,
    request,
    slot_prompt,
    slot_cont,
):
    shard_rows, width = value_rows.shape
    owners, capacity = request.shape[2:]
    slots = owners * capacity
    rows = x_prompt.shape[1]
    cols = w_qkv.shape[2]
    block = cols // owners
    side, depth = grid_of(lax.axis_size("dp"), lax.axis_size("fsdp"))

    asked = lax.all_to_all(request[:, 0], ALL, split_axis=1, concat_axis=1, tiled=True)
    serve_pick = one_hot(asked.transpose(1, 0, 2).reshape(-1), shard_rows)
    served = mm(serve_pick, value_rows).astype(BF).reshape(owners, 2 * capacity, width)
    table = lax.all_to_all(served, ALL, split_axis=0, concat_axis=0, tiled=True)
    table = table.reshape(owners, 2, capacity, width).transpose(1, 0, 2, 3).reshape(2, slots, width)
    offsets = jnp.maximum(request[:, 0].reshape(2, slots), 0)
    picked = (jnp.arange(slots, dtype=jnp.int32) // capacity)[None] * shard_rows + offsets
    ids = jnp.stack([picked // SUB, picked % SUB], axis=1).reshape(4, slots)
    picks = jnp.stack([slot_prompt[0], slot_cont[0]]).transpose(3, 0, 2, 1)
    counts, (qkv_full,) = gather_and_count(
        side, depth, (w_qkv,), picks.reshape(picks.shape[0], -1), slots, rows, 0
    )

    x_rows = jnp.concatenate([x_prompt[0], x_cont[0]], axis=0).astype(F32)
    dy_low = jnp.concatenate([cot_prompt[0], cot_cont[0]], axis=0)
    normed, inverse = normalize(x_rows, gain_attn)
    normed = normed.astype(BF)
    queries = mm(normed, qkv_full[0]).astype(BF)
    keys = mm(normed, qkv_full[1]).astype(BF)
    vals = mm(normed, qkv_full[2]).astype(BF)
    (att, lse, all_keys, all_vals), full = attention_forward(
        side,
        depth,
        queries,
        keys,
        vals,
        (w_attn_out, w_mem_query, sub_keys, w_gate, w_mem_out),
        1,
    )
    attn_out_full, query_full, keys_full, gate_full, mem_out_full = full
    hidden = x_rows + mm(att, attn_out_full)
    normed2, inverse2 = normalize(hidden, gain_mem)
    normed2 = normed2.astype(BF)

    mquery = mm(normed2, query_full).astype(BF)
    gate_pre = mm(normed2, gate_full)
    weights, mixing = slot_weights(ids, counts, mquery, keys_full)
    memory_out = jnp.concatenate([mm_l(mixing[part], table[part]) for part in range(2)], axis=0)
    sigmoid_gate = jax.nn.sigmoid(gate_pre)
    blended = (memory_out * (gate_pre * sigmoid_gate)).astype(BF)
    out = (hidden + mm(blended, mem_out_full)).astype(BF)

    grad_blend = mm_t(dy_low, mem_out_full)
    grad_mem_out = mm_l(blended, dy_low)
    grad_memory = (grad_blend * gate_pre * sigmoid_gate).astype(BF)
    grad_gate = (
        grad_blend * memory_out * sigmoid_gate * (1.0 + gate_pre * (1.0 - sigmoid_gate))
    ).astype(BF)
    slot_grads = [
        mm(mixing[part], grad_memory[part * rows : (part + 1) * rows]).astype(BF)
        for part in range(2)
    ]
    arrived = lax.all_to_all(
        jnp.stack([piece.reshape(owners, capacity, width) for piece in slot_grads], axis=1),
        ALL,
        split_axis=0,
        concat_axis=0,
        tiled=True,
    )
    grad_query, grad_keys = slot_weights_back(
        ids, weights, table, grad_memory, mquery, keys_full, block
    )
    grad_normed2 = mm_t(grad_query, query_full) + mm_t(grad_gate, gate_full)
    grad_query_w = mm_l(normed2, grad_query).astype(BF)
    grad_gate_w = mm_l(normed2, grad_gate).astype(BF)
    back, gain_mem_part = norm_backward(hidden, inverse2, gain_mem, grad_normed2)
    grad_hidden = dy_low.astype(F32) + back
    hidden_low = grad_hidden.astype(BF)
    grad_attn_out = mm_l(att, hidden_low).astype(BF)
    grad_att = mm_t(hidden_low, attn_out_full).astype(BF)
    grad_att, arrived = lax.optimization_barrier((grad_att, arrived))
    grad_rows = mm_l(serve_pick, arrived.reshape(owners * 2 * capacity, width))
    (grad_q, grad_k, grad_v), early = attention_backward(
        side,
        depth,
        queries,
        keys,
        vals,
        all_keys,
        all_vals,
        lse,
        att,
        grad_att,
        (grad_query_w, grad_keys, grad_gate_w, grad_mem_out.astype(BF), grad_attn_out),
        2,
    )
    grad_normed = (
        mm_t(grad_q, qkv_full[0]) + mm_t(grad_k, qkv_full[1]) + mm_t(grad_v, qkv_full[2])
    )
    grad_x, gain_attn_part = norm_backward(x_rows, inverse, gain_attn, grad_normed)
    grad_x = grad_hidden + grad_x
    grad_qkv = jnp.stack([mm_l(normed, piece).astype(BF) for piece in (grad_q, grad_k, grad_v)])
    gains = jnp.concatenate([gain_attn_part, gain_mem_part]).reshape(2 * cols // 128, 128)
    qkv_shard, gain_sums = reduce_grads(side, depth, (grad_qkv,), gains, 3)
    own = lax.axis_index("dp") * depth + lax.axis_index("fsdp")
    gain_shards = lax.dynamic_index_in_dim(
        gain_sums.reshape(2, owners, block), own, axis=1, keepdims=False
    )
    sub_shard = early[1].reshape(block, 2, HALF).transpose(1, 0, 2).reshape(2 * block, HALF)
    return (
        out[None, :rows],
        out[None, rows:],
        grad_x[None, :rows],
        grad_x[None, rows:],
        gain_shards[0],
        gain_shards[1],
        qkv_shard,
        early[4],
        early[0],
        sub_shard,
        early[2],
        early[3],
        grad_rows,
    )


def solution(mesh):
    in_specs = (
        P("dp", "fsdp", None),
        P("dp", "fsdp", None),
        P("dp", "fsdp", None),
        P("dp", "fsdp", None),
        P(),
        P(),
        P(None, "fsdp", None),
        P("fsdp", None),
        P("fsdp", None),
        P("fsdp", None),
        P("fsdp", None),
        P("fsdp", None),
        P(("dp", "fsdp"), None),
        P(None, ("dp", "fsdp"), None, None),
        P("dp", "fsdp", None, None),
        P("dp", "fsdp", None, None),
    )
    out_specs = (
        P("dp", "fsdp", None),
        P("dp", "fsdp", None),
        P("dp", "fsdp", None),
        P("dp", "fsdp", None),
        P(("dp", "fsdp")),
        P(("dp", "fsdp")),
        P(None, ("dp", "fsdp"), None),
        P(("dp", "fsdp"), None),
        P(("dp", "fsdp"), None),
        P(("dp", "fsdp"), None),
        P(("dp", "fsdp"), None),
        P(("dp", "fsdp"), None),
        P(("dp", "fsdp"), None),
    )
    return jax.shard_map(
        per_device, mesh=mesh, in_specs=in_specs, out_specs=out_specs, check_vma=False
    )
```

```python
import functools
import jax
import jax.numpy as jnp
from jax import lax
from jax.experimental import pallas as pl
from jax.experimental.pallas import tpu as pltpu
from jax.sharding import PartitionSpec as P
BF = jnp.bfloat16
F32 = jnp.float32
ALL = ("dp", "fsdp")
MESH = pl.DeviceIdType.MESH
LAG = 2
GATHER_LAG = 2
GATHER_RATE = 1
COLLECT_LAG = 2
AHEAD = 3
HOP_LAG = 1
FIRST_PIECE = 512
LAST_PIECE = 512
PAIR = 128
HDIM = 64
MH = 4
HALF = 512
SUB = 256
NEVER = -1e30


def mm(left, right):
    return jnp.dot(left, right, preferred_element_type=F32)


def mm_t(left, right):
    return lax.dot_general(left, right, (((1,), (1,)), ((), ())), preferred_element_type=F32)


def mm_l(left, right):
    return lax.dot_general(left, right, (((0,), (0,)), ((), ())), preferred_element_type=F32)


def normalize(matrix, gain_vec):
    inverse = lax.rsqrt(jnp.mean(matrix * matrix, axis=-1, keepdims=True) + 1e-05)
    return (matrix * inverse * gain_vec, inverse)


def norm_backward(matrix, inverse, gain_vec, grad_normed):
    scaled = gain_vec * grad_normed
    cubed = inverse * inverse * inverse
    grad_matrix = inverse * scaled - matrix * cubed * jnp.mean(
        matrix * scaled, axis=-1, keepdims=True
    )
    return (grad_matrix, jnp.sum(grad_normed * matrix * inverse, axis=0))


def grid_of(plane, depth):
    side = 1
    while 2 * side * side < plane:
        side += 1
    return side, depth


def place(side):
    dp = lax.axis_index("dp")
    return (dp // (2 * side), (dp // 2) % side, dp % 2, lax.axis_index("fsdp"))


def device_at(side, y, x, core, z):
    return ((y * side + x) * 2 + core, z)


def greet(side, depth):
    y, x, core, z = place(side)
    barrier = pltpu.get_barrier_semaphore()
    peers = [device_at(side, y, x, 1 - core, z)]
    for hop in range(1, side):
        peers.append(device_at(side, y, (x + hop) % side, core, z))
        peers.append(device_at(side, (y + hop) % side, x, core, z))
    for hop in range(1, depth):
        peers.append(device_at(side, y, x, core, (z + hop) % depth))
    for peer in peers:
        pl.semaphore_signal(barrier, inc=1, device_id=peer, device_id_type=MESH)
    pl.semaphore_wait(barrier, len(peers))


def remote(source, target, send_sem, recv_sem, peer):
    return pltpu.make_async_remote_copy(
        src_ref=source,
        dst_ref=target,
        send_sem=send_sem,
        recv_sem=recv_sem,
        device_id=peer,
        device_id_type=MESH,
    )


class Gather:
    def __init__(self, side, depth, shards, piece=1024):
        self.side, self.depth = side, depth
        self.views, self.outs, self.shapes, self.held, self.layout = [], [], [], [], []
        plane = 2 * side * side
        for shard in shards:
            rows, cols = shard.shape[-2:]
            block, width = rows // plane, min(cols, piece)
            lead = shard.shape[:-2]
            self.views.append(shard.reshape(lead + (side, side, 2, block, cols)))
            leads = range(lead[0]) if lead else (None,)
            self.layout.append(
                [(number, start) for number in leads for start in range(0, cols, width)]
            )
            self.outs.append(
                jax.ShapeDtypeStruct(lead + (depth, side, side, 2, block, cols), BF)
            )
            self.shapes.append(lead + (depth * rows, cols))
            self.held.append(
                pltpu.VMEM((len(self.layout[-1]), side, side, 2, block, width), BF)
            )
        self.count = count = sum(len(columns) for columns in self.layout)
        self.steps = count + depth - 2 + 3 * GATHER_LAG
        dma = pltpu.SemaphoreType.DMA
        self.scratch = self.held + [
            dma((count,)),
            dma((count,)),
            dma((count, depth)),
            dma((count, depth)),
            dma((count, depth)),
            dma((count, depth, side - 1)),
            dma((count, depth, side - 1)),
            dma((count, depth, side - 1)),
            dma((count, depth, side - 1)),
            dma((count, depth)),
            dma((count, depth)),
        ]

    def restore(self, full):
        return [one.reshape(shape) for one, shape in zip(full, self.shapes)]

    def bind(self, sources, outs, scratch):
        self.sources, self.results = sources, outs
        n_in = len(self.layout)
        self.holders = scratch[:n_in]
        (self.in_sem, self.out_sem, self.right_send, self.left_send, self.deep_recv,
         self.one_send, self.one_recv, self.two_send, self.two_recv, self.core_send,
         self.core_recv) = scratch[n_in:]
        self.pieces = []
        for number, columns in enumerate(self.layout):
            width = self.holders[number].shape[-1]
            width = width if sources[number].shape[-1] > width else None
            for inner, (lead, start) in enumerate(columns):
                self.pieces.append((number, lead, start, width, inner))

    def cut(self, refs, k, *spot):
        number, lead, start, width = self.pieces[k][:4]
        ref = refs[number] if lead is None else refs[number].at[lead]
        ref = ref.at[spot] if spot else ref
        if width is None:
            return ref
        return ref.at[(slice(None),) * (len(ref.shape) - 1) + (pl.ds(start, width),)]

    def along_z(self, k, zp, move, source=None):
        y, x, core, z = place(self.side)
        target = self.cut(self.results, k, zp, y, x, core)
        send = self.right_send if move > 0 else self.left_send
        return remote(target if source is None else source, target, send.at[k, zp],
                      self.deep_recv.at[k, zp], device_at(self.side, y, x, core, z + move))

    def one_copy(self, k, zp, hop):
        side = self.side
        y, x, core, z = place(side)
        peer = device_at(side, y, (x + hop) % side, core, z) if k % 2 == 0 else device_at(
            side, (y + hop) % side, x, core, z)
        ref = self.cut(self.results, k, zp, y, x, core)
        return remote(ref, ref, self.one_send.at[k, zp, hop - 1],
                      self.one_recv.at[k, zp, hop - 1], peer)

    def two_copy(self, k, zp, hop):
        side = self.side
        y, x, core, z = place(side)
        x_first = k % 2 == 0
        peer = device_at(side, (y + hop) % side, x, core, z) if x_first else device_at(
            side, y, (x + hop) % side, core, z)
        ref = (self.cut(self.results, k, zp, y, slice(None), core) if x_first
               else self.cut(self.results, k, zp, slice(None), x, core))
        return remote(ref, ref, self.two_send.at[k, zp, hop - 1],
                      self.two_recv.at[k, zp, hop - 1], peer)

    def core_copy(self, k, zp):
        y, x, core, z = place(self.side)
        ref = self.cut(self.results, k, zp, slice(None), slice(None), core)
        return remote(ref, ref, self.core_send.at[k, zp], self.core_recv.at[k, zp],
                      device_at(self.side, y, x, 1 - core, z))

    def take(self, k):
        number, inner = self.pieces[k][0], self.pieces[k][4]
        return pltpu.make_async_copy(self.cut(self.sources, k), self.holders[number].at[inner],
                                     self.in_sem.at[k])

    def put(self, k):
        z = place(self.side)[3]
        number, inner = self.pieces[k][0], self.pieces[k][4]
        return pltpu.make_async_copy(self.holders[number].at[inner],
                                     self.cut(self.results, k, z), self.out_sem.at[k])

    def start(self):
        y, x, core, z = place(self.side)
        for k in range(self.count):
            self.take(k).start()
            own = self.cut(self.sources, k, y, x, core)

            @pl.when(z < self.depth - 1)
            def _(k=k, own=own):
                self.along_z(k, z, 1, own).start()

            @pl.when(z > 0)
            def _(k=k, own=own):
                self.along_z(k, z, -1, own).start()

    def step(self, i):
        side, depth = self.side, self.depth
        z = place(side)[3]
        if i < self.count:
            self.take(i).wait()
            self.put(i).start()
        for stage in range(4):
            for distance in range(1, depth):
                k = i - stage * GATHER_LAG - (distance - 1)
                if not 0 <= k < self.count:
                    continue
                for sign in (1, -1):
                    zp = z + sign * distance

                    @pl.when(jnp.logical_and(zp >= 0, zp < depth))
                    def _(k=k, zp=zp, sign=sign, stage=stage):
                        self.arrival(stage, k, zp, sign)

    def arrival(self, stage, k, zp, sign):
        side, depth = self.side, self.depth
        z = place(side)[3]
        if stage == 0:
            self.along_z(k, zp, 1).wait_recv()

            @pl.when(z < depth - 1 if sign < 0 else z > 0)
            def _():
                self.along_z(k, zp, -sign).start()

            for hop in range(1, side):
                self.one_copy(k, zp, hop).start()
        elif stage == 1:
            for hop in range(1, side):
                self.one_copy(k, zp, hop).wait_recv()
            for hop in range(1, side):
                self.two_copy(k, zp, hop).start()
        elif stage == 2:
            for hop in range(1, side):
                self.two_copy(k, zp, hop).wait_recv()
            self.core_copy(k, zp).start()
        else:
            self.core_copy(k, zp).wait_recv()

    def finish(self):
        side, depth = self.side, self.depth
        z = place(side)[3]
        for k in range(self.count):
            self.put(k).wait()
            for zp in range(depth):
                @pl.when(jnp.logical_and(zp <= z, z < depth - 1))
                def _(k=k, zp=zp):
                    self.along_z(k, zp, 1).wait_send()

                @pl.when(jnp.logical_and(zp >= z, z > 0))
                def _(k=k, zp=zp):
                    self.along_z(k, zp, -1).wait_send()

                @pl.when(zp != z)
                def _(k=k, zp=zp):
                    for hop in range(1, side):
                        self.one_copy(k, zp, hop).wait_send()
                        self.two_copy(k, zp, hop).wait_send()
                    self.core_copy(k, zp).wait_send()


class Reduce:
    def __init__(self, side, depth, grads, gains=None, piece=1024):
        self.side, self.depth = side, depth
        self.layout, self.views, self.outs = [], [], []
        self.width = width = piece
        devices = 2 * side * side * depth
        for grad in grads:
            rows, cols = grad.shape[-2:]
            self.block = block = rows // devices
            lead = grad.shape[:-2]
            self.views.append(grad.reshape(lead + (side, side, 2, depth, block, cols)))
            leads = range(lead[0]) if lead else (None,)
            self.layout.append(
                [(number, start) for number in leads for start in range(0, cols, width)]
            )
            self.outs.append(jax.ShapeDtypeStruct(lead + (block, cols), F32))
        self.count = count = sum(len(columns) for columns in self.layout)
        self.steps = count + 3 * LAG
        self.gains = gains is not None
        most = max(side, depth) - 1
        dma = pltpu.SemaphoreType.DMA
        self.scratch = [
            pltpu.VMEM((count, side, side, depth, block, width), BF),
            pltpu.VMEM((count, side, side, depth, block, width), BF),
            pltpu.VMEM((count, side - 1, side, depth, block, width), BF),
            pltpu.VMEM((count, side - 1, depth, block, width), BF),
            pltpu.VMEM((count, depth - 1, block, width), BF),
            pltpu.VMEM((count, block, width), F32),
            dma((count,)),
            dma((count,)),
            dma((count,)),
            dma((count, side - 1)),
            dma((count, side - 1)),
            dma((count, side - 1)),
            dma((count, side - 1)),
            dma((count, depth - 1)),
            dma((count, depth - 1)),
        ]
        if self.gains:
            self.views.append(gains)
            self.outs.append(jax.ShapeDtypeStruct(gains.shape, F32))
            self.scratch += [
                pltpu.VMEM((4,) + gains.shape, F32),
                pltpu.VMEM((4, most) + gains.shape, F32),
                dma((4, most)),
                dma((4, most)),
            ]
        any_space, vmem = pl.BlockSpec(memory_space=pl.ANY), pl.BlockSpec(memory_space=pltpu.VMEM)
        self.in_specs = [any_space] * len(self.layout) + [vmem] * self.gains
        self.out_specs = [vmem] * len(self.views)

    def bind(self, sources, outs, scratch):
        (self.mine, self.got_core, self.got_one, self.got_two, self.got_deep, self.total,
         self.local_sem, self.core_send, self.core_recv, self.one_send, self.one_recv,
         self.two_send, self.two_recv, self.deep_send, self.deep_recv) = scratch[:15]
        self.results = outs
        if self.gains:
            self.gain_in, self.gain_out = sources[-1], outs[-1]
            self.gain_sum, self.gain_got, self.gain_send, self.gain_recv = scratch[15:]
        self.pieces = []
        for number, columns in enumerate(self.layout):
            for lead, start in columns:
                ref = sources[number] if lead is None else sources[number].at[lead]
                self.pieces.append((ref, number, lead, start))

    def core_wait(self, k):
        y, x, core, z = place(self.side)
        return remote(self.got_core.at[k], self.got_core.at[k], self.core_send.at[k],
                      self.core_recv.at[k], device_at(self.side, y, x, 1 - core, z))

    def start(self):
        y, x, core, z = place(self.side)
        for k, (ref, _, _, start) in enumerate(self.pieces):
            spot = pl.ds(start, self.width)
            remote(ref.at[:, :, 1 - core, :, :, spot], self.got_core.at[k], self.core_send.at[k],
                   self.core_recv.at[k], device_at(self.side, y, x, 1 - core, z)).start()
            pltpu.make_async_copy(ref.at[:, :, core, :, :, spot], self.mine.at[k],
                                  self.local_sem.at[k]).start()
        if self.gains:
            self.gain_copy(0, 0).start()

    def one_copy(self, k, hop, x_first):
        side = self.side
        y, x, core, z = place(side)
        peer = device_at(side, y, (x + hop) % side, core, z) if x_first else device_at(
            side, (y + hop) % side, x, core, z)
        source = (self.mine.at[k, :, (x + hop) % side] if x_first
                  else self.mine.at[k, (y + hop) % side])
        return remote(source, self.got_one.at[k, hop - 1], self.one_send.at[k, hop - 1],
                      self.one_recv.at[k, hop - 1], peer)

    def two_copy(self, k, hop, x_first):
        side = self.side
        y, x, core, z = place(side)
        peer = device_at(side, (y + hop) % side, x, core, z) if x_first else device_at(
            side, y, (x + hop) % side, core, z)
        source = (self.mine.at[k, (y + hop) % side, x] if x_first
                  else self.mine.at[k, y, (x + hop) % side])
        return remote(source, self.got_two.at[k, hop - 1], self.two_send.at[k, hop - 1],
                      self.two_recv.at[k, hop - 1], peer)

    def deep_copy(self, k, hop):
        y, x, core, z = place(self.side)
        there = (z + hop) % self.depth
        return remote(self.mine.at[k, y, x, there], self.got_deep.at[k, hop - 1],
                      self.deep_send.at[k, hop - 1], self.deep_recv.at[k, hop - 1],
                      device_at(self.side, y, x, core, there))

    def gain_count(self, stage):
        return (1, self.side - 1, self.side - 1, self.depth - 1)[stage]

    def gain_copy(self, stage, number):
        side, depth, hop = self.side, self.depth, number + 1
        y, x, core, z = place(side)
        peer = (
            device_at(side, y, x, 1 - core, z),
            device_at(side, y, (x + hop) % side, core, z),
            device_at(side, (y + hop) % side, x, core, z),
            device_at(side, y, x, core, (z + hop) % depth),
        )[stage]
        source = self.gain_in if stage == 0 else self.gain_sum.at[stage - 1]
        return remote(source, self.gain_got.at[stage, number], self.gain_send.at[stage, number],
                      self.gain_recv.at[stage, number], peer)

    def both_orders(self, k, action):
        @pl.when(k % 2 == 0)
        def _():
            action(True)

        @pl.when(k % 2 == 1)
        def _():
            action(False)

    def added(self, base, others):
        if len(others) == 1:
            return base + others[0]
        value = base.astype(F32)
        for other in others:
            value = value + other.astype(F32)
        return value.astype(base.dtype)

    def after_core(self, k):
        side, depth, mine, got = self.side, self.depth, self.mine, self.got_core
        self.core_wait(k).wait_recv()
        pltpu.make_async_copy(got.at[k], mine.at[k], self.local_sem.at[k]).wait()

        def add(index, carry):
            spot = (k, index // (side * depth), (index // depth) % side, index % depth)
            mine[spot] = mine[spot] + got[spot]
            return carry

        lax.fori_loop(0, side * side * depth, add, 0)

        def send(x_first):
            for hop in range(1, side):
                self.one_copy(k, hop, x_first).start()

        self.both_orders(k, send)

    def after_one(self, k):
        side, depth, mine = self.side, self.depth, self.mine
        y, x, core, z = place(side)

        def finish(x_first):
            for hop in range(1, side):
                self.one_copy(k, hop, x_first).wait_recv()

            def add(index, carry):
                a, c = index // depth, index % depth
                spot = (k, a, x, c) if x_first else (k, y, a, c)
                mine[spot] = self.added(
                    mine[spot], [self.got_one[k, hop, a, c] for hop in range(side - 1)]
                )
                return carry

            lax.fori_loop(0, side * depth, add, 0)
            for hop in range(1, side):
                self.two_copy(k, hop, x_first).start()

        self.both_orders(k, finish)

    def after_two(self, k):
        side, depth, mine = self.side, self.depth, self.mine
        y, x, core, z = place(side)

        def finish(x_first):
            for hop in range(1, side):
                self.two_copy(k, hop, x_first).wait_recv()

        self.both_orders(k, finish)

        def add(c, carry):
            mine[k, y, x, c] = self.added(
                mine[k, y, x, c], [self.got_two[k, hop, c] for hop in range(side - 1)]
            )
            return carry

        lax.fori_loop(0, depth, add, 0)
        for hop in range(1, depth):
            self.deep_copy(k, hop).start()

    def after_deep(self, k):
        y, x, core, z = place(self.side)
        for hop in range(1, self.depth):
            self.deep_copy(k, hop).wait_recv()
        value = self.mine[k, y, x, z].astype(F32)
        for hop in range(self.depth - 1):
            value = value + self.got_deep[k, hop].astype(F32)
        self.total[k] = value

    def step(self, i):
        stages = (self.after_core, self.after_one, self.after_two, self.after_deep)
        for number, action in enumerate(stages):
            lag = number * LAG

            @pl.when(jnp.logical_and(i >= lag, i < self.count + lag))
            def _(lag=lag, action=action):
                action(i - lag)

        for stage in range(4 if self.gains else 0):
            @pl.when(i == stage + 1)
            def _(stage=stage):
                value = self.gain_in[...] if stage == 0 else self.gain_sum[stage - 1]
                for number in range(self.gain_count(stage)):
                    self.gain_copy(stage, number).wait_recv()
                    value = value + self.gain_got[stage, number]
                self.gain_sum[stage] = value
                if stage < 3:
                    for number in range(self.gain_count(stage + 1)):
                        self.gain_copy(stage + 1, number).start()

    def finish(self):
        if self.gains:
            self.gain_out[...] = self.gain_sum[3]
        for k, (_, number, lead, start) in enumerate(self.pieces):
            spot = (slice(None), pl.ds(start, self.width))
            if lead is None:
                self.results[number][spot] = self.total[k]
            else:
                self.results[number][(lead,) + spot] = self.total[k]

        def drain(k, carry):
            self.core_wait(k).wait_send()

            def sent(x_first):
                for hop in range(1, self.side):
                    self.one_copy(k, hop, x_first).wait_send()
                    self.two_copy(k, hop, x_first).wait_send()

            self.both_orders(k, sent)
            for hop in range(1, self.depth):
                self.deep_copy(k, hop).wait_send()
            return carry

        lax.fori_loop(0, self.count, drain, 0)
        for stage in range(4 if self.gains else 0):
            for number in range(self.gain_count(stage)):
                self.gain_copy(stage, number).wait_send()


def split_refs(refs, *counts):
    groups, at = [], 0
    for count in counts:
        groups.append(refs[at : at + count])
        at += count
    return groups + [refs[at:]]


def params(call_id, mib):
    return pltpu.CompilerParams(
        collective_id=call_id, has_side_effects=True, vmem_limit_bytes=mib * 1024 * 1024
    )


def gather_kernel(plan, slots, rows, *refs):
    n = len(plan.views)
    (picks_ref,), sources, (counts_ref,), outs, scratch = split_refs(refs, 1, n, 1, n)
    plan.bind(sources, outs, scratch)
    blocks = picks_ref.shape[1] // 128
    turns = max(plan.steps, blocks)
    greet(plan.side, plan.depth)
    plan.start()

    def run(i, carry):
        for number in range(plan.steps):
            @pl.when(i == number)
            def _(number=number):
                plan.step(number)

        @pl.when(i < blocks)
        def _():
            count_block(i, rows, slots, picks_ref, counts_ref)

        return carry

    lax.fori_loop(0, turns, run, 0)
    plan.finish()


def gather_and_count(side, depth, shards, picks, slots, rows, call_id):
    plan = Gather(side, depth, shards, FIRST_PIECE)
    any_space, vmem = pl.BlockSpec(memory_space=pl.ANY), pl.BlockSpec(memory_space=pltpu.VMEM)
    results = pl.pallas_call(
        functools.partial(gather_kernel, plan, slots, rows),
        out_shape=(jax.ShapeDtypeStruct((2, MH, slots, rows), BF),) + tuple(plan.outs),
        in_specs=[vmem] + [any_space] * len(plan.views),
        out_specs=(vmem,) + (any_space,) * len(plan.views),
        scratch_shapes=plan.scratch,
        compiler_params=params(call_id, 32),
    )(picks, *plan.views)
    return results[0], plan.restore(results[1:])


def reduce_kernel(plan, *refs):
    n = len(plan.views)
    sources, outs, scratch = split_refs(refs, n, n)
    plan.bind(sources, outs, scratch)
    greet(plan.side, plan.depth)
    plan.start()

    def run(i, carry):
        plan.step(i)
        return carry

    lax.fori_loop(0, max(plan.steps, 5), run, 0)
    plan.finish()


def reduce_grads(side, depth, grads, gains, call_id):
    plan = Reduce(side, depth, grads, gains, LAST_PIECE)
    return pl.pallas_call(
        functools.partial(reduce_kernel, plan),
        out_shape=tuple(plan.outs),
        in_specs=plan.in_specs,
        out_specs=tuple(plan.out_specs),
        scratch_shapes=plan.scratch,
        compiler_params=params(call_id, 60),
    )(*plan.views)


def half_masks(width):
    lane = lax.broadcasted_iota(jnp.int32, (1, width), 1)
    return (lane < width // 2, lane >= width // 2)


def dot_rows(left, right):
    return lax.dot_general(left, right, (((1,), (1,)), ((), ())), preferred_element_type=F32)


def dot_first(left, right):
    return lax.dot_general(left, right, (((0,), (0,)), ((), ())), preferred_element_type=F32)


def dot_plain(left, right):
    return lax.dot_general(left, right, (((1,), (0,)), ((), ())), preferred_element_type=F32)


def prompt_mask(scores, chunk, z, rows):
    key = lax.broadcasted_iota(jnp.int32, scores.shape, 0) + chunk * rows
    query = lax.broadcasted_iota(jnp.int32, scores.shape, 1)
    seen = jnp.logical_or(query >= rows, key <= query + z * rows)
    return jnp.where(seen, scores, NEVER)


def own_mask(scores):
    key = lax.broadcasted_iota(jnp.int32, scores.shape, 0)
    query = lax.broadcasted_iota(jnp.int32, scores.shape, 1)
    return jnp.where(key <= query, scores, NEVER)


def forward_pair(p, z, rows, depth, q_ref, k_ref, v_ref, keys, vals, att_ref, lse_ref):
    cols = pl.ds(pl.multiple_of(p * PAIR, PAIR), PAIR)
    q_pair = q_ref[:, cols] * jnp.asarray(0.125, BF)
    k_own, v_own = k_ref[pl.ds(rows, rows), cols], v_ref[pl.ds(rows, rows), cols]
    outs = []
    for head, mask in enumerate(half_masks(PAIR)):
        q_head = jnp.where(mask, q_pair, jnp.zeros_like(q_pair))
        scores = [
            prompt_mask(dot_rows(keys[p, chunk], q_head), chunk, z, rows) for chunk in range(depth)
        ]
        own = own_mask(dot_rows(k_own, q_head[rows:]))
        top = jnp.max(scores[0], axis=0, keepdims=True)
        for piece in scores[1:]:
            top = jnp.maximum(top, jnp.max(piece, axis=0, keepdims=True))
        top_c = jnp.maximum(top[:, rows:], jnp.max(own, axis=0, keepdims=True))
        top = jnp.concatenate([top[:, :rows], top_c], axis=1)
        total = jnp.zeros_like(top)
        out = jnp.zeros((PAIR, 2 * rows), F32)
        for chunk in range(depth):
            expo = jnp.exp(scores[chunk] - top)
            total = total + jnp.sum(expo, axis=0, keepdims=True)
            out = out + dot_first(vals[p, chunk], expo.astype(BF))
        expo = jnp.exp(own - top_c)
        total_c = total[:, rows:] + jnp.sum(expo, axis=0, keepdims=True)
        out_c = out[:, rows:] + dot_first(v_own, expo.astype(BF))
        total = jnp.concatenate([total[:, :rows], total_c], axis=1)
        out = jnp.concatenate([out[:, :rows], out_c], axis=1) / total
        lse_ref[pl.ds(2 * p + head, 1), :] = top + jnp.log(total)
        outs.append(out[head * HDIM : (head + 1) * HDIM])
    att_ref[:, cols] = jnp.concatenate(outs, axis=0).T.astype(BF)


def backward_pair(p, z, rows, depth, q_ref, k_ref, v_ref, keys, vals, lse_ref, att_ref, g_ref,
                  dq_ref, dk_ref, dv_ref, part):
    cols = pl.ds(pl.multiple_of(p * PAIR, PAIR), PAIR)
    own_rows = pl.ds(rows, rows)
    q_pair = q_ref[:, cols] * jnp.asarray(0.125, BF)
    g_pair = g_ref[:, cols]
    k_own, v_own = k_ref[own_rows, cols], v_ref[own_rows, cols]
    pulled = (g_pair.astype(F32) * att_ref[:, cols].astype(F32)).T
    masks = half_masks(PAIR)
    q_heads = [jnp.where(mask, q_pair, jnp.zeros_like(q_pair)) for mask in masks]
    g_heads = [jnp.where(mask, g_pair, jnp.zeros_like(g_pair)) for mask in masks]
    lses = [lse_ref[pl.ds(2 * p + head, 1), :] for head in range(2)]
    deltas = [
        jnp.sum(pulled[head * HDIM : (head + 1) * HDIM], axis=0, keepdims=True)
        for head in range(2)
    ]
    dq = [jnp.zeros((PAIR, 2 * rows), F32) for _ in range(2)]
    for chunk in range(depth):
        dk = jnp.zeros((rows, PAIR), F32)
        dv = jnp.zeros((rows, PAIR), F32)
        k_chunk, v_chunk = keys[p, chunk], vals[p, chunk]
        for head in range(2):
            scores = prompt_mask(dot_rows(k_chunk, q_heads[head]), chunk, z, rows)
            prob = jnp.exp(scores - lses[head])
            d_prob = dot_rows(v_chunk, g_heads[head])
            d_score = (prob * (d_prob - deltas[head])).astype(BF)
            dv = dv + dot_plain(prob.astype(BF), g_heads[head])
            dk = dk + dot_plain(d_score, q_heads[head])
            dq[head] = dq[head] + dot_first(k_chunk, d_score)
        part[p, chunk, 0] = dk.astype(BF)
        part[p, chunk, 1] = dv.astype(BF)
    dk = jnp.zeros((rows, PAIR), F32)
    dv = jnp.zeros((rows, PAIR), F32)
    for head in range(2):
        q_head, g_head = q_heads[head][rows:], g_heads[head][rows:]
        scores = own_mask(dot_rows(k_own, q_head))
        prob = jnp.exp(scores - lses[head][:, rows:])
        d_prob = dot_rows(v_own, g_head)
        d_score = (prob * (d_prob - deltas[head][:, rows:])).astype(BF)
        dv = dv + dot_plain(prob.astype(BF), g_head)
        dk = dk + dot_plain(d_score, q_head)
        more = dot_first(k_own, d_score)
        dq[head] = jnp.concatenate([dq[head][:, :rows], dq[head][:, rows:] + more], axis=1)
    dk_ref[own_rows, cols] = dk.astype(BF)
    dv_ref[own_rows, cols] = dv.astype(BF)
    both = jnp.concatenate([dq[0][:HDIM], dq[1][HDIM:]], axis=0) * 0.125
    dq_ref[:, cols] = both.T.astype(BF)


class Exchange:
    def __init__(self, depth, rows, pairs):
        self.depth, self.rows, self.pairs = depth, rows, pairs
        dma = pltpu.SemaphoreType.DMA
        self.scratch = [dma((2, 2, pairs, depth)), dma((2, pairs, depth))]

    def bind(self, owned, gathered, scratch):
        self.owned, self.gathered = owned, gathered
        self.send_sem, self.recv_sem = scratch

    def hop(self, kind, p, zp, move, own=False):
        target = self.gathered[kind].at[p, zp]
        cols = pl.ds(pl.multiple_of(p * PAIR, PAIR), PAIR)
        source = self.owned[kind].at[pl.ds(0, self.rows), cols] if own else target
        z = lax.axis_index("fsdp")
        return remote(source, target, self.send_sem.at[kind, (move + 1) // 2, p, zp],
                      self.recv_sem.at[kind, p, zp], (lax.axis_index("dp"), z + move))

    def offer(self, p):
        z = lax.axis_index("fsdp")
        for move in (1, -1):
            @pl.when(z < self.depth - 1 if move > 0 else z > 0)
            def _(move=move):
                for kind in range(2):
                    self.hop(kind, p, z, move, own=True).start()
        cols = pl.ds(pl.multiple_of(p * PAIR, PAIR), PAIR)
        for kind in range(2):
            self.gathered[kind][p, z] = self.owned[kind][pl.ds(0, self.rows), cols]

    def step(self, i):
        z = lax.axis_index("fsdp")
        for distance in range(1, self.depth):
            p = i - (distance - 1) * HOP_LAG
            for sign in (1, -1):
                zp = z + sign * distance
                seen = jnp.logical_and(zp >= 0, zp < self.depth)

                @pl.when(jnp.logical_and(seen, jnp.logical_and(p >= 0, p < self.pairs)))
                def _(p=p, zp=zp, sign=sign):
                    for kind in range(2):
                        self.hop(kind, p, zp, 1).wait_recv()

                    @pl.when(z < self.depth - 1 if sign < 0 else z > 0)
                    def _():
                        for kind in range(2):
                            self.hop(kind, p, zp, -sign).start()

    def finish(self):
        z = lax.axis_index("fsdp")

        def drain(p, carry):
            for zp in range(self.depth):
                for move in (1, -1):
                    far = zp <= z if move > 0 else zp >= z
                    inner = z < self.depth - 1 if move > 0 else z > 0

                    @pl.when(jnp.logical_and(far, inner))
                    def _(zp=zp, move=move):
                        for kind in range(2):
                            self.hop(kind, p, zp, move).wait_send()
            return carry

        lax.fori_loop(0, self.pairs, drain, 0)


def forward_kernel(gather, exchange, *refs):
    depth, rows, pairs = exchange.depth, exchange.rows, exchange.pairs
    n = len(gather.views)
    (q_ref, k_ref, v_ref), shards, (att_ref, lse_ref, keys, vals), full, swap, rest = split_refs(
        refs, 3, n, 4, n, len(exchange.scratch))
    gather.bind(shards, full, rest)
    exchange.bind((k_ref, v_ref), (keys, vals), swap)
    z = lax.axis_index("fsdp")
    greet(gather.side, depth)
    ahead = min(AHEAD, pairs)
    for p in range(ahead):
        exchange.offer(p)
    gather.start()
    delay = (depth - 2) * HOP_LAG + 1
    turns = pairs + delay

    def run(i, carry):
        @pl.when(i + ahead < pairs)
        def _():
            exchange.offer(i + ahead)

        exchange.step(i)
        for turn in range(turns):
            @pl.when(i == turn)
            def _(turn=turn):
                for number in range(turn * GATHER_RATE, min((turn + 1) * GATHER_RATE, gather.steps)):
                    gather.step(number)

        @pl.when(i >= delay)
        def _():
            forward_pair(i - delay, z, rows, depth, q_ref, k_ref, v_ref, keys, vals, att_ref,
                         lse_ref)

        return carry

    lax.fori_loop(0, turns, run, 0)
    for number in range(turns * GATHER_RATE, gather.steps):
        gather.step(number)
    exchange.finish()
    gather.finish()


def attention_forward(side, depth, q, k, v, shards, call_id):
    rows, width = q.shape[0] // 2, q.shape[1]
    pairs = width // PAIR
    gather, exchange = Gather(side, depth, shards), Exchange(depth, rows, pairs)
    any_space, vmem = pl.BlockSpec(memory_space=pl.ANY), pl.BlockSpec(memory_space=pltpu.VMEM)
    spread = jax.ShapeDtypeStruct((pairs, depth, rows, PAIR), BF)
    results = pl.pallas_call(
        functools.partial(forward_kernel, gather, exchange),
        out_shape=(
            jax.ShapeDtypeStruct(q.shape, BF),
            jax.ShapeDtypeStruct((2 * pairs, 2 * rows), F32),
            spread,
            spread,
        )
        + tuple(gather.outs),
        in_specs=[vmem] * 3 + [any_space] * len(gather.views),
        out_specs=(vmem,) * 4 + (any_space,) * len(gather.views),
        scratch_shapes=exchange.scratch + gather.scratch,
        compiler_params=params(call_id, 56),
    )(q, k, v, *gather.views)
    return results[:4], gather.restore(results[4:])


class Collect:
    def __init__(self, depth, rows, pairs):
        self.depth, self.rows, self.pairs = depth, rows, pairs
        dma = pltpu.SemaphoreType.DMA
        shape = (pairs, depth, 2, rows, PAIR)
        self.scratch = [
            pltpu.VMEM(shape, BF),
            pltpu.VMEM(shape, BF),
            pltpu.VMEM(shape, BF),
            pltpu.VMEM((2, rows, PAIR), F32),
            dma((2, pairs, depth)),
            dma((2, pairs, depth)),
        ]
        self.steps = pairs + (depth - 1) * COLLECT_LAG + 1

    def bind(self, scratch):
        (self.part, self.from_left, self.from_right, self.whole, self.send_sem,
         self.recv_sem) = scratch

    def hop(self, p, zd, move):
        z = lax.axis_index("fsdp")
        target = self.from_left if move > 0 else self.from_right
        way = (move + 1) // 2
        return remote(self.part.at[p, zd], target.at[p, zd], self.send_sem.at[way, p, zd],
                      self.recv_sem.at[way, p, zd], (lax.axis_index("dp"), z + move))

    def flow(self, p, move):
        depth = self.depth
        z = lax.axis_index("fsdp")
        first = z == 0 if move > 0 else z == depth - 1
        arrived = self.from_left if move > 0 else self.from_right
        for zd in range(depth - 1, -1, -1) if move > 0 else range(depth):
            beyond = zd > z if move > 0 else zd < z

            @pl.when(jnp.logical_and(jnp.logical_not(first), jnp.logical_or(beyond, zd == z)))
            def _(zd=zd):
                self.hop(p, zd, move).wait_recv()

                def add(part, carry):
                    self.part[p, zd, part] = self.part[p, zd, part] + arrived[p, zd, part]
                    return carry

                @pl.when(zd != z)
                def _():
                    lax.fori_loop(0, 2, add, 0)

            @pl.when(beyond)
            def _(zd=zd):
                self.hop(p, zd, move).start()

    def step(self, i):
        depth = self.depth
        z = lax.axis_index("fsdp")
        for move in (1, -1):
            stage = z if move > 0 else depth - 1 - z
            p = i - stage * COLLECT_LAG

            @pl.when(jnp.logical_and(p >= 0, p < self.pairs))
            def _(p=p, move=move):
                self.flow(p, move)

    def result(self, p):
        z = lax.axis_index("fsdp")
        depth = self.depth
        whole = self.whole
        whole[...] = self.part[p, z].astype(F32)

        @pl.when(z > 0)
        def _():
            whole[...] = whole[...] + self.from_left[p, z].astype(F32)

        @pl.when(z < depth - 1)
        def _():
            whole[...] = whole[...] + self.from_right[p, z].astype(F32)

        return whole[...]

    def finish(self):
        depth = self.depth
        z = lax.axis_index("fsdp")

        def drain(p, carry):
            for zd in range(depth):
                for move in (1, -1):
                    @pl.when(zd > z if move > 0 else zd < z)
                    def _(zd=zd, move=move):
                        self.hop(p, zd, move).wait_send()
            return carry

        lax.fori_loop(0, self.pairs, drain, 0)


def backward_kernel(plan, collect, *refs):
    depth, rows, pairs = collect.depth, collect.rows, collect.pairs
    n = len(plan.views)
    ins, sources, (dq_ref, dk_ref, dv_ref), sums, swap, rest = split_refs(
        refs, 8, n, 3, n, len(collect.scratch))
    q_ref, k_ref, v_ref, keys, vals, lse_ref, att_ref, g_ref = ins
    plan.bind(sources, sums, rest)
    collect.bind(swap)
    z = lax.axis_index("fsdp")
    greet(plan.side, depth)
    plan.start()
    last = (depth - 1) * COLLECT_LAG

    def run(i, carry):
        @pl.when(i < pairs)
        def _():
            backward_pair(i, z, rows, depth, q_ref, k_ref, v_ref, keys, vals, lse_ref, att_ref,
                          g_ref, dq_ref, dk_ref, dv_ref, collect.part)

        collect.step(i)
        plan.step(i)

        @pl.when(jnp.logical_and(i >= last, i < last + pairs))
        def _():
            p = i - last
            cols = pl.ds(pl.multiple_of(p * PAIR, PAIR), PAIR)
            value = collect.result(p)
            dk_ref[pl.ds(0, rows), cols] = value[0].astype(BF)
            dv_ref[pl.ds(0, rows), cols] = value[1].astype(BF)

        return carry

    lax.fori_loop(0, max(pairs + last, plan.steps), run, 0)
    collect.finish()
    plan.finish()


def attention_backward(side, depth, q, k, v, keys, vals, lse, att, grad_att, grads, call_id):
    rows, width = q.shape[0] // 2, q.shape[1]
    plan, collect = Reduce(side, depth, grads), Collect(depth, rows, width // PAIR)
    vmem = pl.BlockSpec(memory_space=pltpu.VMEM)
    results = pl.pallas_call(
        functools.partial(backward_kernel, plan, collect),
        out_shape=(jax.ShapeDtypeStruct(q.shape, BF),) * 3 + tuple(plan.outs),
        in_specs=[vmem] * 8 + plan.in_specs,
        out_specs=(vmem,) * 3 + tuple(plan.out_specs),
        scratch_shapes=collect.scratch + plan.scratch,
        compiler_params=params(call_id, 62),
    )(q, k, v, keys, vals, lse, att, grad_att, *plan.views)
    return results[:3], results[3:]


def count_block(b, rows, slots, picks_ref, counts_ref):
    low, per_word, bits = 16, 5, 6
    groups = -(-(slots // low) // per_word)
    per_head = rows // 128
    cols = pl.ds(pl.multiple_of(b * 128, 128), 128)
    picks = picks_ref[:, cols]
    high = jnp.right_shift(picks, 4)
    group = jnp.right_shift(high * 13, 6)
    word = group * low + jnp.bitwise_and(picks, low - 1)
    unit = jnp.left_shift(jnp.ones_like(picks), bits * (high - per_word * group))
    spot = lax.broadcasted_iota(jnp.int32, (groups * low, 128), 0)
    words = jnp.zeros((groups * low, 128), jnp.int32)
    for pick in range(picks.shape[0]):
        words = words + jnp.where(spot == word[pick : pick + 1], unit[pick : pick + 1], 0)
    part, head = b // (per_head * MH), (b // per_head) % MH
    lanes = pl.ds(pl.multiple_of((b % per_head) * 128, 128), 128)
    for tile in range(slots // low):
        piece = words[(tile // per_word) * low : (tile // per_word + 1) * low]
        count = jnp.bitwise_and(jnp.right_shift(piece, bits * (tile % per_word)), 2**bits - 1)
        counts_ref[part, head, pl.ds(tile * low, low), lanes] = count.astype(F32).astype(BF)


def selector(ids_ref, index, count):
    ids = ids_ref[pl.ds(index, 1), :]
    spot = lax.broadcasted_iota(jnp.int32, (count, ids.shape[1]), 0)
    return jnp.where(spot == ids, 1.0, 0.0).astype(BF)


def picks_kernel(ids_ref, counts_ref, query_ref, keys_ref, weight_ref, mixing_ref, total):
    part, head = pl.program_id(0), pl.program_id(1)
    scores = None
    for half in range(2):
        pick = selector(ids_ref, 2 * part + half, SUB)
        slot_keys = dot_first(pick, keys_ref[half * SUB : (half + 1) * SUB]).astype(BF)
        piece = dot_rows(slot_keys, query_ref[:, half * HALF : (half + 1) * HALF])
        scores = piece if scores is None else scores + piece
    count = counts_ref[0, 0].astype(F32)
    named = count > 0.0
    top = jnp.max(jnp.where(named, scores, -jnp.inf), axis=0, keepdims=True)
    raised = jnp.where(named, count * jnp.exp(scores - top), 0.0)
    weight = raised / jnp.sum(raised, axis=0, keepdims=True)
    weight_ref[0, 0] = weight

    @pl.when(head == 0)
    def _():
        total[...] = weight

    @pl.when(head > 0)
    def _():
        total[...] = total[...] + weight

    @pl.when(head == MH - 1)
    def _():
        mixing_ref[0] = total[...].astype(BF)


def slot_weights(ids, counts, mquery, keys_full):
    slots, rows = counts.shape[2:]
    return pl.pallas_call(
        picks_kernel,
        grid=(2, MH),
        out_shape=(
            jax.ShapeDtypeStruct(counts.shape, F32),
            jax.ShapeDtypeStruct((2, slots, rows), BF),
        ),
        in_specs=[
            pl.BlockSpec(ids.shape, lambda u, m: (0, 0)),
            pl.BlockSpec((1, 1, slots, rows), lambda u, m: (u, m, 0, 0)),
            pl.BlockSpec((rows, 2 * HALF), lambda u, m: (u, m)),
            pl.BlockSpec((2 * SUB, HALF), lambda u, m: (m, 0)),
        ],
        out_specs=(
            pl.BlockSpec((1, 1, slots, rows), lambda u, m: (u, m, 0, 0)),
            pl.BlockSpec((1, slots, rows), lambda u, m: (u, 0, 0)),
        ),
        scratch_shapes=[pltpu.VMEM((slots, rows), F32)],
        cost_estimate=pl.CostEstimate(
            flops=2 * 2 * MH * slots * 2 * HALF * (SUB + rows),
            bytes_accessed=24 * 2**20,
            transcendentals=2 * MH * slots * rows,
        ),
    )(ids, counts, mquery, keys_full)


def picks_back_kernel(block, ids_ref, weight_ref, table_ref, memory_ref, query_ref, keys_ref,
                      grad_query_ref, grad_keys_ref, grad_mixing, total):
    head, part = pl.program_id(0), pl.program_id(1)

    @pl.when(head == 0)
    def _():
        grad_mixing[part] = dot_rows(table_ref[0], memory_ref[...])

    weight = weight_ref[0, 0]
    pulled = weight * grad_mixing[part]
    grad = pulled - weight * jnp.sum(pulled, axis=0, keepdims=True)
    high = grad.astype(BF)
    low = (grad - high.astype(F32)).astype(BF)
    for half in range(2):
        pick = selector(ids_ref, 2 * part + half, SUB)
        sub = (dot_plain(pick, high) + dot_plain(pick, low)).astype(BF)
        span = slice(half * HALF, (half + 1) * HALF)
        keys = keys_ref[half * SUB : (half + 1) * SUB]
        grad_query_ref[:, span] = dot_first(sub, keys).astype(BF)
        piece = dot_plain(sub, query_ref[:, span])
        rows = slice(half * SUB, (half + 1) * SUB)

        @pl.when(part == 0)
        def _(piece=piece, rows=rows):
            total[rows] = piece

        @pl.when(part == 1)
        def _(piece=piece, rows=rows):
            total[rows] = total[rows] + piece

    @pl.when(part == 1)
    def _():
        for shard in range(SUB // block):
            for side in range(2):
                start = (2 * shard + side) * block
                grad_keys_ref[shard * block : (shard + 1) * block, side * HALF : (side + 1) * HALF] = (
                    total[start : start + block].astype(BF))


def slot_weights_back(ids, weights, table, grad_memory, mquery, keys_full, block):
    slots, rows = weights.shape[2:]
    width = table.shape[2]
    return pl.pallas_call(
        functools.partial(picks_back_kernel, block),
        grid=(MH, 2),
        out_shape=(
            jax.ShapeDtypeStruct(mquery.shape, BF),
            jax.ShapeDtypeStruct((MH * SUB, 2 * HALF), BF),
        ),
        in_specs=[
            pl.BlockSpec(ids.shape, lambda m, u: (0, 0)),
            pl.BlockSpec((1, 1, slots, rows), lambda m, u: (u, m, 0, 0)),
            pl.BlockSpec((1, slots, width), lambda m, u: (jnp.where(m == 0, u, 1), 0, 0)),
            pl.BlockSpec((rows, width), lambda m, u: (jnp.where(m == 0, u, 1), 0)),
            pl.BlockSpec((rows, 2 * HALF), lambda m, u: (u, m)),
            pl.BlockSpec((2 * SUB, HALF), lambda m, u: (m, 0)),
        ],
        out_specs=(
            pl.BlockSpec((rows, 2 * HALF), lambda m, u: (u, m)),
            pl.BlockSpec((SUB, 2 * HALF), lambda m, u: (m, 0)),
        ),
        scratch_shapes=[pltpu.VMEM((2, slots, rows), F32), pltpu.VMEM((2 * SUB, HALF), F32)],
        cost_estimate=pl.CostEstimate(
            flops=2 * 2 * MH * slots * rows * (4 * SUB + 4 * HALF),
            bytes_accessed=24 * 2**20,
            transcendentals=0,
        ),
    )(ids, weights, table, grad_memory, mquery, keys_full)


def one_hot(ids, count):
    return (ids[:, None] == jnp.arange(count, dtype=jnp.int32)[None, :]).astype(BF)


def per_device(
    x_prompt,
    x_cont,
    cot_prompt,
    cot_cont,
    gain_attn,
    gain_mem,
    w_qkv,
    w_attn_out,
    w_mem_query,
    sub_keys,
    w_gate,
    w_mem_out,
    value_rows,
    request,
    slot_prompt,
    slot_cont,
):
    shard_rows, width = value_rows.shape
    owners, capacity = request.shape[2:]
    slots = owners * capacity
    rows = x_prompt.shape[1]
    cols = w_qkv.shape[2]
    block = cols // owners
    side, depth = grid_of(lax.axis_size("dp"), lax.axis_size("fsdp"))

    asked = lax.all_to_all(request[:, 0], ALL, split_axis=1, concat_axis=1, tiled=True)
    serve_picks = [one_hot(asked[part].reshape(-1), shard_rows) for part in range(2)]

    def swap(values):
        values = values.reshape(owners, capacity, width)
        swapped = lax.all_to_all(values, ALL, split_axis=0, concat_axis=0, tiled=True)
        return swapped.reshape(slots, width)

    served = [mm(pick, value_rows).astype(BF) for pick in serve_picks]
    offsets = jnp.maximum(request[:, 0].reshape(2, slots), 0)
    picked = (jnp.arange(slots, dtype=jnp.int32) // capacity)[None] * shard_rows + offsets
    ids = jnp.stack([picked // SUB, picked % SUB], axis=1).reshape(4, slots)
    picks = jnp.stack([slot_prompt[0], slot_cont[0]]).transpose(3, 0, 2, 1)
    picks, served = lax.optimization_barrier((picks, served))
    tables = [swap(served[0])]
    counts, (qkv_full,) = gather_and_count(
        side, depth, (w_qkv,), picks.reshape(picks.shape[0], -1), slots, rows, 0
    )

    x_rows = jnp.concatenate([x_prompt[0], x_cont[0]], axis=0).astype(F32)
    dy_low = jnp.concatenate([cot_prompt[0], cot_cont[0]], axis=0)
    normed, inverse = normalize(x_rows, gain_attn)
    normed = normed.astype(BF)
    queries = mm(normed, qkv_full[0]).astype(BF)
    keys = mm(normed, qkv_full[1]).astype(BF)
    vals = mm(normed, qkv_full[2]).astype(BF)
    queries, tables[0] = lax.optimization_barrier((queries, tables[0]))
    (att, lse, all_keys, all_vals), full = attention_forward(
        side,
        depth,
        queries,
        keys,
        vals,
        (w_attn_out, w_mem_query, sub_keys, w_gate, w_mem_out),
        1,
    )
    attn_out_full, query_full, keys_full, gate_full, mem_out_full = full
    att, late = lax.optimization_barrier((att, served[1]))
    tables.append(swap(late))
    hidden = x_rows + mm(att, attn_out_full)
    normed2, inverse2 = normalize(hidden, gain_mem)
    normed2 = normed2.astype(BF)

    mquery = mm(normed2, query_full).astype(BF)
    gate_pre = mm(normed2, gate_full)
    weights, mixing = slot_weights(ids, counts, mquery, keys_full)
    memory_out = jnp.concatenate([mm_l(mixing[part], tables[part]) for part in range(2)], axis=0)
    sigmoid_gate = jax.nn.sigmoid(gate_pre)
    blended = (memory_out * (gate_pre * sigmoid_gate)).astype(BF)
    out = (hidden + mm(blended, mem_out_full)).astype(BF)

    grad_blend = mm_t(dy_low, mem_out_full)
    grad_mem_out = mm_l(blended, dy_low)
    grad_memory = (grad_blend * gate_pre * sigmoid_gate).astype(BF)
    grad_gate = (
        grad_blend * memory_out * sigmoid_gate * (1.0 + gate_pre * (1.0 - sigmoid_gate))
    ).astype(BF)
    slot_grads = [
        mm(mixing[part], grad_memory[part * rows : (part + 1) * rows]).astype(BF)
        for part in range(2)
    ]
    arrived = swap(slot_grads[1])
    grad_query, grad_keys = slot_weights_back(
        ids, weights, jnp.stack(tables), grad_memory, mquery, keys_full, block
    )
    grad_normed2 = mm_t(grad_query, query_full) + mm_t(grad_gate, gate_full)
    grad_query_w = mm_l(normed2, grad_query).astype(BF)
    grad_gate_w = mm_l(normed2, grad_gate).astype(BF)
    back, gain_mem_part = norm_backward(hidden, inverse2, gain_mem, grad_normed2)
    grad_hidden = dy_low.astype(F32) + back
    hidden_low = grad_hidden.astype(BF)
    grad_attn_out = mm_l(att, hidden_low).astype(BF)
    grad_att = mm_t(hidden_low, attn_out_full).astype(BF)
    grad_att, arrived = lax.optimization_barrier((grad_att, arrived))
    (grad_q, grad_k, grad_v), early = attention_backward(
        side,
        depth,
        queries,
        keys,
        vals,
        all_keys,
        all_vals,
        lse,
        att,
        grad_att,
        (grad_query_w, grad_keys, grad_gate_w, grad_mem_out.astype(BF), grad_attn_out),
        2,
    )
    grad_q, late = lax.optimization_barrier((grad_q, slot_grads[0]))
    grad_rows = mm_l(
        jnp.concatenate(serve_picks, axis=0), jnp.concatenate([swap(late), arrived], axis=0)
    )
    grad_normed = (
        mm_t(grad_q, qkv_full[0]) + mm_t(grad_k, qkv_full[1]) + mm_t(grad_v, qkv_full[2])
    )
    grad_x, gain_attn_part = norm_backward(x_rows, inverse, gain_attn, grad_normed)
    grad_x = grad_hidden + grad_x
    grad_qkv = jnp.stack([mm_l(normed, piece).astype(BF) for piece in (grad_q, grad_k, grad_v)])
    gains = jnp.concatenate([gain_attn_part, gain_mem_part]).reshape(2 * cols // 128, 128)
    qkv_shard, gain_sums = reduce_grads(side, depth, (grad_qkv,), gains, 3)
    own = lax.axis_index("dp") * depth + lax.axis_index("fsdp")
    gain_shards = lax.dynamic_index_in_dim(
        gain_sums.reshape(2, owners, block), own, axis=1, keepdims=False
    )
    sub_shard = early[1].reshape(block, 2, HALF).transpose(1, 0, 2).reshape(2 * block, HALF)
    return (
        out[None, :rows],
        out[None, rows:],
        grad_x[None, :rows],
        grad_x[None, rows:],
        gain_shards[0],
        gain_shards[1],
        qkv_shard,
        early[4],
        early[0],
        sub_shard,
        early[2],
        early[3],
        grad_rows,
    )


def solution(mesh):
    in_specs = (
        P("dp", "fsdp", None),
        P("dp", "fsdp", None),
        P("dp", "fsdp", None),
        P("dp", "fsdp", None),
        P(),
        P(),
        P(None, "fsdp", None),
        P("fsdp", None),
        P("fsdp", None),
        P("fsdp", None),
        P("fsdp", None),
        P("fsdp", None),
        P(("dp", "fsdp"), None),
        P(None, ("dp", "fsdp"), None, None),
        P("dp", "fsdp", None, None),
        P("dp", "fsdp", None, None),
    )
    out_specs = (
        P("dp", "fsdp", None),
        P("dp", "fsdp", None),
        P("dp", "fsdp", None),
        P("dp", "fsdp", None),
        P(("dp", "fsdp")),
        P(("dp", "fsdp")),
        P(None, ("dp", "fsdp"), None),
        P(("dp", "fsdp"), None),
        P(("dp", "fsdp"), None),
        P(("dp", "fsdp"), None),
        P(("dp", "fsdp"), None),
        P(("dp", "fsdp"), None),
        P(("dp", "fsdp"), None),
    )
    return jax.shard_map(
        per_device, mesh=mesh, in_specs=in_specs, out_specs=out_specs, check_vma=False
    )
```

```python
import functools
import jax
import jax.numpy as jnp
from jax import lax
from jax.experimental import pallas as pl
from jax.experimental.pallas import tpu as pltpu
from jax.sharding import PartitionSpec as P
BF = jnp.bfloat16
F32 = jnp.float32
ALL = ("dp", "fsdp")
MESH = pl.DeviceIdType.MESH
LAG = 2
GATHER_LAG = 2
REST_START = 1
REST_DELAY = 8
DEEP_AT = 10
COLLECT_LAG = 2
AHEAD = 3
HOP_LAG = 1
FIRST_PIECE = 1024
PAIR = 128
HDIM = 64
MH = 4
HALF = 512
SUB = 256
NEVER = -1e30


def mm(left, right):
    return jnp.dot(left, right, preferred_element_type=F32)


def mm_t(left, right):
    return lax.dot_general(left, right, (((1,), (1,)), ((), ())), preferred_element_type=F32)


def mm_l(left, right):
    return lax.dot_general(left, right, (((0,), (0,)), ((), ())), preferred_element_type=F32)


def normalize(matrix, gain_vec):
    inverse = lax.rsqrt(jnp.mean(matrix * matrix, axis=-1, keepdims=True) + 1e-05)
    return (matrix * inverse * gain_vec, inverse)


def norm_backward(matrix, inverse, gain_vec, grad_normed):
    scaled = gain_vec * grad_normed
    cubed = inverse * inverse * inverse
    grad_matrix = inverse * scaled - matrix * cubed * jnp.mean(
        matrix * scaled, axis=-1, keepdims=True
    )
    return (grad_matrix, jnp.sum(grad_normed * matrix * inverse, axis=0))


def grid_of(plane, depth):
    side = 1
    while 2 * side * side < plane:
        side += 1
    return side, depth


def place(side):
    dp = lax.axis_index("dp")
    return (dp // (2 * side), (dp // 2) % side, dp % 2, lax.axis_index("fsdp"))


def device_at(side, y, x, core, z):
    return ((y * side + x) * 2 + core, z)


def greet(side, depth):
    y, x, core, z = place(side)
    barrier = pltpu.get_barrier_semaphore()
    peers = [device_at(side, y, x, 1 - core, z)]
    for hop in range(1, side):
        peers.append(device_at(side, y, (x + hop) % side, core, z))
        peers.append(device_at(side, (y + hop) % side, x, core, z))
    for hop in range(1, depth):
        peers.append(device_at(side, y, x, core, (z + hop) % depth))
    for peer in peers:
        pl.semaphore_signal(barrier, inc=1, device_id=peer, device_id_type=MESH)
    pl.semaphore_wait(barrier, len(peers))


def remote(source, target, send_sem, recv_sem, peer):
    return pltpu.make_async_remote_copy(
        src_ref=source,
        dst_ref=target,
        send_sem=send_sem,
        recv_sem=recv_sem,
        device_id=peer,
        device_id_type=MESH,
    )


class Gather:
    def __init__(self, side, depth, shards, piece=1024):
        self.side, self.depth = side, depth
        self.views, self.outs, self.shapes, self.held, self.layout = [], [], [], [], []
        plane = 2 * side * side
        for shard in shards:
            rows, cols = shard.shape[-2:]
            block, width = rows // plane, min(cols, piece)
            lead = shard.shape[:-2]
            self.views.append(shard.reshape(lead + (side, side, 2, block, cols)))
            leads = range(lead[0]) if lead else (None,)
            self.layout.append(
                [(number, start) for number in leads for start in range(0, cols, width)]
            )
            self.outs.append(
                jax.ShapeDtypeStruct(lead + (depth, side, side, 2, block, cols), BF)
            )
            self.shapes.append(lead + (depth * rows, cols))
            self.held.append(
                pltpu.VMEM((len(self.layout[-1]), side, side, 2, block, width), BF)
            )
        self.count = count = sum(len(columns) for columns in self.layout)
        self.steps = count + depth - 2 + 3 * GATHER_LAG
        dma = pltpu.SemaphoreType.DMA
        self.scratch = self.held + [
            dma((count,)),
            dma((count,)),
            dma((count, depth)),
            dma((count, depth)),
            dma((count, depth)),
            dma((count, depth, side - 1)),
            dma((count, depth, side - 1)),
            dma((count, depth, side - 1)),
            dma((count, depth, side - 1)),
            dma((count, depth)),
            dma((count, depth)),
        ]

    def restore(self, full):
        return [one.reshape(shape) for one, shape in zip(full, self.shapes)]

    def bind(self, sources, outs, scratch):
        self.sources, self.results = sources, outs
        n_in = len(self.layout)
        self.holders = scratch[:n_in]
        (self.in_sem, self.out_sem, self.right_send, self.left_send, self.deep_recv,
         self.one_send, self.one_recv, self.two_send, self.two_recv, self.core_send,
         self.core_recv) = scratch[n_in:]
        self.pieces = []
        for number, columns in enumerate(self.layout):
            width = self.holders[number].shape[-1]
            width = width if sources[number].shape[-1] > width else None
            for inner, (lead, start) in enumerate(columns):
                self.pieces.append((number, lead, start, width, inner))

    def cut(self, refs, k, *spot):
        number, lead, start, width = self.pieces[k][:4]
        ref = refs[number] if lead is None else refs[number].at[lead]
        ref = ref.at[spot] if spot else ref
        if width is None:
            return ref
        return ref.at[(slice(None),) * (len(ref.shape) - 1) + (pl.ds(start, width),)]

    def along_z(self, k, zp, move, source=None):
        y, x, core, z = place(self.side)
        target = self.cut(self.results, k, zp, y, x, core)
        send = self.right_send if move > 0 else self.left_send
        return remote(target if source is None else source, target, send.at[k, zp],
                      self.deep_recv.at[k, zp], device_at(self.side, y, x, core, z + move))

    def one_copy(self, k, zp, hop):
        side = self.side
        y, x, core, z = place(side)
        peer = device_at(side, y, (x + hop) % side, core, z) if k % 2 == 0 else device_at(
            side, (y + hop) % side, x, core, z)
        ref = self.cut(self.results, k, zp, y, x, core)
        return remote(ref, ref, self.one_send.at[k, zp, hop - 1],
                      self.one_recv.at[k, zp, hop - 1], peer)

    def two_copy(self, k, zp, hop):
        side = self.side
        y, x, core, z = place(side)
        x_first = k % 2 == 0
        peer = device_at(side, (y + hop) % side, x, core, z) if x_first else device_at(
            side, y, (x + hop) % side, core, z)
        ref = (self.cut(self.results, k, zp, y, slice(None), core) if x_first
               else self.cut(self.results, k, zp, slice(None), x, core))
        return remote(ref, ref, self.two_send.at[k, zp, hop - 1],
                      self.two_recv.at[k, zp, hop - 1], peer)

    def core_copy(self, k, zp):
        y, x, core, z = place(self.side)
        ref = self.cut(self.results, k, zp, slice(None), slice(None), core)
        return remote(ref, ref, self.core_send.at[k, zp], self.core_recv.at[k, zp],
                      device_at(self.side, y, x, 1 - core, z))

    def take(self, k):
        number, inner = self.pieces[k][0], self.pieces[k][4]
        return pltpu.make_async_copy(self.cut(self.sources, k), self.holders[number].at[inner],
                                     self.in_sem.at[k])

    def put(self, k):
        z = place(self.side)[3]
        number, inner = self.pieces[k][0], self.pieces[k][4]
        return pltpu.make_async_copy(self.holders[number].at[inner],
                                     self.cut(self.results, k, z), self.out_sem.at[k])

    def start(self, k):
        y, x, core, z = place(self.side)
        self.take(k).start()
        own = self.cut(self.sources, k, y, x, core)

        @pl.when(z < self.depth - 1)
        def _():
            self.along_z(k, z, 1, own).start()

        @pl.when(z > 0)
        def _():
            self.along_z(k, z, -1, own).start()

    def step(self, i):
        side, depth = self.side, self.depth
        z = place(side)[3]
        if i < self.count:
            self.take(i).wait()
            self.put(i).start()
        for stage in range(4):
            for distance in range(1, depth):
                k = i - stage * GATHER_LAG - (distance - 1)
                if not 0 <= k < self.count:
                    continue
                for sign in (1, -1):
                    zp = z + sign * distance

                    @pl.when(jnp.logical_and(zp >= 0, zp < depth))
                    def _(k=k, zp=zp, sign=sign, stage=stage):
                        self.arrival(stage, k, zp, sign)

    def arrival(self, stage, k, zp, sign):
        side, depth = self.side, self.depth
        z = place(side)[3]
        if stage == 0:
            self.along_z(k, zp, 1).wait_recv()

            @pl.when(z < depth - 1 if sign < 0 else z > 0)
            def _():
                self.along_z(k, zp, -sign).start()

            for hop in range(1, side):
                self.one_copy(k, zp, hop).start()
        elif stage == 1:
            for hop in range(1, side):
                self.one_copy(k, zp, hop).wait_recv()
            for hop in range(1, side):
                self.two_copy(k, zp, hop).start()
        elif stage == 2:
            for hop in range(1, side):
                self.two_copy(k, zp, hop).wait_recv()
            self.core_copy(k, zp).start()
        else:
            self.core_copy(k, zp).wait_recv()

    def settle(self):
        for k in range(self.count):
            self.put(k).wait()

    def finish(self):
        side, depth = self.side, self.depth
        z = place(side)[3]
        for k in range(self.count):
            for zp in range(depth):
                @pl.when(jnp.logical_and(zp <= z, z < depth - 1))
                def _(k=k, zp=zp):
                    self.along_z(k, zp, 1).wait_send()

                @pl.when(jnp.logical_and(zp >= z, z > 0))
                def _(k=k, zp=zp):
                    self.along_z(k, zp, -1).wait_send()

                @pl.when(zp != z)
                def _(k=k, zp=zp):
                    for hop in range(1, side):
                        self.one_copy(k, zp, hop).wait_send()
                        self.two_copy(k, zp, hop).wait_send()
                    self.core_copy(k, zp).wait_send()


class Reduce:
    def __init__(self, side, depth, grads, piece, deep_at):
        self.side, self.depth, self.deep_at = side, depth, deep_at
        self.layout, self.views, self.outs = [], [], []
        self.width = width = piece
        devices = 2 * side * side * depth
        for grad in grads:
            rows, cols = grad.shape[-2:]
            self.block = block = rows // devices
            lead = grad.shape[:-2]
            self.views.append(lead + (side, side, 2, depth, block, cols))
            leads = range(lead[0]) if lead else (None,)
            self.layout += [
                (len(self.outs), number, start) for number in leads for start in range(0, cols, width)
            ]
            self.outs.append(jax.ShapeDtypeStruct(lead + (block, cols), F32))
        self.count = count = len(self.layout)
        self.steps = count + deep_at + LAG
        dma = pltpu.SemaphoreType.DMA
        self.scratch = [
            pltpu.VMEM((count, side, side, depth, block, width), BF),
            pltpu.VMEM((count, side, side, depth, block, width), BF),
            pltpu.VMEM((count, side - 1, side, depth, block, width), BF),
            pltpu.VMEM((count, side - 1, depth, block, width), BF),
            pltpu.VMEM((count, depth - 1, block, width), BF),
            pltpu.VMEM((count, block, width), F32),
            dma((count,)),
            dma((count,)),
            dma((count,)),
            dma((count, side - 1)),
            dma((count, side - 1)),
            dma((count, side - 1)),
            dma((count, side - 1)),
            dma((count, depth - 1)),
            dma((count, depth - 1)),
        ]

    def bind(self, sources, outs, scratch):
        (self.mine, self.got_core, self.got_one, self.got_two, self.got_deep, self.total,
         self.local_sem, self.core_send, self.core_recv, self.one_send, self.one_recv,
         self.two_send, self.two_recv, self.deep_send, self.deep_recv) = scratch
        self.results, self.sources = outs, sources

    def core_copy(self, k, source):
        y, x, core, z = place(self.side)
        return remote(source, self.got_core.at[k], self.core_send.at[k],
                      self.core_recv.at[k], device_at(self.side, y, x, 1 - core, z))

    def start(self, k):
        core = place(self.side)[2]
        self.core_copy(k, self.sources(k, 1 - core)).start()
        pltpu.make_async_copy(self.sources(k, core), self.mine.at[k], self.local_sem.at[k]).start()

    def one_copy(self, k, hop, x_first):
        side = self.side
        y, x, core, z = place(side)
        peer = device_at(side, y, (x + hop) % side, core, z) if x_first else device_at(
            side, (y + hop) % side, x, core, z)
        source = (self.mine.at[k, :, (x + hop) % side] if x_first
                  else self.mine.at[k, (y + hop) % side])
        return remote(source, self.got_one.at[k, hop - 1], self.one_send.at[k, hop - 1],
                      self.one_recv.at[k, hop - 1], peer)

    def two_copy(self, k, hop, x_first):
        side = self.side
        y, x, core, z = place(side)
        peer = device_at(side, (y + hop) % side, x, core, z) if x_first else device_at(
            side, y, (x + hop) % side, core, z)
        source = (self.mine.at[k, (y + hop) % side, x] if x_first
                  else self.mine.at[k, y, (x + hop) % side])
        return remote(source, self.got_two.at[k, hop - 1], self.two_send.at[k, hop - 1],
                      self.two_recv.at[k, hop - 1], peer)

    def deep_copy(self, k, hop):
        y, x, core, z = place(self.side)
        there = (z + hop) % self.depth
        return remote(self.mine.at[k, y, x, there], self.got_deep.at[k, hop - 1],
                      self.deep_send.at[k, hop - 1], self.deep_recv.at[k, hop - 1],
                      device_at(self.side, y, x, core, there))

    def both_orders(self, k, action):
        @pl.when(k % 2 == 0)
        def _():
            action(True)

        @pl.when(k % 2 == 1)
        def _():
            action(False)

    def added(self, base, others):
        if len(others) == 1:
            return base + others[0]
        value = base.astype(F32)
        for other in others:
            value = value + other.astype(F32)
        return value.astype(base.dtype)

    def after_core(self, k):
        side, depth, mine, got = self.side, self.depth, self.mine, self.got_core
        self.core_copy(k, got.at[k]).wait_recv()
        pltpu.make_async_copy(got.at[k], mine.at[k], self.local_sem.at[k]).wait()

        def add(index, carry):
            spot = (k, index // (side * depth), (index // depth) % side, index % depth)
            mine[spot] = mine[spot] + got[spot]
            return carry

        lax.fori_loop(0, side * side * depth, add, 0)

        def send(x_first):
            for hop in range(1, side):
                self.one_copy(k, hop, x_first).start()

        self.both_orders(k, send)

    def after_one(self, k):
        side, depth, mine = self.side, self.depth, self.mine
        y, x, core, z = place(side)

        def finish(x_first):
            for hop in range(1, side):
                self.one_copy(k, hop, x_first).wait_recv()

            def add(index, carry):
                a, c = index // depth, index % depth
                spot = (k, a, x, c) if x_first else (k, y, a, c)
                mine[spot] = self.added(
                    mine[spot], [self.got_one[k, hop, a, c] for hop in range(side - 1)]
                )
                return carry

            lax.fori_loop(0, side * depth, add, 0)
            for hop in range(1, side):
                self.two_copy(k, hop, x_first).start()

        self.both_orders(k, finish)

    def after_two(self, k):
        side, depth, mine = self.side, self.depth, self.mine
        y, x, core, z = place(side)

        def finish(x_first):
            for hop in range(1, side):
                self.two_copy(k, hop, x_first).wait_recv()

        self.both_orders(k, finish)

        def add(c, carry):
            mine[k, y, x, c] = self.added(
                mine[k, y, x, c], [self.got_two[k, hop, c] for hop in range(side - 1)]
            )
            return carry

        lax.fori_loop(0, depth, add, 0)

    def send_deep(self, k):
        for hop in range(1, self.depth):
            self.deep_copy(k, hop).start()

    def after_deep(self, k):
        y, x, core, z = place(self.side)
        for hop in range(1, self.depth):
            self.deep_copy(k, hop).wait_recv()
        value = self.mine[k, y, x, z].astype(F32)
        for hop in range(self.depth - 1):
            value = value + self.got_deep[k, hop].astype(F32)
        self.total[k] = value

    def step(self, i):
        stages = (
            (0, self.after_core),
            (LAG, self.after_one),
            (2 * LAG, self.after_two),
            (self.deep_at, self.send_deep),
            (self.deep_at + LAG, self.after_deep),
        )
        for lag, action in stages:
            @pl.when(jnp.logical_and(i >= lag, i < self.count + lag))
            def _(lag=lag, action=action):
                action(i - lag)

    def finish(self):
        for k, (number, lead, start) in enumerate(self.layout):
            spot = (slice(None), pl.ds(start, self.width))
            if lead is None:
                self.results[number][spot] = self.total[k]
            else:
                self.results[number][(lead,) + spot] = self.total[k]

        def drain(k, carry):
            self.core_copy(k, self.got_core.at[k]).wait_send()

            def sent(x_first):
                for hop in range(1, self.side):
                    self.one_copy(k, hop, x_first).wait_send()
                    self.two_copy(k, hop, x_first).wait_send()

            self.both_orders(k, sent)
            for hop in range(1, self.depth):
                self.deep_copy(k, hop).wait_send()
            return carry

        lax.fori_loop(0, self.count, drain, 0)


def split_refs(refs, *counts):
    groups, at = [], 0
    for count in counts:
        groups.append(refs[at : at + count])
        at += count
    return groups + [refs[at:]]


def params(call_id, mib):
    return pltpu.CompilerParams(
        collective_id=call_id, has_side_effects=True, vmem_limit_bytes=mib * 1024 * 1024
    )


def half_masks(width):
    lane = lax.broadcasted_iota(jnp.int32, (1, width), 1)
    return (lane < width // 2, lane >= width // 2)


def dot_rows(left, right):
    return lax.dot_general(left, right, (((1,), (1,)), ((), ())), preferred_element_type=F32)


def dot_first(left, right):
    return lax.dot_general(left, right, (((0,), (0,)), ((), ())), preferred_element_type=F32)


def dot_plain(left, right):
    return lax.dot_general(left, right, (((1,), (0,)), ((), ())), preferred_element_type=F32)


def prompt_mask(scores, chunk, z, rows):
    key = lax.broadcasted_iota(jnp.int32, scores.shape, 0) + chunk * rows
    query = lax.broadcasted_iota(jnp.int32, scores.shape, 1)
    seen = jnp.logical_or(query >= rows, key <= query + z * rows)
    return jnp.where(seen, scores, NEVER)


def own_mask(scores):
    key = lax.broadcasted_iota(jnp.int32, scores.shape, 0)
    query = lax.broadcasted_iota(jnp.int32, scores.shape, 1)
    return jnp.where(key <= query, scores, NEVER)


def forward_pair(p, z, rows, depth, q_ref, k_ref, v_ref, keys, vals, att_ref, lse_ref):
    cols = pl.ds(pl.multiple_of(p * PAIR, PAIR), PAIR)
    q_pair = q_ref[:, cols] * jnp.asarray(0.125, BF)
    k_own, v_own = k_ref[pl.ds(rows, rows), cols], v_ref[pl.ds(rows, rows), cols]
    outs = []
    for head, mask in enumerate(half_masks(PAIR)):
        q_head = jnp.where(mask, q_pair, jnp.zeros_like(q_pair))
        scores = [
            prompt_mask(dot_rows(keys[p, chunk], q_head), chunk, z, rows) for chunk in range(depth)
        ]
        own = own_mask(dot_rows(k_own, q_head[rows:]))
        top = jnp.max(scores[0], axis=0, keepdims=True)
        for piece in scores[1:]:
            top = jnp.maximum(top, jnp.max(piece, axis=0, keepdims=True))
        top_c = jnp.maximum(top[:, rows:], jnp.max(own, axis=0, keepdims=True))
        top = jnp.concatenate([top[:, :rows], top_c], axis=1)
        total = jnp.zeros_like(top)
        out = jnp.zeros((PAIR, 2 * rows), F32)
        for chunk in range(depth):
            expo = jnp.exp(scores[chunk] - top)
            total = total + jnp.sum(expo, axis=0, keepdims=True)
            out = out + dot_first(vals[p, chunk], expo.astype(BF))
        expo = jnp.exp(own - top_c)
        total_c = total[:, rows:] + jnp.sum(expo, axis=0, keepdims=True)
        out_c = out[:, rows:] + dot_first(v_own, expo.astype(BF))
        total = jnp.concatenate([total[:, :rows], total_c], axis=1)
        out = jnp.concatenate([out[:, :rows], out_c], axis=1) / total
        lse_ref[pl.ds(2 * p + head, 1), :] = top + jnp.log(total)
        outs.append(out[head * HDIM : (head + 1) * HDIM])
    att_ref[:, cols] = jnp.concatenate(outs, axis=0).T.astype(BF)


def backward_pair(p, z, rows, depth, q_ref, k_ref, v_ref, keys, vals, lse_ref, att_ref, g_ref,
                  dq_ref, dk_ref, dv_ref, part):
    cols = pl.ds(pl.multiple_of(p * PAIR, PAIR), PAIR)
    own_rows = pl.ds(rows, rows)
    q_pair = q_ref[:, cols] * jnp.asarray(0.125, BF)
    g_pair = g_ref[:, cols]
    k_own, v_own = k_ref[own_rows, cols], v_ref[own_rows, cols]
    pulled = (g_pair.astype(F32) * att_ref[:, cols].astype(F32)).T
    masks = half_masks(PAIR)
    q_heads = [jnp.where(mask, q_pair, jnp.zeros_like(q_pair)) for mask in masks]
    g_heads = [jnp.where(mask, g_pair, jnp.zeros_like(g_pair)) for mask in masks]
    lses = [lse_ref[pl.ds(2 * p + head, 1), :] for head in range(2)]
    deltas = [
        jnp.sum(pulled[head * HDIM : (head + 1) * HDIM], axis=0, keepdims=True)
        for head in range(2)
    ]
    dq = [jnp.zeros((PAIR, 2 * rows), F32) for _ in range(2)]
    for chunk in range(depth):
        dk = jnp.zeros((rows, PAIR), F32)
        dv = jnp.zeros((rows, PAIR), F32)
        k_chunk, v_chunk = keys[p, chunk], vals[p, chunk]
        for head in range(2):
            scores = prompt_mask(dot_rows(k_chunk, q_heads[head]), chunk, z, rows)
            prob = jnp.exp(scores - lses[head])
            d_prob = dot_rows(v_chunk, g_heads[head])
            d_score = (prob * (d_prob - deltas[head])).astype(BF)
            dv = dv + dot_plain(prob.astype(BF), g_heads[head])
            dk = dk + dot_plain(d_score, q_heads[head])
            dq[head] = dq[head] + dot_first(k_chunk, d_score)
        part[p, chunk, 0] = dk.astype(BF)
        part[p, chunk, 1] = dv.astype(BF)
    dk = jnp.zeros((rows, PAIR), F32)
    dv = jnp.zeros((rows, PAIR), F32)
    for head in range(2):
        q_head, g_head = q_heads[head][rows:], g_heads[head][rows:]
        scores = own_mask(dot_rows(k_own, q_head))
        prob = jnp.exp(scores - lses[head][:, rows:])
        d_prob = dot_rows(v_own, g_head)
        d_score = (prob * (d_prob - deltas[head][:, rows:])).astype(BF)
        dv = dv + dot_plain(prob.astype(BF), g_head)
        dk = dk + dot_plain(d_score, q_head)
        more = dot_first(k_own, d_score)
        dq[head] = jnp.concatenate([dq[head][:, :rows], dq[head][:, rows:] + more], axis=1)
    dk_ref[own_rows, cols] = dk.astype(BF)
    dv_ref[own_rows, cols] = dv.astype(BF)
    both = jnp.concatenate([dq[0][:HDIM], dq[1][HDIM:]], axis=0) * 0.125
    dq_ref[:, cols] = both.T.astype(BF)


class Exchange:
    def __init__(self, depth, rows, pairs):
        self.depth, self.rows, self.pairs = depth, rows, pairs
        dma = pltpu.SemaphoreType.DMA
        self.scratch = [dma((2, 2, pairs, depth)), dma((2, pairs, depth))]

    def bind(self, owned, gathered, scratch):
        self.owned, self.gathered = owned, gathered
        self.send_sem, self.recv_sem = scratch

    def hop(self, kind, p, zp, move, own=False):
        target = self.gathered[kind].at[p, zp]
        cols = pl.ds(pl.multiple_of(p * PAIR, PAIR), PAIR)
        source = self.owned[kind].at[pl.ds(0, self.rows), cols] if own else target
        z = lax.axis_index("fsdp")
        return remote(source, target, self.send_sem.at[kind, (move + 1) // 2, p, zp],
                      self.recv_sem.at[kind, p, zp], (lax.axis_index("dp"), z + move))

    def offer(self, p):
        z = lax.axis_index("fsdp")
        for move in (1, -1):
            @pl.when(z < self.depth - 1 if move > 0 else z > 0)
            def _(move=move):
                for kind in range(2):
                    self.hop(kind, p, z, move, own=True).start()
        cols = pl.ds(pl.multiple_of(p * PAIR, PAIR), PAIR)
        for kind in range(2):
            self.gathered[kind][p, z] = self.owned[kind][pl.ds(0, self.rows), cols]

    def step(self, i):
        z = lax.axis_index("fsdp")
        for distance in range(1, self.depth):
            p = i - (distance - 1) * HOP_LAG
            for sign in (1, -1):
                zp = z + sign * distance
                seen = jnp.logical_and(zp >= 0, zp < self.depth)

                @pl.when(jnp.logical_and(seen, jnp.logical_and(p >= 0, p < self.pairs)))
                def _(p=p, zp=zp, sign=sign):
                    for kind in range(2):
                        self.hop(kind, p, zp, 1).wait_recv()

                    @pl.when(z < self.depth - 1 if sign < 0 else z > 0)
                    def _():
                        for kind in range(2):
                            self.hop(kind, p, zp, -sign).start()

    def finish(self):
        z = lax.axis_index("fsdp")

        def drain(p, carry):
            for zp in range(self.depth):
                for move in (1, -1):
                    far = zp <= z if move > 0 else zp >= z
                    inner = z < self.depth - 1 if move > 0 else z > 0

                    @pl.when(jnp.logical_and(far, inner))
                    def _(zp=zp, move=move):
                        for kind in range(2):
                            self.hop(kind, p, zp, move).wait_send()
            return carry

        lax.fori_loop(0, self.pairs, drain, 0)


def project(normed_ref, weight, out_ref):
    width = 2 * PAIR

    def run(part, carry):
        cols = pl.ds(pl.multiple_of(part * width, width), width)
        piece = weight[..., cols].reshape(normed_ref.shape[1], width)
        out_ref[:, cols] = dot_plain(normed_ref[...], piece).astype(BF)
        return carry

    lax.fori_loop(0, out_ref.shape[1] // width, run, 0)


def forward_kernel(first, rest, exchange, slots, *refs):
    depth, rows, pairs = exchange.depth, exchange.rows, exchange.pairs
    n = len(rest.views)
    ((picks_ref, normed_ref), shard, shards, outs, (qkv,), full, swap, held,
     others) = split_refs(refs, 2, 1, n, 8, 1, n, len(exchange.scratch), len(first.scratch))
    counts_ref, q_ref, k_ref, v_ref, att_ref, lse_ref, keys, vals = outs
    first.bind(shard, (qkv,), held)
    rest.bind(shards, full, others)
    exchange.bind((k_ref, v_ref), (keys, vals), swap)
    z = lax.axis_index("fsdp")
    blocks = picks_ref.shape[1] // 128
    per_turn = -(-blocks // first.steps)
    greet(first.side, depth)
    for k in range(first.count):
        first.start(k)

    def gather(i, carry):
        for turn in range(first.steps):
            @pl.when(i == turn)
            def _(turn=turn):
                first.step(turn)
                if 0 <= turn - REST_START < rest.count:
                    rest.start(turn - REST_START)
                if turn >= REST_DELAY:
                    rest.step(turn - REST_DELAY)

        for inner in range(per_turn):
            block = i * per_turn + inner

            @pl.when(block < blocks)
            def _(block=block):
                count_block(block, rows, slots, picks_ref, counts_ref)

        return carry

    lax.fori_loop(0, first.steps, gather, 0)
    for k in range(max(0, first.steps - REST_START), rest.count):
        rest.start(k)
    first.settle()
    project(normed_ref, qkv.at[1], k_ref)
    project(normed_ref, qkv.at[2], v_ref)
    ahead = min(AHEAD, pairs)
    for p in range(ahead):
        exchange.offer(p)
    project(normed_ref, qkv.at[0], q_ref)
    done = max(0, first.steps - REST_DELAY)
    delay = (depth - 2) * HOP_LAG + 1
    turns = pairs + delay

    def run(i, carry):
        @pl.when(i + ahead < pairs)
        def _():
            exchange.offer(i + ahead)

        exchange.step(i)
        for turn in range(turns):
            number = done + turn
            if number < rest.steps:
                @pl.when(i == turn)
                def _(number=number):
                    rest.step(number)

        @pl.when(i >= delay)
        def _():
            forward_pair(i - delay, z, rows, depth, q_ref, k_ref, v_ref, keys, vals, att_ref,
                         lse_ref)

        return carry

    lax.fori_loop(0, turns, run, 0)
    for number in range(done + turns, rest.steps):
        rest.step(number)
    exchange.finish()
    rest.settle()
    first.finish()
    rest.finish()


def attention_forward(side, depth, picks, normed, w_qkv, shards, slots, call_id):
    rows, width = normed.shape[0] // 2, normed.shape[1]
    pairs = width // PAIR
    first, rest = Gather(side, depth, (w_qkv,), FIRST_PIECE), Gather(side, depth, shards)
    exchange = Exchange(depth, rows, pairs)
    any_space, vmem = pl.BlockSpec(memory_space=pl.ANY), pl.BlockSpec(memory_space=pltpu.VMEM)
    spread = jax.ShapeDtypeStruct((pairs, depth, rows, PAIR), BF)
    flat = jax.ShapeDtypeStruct(normed.shape, BF)
    results = pl.pallas_call(
        functools.partial(forward_kernel, first, rest, exchange, slots),
        out_shape=(
            jax.ShapeDtypeStruct((2, MH, slots, rows), BF),
            flat,
            flat,
            flat,
            flat,
            jax.ShapeDtypeStruct((2 * pairs, 2 * rows), F32),
            spread,
            spread,
        )
        + tuple(first.outs)
        + tuple(rest.outs),
        in_specs=[vmem] * 2 + [any_space] * (1 + len(rest.views)),
        out_specs=(vmem,) * 9 + (any_space,) * len(rest.views),
        scratch_shapes=exchange.scratch + first.scratch + rest.scratch,
        compiler_params=params(call_id, 56),
    )(picks, normed, *first.views, *rest.views)
    return results[:8], first.restore(results[8:9])[0], rest.restore(results[9:])


class Collect:
    def __init__(self, depth, rows, pairs):
        self.depth, self.rows, self.pairs = depth, rows, pairs
        dma = pltpu.SemaphoreType.DMA
        shape = (pairs, depth, 2, rows, PAIR)
        self.scratch = [
            pltpu.VMEM(shape, BF),
            pltpu.VMEM(shape, BF),
            pltpu.VMEM((pairs, 2, rows, PAIR), BF),
            pltpu.VMEM((2, rows, PAIR), F32),
            dma((2, pairs, depth)),
            dma((2, pairs, depth)),
        ]
        self.steps = pairs + (depth - 1) * COLLECT_LAG + 1

    def bind(self, scratch):
        (self.part, self.arrived, self.second, self.whole, self.send_sem,
         self.recv_sem) = scratch

    def hop(self, p, zd, move, final):
        z = lax.axis_index("fsdp")
        way = (move + 1) // 2
        target = self.second.at[p] if final and move < 0 else self.arrived.at[p, zd]
        return remote(self.part.at[p, zd], target, self.send_sem.at[way, p, zd],
                      self.recv_sem.at[way, p, zd], (lax.axis_index("dp"), z + move))

    def flow(self, p, move):
        depth = self.depth
        z = lax.axis_index("fsdp")
        first = z == 0 if move > 0 else z == depth - 1
        for zd in range(depth - 1, -1, -1) if move > 0 else range(depth):
            beyond = zd > z if move > 0 else zd < z

            @pl.when(jnp.logical_and(jnp.logical_not(first), beyond))
            def _(zd=zd):
                self.hop(p, zd, move, False).wait_recv()

                def add(part, carry):
                    self.part[p, zd, part] = self.part[p, zd, part] + self.arrived[p, zd, part]
                    return carry

                lax.fori_loop(0, 2, add, 0)

            @pl.when(jnp.logical_and(jnp.logical_not(first), zd == z))
            def _(zd=zd):
                self.hop(p, zd, move, True).wait_recv()

            @pl.when(zd == z + move)
            def _(zd=zd):
                self.hop(p, zd, move, True).start()

            @pl.when(jnp.logical_and(beyond, zd != z + move))
            def _(zd=zd):
                self.hop(p, zd, move, False).start()

    def step(self, i):
        depth = self.depth
        z = lax.axis_index("fsdp")
        for move in (1, -1):
            stage = z if move > 0 else depth - 1 - z
            p = i - stage * COLLECT_LAG

            @pl.when(jnp.logical_and(p >= 0, p < self.pairs))
            def _(p=p, move=move):
                self.flow(p, move)

    def result(self, p):
        z = lax.axis_index("fsdp")
        depth = self.depth
        whole = self.whole
        whole[...] = self.part[p, z].astype(F32)

        @pl.when(z > 0)
        def _():
            whole[...] = whole[...] + self.arrived[p, z].astype(F32)

        @pl.when(z < depth - 1)
        def _():
            whole[...] = whole[...] + self.second[p].astype(F32)

        return whole[...]

    def finish(self):
        depth = self.depth
        z = lax.axis_index("fsdp")

        def drain(p, carry):
            for zd in range(depth):
                for move in (1, -1):
                    @pl.when(zd > z if move > 0 else zd < z)
                    def _(zd=zd, move=move):
                        self.hop(p, zd, move, False).wait_send()
            return carry

        lax.fori_loop(0, self.pairs, drain, 0)


def produce(late, stage, kind, half, normed_ref, grad_ref):
    side, depth, block, width = late.side, late.depth, late.block, late.width
    k = 2 * kind + half
    run = depth * block
    for start in range(0, normed_ref.shape[1], 2 * PAIR):
        value = dot_first(
            normed_ref[:, start : start + 2 * PAIR], grad_ref[:, half * width : (half + 1) * width]
        ).astype(BF)
        for row in range(0, 2 * PAIR, run):
            number = (start + row) // run
            y, x, core = number // (2 * side), (number // 2) % side, number % 2
            stage[k, y, x, :, :, core * width : (core + 1) * width] = value[row : row + run].reshape(
                depth, block, width)


def backward_kernel(early, late, collect, *refs):
    side, depth, rows, pairs = early.side, collect.depth, collect.rows, collect.pairs
    n = len(early.views)
    ins, grads, (dq_ref, dk_ref, dv_ref), sums, (qkv_sum,), swap, first, second = split_refs(
        refs, 9, n, 3, n, 1, len(collect.scratch), len(early.scratch))
    q_ref, k_ref, v_ref, keys, vals, lse_ref, att_ref, g_ref, normed_ref = ins

    def part_of(k, half):
        number, lead, start = early.layout[k]
        ref = grads[number] if lead is None else grads[number].at[lead]
        return ref.at[:, :, half, :, :, pl.ds(start, early.width)]

    early.bind(part_of, sums, first)
    stage = early.got_core

    def late_part(k, half):
        lanes = pl.ds(pl.multiple_of(half * late.width, late.width), late.width)
        return stage.at[k, :, :, :, :, lanes]

    late.bind(late_part, (qkv_sum,), second)
    collect.bind(swap)
    z = lax.axis_index("fsdp")
    greet(side, depth)
    for k in range(early.count):
        early.start(k)
    last = (depth - 1) * COLLECT_LAG
    ready = max(pairs, early.count)
    settled = max(pairs + last, ready + 2)
    late_at = settled - 1
    due = [ready, ready + 1, settled, settled + 1, settled + 2, settled + 3]

    def run(i, carry):
        @pl.when(i < pairs)
        def _():
            backward_pair(i, z, rows, depth, q_ref, k_ref, v_ref, keys, vals, lse_ref, att_ref,
                          g_ref, dq_ref, dk_ref, dv_ref, collect.part)

        collect.step(i)
        early.step(i)

        @pl.when(jnp.logical_and(i >= last, i < last + pairs))
        def _():
            p = i - last
            cols = pl.ds(pl.multiple_of(p * PAIR, PAIR), PAIR)
            value = collect.result(p)
            dk_ref[pl.ds(0, rows), cols] = value[0].astype(BF)
            dv_ref[pl.ds(0, rows), cols] = value[1].astype(BF)

        late.step(i - late_at)
        for number, when in enumerate(due):
            @pl.when(i == when)
            def _(number=number):
                kind = number // 2
                produce(late, stage, kind, number % 2, normed_ref, (dq_ref, dk_ref, dv_ref)[kind])
                late.start(number)

        return carry

    lax.fori_loop(0, max(early.steps, late_at + late.steps), run, 0)
    collect.finish()
    early.finish()
    late.finish()


def attention_backward(side, depth, q, k, v, keys, vals, lse, att, grad_att, normed, grads, w_qkv,
                       call_id):
    rows, width = q.shape[0] // 2, q.shape[1]
    early = Reduce(side, depth, grads, width, DEEP_AT)
    late = Reduce(side, depth, (w_qkv,), width // 2, 2 * LAG)
    collect = Collect(depth, rows, width // PAIR)
    any_space, vmem = pl.BlockSpec(memory_space=pl.ANY), pl.BlockSpec(memory_space=pltpu.VMEM)
    results = pl.pallas_call(
        functools.partial(backward_kernel, early, late, collect),
        out_shape=(jax.ShapeDtypeStruct(q.shape, BF),) * 3 + tuple(early.outs) + tuple(late.outs),
        in_specs=[vmem] * 9 + [any_space] * len(grads),
        out_specs=(vmem,) * (4 + len(grads)),
        scratch_shapes=collect.scratch + early.scratch + late.scratch,
        compiler_params=params(call_id, 63),
    )(
        q,
        k,
        v,
        keys,
        vals,
        lse,
        att,
        grad_att,
        normed,
        *[grad.reshape(view) for grad, view in zip(grads, early.views)],
    )
    return results[:3], results[3:-1], results[-1]


def count_block(b, rows, slots, picks_ref, counts_ref):
    low, per_word, bits = 16, 5, 6
    groups = -(-(slots // low) // per_word)
    per_head = rows // 128
    cols = pl.ds(pl.multiple_of(b * 128, 128), 128)
    picks = picks_ref[:, cols]
    high = jnp.right_shift(picks, 4)
    group = jnp.right_shift(high * 13, 6)
    word = group * low + jnp.bitwise_and(picks, low - 1)
    unit = jnp.left_shift(jnp.ones_like(picks), bits * (high - per_word * group))
    spot = lax.broadcasted_iota(jnp.int32, (groups * low, 128), 0)
    words = jnp.zeros((groups * low, 128), jnp.int32)
    for pick in range(picks.shape[0]):
        words = words + jnp.where(spot == word[pick : pick + 1], unit[pick : pick + 1], 0)
    part, head = b // (per_head * MH), (b // per_head) % MH
    lanes = pl.ds(pl.multiple_of((b % per_head) * 128, 128), 128)
    for tile in range(slots // low):
        piece = words[(tile // per_word) * low : (tile // per_word + 1) * low]
        count = jnp.bitwise_and(jnp.right_shift(piece, bits * (tile % per_word)), 2**bits - 1)
        counts_ref[part, head, pl.ds(tile * low, low), lanes] = count.astype(F32).astype(BF)


def selector(ids_ref, index, count):
    ids = ids_ref[pl.ds(index, 1), :]
    spot = lax.broadcasted_iota(jnp.int32, (count, ids.shape[1]), 0)
    return jnp.where(spot == ids, 1.0, 0.0).astype(BF)


def picks_kernel(ids_ref, counts_ref, query_ref, keys_ref, weight_ref, mixing_ref, total):
    part, head = pl.program_id(0), pl.program_id(1)
    scores = None
    for half in range(2):
        pick = selector(ids_ref, 2 * part + half, SUB)
        slot_keys = dot_first(pick, keys_ref[half * SUB : (half + 1) * SUB]).astype(BF)
        piece = dot_rows(slot_keys, query_ref[:, half * HALF : (half + 1) * HALF])
        scores = piece if scores is None else scores + piece
    count = counts_ref[0, 0].astype(F32)
    named = count > 0.0
    top = jnp.max(jnp.where(named, scores, -jnp.inf), axis=0, keepdims=True)
    raised = jnp.where(named, count * jnp.exp(scores - top), 0.0)
    weight = raised / jnp.sum(raised, axis=0, keepdims=True)
    weight_ref[0, 0] = weight

    @pl.when(head == 0)
    def _():
        total[...] = weight

    @pl.when(head > 0)
    def _():
        total[...] = total[...] + weight

    @pl.when(head == MH - 1)
    def _():
        mixing_ref[0] = total[...].astype(BF)


def slot_weights(ids, counts, mquery, keys_full):
    slots, rows = counts.shape[2:]
    return pl.pallas_call(
        picks_kernel,
        grid=(2, MH),
        out_shape=(
            jax.ShapeDtypeStruct(counts.shape, F32),
            jax.ShapeDtypeStruct((2, slots, rows), BF),
        ),
        in_specs=[
            pl.BlockSpec(ids.shape, lambda u, m: (0, 0)),
            pl.BlockSpec((1, 1, slots, rows), lambda u, m: (u, m, 0, 0)),
            pl.BlockSpec((rows, 2 * HALF), lambda u, m: (u, m)),
            pl.BlockSpec((2 * SUB, HALF), lambda u, m: (m, 0)),
        ],
        out_specs=(
            pl.BlockSpec((1, 1, slots, rows), lambda u, m: (u, m, 0, 0)),
            pl.BlockSpec((1, slots, rows), lambda u, m: (u, 0, 0)),
        ),
        scratch_shapes=[pltpu.VMEM((slots, rows), F32)],
        cost_estimate=pl.CostEstimate(
            flops=2 * 2 * MH * slots * 2 * HALF * (SUB + rows),
            bytes_accessed=24 * 2**20,
            transcendentals=2 * MH * slots * rows,
        ),
    )(ids, counts, mquery, keys_full)


def picks_back_kernel(block, ids_ref, weight_ref, table_ref, memory_ref, query_ref, keys_ref,
                      grad_query_ref, grad_keys_ref, grad_mixing, total):
    head, part = pl.program_id(0), pl.program_id(1)

    @pl.when(head == 0)
    def _():
        grad_mixing[part] = dot_rows(table_ref[0], memory_ref[...])

    weight = weight_ref[0, 0]
    pulled = weight * grad_mixing[part]
    grad = pulled - weight * jnp.sum(pulled, axis=0, keepdims=True)
    high = grad.astype(BF)
    low = (grad - high.astype(F32)).astype(BF)
    for half in range(2):
        pick = selector(ids_ref, 2 * part + half, SUB)
        sub = (dot_plain(pick, high) + dot_plain(pick, low)).astype(BF)
        span = slice(half * HALF, (half + 1) * HALF)
        keys = keys_ref[half * SUB : (half + 1) * SUB]
        grad_query_ref[:, span] = dot_first(sub, keys).astype(BF)
        piece = dot_plain(sub, query_ref[:, span])
        rows = slice(half * SUB, (half + 1) * SUB)

        @pl.when(part == 0)
        def _(piece=piece, rows=rows):
            total[rows] = piece

        @pl.when(part == 1)
        def _(piece=piece, rows=rows):
            total[rows] = total[rows] + piece

    @pl.when(part == 1)
    def _():
        for shard in range(SUB // block):
            for side in range(2):
                start = (2 * shard + side) * block
                grad_keys_ref[shard * block : (shard + 1) * block, side * HALF : (side + 1) * HALF] = (
                    total[start : start + block].astype(BF))


def slot_weights_back(ids, weights, table, grad_memory, mquery, keys_full, block):
    slots, rows = weights.shape[2:]
    width = table.shape[2]
    return pl.pallas_call(
        functools.partial(picks_back_kernel, block),
        grid=(MH, 2),
        out_shape=(
            jax.ShapeDtypeStruct(mquery.shape, BF),
            jax.ShapeDtypeStruct((MH * SUB, 2 * HALF), BF),
        ),
        in_specs=[
            pl.BlockSpec(ids.shape, lambda m, u: (0, 0)),
            pl.BlockSpec((1, 1, slots, rows), lambda m, u: (u, m, 0, 0)),
            pl.BlockSpec((1, slots, width), lambda m, u: (jnp.where(m == 0, u, 1), 0, 0)),
            pl.BlockSpec((rows, width), lambda m, u: (jnp.where(m == 0, u, 1), 0)),
            pl.BlockSpec((rows, 2 * HALF), lambda m, u: (u, m)),
            pl.BlockSpec((2 * SUB, HALF), lambda m, u: (m, 0)),
        ],
        out_specs=(
            pl.BlockSpec((rows, 2 * HALF), lambda m, u: (u, m)),
            pl.BlockSpec((SUB, 2 * HALF), lambda m, u: (m, 0)),
        ),
        scratch_shapes=[pltpu.VMEM((2, slots, rows), F32), pltpu.VMEM((2 * SUB, HALF), F32)],
        cost_estimate=pl.CostEstimate(
            flops=2 * 2 * MH * slots * rows * (4 * SUB + 4 * HALF),
            bytes_accessed=24 * 2**20,
            transcendentals=0,
        ),
    )(ids, weights, table, grad_memory, mquery, keys_full)


def one_hot(ids, count):
    return (ids[:, None] == jnp.arange(count, dtype=jnp.int32)[None, :]).astype(BF)


def per_device(
    x_prompt,
    x_cont,
    cot_prompt,
    cot_cont,
    gain_attn,
    gain_mem,
    w_qkv,
    w_attn_out,
    w_mem_query,
    sub_keys,
    w_gate,
    w_mem_out,
    value_rows,
    request,
    slot_prompt,
    slot_cont,
):
    shard_rows, width = value_rows.shape
    owners, capacity = request.shape[2:]
    slots = owners * capacity
    rows = x_prompt.shape[1]
    cols = w_qkv.shape[2]
    block = cols // owners
    side, depth = grid_of(lax.axis_size("dp"), lax.axis_size("fsdp"))

    asked = lax.all_to_all(request[:, 0], ALL, split_axis=1, concat_axis=1, tiled=True)
    serve_picks = [one_hot(asked[part].reshape(-1), shard_rows) for part in range(2)]

    def swap(values):
        values = values.reshape(owners, capacity, width)
        swapped = lax.all_to_all(values, ALL, split_axis=0, concat_axis=0, tiled=True)
        return swapped.reshape(slots, width)

    served = [mm(pick, value_rows).astype(BF) for pick in serve_picks]
    offsets = jnp.maximum(request[:, 0].reshape(2, slots), 0)
    picked = (jnp.arange(slots, dtype=jnp.int32) // capacity)[None] * shard_rows + offsets
    ids = jnp.stack([picked // SUB, picked % SUB], axis=1).reshape(4, slots)
    x_rows = jnp.concatenate([x_prompt[0], x_cont[0]], axis=0).astype(F32)
    dy_low = jnp.concatenate([cot_prompt[0], cot_cont[0]], axis=0)
    normed, inverse = normalize(x_rows, gain_attn)
    normed = normed.astype(BF)
    picks = jnp.stack([slot_prompt[0], slot_cont[0]]).transpose(3, 0, 2, 1)
    picks, served = lax.optimization_barrier((picks.reshape(picks.shape[0], -1), served))
    tables = [swap(served[0])]
    results, qkv_full, full = attention_forward(
        side,
        depth,
        picks,
        normed,
        w_qkv,
        (w_attn_out, w_mem_query, sub_keys, w_gate, w_mem_out),
        slots,
        0,
    )
    counts, queries, keys, vals, att, lse, all_keys, all_vals = results
    attn_out_full, query_full, keys_full, gate_full, mem_out_full = full
    att, late, tables[0] = lax.optimization_barrier((att, served[1], tables[0]))
    tables.append(swap(late))
    hidden = x_rows + mm(att, attn_out_full)
    normed2, inverse2 = normalize(hidden, gain_mem)
    normed2 = normed2.astype(BF)

    mquery = mm(normed2, query_full).astype(BF)
    gate_pre = mm(normed2, gate_full)
    weights, mixing = slot_weights(ids, counts, mquery, keys_full)
    memory_out = jnp.concatenate([mm_l(mixing[part], tables[part]) for part in range(2)], axis=0)
    sigmoid_gate = jax.nn.sigmoid(gate_pre)
    blended = (memory_out * (gate_pre * sigmoid_gate)).astype(BF)
    out = (hidden + mm(blended, mem_out_full)).astype(BF)

    grad_blend = mm_t(dy_low, mem_out_full)
    grad_mem_out = mm_l(blended, dy_low)
    grad_memory = (grad_blend * gate_pre * sigmoid_gate).astype(BF)
    grad_gate = (
        grad_blend * memory_out * sigmoid_gate * (1.0 + gate_pre * (1.0 - sigmoid_gate))
    ).astype(BF)
    slot_grads = [
        mm(mixing[part], grad_memory[part * rows : (part + 1) * rows]).astype(BF)
        for part in range(2)
    ]
    arrived = [None, swap(slot_grads[1])]
    grad_query, grad_keys = slot_weights_back(
        ids, weights, jnp.stack(tables), grad_memory, mquery, keys_full, block
    )
    grad_query, arrived[1], late = lax.optimization_barrier((grad_query, arrived[1], slot_grads[0]))
    arrived[0] = swap(late)
    grad_normed2 = mm_t(grad_query, query_full) + mm_t(grad_gate, gate_full)
    grad_query_w = mm_l(normed2, grad_query).astype(BF)
    grad_gate_w = mm_l(normed2, grad_gate).astype(BF)
    back, gain_mem_part = norm_backward(hidden, inverse2, gain_mem, grad_normed2)
    grad_hidden = dy_low.astype(F32) + back
    hidden_low = grad_hidden.astype(BF)
    grad_attn_out = mm_l(att, hidden_low).astype(BF)
    grad_att = mm_t(hidden_low, attn_out_full).astype(BF)
    grad_att, arrived = lax.optimization_barrier((grad_att, arrived))
    (grad_q, grad_k, grad_v), early, qkv_shard = attention_backward(
        side,
        depth,
        queries,
        keys,
        vals,
        all_keys,
        all_vals,
        lse,
        att,
        grad_att,
        normed,
        (grad_query_w, grad_keys, grad_gate_w, grad_mem_out.astype(BF), grad_attn_out),
        qkv_full,
        1,
    )
    grad_rows = mm_l(jnp.concatenate(serve_picks, axis=0), jnp.concatenate(arrived, axis=0))
    grad_normed = (
        mm_t(grad_q, qkv_full[0]) + mm_t(grad_k, qkv_full[1]) + mm_t(grad_v, qkv_full[2])
    )
    grad_x, gain_attn_part = norm_backward(x_rows, inverse, gain_attn, grad_normed)
    grad_x = grad_hidden + grad_x
    gains = jnp.stack([gain_attn_part, gain_mem_part]).reshape(2, owners, block)
    gains = lax.all_to_all(gains.transpose(1, 0, 2), ALL, split_axis=0, concat_axis=0, tiled=True)
    gain_shards = jnp.sum(gains, axis=0)
    sub_shard = early[1].reshape(block, 2, HALF).transpose(1, 0, 2).reshape(2 * block, HALF)
    return (
        out[None, :rows],
        out[None, rows:],
        grad_x[None, :rows],
        grad_x[None, rows:],
        gain_shards[0],
        gain_shards[1],
        qkv_shard,
        early[4],
        early[0],
        sub_shard,
        early[2],
        early[3],
        grad_rows,
    )


def solution(mesh):
    in_specs = (
        P("dp", "fsdp", None),
        P("dp", "fsdp", None),
        P("dp", "fsdp", None),
        P("dp", "fsdp", None),
        P(),
        P(),
        P(None, "fsdp", None),
        P("fsdp", None),
        P("fsdp", None),
        P("fsdp", None),
        P("fsdp", None),
        P("fsdp", None),
        P(("dp", "fsdp"), None),
        P(None, ("dp", "fsdp"), None, None),
        P("dp", "fsdp", None, None),
        P("dp", "fsdp", None, None),
    )
    out_specs = (
        P("dp", "fsdp", None),
        P("dp", "fsdp", None),
        P("dp", "fsdp", None),
        P("dp", "fsdp", None),
        P(("dp", "fsdp")),
        P(("dp", "fsdp")),
        P(None, ("dp", "fsdp"), None),
        P(("dp", "fsdp"), None),
        P(("dp", "fsdp"), None),
        P(("dp", "fsdp"), None),
        P(("dp", "fsdp"), None),
        P(("dp", "fsdp"), None),
        P(("dp", "fsdp"), None),
    )
    return jax.shard_map(
        per_device, mesh=mesh, in_specs=in_specs, out_specs=out_specs, check_vma=False
    )
```

```python
import functools
import jax
import jax.numpy as jnp
from jax import lax
from jax.experimental import pallas as pl
from jax.experimental.pallas import tpu as pltpu
from jax.sharding import PartitionSpec as P
BF = jnp.bfloat16
F32 = jnp.float32
ALL = ("dp", "fsdp")
MESH = pl.DeviceIdType.MESH
LAG = 3
GATHER_LAG = 3
REST_START = 1
REST_DELAY = 8
DEEP_AT = 10
COLLECT_LAG = 2
AHEAD = 3
HOP_LAG = 1
PAIR = 128
HDIM = 64
MH = 4
HALF = 512
SUB = 256
NEVER = -1e30


def mm(left, right):
    return jnp.dot(left, right, preferred_element_type=F32)


def mm_t(left, right):
    return lax.dot_general(left, right, (((1,), (1,)), ((), ())), preferred_element_type=F32)


def mm_l(left, right):
    return lax.dot_general(left, right, (((0,), (0,)), ((), ())), preferred_element_type=F32)


def normalize(matrix, gain_vec):
    inverse = lax.rsqrt(jnp.mean(matrix * matrix, axis=-1, keepdims=True) + 1e-05)
    return (matrix * inverse * gain_vec, inverse)


def norm_backward(matrix, inverse, gain_vec, grad_normed):
    scaled = gain_vec * grad_normed
    cubed = inverse * inverse * inverse
    grad_matrix = inverse * scaled - matrix * cubed * jnp.mean(
        matrix * scaled, axis=-1, keepdims=True
    )
    return (grad_matrix, jnp.sum(grad_normed * matrix * inverse, axis=0))


def grid_of(plane, depth):
    side = 1
    while 2 * side * side < plane:
        side += 1
    return side, depth


def place(side):
    dp = lax.axis_index("dp")
    return (dp // (2 * side), (dp // 2) % side, dp % 2, lax.axis_index("fsdp"))


def device_at(side, y, x, core, z):
    return ((y * side + x) * 2 + core, z)


def greet(side, depth):
    y, x, core, z = place(side)
    barrier = pltpu.get_barrier_semaphore()
    peers = [device_at(side, y, x, 1 - core, z)]
    for hop in range(1, side):
        peers.append(device_at(side, y, (x + hop) % side, core, z))
        peers.append(device_at(side, (y + hop) % side, x, core, z))
    for hop in range(1, depth):
        peers.append(device_at(side, y, x, core, (z + hop) % depth))
    for peer in peers:
        pl.semaphore_signal(barrier, inc=1, device_id=peer, device_id_type=MESH)
    pl.semaphore_wait(barrier, len(peers))


def remote(source, target, send_sem, recv_sem, peer):
    return pltpu.make_async_remote_copy(
        src_ref=source,
        dst_ref=target,
        send_sem=send_sem,
        recv_sem=recv_sem,
        device_id=peer,
        device_id_type=MESH,
    )


class Gather:
    def __init__(self, side, depth, shards, piece=1024):
        self.side, self.depth = side, depth
        self.views, self.outs, self.shapes, self.held, self.layout = [], [], [], [], []
        plane = 2 * side * side
        for shard in shards:
            rows, cols = shard.shape[-2:]
            block, width = rows // plane, min(cols, piece)
            lead = shard.shape[:-2]
            self.views.append(shard.reshape(lead + (side, side, 2, block, cols)))
            leads = range(lead[0]) if lead else (None,)
            self.layout.append(
                [(number, start) for number in leads for start in range(0, cols, width)]
            )
            self.outs.append(
                jax.ShapeDtypeStruct(lead + (depth, side, side, 2, block, cols), BF)
            )
            self.shapes.append(lead + (depth * rows, cols))
            self.held.append(
                pltpu.VMEM((len(self.layout[-1]), side, side, 2, block, width), BF)
            )
        self.count = count = sum(len(columns) for columns in self.layout)
        self.steps = count + depth - 2 + 3 * GATHER_LAG
        dma = pltpu.SemaphoreType.DMA
        self.scratch = self.held + [
            dma((count,)),
            dma((count,)),
            dma((count, depth)),
            dma((count, depth)),
            dma((count, depth)),
            dma((count, depth, side - 1)),
            dma((count, depth, side - 1)),
            dma((count, depth, side - 1)),
            dma((count, depth, side - 1)),
            dma((count, depth)),
            dma((count, depth)),
        ]

    def restore(self, full):
        return [one.reshape(shape) for one, shape in zip(full, self.shapes)]

    def bind(self, sources, outs, scratch):
        self.sources, self.results = sources, outs
        n_in = len(self.layout)
        self.holders = scratch[:n_in]
        (self.in_sem, self.out_sem, self.right_send, self.left_send, self.deep_recv,
         self.one_send, self.one_recv, self.two_send, self.two_recv, self.core_send,
         self.core_recv) = scratch[n_in:]
        self.pieces = []
        for number, columns in enumerate(self.layout):
            width = self.holders[number].shape[-1]
            width = width if sources[number].shape[-1] > width else None
            for inner, (lead, start) in enumerate(columns):
                self.pieces.append((number, lead, start, width, inner))

    def cut(self, refs, k, *spot):
        number, lead, start, width = self.pieces[k][:4]
        ref = refs[number] if lead is None else refs[number].at[lead]
        ref = ref.at[spot] if spot else ref
        if width is None:
            return ref
        return ref.at[(slice(None),) * (len(ref.shape) - 1) + (pl.ds(start, width),)]

    def along_z(self, k, zp, move, source=None):
        y, x, core, z = place(self.side)
        target = self.cut(self.results, k, zp, y, x, core)
        send = self.right_send if move > 0 else self.left_send
        return remote(target if source is None else source, target, send.at[k, zp],
                      self.deep_recv.at[k, zp], device_at(self.side, y, x, core, z + move))

    def one_copy(self, k, zp, hop):
        side = self.side
        y, x, core, z = place(side)
        peer = device_at(side, y, (x + hop) % side, core, z) if k % 2 == 0 else device_at(
            side, (y + hop) % side, x, core, z)
        ref = self.cut(self.results, k, zp, y, x, core)
        return remote(ref, ref, self.one_send.at[k, zp, hop - 1],
                      self.one_recv.at[k, zp, hop - 1], peer)

    def two_copy(self, k, zp, hop):
        side = self.side
        y, x, core, z = place(side)
        x_first = k % 2 == 0
        peer = device_at(side, (y + hop) % side, x, core, z) if x_first else device_at(
            side, y, (x + hop) % side, core, z)
        ref = (self.cut(self.results, k, zp, y, slice(None), core) if x_first
               else self.cut(self.results, k, zp, slice(None), x, core))
        return remote(ref, ref, self.two_send.at[k, zp, hop - 1],
                      self.two_recv.at[k, zp, hop - 1], peer)

    def core_copy(self, k, zp):
        y, x, core, z = place(self.side)
        ref = self.cut(self.results, k, zp, slice(None), slice(None), core)
        return remote(ref, ref, self.core_send.at[k, zp], self.core_recv.at[k, zp],
                      device_at(self.side, y, x, 1 - core, z))

    def take(self, k):
        number, inner = self.pieces[k][0], self.pieces[k][4]
        return pltpu.make_async_copy(self.cut(self.sources, k), self.holders[number].at[inner],
                                     self.in_sem.at[k])

    def put(self, k):
        z = place(self.side)[3]
        number, inner = self.pieces[k][0], self.pieces[k][4]
        return pltpu.make_async_copy(self.holders[number].at[inner],
                                     self.cut(self.results, k, z), self.out_sem.at[k])

    def start(self, k):
        y, x, core, z = place(self.side)
        self.take(k).start()
        own = self.cut(self.sources, k, y, x, core)

        @pl.when(z < self.depth - 1)
        def _():
            self.along_z(k, z, 1, own).start()

        @pl.when(z > 0)
        def _():
            self.along_z(k, z, -1, own).start()

    def step(self, i):
        side, depth = self.side, self.depth
        z = place(side)[3]
        if i < self.count:
            self.take(i).wait()
            self.put(i).start()
        for stage in range(4):
            for distance in range(1, depth):
                k = i - stage * GATHER_LAG - (distance - 1)
                if not 0 <= k < self.count:
                    continue
                for sign in (1, -1):
                    zp = z + sign * distance

                    @pl.when(jnp.logical_and(zp >= 0, zp < depth))
                    def _(k=k, zp=zp, sign=sign, stage=stage):
                        self.arrival(stage, k, zp, sign)

    def arrival(self, stage, k, zp, sign):
        side, depth = self.side, self.depth
        z = place(side)[3]
        if stage == 0:
            self.along_z(k, zp, 1).wait_recv()

            @pl.when(z < depth - 1 if sign < 0 else z > 0)
            def _():
                self.along_z(k, zp, -sign).start()

            for hop in range(1, side):
                self.one_copy(k, zp, hop).start()
        elif stage == 1:
            for hop in range(1, side):
                self.one_copy(k, zp, hop).wait_recv()
            for hop in range(1, side):
                self.two_copy(k, zp, hop).start()
        elif stage == 2:
            for hop in range(1, side):
                self.two_copy(k, zp, hop).wait_recv()
            self.core_copy(k, zp).start()
        else:
            self.core_copy(k, zp).wait_recv()

    def settle(self):
        for k in range(self.count):
            self.put(k).wait()

    def finish(self):
        side, depth = self.side, self.depth
        z = place(side)[3]
        for k in range(self.count):
            for zp in range(depth):
                @pl.when(jnp.logical_and(zp <= z, z < depth - 1))
                def _(k=k, zp=zp):
                    self.along_z(k, zp, 1).wait_send()

                @pl.when(jnp.logical_and(zp >= z, z > 0))
                def _(k=k, zp=zp):
                    self.along_z(k, zp, -1).wait_send()

                @pl.when(zp != z)
                def _(k=k, zp=zp):
                    for hop in range(1, side):
                        self.one_copy(k, zp, hop).wait_send()
                        self.two_copy(k, zp, hop).wait_send()
                    self.core_copy(k, zp).wait_send()


class Reduce:
    def __init__(self, side, depth, grads, piece, deep_at):
        self.side, self.depth, self.deep_at = side, depth, deep_at
        self.layout, self.views, self.outs = [], [], []
        self.width = width = piece
        devices = 2 * side * side * depth
        for grad in grads:
            rows, cols = grad.shape[-2:]
            self.block = block = rows // devices
            lead = grad.shape[:-2]
            self.views.append(lead + (side, side, 2, depth, block, cols))
            leads = range(lead[0]) if lead else (None,)
            self.layout += [
                (len(self.outs), number, start) for number in leads for start in range(0, cols, width)
            ]
            self.outs.append(jax.ShapeDtypeStruct(lead + (block, cols), F32))
        self.count = count = len(self.layout)
        self.steps = count + deep_at + LAG
        dma = pltpu.SemaphoreType.DMA
        self.scratch = [
            pltpu.VMEM((count, side, side, depth, block, width), BF),
            pltpu.VMEM((count, side, side, depth, block, width), BF),
            pltpu.VMEM((count, side - 1, side, depth, block, width), BF),
            pltpu.VMEM((count, side - 1, depth, block, width), BF),
            pltpu.VMEM((count, depth - 1, block, width), BF),
            pltpu.VMEM((count, block, width), F32),
            dma((count,)),
            dma((count,)),
            dma((count,)),
            dma((count, side - 1)),
            dma((count, side - 1)),
            dma((count, side - 1)),
            dma((count, side - 1)),
            dma((count, depth - 1)),
            dma((count, depth - 1)),
        ]

    def bind(self, sources, outs, scratch):
        (self.mine, self.got_core, self.got_one, self.got_two, self.got_deep, self.total,
         self.local_sem, self.core_send, self.core_recv, self.one_send, self.one_recv,
         self.two_send, self.two_recv, self.deep_send, self.deep_recv) = scratch
        self.results, self.sources = outs, sources

    def core_copy(self, k, source):
        y, x, core, z = place(self.side)
        return remote(source, self.got_core.at[k], self.core_send.at[k],
                      self.core_recv.at[k], device_at(self.side, y, x, 1 - core, z))

    def start(self, k):
        core = place(self.side)[2]
        self.core_copy(k, self.sources(k, 1 - core)).start()
        pltpu.make_async_copy(self.sources(k, core), self.mine.at[k], self.local_sem.at[k]).start()

    def one_copy(self, k, hop, x_first):
        side = self.side
        y, x, core, z = place(side)
        peer = device_at(side, y, (x + hop) % side, core, z) if x_first else device_at(
            side, (y + hop) % side, x, core, z)
        source = (self.mine.at[k, :, (x + hop) % side] if x_first
                  else self.mine.at[k, (y + hop) % side])
        return remote(source, self.got_one.at[k, hop - 1], self.one_send.at[k, hop - 1],
                      self.one_recv.at[k, hop - 1], peer)

    def two_copy(self, k, hop, x_first):
        side = self.side
        y, x, core, z = place(side)
        peer = device_at(side, (y + hop) % side, x, core, z) if x_first else device_at(
            side, y, (x + hop) % side, core, z)
        source = (self.mine.at[k, (y + hop) % side, x] if x_first
                  else self.mine.at[k, y, (x + hop) % side])
        return remote(source, self.got_two.at[k, hop - 1], self.two_send.at[k, hop - 1],
                      self.two_recv.at[k, hop - 1], peer)

    def deep_copy(self, k, hop):
        y, x, core, z = place(self.side)
        there = (z + hop) % self.depth
        return remote(self.mine.at[k, y, x, there], self.got_deep.at[k, hop - 1],
                      self.deep_send.at[k, hop - 1], self.deep_recv.at[k, hop - 1],
                      device_at(self.side, y, x, core, there))

    def both_orders(self, k, action):
        @pl.when(k % 2 == 0)
        def _():
            action(True)

        @pl.when(k % 2 == 1)
        def _():
            action(False)

    def added(self, base, others):
        if len(others) == 1:
            return base + others[0]
        value = base.astype(F32)
        for other in others:
            value = value + other.astype(F32)
        return value.astype(base.dtype)

    def after_core(self, k):
        side, depth, mine, got = self.side, self.depth, self.mine, self.got_core
        self.core_copy(k, got.at[k]).wait_recv()
        pltpu.make_async_copy(got.at[k], mine.at[k], self.local_sem.at[k]).wait()

        def add(index, carry):
            spot = (k, index // (side * depth), (index // depth) % side, index % depth)
            mine[spot] = mine[spot] + got[spot]
            return carry

        lax.fori_loop(0, side * side * depth, add, 0)

        def send(x_first):
            for hop in range(1, side):
                self.one_copy(k, hop, x_first).start()

        self.both_orders(k, send)

    def after_one(self, k):
        side, depth, mine = self.side, self.depth, self.mine
        y, x, core, z = place(side)

        def finish(x_first):
            for hop in range(1, side):
                self.one_copy(k, hop, x_first).wait_recv()

            def add(index, carry):
                a, c = index // depth, index % depth
                spot = (k, a, x, c) if x_first else (k, y, a, c)
                mine[spot] = self.added(
                    mine[spot], [self.got_one[k, hop, a, c] for hop in range(side - 1)]
                )
                return carry

            lax.fori_loop(0, side * depth, add, 0)
            for hop in range(1, side):
                self.two_copy(k, hop, x_first).start()

        self.both_orders(k, finish)

    def after_two(self, k):
        side, depth, mine = self.side, self.depth, self.mine
        y, x, core, z = place(side)

        def finish(x_first):
            for hop in range(1, side):
                self.two_copy(k, hop, x_first).wait_recv()

        self.both_orders(k, finish)

        def add(c, carry):
            mine[k, y, x, c] = self.added(
                mine[k, y, x, c], [self.got_two[k, hop, c] for hop in range(side - 1)]
            )
            return carry

        lax.fori_loop(0, depth, add, 0)

    def send_deep(self, k):
        for hop in range(1, self.depth):
            self.deep_copy(k, hop).start()

    def after_deep(self, k):
        y, x, core, z = place(self.side)
        for hop in range(1, self.depth):
            self.deep_copy(k, hop).wait_recv()
        value = self.mine[k, y, x, z].astype(F32)
        for hop in range(self.depth - 1):
            value = value + self.got_deep[k, hop].astype(F32)
        self.total[k] = value

    def step(self, i):
        stages = (
            (0, self.after_core),
            (LAG, self.after_one),
            (2 * LAG, self.after_two),
            (self.deep_at, self.send_deep),
            (self.deep_at + LAG, self.after_deep),
        )
        for lag, action in stages:
            @pl.when(jnp.logical_and(i >= lag, i < self.count + lag))
            def _(lag=lag, action=action):
                action(i - lag)

    def finish(self):
        for k, (number, lead, start) in enumerate(self.layout):
            spot = (slice(None), pl.ds(start, self.width))
            if lead is None:
                self.results[number][spot] = self.total[k]
            else:
                self.results[number][(lead,) + spot] = self.total[k]

        def drain(k, carry):
            self.core_copy(k, self.got_core.at[k]).wait_send()

            def sent(x_first):
                for hop in range(1, self.side):
                    self.one_copy(k, hop, x_first).wait_send()
                    self.two_copy(k, hop, x_first).wait_send()

            self.both_orders(k, sent)
            for hop in range(1, self.depth):
                self.deep_copy(k, hop).wait_send()
            return carry

        lax.fori_loop(0, self.count, drain, 0)


def split_refs(refs, *counts):
    groups, at = [], 0
    for count in counts:
        groups.append(refs[at : at + count])
        at += count
    return groups + [refs[at:]]


def params(call_id, mib):
    return pltpu.CompilerParams(
        collective_id=call_id, has_side_effects=True, vmem_limit_bytes=mib * 1024 * 1024
    )


def half_masks(width):
    lane = lax.broadcasted_iota(jnp.int32, (1, width), 1)
    return (lane < width // 2, lane >= width // 2)


def dot_rows(left, right):
    return lax.dot_general(left, right, (((1,), (1,)), ((), ())), preferred_element_type=F32)


def dot_first(left, right):
    return lax.dot_general(left, right, (((0,), (0,)), ((), ())), preferred_element_type=F32)


def dot_plain(left, right):
    return lax.dot_general(left, right, (((1,), (0,)), ((), ())), preferred_element_type=F32)


def prompt_mask(scores, chunk, z, rows):
    key = lax.broadcasted_iota(jnp.int32, scores.shape, 0) + chunk * rows
    query = lax.broadcasted_iota(jnp.int32, scores.shape, 1)
    seen = jnp.logical_or(query >= rows, key <= query + z * rows)
    return jnp.where(seen, scores, NEVER)


def own_mask(scores):
    key = lax.broadcasted_iota(jnp.int32, scores.shape, 0)
    query = lax.broadcasted_iota(jnp.int32, scores.shape, 1)
    return jnp.where(key <= query, scores, NEVER)


def forward_pair(p, z, rows, depth, q_ref, k_ref, v_ref, keys, vals, att_ref, lse_ref):
    cols = pl.ds(pl.multiple_of(p * PAIR, PAIR), PAIR)
    q_pair = q_ref[:, cols] * jnp.asarray(0.125, BF)
    k_own, v_own = k_ref[pl.ds(rows, rows), cols], v_ref[pl.ds(rows, rows), cols]
    outs = []
    for head, mask in enumerate(half_masks(PAIR)):
        q_head = jnp.where(mask, q_pair, jnp.zeros_like(q_pair))
        scores = [
            prompt_mask(dot_rows(keys[p, chunk], q_head), chunk, z, rows) for chunk in range(depth)
        ]
        own = own_mask(dot_rows(k_own, q_head[rows:]))
        top = jnp.max(scores[0], axis=0, keepdims=True)
        for piece in scores[1:]:
            top = jnp.maximum(top, jnp.max(piece, axis=0, keepdims=True))
        top_c = jnp.maximum(top[:, rows:], jnp.max(own, axis=0, keepdims=True))
        top = jnp.concatenate([top[:, :rows], top_c], axis=1)
        total = jnp.zeros_like(top)
        out = jnp.zeros((PAIR, 2 * rows), F32)
        for chunk in range(depth):
            expo = jnp.exp(scores[chunk] - top)
            total = total + jnp.sum(expo, axis=0, keepdims=True)
            out = out + dot_first(vals[p, chunk], expo.astype(BF))
        expo = jnp.exp(own - top_c)
        total_c = total[:, rows:] + jnp.sum(expo, axis=0, keepdims=True)
        out_c = out[:, rows:] + dot_first(v_own, expo.astype(BF))
        total = jnp.concatenate([total[:, :rows], total_c], axis=1)
        out = jnp.concatenate([out[:, :rows], out_c], axis=1) / total
        lse_ref[pl.ds(2 * p + head, 1), :] = top + jnp.log(total)
        outs.append(out[head * HDIM : (head + 1) * HDIM])
    att_ref[:, cols] = jnp.concatenate(outs, axis=0).T.astype(BF)


def backward_pair(p, z, rows, depth, q_ref, k_ref, v_ref, keys, vals, lse_ref, att_ref, g_ref,
                  dq_ref, dk_ref, dv_ref, part):
    cols = pl.ds(pl.multiple_of(p * PAIR, PAIR), PAIR)
    own_rows = pl.ds(rows, rows)
    q_pair = q_ref[:, cols] * jnp.asarray(0.125, BF)
    g_pair = g_ref[:, cols]
    k_own, v_own = k_ref[own_rows, cols], v_ref[own_rows, cols]
    pulled = (g_pair.astype(F32) * att_ref[:, cols].astype(F32)).T
    masks = half_masks(PAIR)
    q_heads = [jnp.where(mask, q_pair, jnp.zeros_like(q_pair)) for mask in masks]
    g_heads = [jnp.where(mask, g_pair, jnp.zeros_like(g_pair)) for mask in masks]
    lses = [lse_ref[pl.ds(2 * p + head, 1), :] for head in range(2)]
    deltas = [
        jnp.sum(pulled[head * HDIM : (head + 1) * HDIM], axis=0, keepdims=True)
        for head in range(2)
    ]
    dq = [jnp.zeros((PAIR, 2 * rows), F32) for _ in range(2)]
    for chunk in range(depth):
        dk = jnp.zeros((rows, PAIR), F32)
        dv = jnp.zeros((rows, PAIR), F32)
        k_chunk, v_chunk = keys[p, chunk], vals[p, chunk]
        for head in range(2):
            scores = prompt_mask(dot_rows(k_chunk, q_heads[head]), chunk, z, rows)
            prob = jnp.exp(scores - lses[head])
            d_prob = dot_rows(v_chunk, g_heads[head])
            d_score = (prob * (d_prob - deltas[head])).astype(BF)
            dv = dv + dot_plain(prob.astype(BF), g_heads[head])
            dk = dk + dot_plain(d_score, q_heads[head])
            dq[head] = dq[head] + dot_first(k_chunk, d_score)
        part[p, chunk, 0] = dk.astype(BF)
        part[p, chunk, 1] = dv.astype(BF)
    dk = jnp.zeros((rows, PAIR), F32)
    dv = jnp.zeros((rows, PAIR), F32)
    for head in range(2):
        q_head, g_head = q_heads[head][rows:], g_heads[head][rows:]
        scores = own_mask(dot_rows(k_own, q_head))
        prob = jnp.exp(scores - lses[head][:, rows:])
        d_prob = dot_rows(v_own, g_head)
        d_score = (prob * (d_prob - deltas[head][:, rows:])).astype(BF)
        dv = dv + dot_plain(prob.astype(BF), g_head)
        dk = dk + dot_plain(d_score, q_head)
        more = dot_first(k_own, d_score)
        dq[head] = jnp.concatenate([dq[head][:, :rows], dq[head][:, rows:] + more], axis=1)
    dk_ref[own_rows, cols] = dk.astype(BF)
    dv_ref[own_rows, cols] = dv.astype(BF)
    both = jnp.concatenate([dq[0][:HDIM], dq[1][HDIM:]], axis=0) * 0.125
    dq_ref[:, cols] = both.T.astype(BF)


class Exchange:
    def __init__(self, depth, rows, pairs):
        self.depth, self.rows, self.pairs = depth, rows, pairs
        dma = pltpu.SemaphoreType.DMA
        self.scratch = [dma((2, 2, pairs, depth)), dma((2, pairs, depth))]

    def bind(self, owned, gathered, scratch):
        self.owned, self.gathered = owned, gathered
        self.send_sem, self.recv_sem = scratch

    def hop(self, kind, p, zp, move, own=False):
        target = self.gathered[kind].at[p, zp]
        cols = pl.ds(pl.multiple_of(p * PAIR, PAIR), PAIR)
        source = self.owned[kind].at[pl.ds(0, self.rows), cols] if own else target
        z = lax.axis_index("fsdp")
        return remote(source, target, self.send_sem.at[kind, (move + 1) // 2, p, zp],
                      self.recv_sem.at[kind, p, zp], (lax.axis_index("dp"), z + move))

    def offer(self, p):
        z = lax.axis_index("fsdp")
        for move in (1, -1):
            @pl.when(z < self.depth - 1 if move > 0 else z > 0)
            def _(move=move):
                for kind in range(2):
                    self.hop(kind, p, z, move, own=True).start()
        cols = pl.ds(pl.multiple_of(p * PAIR, PAIR), PAIR)
        for kind in range(2):
            self.gathered[kind][p, z] = self.owned[kind][pl.ds(0, self.rows), cols]

    def step(self, i):
        z = lax.axis_index("fsdp")
        for distance in range(1, self.depth):
            p = i - (distance - 1) * HOP_LAG
            for sign in (1, -1):
                zp = z + sign * distance
                seen = jnp.logical_and(zp >= 0, zp < self.depth)

                @pl.when(jnp.logical_and(seen, jnp.logical_and(p >= 0, p < self.pairs)))
                def _(p=p, zp=zp, sign=sign):
                    for kind in range(2):
                        self.hop(kind, p, zp, 1).wait_recv()

                    @pl.when(z < self.depth - 1 if sign < 0 else z > 0)
                    def _():
                        for kind in range(2):
                            self.hop(kind, p, zp, -sign).start()

    def finish(self):
        z = lax.axis_index("fsdp")

        def drain(p, carry):
            for zp in range(self.depth):
                for move in (1, -1):
                    far = zp <= z if move > 0 else zp >= z
                    inner = z < self.depth - 1 if move > 0 else z > 0

                    @pl.when(jnp.logical_and(far, inner))
                    def _(zp=zp, move=move):
                        for kind in range(2):
                            self.hop(kind, p, zp, move).wait_send()
            return carry

        lax.fori_loop(0, self.pairs, drain, 0)


def project(normed_ref, weight, out_ref):
    width = 2 * PAIR

    def run(part, carry):
        cols = pl.ds(pl.multiple_of(part * width, width), width)
        piece = weight[..., cols].reshape(normed_ref.shape[1], width)
        out_ref[:, cols] = dot_plain(normed_ref[...], piece).astype(BF)
        return carry

    lax.fori_loop(0, out_ref.shape[1] // width, run, 0)


def forward_kernel(first, rest, exchange, slots, *refs):
    depth, rows, pairs = exchange.depth, exchange.rows, exchange.pairs
    n = len(rest.views)
    ((picks_ref, normed_ref), shard, shards, outs, weights, full, swap, held,
     others) = split_refs(refs, 2, 3, n, 8, 3, n, len(exchange.scratch), len(first.scratch))
    counts_ref, q_ref, k_ref, v_ref, att_ref, lse_ref, keys, vals = outs
    first.bind(shard, weights, held)
    rest.bind(shards, full, others)
    exchange.bind((k_ref, v_ref), (keys, vals), swap)
    z = lax.axis_index("fsdp")
    blocks = picks_ref.shape[1] // 128
    head = depth - 2 + 3 * GATHER_LAG
    per_turn = -(-blocks // head)
    greet(first.side, depth)
    for k in range(first.count):
        first.start(k)

    def both(turn):
        first.step(turn)
        if 0 <= turn - REST_START < rest.count:
            rest.start(turn - REST_START)
        if turn >= REST_DELAY:
            rest.step(turn - REST_DELAY)

    def gather(i, carry):
        for turn in range(head):
            @pl.when(i == turn)
            def _(turn=turn):
                both(turn)

        for inner in range(per_turn):
            block = i * per_turn + inner

            @pl.when(block < blocks)
            def _(block=block):
                count_block(block, rows, slots, picks_ref, counts_ref)

        return carry

    lax.fori_loop(0, head, gather, 0)
    ahead = min(AHEAD, pairs)
    for k, out_ref in enumerate((k_ref, v_ref, q_ref)):
        both(head + k)
        first.put(k).wait()
        project(normed_ref, weights[k], out_ref)
        if k == 1:
            for p in range(ahead):
                exchange.offer(p)
    for k in range(max(0, first.steps - REST_START), rest.count):
        rest.start(k)
    done = max(0, first.steps - REST_DELAY)
    delay = (depth - 2) * HOP_LAG + 1
    turns = pairs + delay

    def run(i, carry):
        @pl.when(i + ahead < pairs)
        def _():
            exchange.offer(i + ahead)

        exchange.step(i)
        for turn in range(turns):
            number = done + turn
            if number < rest.steps:
                @pl.when(i == turn)
                def _(number=number):
                    rest.step(number)

        @pl.when(i >= delay)
        def _():
            forward_pair(i - delay, z, rows, depth, q_ref, k_ref, v_ref, keys, vals, att_ref,
                         lse_ref)

        return carry

    lax.fori_loop(0, turns, run, 0)
    for number in range(done + turns, rest.steps):
        rest.step(number)
    exchange.finish()
    rest.settle()
    first.finish()
    rest.finish()


def attention_forward(side, depth, picks, normed, projections, shards, slots, call_id):
    rows, width = normed.shape[0] // 2, normed.shape[1]
    pairs = width // PAIR
    first, rest = Gather(side, depth, projections), Gather(side, depth, shards)
    exchange = Exchange(depth, rows, pairs)
    any_space, vmem = pl.BlockSpec(memory_space=pl.ANY), pl.BlockSpec(memory_space=pltpu.VMEM)
    spread = jax.ShapeDtypeStruct((pairs, depth, rows, PAIR), BF)
    flat = jax.ShapeDtypeStruct(normed.shape, BF)
    results = pl.pallas_call(
        functools.partial(forward_kernel, first, rest, exchange, slots),
        out_shape=(
            jax.ShapeDtypeStruct((2, MH, slots, rows), BF),
            flat,
            flat,
            flat,
            flat,
            jax.ShapeDtypeStruct((2 * pairs, 2 * rows), F32),
            spread,
            spread,
        )
        + tuple(first.outs)
        + tuple(rest.outs),
        in_specs=[vmem] * 2 + [any_space] * (3 + len(rest.views)),
        out_specs=(vmem,) * 11 + (any_space,) * len(rest.views),
        scratch_shapes=exchange.scratch + first.scratch + rest.scratch,
        compiler_params=params(call_id, 56),
    )(picks, normed, *first.views, *rest.views)
    return results[:8], first.restore(results[8:11]), rest.restore(results[11:])


class Collect:
    def __init__(self, depth, rows, pairs):
        self.depth, self.rows, self.pairs = depth, rows, pairs
        dma = pltpu.SemaphoreType.DMA
        shape = (pairs, depth, 2, rows, PAIR)
        self.scratch = [
            pltpu.VMEM(shape, BF),
            pltpu.VMEM(shape, BF),
            pltpu.VMEM((pairs, 2, rows, PAIR), BF),
            pltpu.VMEM((2, rows, PAIR), F32),
            dma((2, pairs, depth)),
            dma((2, pairs, depth)),
        ]
        self.steps = pairs + (depth - 1) * COLLECT_LAG + 1

    def bind(self, scratch):
        (self.part, self.arrived, self.second, self.whole, self.send_sem,
         self.recv_sem) = scratch

    def hop(self, p, zd, move, final):
        z = lax.axis_index("fsdp")
        way = (move + 1) // 2
        target = self.second.at[p] if final and move < 0 else self.arrived.at[p, zd]
        return remote(self.part.at[p, zd], target, self.send_sem.at[way, p, zd],
                      self.recv_sem.at[way, p, zd], (lax.axis_index("dp"), z + move))

    def flow(self, p, move):
        depth = self.depth
        z = lax.axis_index("fsdp")
        first = z == 0 if move > 0 else z == depth - 1
        for zd in range(depth - 1, -1, -1) if move > 0 else range(depth):
            beyond = zd > z if move > 0 else zd < z

            @pl.when(jnp.logical_and(jnp.logical_not(first), beyond))
            def _(zd=zd):
                self.hop(p, zd, move, False).wait_recv()

                def add(part, carry):
                    self.part[p, zd, part] = self.part[p, zd, part] + self.arrived[p, zd, part]
                    return carry

                lax.fori_loop(0, 2, add, 0)

            @pl.when(jnp.logical_and(jnp.logical_not(first), zd == z))
            def _(zd=zd):
                self.hop(p, zd, move, True).wait_recv()

            @pl.when(zd == z + move)
            def _(zd=zd):
                self.hop(p, zd, move, True).start()

            @pl.when(jnp.logical_and(beyond, zd != z + move))
            def _(zd=zd):
                self.hop(p, zd, move, False).start()

    def step(self, i):
        depth = self.depth
        z = lax.axis_index("fsdp")
        for move in (1, -1):
            stage = z if move > 0 else depth - 1 - z
            p = i - stage * COLLECT_LAG

            @pl.when(jnp.logical_and(p >= 0, p < self.pairs))
            def _(p=p, move=move):
                self.flow(p, move)

    def result(self, p):
        z = lax.axis_index("fsdp")
        depth = self.depth
        whole = self.whole
        whole[...] = self.part[p, z].astype(F32)

        @pl.when(z > 0)
        def _():
            whole[...] = whole[...] + self.arrived[p, z].astype(F32)

        @pl.when(z < depth - 1)
        def _():
            whole[...] = whole[...] + self.second[p].astype(F32)

        return whole[...]

    def finish(self):
        depth = self.depth
        z = lax.axis_index("fsdp")

        def drain(p, carry):
            for zd in range(depth):
                for move in (1, -1):
                    @pl.when(zd > z if move > 0 else zd < z)
                    def _(zd=zd, move=move):
                        self.hop(p, zd, move, False).wait_send()
            return carry

        lax.fori_loop(0, self.pairs, drain, 0)


def produce(late, stage, kind, half, normed_ref, grad_ref):
    side, depth, block, width = late.side, late.depth, late.block, late.width
    k = 2 * kind + half
    run = depth * block
    for start in range(0, normed_ref.shape[1], 2 * PAIR):
        value = dot_first(
            normed_ref[:, start : start + 2 * PAIR], grad_ref[:, half * width : (half + 1) * width]
        ).astype(BF)
        for row in range(0, 2 * PAIR, run):
            number = (start + row) // run
            y, x, core = number // (2 * side), (number // 2) % side, number % 2
            stage[k, y, x, :, :, core * width : (core + 1) * width] = value[row : row + run].reshape(
                depth, block, width)


def backward_kernel(early, late, collect, *refs):
    side, depth, rows, pairs = early.side, collect.depth, collect.rows, collect.pairs
    n = len(early.views)
    ins, grads, (dq_ref, dk_ref, dv_ref), sums, (qkv_sum,), swap, first, second = split_refs(
        refs, 9, n, 3, n, 1, len(collect.scratch), len(early.scratch))
    q_ref, k_ref, v_ref, keys, vals, lse_ref, att_ref, g_ref, normed_ref = ins

    def part_of(k, half):
        number, lead, start = early.layout[k]
        ref = grads[number] if lead is None else grads[number].at[lead]
        return ref.at[:, :, half, :, :, pl.ds(start, early.width)]

    early.bind(part_of, sums, first)
    stage = early.got_core

    def late_part(k, half):
        lanes = pl.ds(pl.multiple_of(half * late.width, late.width), late.width)
        return stage.at[k, :, :, :, :, lanes]

    late.bind(late_part, (qkv_sum,), second)
    collect.bind(swap)
    z = lax.axis_index("fsdp")
    greet(side, depth)
    for k in range(early.count):
        early.start(k)
    last = (depth - 1) * COLLECT_LAG
    ready = max(pairs, early.count)
    settled = max(pairs + last, ready + 2)
    late_at = settled - 1
    due = [ready, ready + 1, settled, settled + 1, settled + 2, settled + 3]

    def run(i, carry):
        @pl.when(i < pairs)
        def _():
            backward_pair(i, z, rows, depth, q_ref, k_ref, v_ref, keys, vals, lse_ref, att_ref,
                          g_ref, dq_ref, dk_ref, dv_ref, collect.part)

        collect.step(i)
        early.step(i)

        @pl.when(jnp.logical_and(i >= last, i < last + pairs))
        def _():
            p = i - last
            cols = pl.ds(pl.multiple_of(p * PAIR, PAIR), PAIR)
            value = collect.result(p)
            dk_ref[pl.ds(0, rows), cols] = value[0].astype(BF)
            dv_ref[pl.ds(0, rows), cols] = value[1].astype(BF)

        late.step(i - late_at)
        for number, when in enumerate(due):
            @pl.when(i == when)
            def _(number=number):
                kind = number // 2
                produce(late, stage, kind, number % 2, normed_ref, (dq_ref, dk_ref, dv_ref)[kind])
                late.start(number)

        return carry

    lax.fori_loop(0, max(early.steps, late_at + late.steps), run, 0)
    collect.finish()
    early.finish()
    late.finish()


def attention_backward(side, depth, q, k, v, keys, vals, lse, att, grad_att, normed, grads, w_qkv,
                       call_id):
    rows, width = q.shape[0] // 2, q.shape[1]
    early = Reduce(side, depth, grads, width, DEEP_AT)
    late = Reduce(side, depth, (w_qkv,), width // 2, 2 * LAG)
    collect = Collect(depth, rows, width // PAIR)
    any_space, vmem = pl.BlockSpec(memory_space=pl.ANY), pl.BlockSpec(memory_space=pltpu.VMEM)
    results = pl.pallas_call(
        functools.partial(backward_kernel, early, late, collect),
        out_shape=(jax.ShapeDtypeStruct(q.shape, BF),) * 3 + tuple(early.outs) + tuple(late.outs),
        in_specs=[vmem] * 9 + [any_space] * len(grads),
        out_specs=(vmem,) * (4 + len(grads)),
        scratch_shapes=collect.scratch + early.scratch + late.scratch,
        compiler_params=params(call_id, 63),
    )(
        q,
        k,
        v,
        keys,
        vals,
        lse,
        att,
        grad_att,
        normed,
        *[grad.reshape(view) for grad, view in zip(grads, early.views)],
    )
    return results[:3], results[3:-1], results[-1]


def count_block(b, rows, slots, picks_ref, counts_ref):
    low, per_word, bits = 16, 5, 6
    groups = -(-(slots // low) // per_word)
    per_head = rows // 128
    cols = pl.ds(pl.multiple_of(b * 128, 128), 128)
    picks = picks_ref[:, cols]
    high = jnp.right_shift(picks, 4)
    group = jnp.right_shift(high * 13, 6)
    word = group * low + jnp.bitwise_and(picks, low - 1)
    unit = jnp.left_shift(jnp.ones_like(picks), bits * (high - per_word * group))
    spot = lax.broadcasted_iota(jnp.int32, (groups * low, 128), 0)
    words = jnp.zeros((groups * low, 128), jnp.int32)
    for pick in range(picks.shape[0]):
        words = words + jnp.where(spot == word[pick : pick + 1], unit[pick : pick + 1], 0)
    part, head = b // (per_head * MH), (b // per_head) % MH
    lanes = pl.ds(pl.multiple_of((b % per_head) * 128, 128), 128)
    for tile in range(slots // low):
        piece = words[(tile // per_word) * low : (tile // per_word + 1) * low]
        count = jnp.bitwise_and(jnp.right_shift(piece, bits * (tile % per_word)), 2**bits - 1)
        counts_ref[part, head, pl.ds(tile * low, low), lanes] = count.astype(F32).astype(BF)


def selector(ids_ref, index, count):
    ids = ids_ref[pl.ds(index, 1), :]
    spot = lax.broadcasted_iota(jnp.int32, (count, ids.shape[1]), 0)
    return jnp.where(spot == ids, 1.0, 0.0).astype(BF)


def picks_kernel(ids_ref, counts_ref, query_ref, keys_ref, weight_ref, mixing_ref, total):
    part, head = pl.program_id(0), pl.program_id(1)
    scores = None
    for half in range(2):
        pick = selector(ids_ref, 2 * part + half, SUB)
        slot_keys = dot_first(pick, keys_ref[half * SUB : (half + 1) * SUB]).astype(BF)
        piece = dot_rows(slot_keys, query_ref[:, half * HALF : (half + 1) * HALF])
        scores = piece if scores is None else scores + piece
    count = counts_ref[0, 0].astype(F32)
    named = count > 0.0
    top = jnp.max(jnp.where(named, scores, -jnp.inf), axis=0, keepdims=True)
    raised = jnp.where(named, count * jnp.exp(scores - top), 0.0)
    weight = raised / jnp.sum(raised, axis=0, keepdims=True)
    weight_ref[0, 0] = weight

    @pl.when(head == 0)
    def _():
        total[...] = weight

    @pl.when(head > 0)
    def _():
        total[...] = total[...] + weight

    @pl.when(head == MH - 1)
    def _():
        mixing_ref[0] = total[...].astype(BF)


def slot_weights(ids, counts, mquery, keys_full):
    slots, rows = counts.shape[2:]
    return pl.pallas_call(
        picks_kernel,
        grid=(2, MH),
        out_shape=(
            jax.ShapeDtypeStruct(counts.shape, F32),
            jax.ShapeDtypeStruct((2, slots, rows), BF),
        ),
        in_specs=[
            pl.BlockSpec(ids.shape, lambda u, m: (0, 0)),
            pl.BlockSpec((1, 1, slots, rows), lambda u, m: (u, m, 0, 0)),
            pl.BlockSpec((rows, 2 * HALF), lambda u, m: (u, m)),
            pl.BlockSpec((2 * SUB, HALF), lambda u, m: (m, 0)),
        ],
        out_specs=(
            pl.BlockSpec((1, 1, slots, rows), lambda u, m: (u, m, 0, 0)),
            pl.BlockSpec((1, slots, rows), lambda u, m: (u, 0, 0)),
        ),
        scratch_shapes=[pltpu.VMEM((slots, rows), F32)],
        cost_estimate=pl.CostEstimate(
            flops=2 * 2 * MH * slots * 2 * HALF * (SUB + rows),
            bytes_accessed=24 * 2**20,
            transcendentals=2 * MH * slots * rows,
        ),
    )(ids, counts, mquery, keys_full)


def picks_back_kernel(block, ids_ref, weight_ref, first_ref, second_ref, memory_ref, query_ref,
                      keys_ref, grad_query_ref, grad_keys_ref, grad_mixing, total):
    head, part = pl.program_id(0), pl.program_id(1)

    for number, table_ref in enumerate((first_ref, second_ref)):
        @pl.when(jnp.logical_and(head == 0, part == number))
        def _(number=number, table_ref=table_ref):
            grad_mixing[number] = dot_rows(table_ref[...], memory_ref[...])

    weight = weight_ref[0, 0]
    pulled = weight * grad_mixing[part]
    grad = pulled - weight * jnp.sum(pulled, axis=0, keepdims=True)
    high = grad.astype(BF)
    low = (grad - high.astype(F32)).astype(BF)
    for half in range(2):
        pick = selector(ids_ref, 2 * part + half, SUB)
        sub = (dot_plain(pick, high) + dot_plain(pick, low)).astype(BF)
        span = slice(half * HALF, (half + 1) * HALF)
        keys = keys_ref[half * SUB : (half + 1) * SUB]
        grad_query_ref[:, span] = dot_first(sub, keys).astype(BF)
        piece = dot_plain(sub, query_ref[:, span])
        rows = slice(half * SUB, (half + 1) * SUB)

        @pl.when(part == 0)
        def _(piece=piece, rows=rows):
            total[rows] = piece

        @pl.when(part == 1)
        def _(piece=piece, rows=rows):
            total[rows] = total[rows] + piece

    @pl.when(part == 1)
    def _():
        for shard in range(SUB // block):
            for side in range(2):
                start = (2 * shard + side) * block
                grad_keys_ref[shard * block : (shard + 1) * block, side * HALF : (side + 1) * HALF] = (
                    total[start : start + block].astype(BF))


def slot_weights_back(ids, weights, tables, grad_memory, mquery, keys_full, block):
    slots, rows = weights.shape[2:]
    width = tables[0].shape[1]
    return pl.pallas_call(
        functools.partial(picks_back_kernel, block),
        grid=(MH, 2),
        out_shape=(
            jax.ShapeDtypeStruct(mquery.shape, BF),
            jax.ShapeDtypeStruct((MH * SUB, 2 * HALF), BF),
        ),
        in_specs=[
            pl.BlockSpec(ids.shape, lambda m, u: (0, 0)),
            pl.BlockSpec((1, 1, slots, rows), lambda m, u: (u, m, 0, 0)),
            pl.BlockSpec((slots, width), lambda m, u: (0, 0)),
            pl.BlockSpec((slots, width), lambda m, u: (0, 0)),
            pl.BlockSpec((rows, width), lambda m, u: (jnp.where(m == 0, u, 1), 0)),
            pl.BlockSpec((rows, 2 * HALF), lambda m, u: (u, m)),
            pl.BlockSpec((2 * SUB, HALF), lambda m, u: (m, 0)),
        ],
        out_specs=(
            pl.BlockSpec((rows, 2 * HALF), lambda m, u: (u, m)),
            pl.BlockSpec((SUB, 2 * HALF), lambda m, u: (m, 0)),
        ),
        scratch_shapes=[pltpu.VMEM((2, slots, rows), F32), pltpu.VMEM((2 * SUB, HALF), F32)],
        cost_estimate=pl.CostEstimate(
            flops=2 * 2 * MH * slots * rows * (4 * SUB + 4 * HALF),
            bytes_accessed=24 * 2**20,
            transcendentals=0,
        ),
    )(ids, weights, *tables, grad_memory, mquery, keys_full)


def one_hot(ids, count):
    return (ids[:, None] == jnp.arange(count, dtype=jnp.int32)[None, :]).astype(BF)


def per_device(
    x_prompt,
    x_cont,
    cot_prompt,
    cot_cont,
    gain_attn,
    gain_mem,
    w_qkv,
    w_attn_out,
    w_mem_query,
    sub_keys,
    w_gate,
    w_mem_out,
    value_rows,
    request,
    slot_prompt,
    slot_cont,
):
    shard_rows, width = value_rows.shape
    owners, capacity = request.shape[2:]
    slots = owners * capacity
    rows = x_prompt.shape[1]
    cols = w_qkv.shape[2]
    block = cols // owners
    side, depth = grid_of(lax.axis_size("dp"), lax.axis_size("fsdp"))

    asked = lax.all_to_all(request[:, 0], ALL, split_axis=1, concat_axis=1, tiled=True)
    def swap(values):
        values = values.reshape(owners, capacity, width)
        swapped = lax.all_to_all(values, ALL, split_axis=0, concat_axis=0, tiled=True)
        return swapped.reshape(slots, width)

    offsets = jnp.maximum(request[:, 0].reshape(2, slots), 0)
    picked = (jnp.arange(slots, dtype=jnp.int32) // capacity)[None] * shard_rows + offsets
    ids = jnp.stack([picked // SUB, picked % SUB], axis=1).reshape(4, slots)
    x_rows = jnp.concatenate([x_prompt[0], x_cont[0]], axis=0).astype(F32)
    dy_low = jnp.concatenate([cot_prompt[0], cot_cont[0]], axis=0)
    normed, inverse = normalize(x_rows, gain_attn)
    normed = normed.astype(BF)
    picks = jnp.stack([slot_prompt[0], slot_cont[0]]).transpose(3, 0, 2, 1)
    picks = picks.reshape(picks.shape[0], -1)
    results, (key_full, value_full, ask_full), full = attention_forward(
        side,
        depth,
        picks,
        normed,
        (w_qkv[1], w_qkv[2], w_qkv[0]),
        (w_attn_out, w_mem_query, sub_keys, w_gate, w_mem_out),
        slots,
        0,
    )
    counts, queries, keys, vals, att, lse, all_keys, all_vals = results
    attn_out_full, query_full, keys_full, gate_full, mem_out_full = full
    att, asked = lax.optimization_barrier((att, asked))
    serve_pick = one_hot(asked.reshape(-1), shard_rows)
    served = mm(serve_pick, value_rows).astype(BF).reshape(2, owners, capacity, width)
    tables = lax.all_to_all(served, ALL, split_axis=1, concat_axis=1, tiled=True)
    tables = tables.reshape(2, slots, width)
    hidden = x_rows + mm(att, attn_out_full)
    normed2, inverse2 = normalize(hidden, gain_mem)
    normed2 = normed2.astype(BF)

    mquery = mm(normed2, query_full).astype(BF)
    gate_pre = mm(normed2, gate_full)
    weights, mixing = slot_weights(ids, counts, mquery, keys_full)
    memory_out = jnp.concatenate([mm_l(mixing[part], tables[part]) for part in range(2)], axis=0)
    sigmoid_gate = jax.nn.sigmoid(gate_pre)
    blended = (memory_out * (gate_pre * sigmoid_gate)).astype(BF)
    out = (hidden + mm(blended, mem_out_full)).astype(BF)

    grad_blend = mm_t(dy_low, mem_out_full)
    grad_mem_out = mm_l(blended, dy_low)
    grad_memory = (grad_blend * gate_pre * sigmoid_gate).astype(BF)
    grad_gate = (
        grad_blend * memory_out * sigmoid_gate * (1.0 + gate_pre * (1.0 - sigmoid_gate))
    ).astype(BF)
    slot_grads = [
        mm(mixing[part], grad_memory[part * rows : (part + 1) * rows]).astype(BF)
        for part in range(2)
    ]
    arrived = [None, swap(slot_grads[1])]
    grad_query, grad_keys = slot_weights_back(
        ids, weights, tables, grad_memory, mquery, keys_full, block
    )
    grad_query, arrived[1], late = lax.optimization_barrier((grad_query, arrived[1], slot_grads[0]))
    arrived[0] = swap(late)
    grad_normed2 = mm_t(grad_query, query_full) + mm_t(grad_gate, gate_full)
    grad_query_w = mm_l(normed2, grad_query).astype(BF)
    grad_gate_w = mm_l(normed2, grad_gate).astype(BF)
    back, gain_mem_part = norm_backward(hidden, inverse2, gain_mem, grad_normed2)
    grad_hidden = dy_low.astype(F32) + back
    hidden_low = grad_hidden.astype(BF)
    grad_attn_out = mm_l(att, hidden_low).astype(BF)
    grad_att = mm_t(hidden_low, attn_out_full).astype(BF)
    grad_att, arrived = lax.optimization_barrier((grad_att, arrived))
    (grad_q, grad_k, grad_v), early, qkv_shard = attention_backward(
        side,
        depth,
        queries,
        keys,
        vals,
        all_keys,
        all_vals,
        lse,
        att,
        grad_att,
        normed,
        (grad_query_w, grad_keys, grad_gate_w, grad_mem_out.astype(BF), grad_attn_out),
        jax.ShapeDtypeStruct((3, cols, cols), BF),
        1,
    )
    grad_rows = mm_l(serve_pick, jnp.concatenate(arrived, axis=0))
    grad_normed = (
        mm_t(grad_q, ask_full) + mm_t(grad_k, key_full) + mm_t(grad_v, value_full)
    )
    grad_x, gain_attn_part = norm_backward(x_rows, inverse, gain_attn, grad_normed)
    grad_x = grad_hidden + grad_x
    gains = jnp.stack([gain_attn_part, gain_mem_part]).reshape(2, owners, block)
    gains = lax.all_to_all(gains.transpose(1, 0, 2), ALL, split_axis=0, concat_axis=0, tiled=True)
    gain_shards = jnp.sum(gains, axis=0)
    sub_shard = early[1].reshape(block, 2, HALF).transpose(1, 0, 2).reshape(2 * block, HALF)
    return (
        out[None, :rows],
        out[None, rows:],
        grad_x[None, :rows],
        grad_x[None, rows:],
        gain_shards[0],
        gain_shards[1],
        qkv_shard,
        early[4],
        early[0],
        sub_shard,
        early[2],
        early[3],
        grad_rows,
    )


def solution(mesh):
    in_specs = (
        P("dp", "fsdp", None),
        P("dp", "fsdp", None),
        P("dp", "fsdp", None),
        P("dp", "fsdp", None),
        P(),
        P(),
        P(None, "fsdp", None),
        P("fsdp", None),
        P("fsdp", None),
        P("fsdp", None),
        P("fsdp", None),
        P("fsdp", None),
        P(("dp", "fsdp"), None),
        P(None, ("dp", "fsdp"), None, None),
        P("dp", "fsdp", None, None),
        P("dp", "fsdp", None, None),
    )
    out_specs = (
        P("dp", "fsdp", None),
        P("dp", "fsdp", None),
        P("dp", "fsdp", None),
        P("dp", "fsdp", None),
        P(("dp", "fsdp")),
        P(("dp", "fsdp")),
        P(None, ("dp", "fsdp"), None),
        P(("dp", "fsdp"), None),
        P(("dp", "fsdp"), None),
        P(("dp", "fsdp"), None),
        P(("dp", "fsdp"), None),
        P(("dp", "fsdp"), None),
        P(("dp", "fsdp"), None),
    )
    return jax.shard_map(
        per_device, mesh=mesh, in_specs=in_specs, out_specs=out_specs, check_vma=False
    )
```

```python
import functools
import jax
import jax.numpy as jnp
from jax import lax
from jax.experimental import pallas as pl
from jax.experimental.pallas import tpu as pltpu
from jax.sharding import PartitionSpec as P
BF = jnp.bfloat16
F32 = jnp.float32
ALL = ("dp", "fsdp")
MESH = pl.DeviceIdType.MESH
LAG = 4
GATHER_LAG = 3
REST_START = 1
REST_DELAY = 6
DEEP_AT = 10
COLLECT_LAG = 2
AHEAD = 3
HOP_LAG = 1
PAIR = 128
HDIM = 64
MH = 4
HALF = 512
SUB = 256
NEVER = -1e30


def mm(left, right):
    return jnp.dot(left, right, preferred_element_type=F32)


def mm_t(left, right):
    return lax.dot_general(left, right, (((1,), (1,)), ((), ())), preferred_element_type=F32)


def mm_l(left, right):
    return lax.dot_general(left, right, (((0,), (0,)), ((), ())), preferred_element_type=F32)


def normalize(matrix, gain_vec):
    inverse = lax.rsqrt(jnp.mean(matrix * matrix, axis=-1, keepdims=True) + 1e-05)
    return (matrix * inverse * gain_vec, inverse)


def norm_backward(matrix, inverse, gain_vec, grad_normed):
    scaled = gain_vec * grad_normed
    cubed = inverse * inverse * inverse
    grad_matrix = inverse * scaled - matrix * cubed * jnp.mean(
        matrix * scaled, axis=-1, keepdims=True
    )
    return (grad_matrix, jnp.sum(grad_normed * matrix * inverse, axis=0))


def grid_of(plane, depth):
    side = 1
    while 2 * side * side < plane:
        side += 1
    return side, depth


def place(side):
    dp = lax.axis_index("dp")
    return (dp // (2 * side), (dp // 2) % side, dp % 2, lax.axis_index("fsdp"))


def device_at(side, y, x, core, z):
    return ((y * side + x) * 2 + core, z)


def greet(side, depth):
    y, x, core, z = place(side)
    barrier = pltpu.get_barrier_semaphore()
    peers = [device_at(side, y, x, 1 - core, z)]
    for hop in range(1, side):
        peers.append(device_at(side, y, (x + hop) % side, core, z))
        peers.append(device_at(side, (y + hop) % side, x, core, z))
    for hop in range(1, depth):
        peers.append(device_at(side, y, x, core, (z + hop) % depth))
    for peer in peers:
        pl.semaphore_signal(barrier, inc=1, device_id=peer, device_id_type=MESH)
    pl.semaphore_wait(barrier, len(peers))


def remote(source, target, send_sem, recv_sem, peer):
    return pltpu.make_async_remote_copy(
        src_ref=source,
        dst_ref=target,
        send_sem=send_sem,
        recv_sem=recv_sem,
        device_id=peer,
        device_id_type=MESH,
    )


class Gather:
    def __init__(self, side, depth, shards, piece=1024):
        self.side, self.depth = side, depth
        self.views, self.outs, self.shapes, self.held, self.layout = [], [], [], [], []
        plane = 2 * side * side
        for shard in shards:
            rows, cols = shard.shape[-2:]
            block, width = rows // plane, min(cols, piece)
            lead = shard.shape[:-2]
            self.views.append(shard.reshape(lead + (side, side, 2, block, cols)))
            leads = range(lead[0]) if lead else (None,)
            self.layout.append(
                [(number, start) for number in leads for start in range(0, cols, width)]
            )
            self.outs.append(
                jax.ShapeDtypeStruct(lead + (depth, side, side, 2, block, cols), BF)
            )
            self.shapes.append(lead + (depth * rows, cols))
            self.held.append(
                pltpu.VMEM((len(self.layout[-1]), side, side, 2, block, width), BF)
            )
        self.count = count = sum(len(columns) for columns in self.layout)
        self.steps = count + depth - 2 + 3 * GATHER_LAG
        dma = pltpu.SemaphoreType.DMA
        self.scratch = self.held + [
            dma((count,)),
            dma((count,)),
            dma((count, depth)),
            dma((count, depth)),
            dma((count, depth)),
            dma((count, depth, side - 1)),
            dma((count, depth, side - 1)),
            dma((count, depth, side - 1)),
            dma((count, depth, side - 1)),
            dma((count, depth)),
            dma((count, depth)),
        ]

    def restore(self, full):
        return [one.reshape(shape) for one, shape in zip(full, self.shapes)]

    def bind(self, sources, outs, scratch):
        self.sources, self.results = sources, outs
        n_in = len(self.layout)
        self.holders = scratch[:n_in]
        (self.in_sem, self.out_sem, self.right_send, self.left_send, self.deep_recv,
         self.one_send, self.one_recv, self.two_send, self.two_recv, self.core_send,
         self.core_recv) = scratch[n_in:]
        self.pieces = []
        for number, columns in enumerate(self.layout):
            width = self.holders[number].shape[-1]
            width = width if sources[number].shape[-1] > width else None
            for inner, (lead, start) in enumerate(columns):
                self.pieces.append((number, lead, start, width, inner))

    def cut(self, refs, k, *spot):
        number, lead, start, width = self.pieces[k][:4]
        ref = refs[number] if lead is None else refs[number].at[lead]
        ref = ref.at[spot] if spot else ref
        if width is None:
            return ref
        return ref.at[(slice(None),) * (len(ref.shape) - 1) + (pl.ds(start, width),)]

    def along_z(self, k, zp, move, source=None):
        y, x, core, z = place(self.side)
        target = self.cut(self.results, k, zp, y, x, core)
        send = self.right_send if move > 0 else self.left_send
        return remote(target if source is None else source, target, send.at[k, zp],
                      self.deep_recv.at[k, zp], device_at(self.side, y, x, core, z + move))

    def one_copy(self, k, zp, hop):
        side = self.side
        y, x, core, z = place(side)
        peer = device_at(side, y, (x + hop) % side, core, z) if k % 2 == 0 else device_at(
            side, (y + hop) % side, x, core, z)
        ref = self.cut(self.results, k, zp, y, x, core)
        return remote(ref, ref, self.one_send.at[k, zp, hop - 1],
                      self.one_recv.at[k, zp, hop - 1], peer)

    def two_copy(self, k, zp, hop):
        side = self.side
        y, x, core, z = place(side)
        x_first = k % 2 == 0
        peer = device_at(side, (y + hop) % side, x, core, z) if x_first else device_at(
            side, y, (x + hop) % side, core, z)
        ref = (self.cut(self.results, k, zp, y, slice(None), core) if x_first
               else self.cut(self.results, k, zp, slice(None), x, core))
        return remote(ref, ref, self.two_send.at[k, zp, hop - 1],
                      self.two_recv.at[k, zp, hop - 1], peer)

    def core_copy(self, k, zp):
        y, x, core, z = place(self.side)
        ref = self.cut(self.results, k, zp, slice(None), slice(None), core)
        return remote(ref, ref, self.core_send.at[k, zp], self.core_recv.at[k, zp],
                      device_at(self.side, y, x, 1 - core, z))

    def take(self, k):
        number, inner = self.pieces[k][0], self.pieces[k][4]
        return pltpu.make_async_copy(self.cut(self.sources, k), self.holders[number].at[inner],
                                     self.in_sem.at[k])

    def put(self, k):
        z = place(self.side)[3]
        number, inner = self.pieces[k][0], self.pieces[k][4]
        return pltpu.make_async_copy(self.holders[number].at[inner],
                                     self.cut(self.results, k, z), self.out_sem.at[k])

    def start(self, k):
        y, x, core, z = place(self.side)
        self.take(k).start()
        own = self.cut(self.sources, k, y, x, core)

        @pl.when(z < self.depth - 1)
        def _():
            self.along_z(k, z, 1, own).start()

        @pl.when(z > 0)
        def _():
            self.along_z(k, z, -1, own).start()

    def step(self, i):
        side, depth = self.side, self.depth
        z = place(side)[3]
        if i < self.count:
            self.take(i).wait()
            self.put(i).start()
        for stage in range(4):
            for distance in range(1, depth):
                k = i - stage * GATHER_LAG - (distance - 1)
                if not 0 <= k < self.count:
                    continue
                for sign in (1, -1):
                    zp = z + sign * distance

                    @pl.when(jnp.logical_and(zp >= 0, zp < depth))
                    def _(k=k, zp=zp, sign=sign, stage=stage):
                        self.arrival(stage, k, zp, sign)

    def arrival(self, stage, k, zp, sign):
        side, depth = self.side, self.depth
        z = place(side)[3]
        if stage == 0:
            self.along_z(k, zp, 1).wait_recv()

            @pl.when(z < depth - 1 if sign < 0 else z > 0)
            def _():
                self.along_z(k, zp, -sign).start()

            for hop in range(1, side):
                self.one_copy(k, zp, hop).start()
        elif stage == 1:
            for hop in range(1, side):
                self.one_copy(k, zp, hop).wait_recv()
            for hop in range(1, side):
                self.two_copy(k, zp, hop).start()
        elif stage == 2:
            for hop in range(1, side):
                self.two_copy(k, zp, hop).wait_recv()
            self.core_copy(k, zp).start()
        else:
            self.core_copy(k, zp).wait_recv()

    def settle(self):
        for k in range(self.count):
            self.put(k).wait()

    def finish(self):
        side, depth = self.side, self.depth
        z = place(side)[3]
        for k in range(self.count):
            for zp in range(depth):
                @pl.when(jnp.logical_and(zp <= z, z < depth - 1))
                def _(k=k, zp=zp):
                    self.along_z(k, zp, 1).wait_send()

                @pl.when(jnp.logical_and(zp >= z, z > 0))
                def _(k=k, zp=zp):
                    self.along_z(k, zp, -1).wait_send()

                @pl.when(zp != z)
                def _(k=k, zp=zp):
                    for hop in range(1, side):
                        self.one_copy(k, zp, hop).wait_send()
                        self.two_copy(k, zp, hop).wait_send()
                    self.core_copy(k, zp).wait_send()


class Reduce:
    def __init__(self, side, depth, grads, piece, deep_at):
        self.side, self.depth, self.deep_at = side, depth, deep_at
        self.layout, self.views, self.outs = [], [], []
        self.width = width = piece
        devices = 2 * side * side * depth
        for grad in grads:
            rows, cols = grad.shape[-2:]
            self.block = block = rows // devices
            lead = grad.shape[:-2]
            self.views.append(lead + (side, side, 2, depth, block, cols))
            leads = range(lead[0]) if lead else (None,)
            self.layout += [
                (len(self.outs), number, start) for number in leads for start in range(0, cols, width)
            ]
            self.outs.append(jax.ShapeDtypeStruct(lead + (block, cols), F32))
        self.count = count = len(self.layout)
        self.steps = count + deep_at + LAG
        dma = pltpu.SemaphoreType.DMA
        self.scratch = [
            pltpu.VMEM((count, side, side, depth, block, width), BF),
            pltpu.VMEM((count, side, side, depth, block, width), BF),
            pltpu.VMEM((count, side - 1, side, depth, block, width), BF),
            pltpu.VMEM((count, side - 1, depth, block, width), BF),
            pltpu.VMEM((count, depth - 1, block, width), BF),
            pltpu.VMEM((count, block, width), F32),
            dma((count,)),
            dma((count,)),
            dma((count,)),
            dma((count, side - 1)),
            dma((count, side - 1)),
            dma((count, side - 1)),
            dma((count, side - 1)),
            dma((count, depth - 1)),
            dma((count, depth - 1)),
        ]

    def bind(self, sources, outs, scratch):
        (self.mine, self.got_core, self.got_one, self.got_two, self.got_deep, self.total,
         self.local_sem, self.core_send, self.core_recv, self.one_send, self.one_recv,
         self.two_send, self.two_recv, self.deep_send, self.deep_recv) = scratch
        self.results, self.sources = outs, sources

    def core_copy(self, k, source):
        y, x, core, z = place(self.side)
        return remote(source, self.got_core.at[k], self.core_send.at[k],
                      self.core_recv.at[k], device_at(self.side, y, x, 1 - core, z))

    def start(self, k):
        core = place(self.side)[2]
        self.core_copy(k, self.sources(k, 1 - core)).start()
        pltpu.make_async_copy(self.sources(k, core), self.mine.at[k], self.local_sem.at[k]).start()

    def one_copy(self, k, hop, x_first):
        side = self.side
        y, x, core, z = place(side)
        peer = device_at(side, y, (x + hop) % side, core, z) if x_first else device_at(
            side, (y + hop) % side, x, core, z)
        source = (self.mine.at[k, :, (x + hop) % side] if x_first
                  else self.mine.at[k, (y + hop) % side])
        return remote(source, self.got_one.at[k, hop - 1], self.one_send.at[k, hop - 1],
                      self.one_recv.at[k, hop - 1], peer)

    def two_copy(self, k, hop, x_first):
        side = self.side
        y, x, core, z = place(side)
        peer = device_at(side, (y + hop) % side, x, core, z) if x_first else device_at(
            side, y, (x + hop) % side, core, z)
        source = (self.mine.at[k, (y + hop) % side, x] if x_first
                  else self.mine.at[k, y, (x + hop) % side])
        return remote(source, self.got_two.at[k, hop - 1], self.two_send.at[k, hop - 1],
                      self.two_recv.at[k, hop - 1], peer)

    def deep_copy(self, k, hop):
        y, x, core, z = place(self.side)
        there = (z + hop) % self.depth
        return remote(self.mine.at[k, y, x, there], self.got_deep.at[k, hop - 1],
                      self.deep_send.at[k, hop - 1], self.deep_recv.at[k, hop - 1],
                      device_at(self.side, y, x, core, there))

    def both_orders(self, k, action):
        @pl.when(k % 2 == 0)
        def _():
            action(True)

        @pl.when(k % 2 == 1)
        def _():
            action(False)

    def added(self, base, others):
        if len(others) == 1:
            return base + others[0]
        value = base.astype(F32)
        for other in others:
            value = value + other.astype(F32)
        return value.astype(base.dtype)

    def after_core(self, k):
        side, depth, mine, got = self.side, self.depth, self.mine, self.got_core
        self.core_copy(k, got.at[k]).wait_recv()
        pltpu.make_async_copy(got.at[k], mine.at[k], self.local_sem.at[k]).wait()

        def add(index, carry):
            spot = (k, index // (side * depth), (index // depth) % side, index % depth)
            mine[spot] = mine[spot] + got[spot]
            return carry

        lax.fori_loop(0, side * side * depth, add, 0)

        def send(x_first):
            for hop in range(1, side):
                self.one_copy(k, hop, x_first).start()

        self.both_orders(k, send)

    def after_one(self, k):
        side, depth, mine = self.side, self.depth, self.mine
        y, x, core, z = place(side)

        def finish(x_first):
            for hop in range(1, side):
                self.one_copy(k, hop, x_first).wait_recv()

            def add(index, carry):
                a, c = index // depth, index % depth
                spot = (k, a, x, c) if x_first else (k, y, a, c)
                mine[spot] = self.added(
                    mine[spot], [self.got_one[k, hop, a, c] for hop in range(side - 1)]
                )
                return carry

            lax.fori_loop(0, side * depth, add, 0)
            for hop in range(1, side):
                self.two_copy(k, hop, x_first).start()

        self.both_orders(k, finish)

    def after_two(self, k):
        side, depth, mine = self.side, self.depth, self.mine
        y, x, core, z = place(side)

        def finish(x_first):
            for hop in range(1, side):
                self.two_copy(k, hop, x_first).wait_recv()

        self.both_orders(k, finish)

        def add(c, carry):
            mine[k, y, x, c] = self.added(
                mine[k, y, x, c], [self.got_two[k, hop, c] for hop in range(side - 1)]
            )
            return carry

        lax.fori_loop(0, depth, add, 0)

    def send_deep(self, k):
        for hop in range(1, self.depth):
            self.deep_copy(k, hop).start()

    def after_deep(self, k):
        y, x, core, z = place(self.side)
        for hop in range(1, self.depth):
            self.deep_copy(k, hop).wait_recv()
        value = self.mine[k, y, x, z].astype(F32)
        for hop in range(self.depth - 1):
            value = value + self.got_deep[k, hop].astype(F32)
        self.total[k] = value

    def step(self, i):
        stages = (
            (0, self.after_core),
            (LAG, self.after_one),
            (2 * LAG, self.after_two),
            (self.deep_at, self.send_deep),
            (self.deep_at + LAG, self.after_deep),
        )
        for lag, action in stages:
            @pl.when(jnp.logical_and(i >= lag, i < self.count + lag))
            def _(lag=lag, action=action):
                action(i - lag)

    def finish(self):
        for k, (number, lead, start) in enumerate(self.layout):
            spot = (slice(None), pl.ds(start, self.width))
            if lead is None:
                self.results[number][spot] = self.total[k]
            else:
                self.results[number][(lead,) + spot] = self.total[k]

        def drain(k, carry):
            self.core_copy(k, self.got_core.at[k]).wait_send()

            def sent(x_first):
                for hop in range(1, self.side):
                    self.one_copy(k, hop, x_first).wait_send()
                    self.two_copy(k, hop, x_first).wait_send()

            self.both_orders(k, sent)
            for hop in range(1, self.depth):
                self.deep_copy(k, hop).wait_send()
            return carry

        lax.fori_loop(0, self.count, drain, 0)


def split_refs(refs, *counts):
    groups, at = [], 0
    for count in counts:
        groups.append(refs[at : at + count])
        at += count
    return groups + [refs[at:]]


def params(call_id, mib):
    return pltpu.CompilerParams(
        collective_id=call_id, has_side_effects=True, vmem_limit_bytes=mib * 1024 * 1024
    )


def half_masks(width):
    lane = lax.broadcasted_iota(jnp.int32, (1, width), 1)
    return (lane < width // 2, lane >= width // 2)


def dot_rows(left, right):
    return lax.dot_general(left, right, (((1,), (1,)), ((), ())), preferred_element_type=F32)


def dot_first(left, right):
    return lax.dot_general(left, right, (((0,), (0,)), ((), ())), preferred_element_type=F32)


def dot_plain(left, right):
    return lax.dot_general(left, right, (((1,), (0,)), ((), ())), preferred_element_type=F32)


def prompt_mask(scores, chunk, z, rows):
    key = lax.broadcasted_iota(jnp.int32, scores.shape, 0) + chunk * rows
    query = lax.broadcasted_iota(jnp.int32, scores.shape, 1)
    seen = jnp.logical_or(query >= rows, key <= query + z * rows)
    return jnp.where(seen, scores, NEVER)


def own_mask(scores):
    key = lax.broadcasted_iota(jnp.int32, scores.shape, 0)
    query = lax.broadcasted_iota(jnp.int32, scores.shape, 1)
    return jnp.where(key <= query, scores, NEVER)


def forward_pair(p, z, rows, depth, q_ref, k_ref, v_ref, keys, vals, att_ref, lse_ref):
    cols = pl.ds(pl.multiple_of(p * PAIR, PAIR), PAIR)
    q_pair = q_ref[:, cols] * jnp.asarray(0.125, BF)
    k_own, v_own = k_ref[pl.ds(rows, rows), cols], v_ref[pl.ds(rows, rows), cols]
    outs = []
    for head, mask in enumerate(half_masks(PAIR)):
        q_head = jnp.where(mask, q_pair, jnp.zeros_like(q_pair))
        scores = [
            prompt_mask(dot_rows(keys[p, chunk], q_head), chunk, z, rows) for chunk in range(depth)
        ]
        own = own_mask(dot_rows(k_own, q_head[rows:]))
        top = jnp.max(scores[0], axis=0, keepdims=True)
        for piece in scores[1:]:
            top = jnp.maximum(top, jnp.max(piece, axis=0, keepdims=True))
        top_c = jnp.maximum(top[:, rows:], jnp.max(own, axis=0, keepdims=True))
        top = jnp.concatenate([top[:, :rows], top_c], axis=1)
        total = jnp.zeros_like(top)
        out = jnp.zeros((PAIR, 2 * rows), F32)
        for chunk in range(depth):
            expo = jnp.exp(scores[chunk] - top)
            total = total + jnp.sum(expo, axis=0, keepdims=True)
            out = out + dot_first(vals[p, chunk], expo.astype(BF))
        expo = jnp.exp(own - top_c)
        total_c = total[:, rows:] + jnp.sum(expo, axis=0, keepdims=True)
        out_c = out[:, rows:] + dot_first(v_own, expo.astype(BF))
        total = jnp.concatenate([total[:, :rows], total_c], axis=1)
        out = jnp.concatenate([out[:, :rows], out_c], axis=1) / total
        lse_ref[pl.ds(2 * p + head, 1), :] = top + jnp.log(total)
        outs.append(out[head * HDIM : (head + 1) * HDIM])
    att_ref[:, cols] = jnp.concatenate(outs, axis=0).T.astype(BF)


def backward_pair(p, z, rows, depth, q_ref, k_ref, v_ref, keys, vals, lse_ref, att_ref, g_ref,
                  dq_ref, dk_ref, dv_ref, part):
    cols = pl.ds(pl.multiple_of(p * PAIR, PAIR), PAIR)
    own_rows = pl.ds(rows, rows)
    q_pair = q_ref[:, cols] * jnp.asarray(0.125, BF)
    g_pair = g_ref[:, cols]
    k_own, v_own = k_ref[own_rows, cols], v_ref[own_rows, cols]
    pulled = (g_pair.astype(F32) * att_ref[:, cols].astype(F32)).T
    masks = half_masks(PAIR)
    q_heads = [jnp.where(mask, q_pair, jnp.zeros_like(q_pair)) for mask in masks]
    g_heads = [jnp.where(mask, g_pair, jnp.zeros_like(g_pair)) for mask in masks]
    lses = [lse_ref[pl.ds(2 * p + head, 1), :] for head in range(2)]
    deltas = [
        jnp.sum(pulled[head * HDIM : (head + 1) * HDIM], axis=0, keepdims=True)
        for head in range(2)
    ]
    dq = [jnp.zeros((PAIR, 2 * rows), F32) for _ in range(2)]
    for chunk in range(depth):
        dk = jnp.zeros((rows, PAIR), F32)
        dv = jnp.zeros((rows, PAIR), F32)
        k_chunk, v_chunk = keys[p, chunk], vals[p, chunk]
        for head in range(2):
            scores = prompt_mask(dot_rows(k_chunk, q_heads[head]), chunk, z, rows)
            prob = jnp.exp(scores - lses[head])
            d_prob = dot_rows(v_chunk, g_heads[head])
            d_score = (prob * (d_prob - deltas[head])).astype(BF)
            dv = dv + dot_plain(prob.astype(BF), g_heads[head])
            dk = dk + dot_plain(d_score, q_heads[head])
            dq[head] = dq[head] + dot_first(k_chunk, d_score)
        part[p, chunk, 0] = dk.astype(BF)
        part[p, chunk, 1] = dv.astype(BF)
    dk = jnp.zeros((rows, PAIR), F32)
    dv = jnp.zeros((rows, PAIR), F32)
    for head in range(2):
        q_head, g_head = q_heads[head][rows:], g_heads[head][rows:]
        scores = own_mask(dot_rows(k_own, q_head))
        prob = jnp.exp(scores - lses[head][:, rows:])
        d_prob = dot_rows(v_own, g_head)
        d_score = (prob * (d_prob - deltas[head][:, rows:])).astype(BF)
        dv = dv + dot_plain(prob.astype(BF), g_head)
        dk = dk + dot_plain(d_score, q_head)
        more = dot_first(k_own, d_score)
        dq[head] = jnp.concatenate([dq[head][:, :rows], dq[head][:, rows:] + more], axis=1)
    dk_ref[own_rows, cols] = dk.astype(BF)
    dv_ref[own_rows, cols] = dv.astype(BF)
    both = jnp.concatenate([dq[0][:HDIM], dq[1][HDIM:]], axis=0) * 0.125
    dq_ref[:, cols] = both.T.astype(BF)


class Exchange:
    def __init__(self, depth, rows, pairs):
        self.depth, self.rows, self.pairs = depth, rows, pairs
        dma = pltpu.SemaphoreType.DMA
        self.scratch = [dma((2, 2, pairs, depth)), dma((2, pairs, depth))]

    def bind(self, owned, gathered, scratch):
        self.owned, self.gathered = owned, gathered
        self.send_sem, self.recv_sem = scratch

    def hop(self, kind, p, zp, move, own=False):
        target = self.gathered[kind].at[p, zp]
        cols = pl.ds(pl.multiple_of(p * PAIR, PAIR), PAIR)
        source = self.owned[kind].at[pl.ds(0, self.rows), cols] if own else target
        z = lax.axis_index("fsdp")
        return remote(source, target, self.send_sem.at[kind, (move + 1) // 2, p, zp],
                      self.recv_sem.at[kind, p, zp], (lax.axis_index("dp"), z + move))

    def offer(self, p):
        z = lax.axis_index("fsdp")
        for move in (1, -1):
            @pl.when(z < self.depth - 1 if move > 0 else z > 0)
            def _(move=move):
                for kind in range(2):
                    self.hop(kind, p, z, move, own=True).start()
        cols = pl.ds(pl.multiple_of(p * PAIR, PAIR), PAIR)
        for kind in range(2):
            self.gathered[kind][p, z] = self.owned[kind][pl.ds(0, self.rows), cols]

    def step(self, i):
        z = lax.axis_index("fsdp")
        for distance in range(1, self.depth):
            p = i - (distance - 1) * HOP_LAG
            for sign in (1, -1):
                zp = z + sign * distance
                seen = jnp.logical_and(zp >= 0, zp < self.depth)

                @pl.when(jnp.logical_and(seen, jnp.logical_and(p >= 0, p < self.pairs)))
                def _(p=p, zp=zp, sign=sign):
                    for kind in range(2):
                        self.hop(kind, p, zp, 1).wait_recv()

                    @pl.when(z < self.depth - 1 if sign < 0 else z > 0)
                    def _():
                        for kind in range(2):
                            self.hop(kind, p, zp, -sign).start()

    def finish(self):
        z = lax.axis_index("fsdp")

        def drain(p, carry):
            for zp in range(self.depth):
                for move in (1, -1):
                    far = zp <= z if move > 0 else zp >= z
                    inner = z < self.depth - 1 if move > 0 else z > 0

                    @pl.when(jnp.logical_and(far, inner))
                    def _(zp=zp, move=move):
                        for kind in range(2):
                            self.hop(kind, p, zp, move).wait_send()
            return carry

        lax.fori_loop(0, self.pairs, drain, 0)


def project(normed_ref, weight, out_ref):
    width = 2 * PAIR

    def run(part, carry):
        cols = pl.ds(pl.multiple_of(part * width, width), width)
        piece = weight[..., cols].reshape(normed_ref.shape[1], width)
        out_ref[:, cols] = dot_plain(normed_ref[...], piece).astype(BF)
        return carry

    lax.fori_loop(0, out_ref.shape[1] // width, run, 0)


def forward_kernel(first, rest, exchange, slots, *refs):
    depth, rows, pairs = exchange.depth, exchange.rows, exchange.pairs
    n = len(rest.views)
    ((picks_ref, normed_ref), shard, shards, outs, weights, full, swap, held,
     others) = split_refs(refs, 2, 3, n, 8, 3, n, len(exchange.scratch), len(first.scratch))
    counts_ref, q_ref, k_ref, v_ref, att_ref, lse_ref, keys, vals = outs
    first.bind(shard, weights, held)
    rest.bind(shards, full, others)
    exchange.bind((k_ref, v_ref), (keys, vals), swap)
    z = lax.axis_index("fsdp")
    blocks = picks_ref.shape[1] // 128
    head = depth - 2 + 3 * GATHER_LAG
    per_turn = -(-blocks // head)
    greet(first.side, depth)
    for k in range(first.count):
        first.start(k)

    def both(turn):
        first.step(turn)
        if 0 <= turn - REST_START < rest.count:
            rest.start(turn - REST_START)
        if turn >= REST_DELAY:
            rest.step(turn - REST_DELAY)

    def gather(i, carry):
        for turn in range(head):
            @pl.when(i == turn)
            def _(turn=turn):
                both(turn)

        for inner in range(per_turn):
            block = i * per_turn + inner

            @pl.when(block < blocks)
            def _(block=block):
                count_block(block, rows, slots, picks_ref, counts_ref)

        return carry

    lax.fori_loop(0, head, gather, 0)
    ahead = min(AHEAD, pairs)
    for k, out_ref in enumerate((k_ref, v_ref, q_ref)):
        both(head + k)
        first.put(k).wait()
        project(normed_ref, weights[k], out_ref)
        if k == 1:
            for p in range(ahead):
                exchange.offer(p)
    for k in range(max(0, first.steps - REST_START), rest.count):
        rest.start(k)
    done = max(0, first.steps - REST_DELAY)
    delay = (depth - 2) * HOP_LAG + 1
    turns = pairs + delay

    def run(i, carry):
        @pl.when(i + ahead < pairs)
        def _():
            exchange.offer(i + ahead)

        exchange.step(i)
        for turn in range(turns):
            number = done + turn
            if number < rest.steps:
                @pl.when(i == turn)
                def _(number=number):
                    rest.step(number)

        @pl.when(i >= delay)
        def _():
            forward_pair(i - delay, z, rows, depth, q_ref, k_ref, v_ref, keys, vals, att_ref,
                         lse_ref)

        return carry

    lax.fori_loop(0, turns, run, 0)
    for number in range(done + turns, rest.steps):
        rest.step(number)
    exchange.finish()
    rest.settle()
    first.finish()
    rest.finish()


def attention_forward(side, depth, picks, normed, projections, shards, slots, call_id):
    rows, width = normed.shape[0] // 2, normed.shape[1]
    pairs = width // PAIR
    first, rest = Gather(side, depth, projections), Gather(side, depth, shards)
    exchange = Exchange(depth, rows, pairs)
    any_space, vmem = pl.BlockSpec(memory_space=pl.ANY), pl.BlockSpec(memory_space=pltpu.VMEM)
    spread = jax.ShapeDtypeStruct((pairs, depth, rows, PAIR), BF)
    flat = jax.ShapeDtypeStruct(normed.shape, BF)
    results = pl.pallas_call(
        functools.partial(forward_kernel, first, rest, exchange, slots),
        out_shape=(
            jax.ShapeDtypeStruct((2, MH, slots, rows), BF),
            flat,
            flat,
            flat,
            flat,
            jax.ShapeDtypeStruct((2 * pairs, 2 * rows), F32),
            spread,
            spread,
        )
        + tuple(first.outs)
        + tuple(rest.outs),
        in_specs=[vmem] * 2 + [any_space] * (3 + len(rest.views)),
        out_specs=(vmem,) * 11 + (any_space,) * len(rest.views),
        scratch_shapes=exchange.scratch + first.scratch + rest.scratch,
        compiler_params=params(call_id, 56),
    )(picks, normed, *first.views, *rest.views)
    return results[:8], first.restore(results[8:11]), rest.restore(results[11:])


class Collect:
    def __init__(self, depth, rows, pairs):
        self.depth, self.rows, self.pairs = depth, rows, pairs
        dma = pltpu.SemaphoreType.DMA
        shape = (pairs, depth, 2, rows, PAIR)
        self.scratch = [
            pltpu.VMEM(shape, BF),
            pltpu.VMEM(shape, BF),
            pltpu.VMEM((pairs, 2, rows, PAIR), BF),
            pltpu.VMEM((2, rows, PAIR), F32),
            dma((2, pairs, depth)),
            dma((2, pairs, depth)),
        ]
        self.steps = pairs + (depth - 1) * COLLECT_LAG + 1

    def bind(self, scratch):
        (self.part, self.arrived, self.second, self.whole, self.send_sem,
         self.recv_sem) = scratch

    def hop(self, p, zd, move, final):
        z = lax.axis_index("fsdp")
        way = (move + 1) // 2
        target = self.second.at[p] if final and move < 0 else self.arrived.at[p, zd]
        return remote(self.part.at[p, zd], target, self.send_sem.at[way, p, zd],
                      self.recv_sem.at[way, p, zd], (lax.axis_index("dp"), z + move))

    def flow(self, p, move):
        depth = self.depth
        z = lax.axis_index("fsdp")
        first = z == 0 if move > 0 else z == depth - 1
        for zd in range(depth - 1, -1, -1) if move > 0 else range(depth):
            beyond = zd > z if move > 0 else zd < z

            @pl.when(jnp.logical_and(jnp.logical_not(first), beyond))
            def _(zd=zd):
                self.hop(p, zd, move, False).wait_recv()

                def add(part, carry):
                    self.part[p, zd, part] = self.part[p, zd, part] + self.arrived[p, zd, part]
                    return carry

                lax.fori_loop(0, 2, add, 0)

            @pl.when(jnp.logical_and(jnp.logical_not(first), zd == z))
            def _(zd=zd):
                self.hop(p, zd, move, True).wait_recv()

            @pl.when(zd == z + move)
            def _(zd=zd):
                self.hop(p, zd, move, True).start()

            @pl.when(jnp.logical_and(beyond, zd != z + move))
            def _(zd=zd):
                self.hop(p, zd, move, False).start()

    def step(self, i):
        depth = self.depth
        z = lax.axis_index("fsdp")
        for move in (1, -1):
            stage = z if move > 0 else depth - 1 - z
            p = i - stage * COLLECT_LAG

            @pl.when(jnp.logical_and(p >= 0, p < self.pairs))
            def _(p=p, move=move):
                self.flow(p, move)

    def result(self, p):
        z = lax.axis_index("fsdp")
        depth = self.depth
        whole = self.whole
        whole[...] = self.part[p, z].astype(F32)

        @pl.when(z > 0)
        def _():
            whole[...] = whole[...] + self.arrived[p, z].astype(F32)

        @pl.when(z < depth - 1)
        def _():
            whole[...] = whole[...] + self.second[p].astype(F32)

        return whole[...]

    def finish(self):
        depth = self.depth
        z = lax.axis_index("fsdp")

        def drain(p, carry):
            for zd in range(depth):
                for move in (1, -1):
                    @pl.when(zd > z if move > 0 else zd < z)
                    def _(zd=zd, move=move):
                        self.hop(p, zd, move, False).wait_send()
            return carry

        lax.fori_loop(0, self.pairs, drain, 0)


def produce(late, stage, kind, half, normed_ref, grad_ref):
    side, depth, block, width = late.side, late.depth, late.block, late.width
    k = 2 * kind + half
    run = depth * block
    for start in range(0, normed_ref.shape[1], 2 * PAIR):
        value = dot_first(
            normed_ref[:, start : start + 2 * PAIR], grad_ref[:, half * width : (half + 1) * width]
        ).astype(BF)
        for row in range(0, 2 * PAIR, run):
            number = (start + row) // run
            y, x, core = number // (2 * side), (number // 2) % side, number % 2
            stage[k, y, x, :, :, core * width : (core + 1) * width] = value[row : row + run].reshape(
                depth, block, width)


def backward_kernel(early, late, collect, *refs):
    side, depth, rows, pairs = early.side, collect.depth, collect.rows, collect.pairs
    n = len(early.views)
    ins, grads, (dq_ref, dk_ref, dv_ref), sums, (qkv_sum,), swap, first, second = split_refs(
        refs, 9, n, 3, n, 1, len(collect.scratch), len(early.scratch))
    q_ref, k_ref, v_ref, keys, vals, lse_ref, att_ref, g_ref, normed_ref = ins

    def part_of(k, half):
        number, lead, start = early.layout[k]
        ref = grads[number] if lead is None else grads[number].at[lead]
        return ref.at[:, :, half, :, :, pl.ds(start, early.width)]

    early.bind(part_of, sums, first)
    stage = early.got_core

    def late_part(k, half):
        lanes = pl.ds(pl.multiple_of(half * late.width, late.width), late.width)
        return stage.at[k, :, :, :, :, lanes]

    late.bind(late_part, (qkv_sum,), second)
    collect.bind(swap)
    z = lax.axis_index("fsdp")
    greet(side, depth)
    for k in range(early.count):
        early.start(k)
    last = (depth - 1) * COLLECT_LAG
    ready = max(pairs, early.count)
    settled = max(pairs + last, ready + 2)
    late_at = settled - 1
    due = [ready, ready + 1, settled, settled + 1, settled + 2, settled + 3]

    def run(i, carry):
        @pl.when(i < pairs)
        def _():
            backward_pair(i, z, rows, depth, q_ref, k_ref, v_ref, keys, vals, lse_ref, att_ref,
                          g_ref, dq_ref, dk_ref, dv_ref, collect.part)

        collect.step(i)
        early.step(i)

        @pl.when(jnp.logical_and(i >= last, i < last + pairs))
        def _():
            p = i - last
            cols = pl.ds(pl.multiple_of(p * PAIR, PAIR), PAIR)
            value = collect.result(p)
            dk_ref[pl.ds(0, rows), cols] = value[0].astype(BF)
            dv_ref[pl.ds(0, rows), cols] = value[1].astype(BF)

        late.step(i - late_at)
        for number, when in enumerate(due):
            @pl.when(i == when)
            def _(number=number):
                kind = number // 2
                produce(late, stage, kind, number % 2, normed_ref, (dq_ref, dk_ref, dv_ref)[kind])
                late.start(number)

        return carry

    lax.fori_loop(0, max(early.steps, late_at + late.steps), run, 0)
    collect.finish()
    early.finish()
    late.finish()


def attention_backward(side, depth, q, k, v, keys, vals, lse, att, grad_att, normed, grads, w_qkv,
                       call_id):
    rows, width = q.shape[0] // 2, q.shape[1]
    early = Reduce(side, depth, grads, width, DEEP_AT)
    late = Reduce(side, depth, (w_qkv,), width // 2, 2 * LAG)
    collect = Collect(depth, rows, width // PAIR)
    any_space, vmem = pl.BlockSpec(memory_space=pl.ANY), pl.BlockSpec(memory_space=pltpu.VMEM)
    results = pl.pallas_call(
        functools.partial(backward_kernel, early, late, collect),
        out_shape=(jax.ShapeDtypeStruct(q.shape, BF),) * 3 + tuple(early.outs) + tuple(late.outs),
        in_specs=[vmem] * 9 + [any_space] * len(grads),
        out_specs=(vmem,) * (4 + len(grads)),
        scratch_shapes=collect.scratch + early.scratch + late.scratch,
        compiler_params=params(call_id, 63),
    )(
        q,
        k,
        v,
        keys,
        vals,
        lse,
        att,
        grad_att,
        normed,
        *[grad.reshape(view) for grad, view in zip(grads, early.views)],
    )
    return results[:3], results[3:-1], results[-1]


def count_block(b, rows, slots, picks_ref, counts_ref):
    low, per_word, bits = 16, 5, 6
    groups = -(-(slots // low) // per_word)
    per_head = rows // 128
    cols = pl.ds(pl.multiple_of(b * 128, 128), 128)
    picks = picks_ref[:, cols]
    high = jnp.right_shift(picks, 4)
    group = jnp.right_shift(high * 13, 6)
    word = group * low + jnp.bitwise_and(picks, low - 1)
    unit = jnp.left_shift(jnp.ones_like(picks), bits * (high - per_word * group))
    spot = lax.broadcasted_iota(jnp.int32, (groups * low, 128), 0)
    words = jnp.zeros((groups * low, 128), jnp.int32)
    for pick in range(picks.shape[0]):
        words = words + jnp.where(spot == word[pick : pick + 1], unit[pick : pick + 1], 0)
    part, head = b // (per_head * MH), (b // per_head) % MH
    lanes = pl.ds(pl.multiple_of((b % per_head) * 128, 128), 128)
    for tile in range(slots // low):
        piece = words[(tile // per_word) * low : (tile // per_word + 1) * low]
        count = jnp.bitwise_and(jnp.right_shift(piece, bits * (tile % per_word)), 2**bits - 1)
        counts_ref[part, head, pl.ds(tile * low, low), lanes] = count.astype(F32).astype(BF)


def selector(ids_ref, index, count):
    ids = ids_ref[pl.ds(index, 1), :]
    spot = lax.broadcasted_iota(jnp.int32, (count, ids.shape[1]), 0)
    return jnp.where(spot == ids, 1.0, 0.0).astype(BF)


def picks_kernel(ids_ref, counts_ref, query_ref, keys_ref, weight_ref, mixing_ref, total):
    head = pl.program_id(0)
    rows = counts_ref.shape[3]
    for part in range(2):
        scores = None
        for half in range(2):
            pick = selector(ids_ref, 2 * part + half, SUB)
            slot_keys = dot_first(pick, keys_ref[half * SUB : (half + 1) * SUB]).astype(BF)
            query = query_ref[part * rows : (part + 1) * rows, half * HALF : (half + 1) * HALF]
            piece = dot_rows(slot_keys, query)
            scores = piece if scores is None else scores + piece
        count = counts_ref[part, 0].astype(F32)
        named = count > 0.0
        top = jnp.max(jnp.where(named, scores, -jnp.inf), axis=0, keepdims=True)
        raised = jnp.where(named, count * jnp.exp(scores - top), 0.0)
        weight = raised / jnp.sum(raised, axis=0, keepdims=True)
        weight_ref[part, 0] = weight

        @pl.when(head == 0)
        def _(part=part, weight=weight):
            total[part] = weight

        @pl.when(head > 0)
        def _(part=part, weight=weight):
            total[part] = total[part] + weight

    @pl.when(head == MH - 1)
    def _():
        mixing_ref[...] = total[...].astype(BF)


def slot_weights(ids, counts, mquery, keys_full):
    slots, rows = counts.shape[2:]
    return pl.pallas_call(
        picks_kernel,
        grid=(MH,),
        out_shape=(
            jax.ShapeDtypeStruct(counts.shape, F32),
            jax.ShapeDtypeStruct((2, slots, rows), BF),
        ),
        in_specs=[
            pl.BlockSpec(ids.shape, lambda m: (0, 0)),
            pl.BlockSpec((2, 1, slots, rows), lambda m: (0, m, 0, 0)),
            pl.BlockSpec((2 * rows, 2 * HALF), lambda m: (0, m)),
            pl.BlockSpec((2 * SUB, HALF), lambda m: (m, 0)),
        ],
        out_specs=(
            pl.BlockSpec((2, 1, slots, rows), lambda m: (0, m, 0, 0)),
            pl.BlockSpec((2, slots, rows), lambda m: (0, 0, 0)),
        ),
        scratch_shapes=[pltpu.VMEM((2, slots, rows), F32)],
        cost_estimate=pl.CostEstimate(
            flops=2 * 2 * MH * slots * 2 * HALF * (SUB + rows),
            bytes_accessed=24 * 2**20,
            transcendentals=2 * MH * slots * rows,
        ),
    )(ids, counts, mquery, keys_full)


def picks_back_kernel(block, ids_ref, weight_ref, table_ref, memory_ref, query_ref, keys_ref,
                      grad_query_ref, grad_keys_ref, grad_mixing):
    head = pl.program_id(0)
    rows = weight_ref.shape[3]

    @pl.when(head == 0)
    def _():
        for part in range(2):
            grad_mixing[part] = dot_rows(
                table_ref[part], memory_ref[part * rows : (part + 1) * rows]
            )

    splits = []
    for part in range(2):
        weight = weight_ref[part, 0]
        pulled = weight * grad_mixing[part]
        grad = pulled - weight * jnp.sum(pulled, axis=0, keepdims=True)
        high = grad.astype(BF)
        splits.append((high, (grad - high.astype(F32)).astype(BF)))
    for half in range(2):
        span = slice(half * HALF, (half + 1) * HALF)
        keys = keys_ref[half * SUB : (half + 1) * SUB]
        subs = []
        for part, (high, low) in enumerate(splits):
            pick = selector(ids_ref, 2 * part + half, SUB)
            subs.append((dot_plain(pick, high) + dot_plain(pick, low)).astype(BF))
        sub = jnp.concatenate(subs, axis=1)
        grad_query_ref[:, span] = dot_first(sub, keys).astype(BF)
        total = dot_plain(sub, query_ref[:, span]).astype(BF)
        for shard in range(SUB // (2 * block)):
            for side in range(2):
                start = (2 * shard + side) * block
                row = half * (SUB // 2) + shard * block
                grad_keys_ref[row : row + block, side * HALF : (side + 1) * HALF] = total[
                    start : start + block
                ]


def slot_weights_back(ids, weights, tables, grad_memory, mquery, keys_full, block):
    slots, rows = weights.shape[2:]
    width = tables.shape[2]
    return pl.pallas_call(
        functools.partial(picks_back_kernel, block),
        grid=(MH,),
        out_shape=(
            jax.ShapeDtypeStruct(mquery.shape, BF),
            jax.ShapeDtypeStruct((MH * SUB, 2 * HALF), BF),
        ),
        in_specs=[
            pl.BlockSpec(ids.shape, lambda m: (0, 0)),
            pl.BlockSpec((2, 1, slots, rows), lambda m: (0, m, 0, 0)),
            pl.BlockSpec((2, slots, width), lambda m: (0, 0, 0)),
            pl.BlockSpec((2 * rows, width), lambda m: (0, 0)),
            pl.BlockSpec((2 * rows, 2 * HALF), lambda m: (0, m)),
            pl.BlockSpec((2 * SUB, HALF), lambda m: (m, 0)),
        ],
        out_specs=(
            pl.BlockSpec((2 * rows, 2 * HALF), lambda m: (0, m)),
            pl.BlockSpec((SUB, 2 * HALF), lambda m: (m, 0)),
        ),
        scratch_shapes=[pltpu.VMEM((2, slots, rows), F32)],
        cost_estimate=pl.CostEstimate(
            flops=2 * 2 * MH * slots * rows * (4 * SUB + 4 * HALF),
            bytes_accessed=24 * 2**20,
            transcendentals=0,
        ),
    )(ids, weights, tables, grad_memory, mquery, keys_full)


def one_hot(ids, count):
    return (ids[:, None] == jnp.arange(count, dtype=jnp.int32)[None, :]).astype(BF)


def per_device(
    x_prompt,
    x_cont,
    cot_prompt,
    cot_cont,
    gain_attn,
    gain_mem,
    w_qkv,
    w_attn_out,
    w_mem_query,
    sub_keys,
    w_gate,
    w_mem_out,
    value_rows,
    request,
    slot_prompt,
    slot_cont,
):
    shard_rows, width = value_rows.shape
    owners, capacity = request.shape[2:]
    slots = owners * capacity
    rows = x_prompt.shape[1]
    cols = w_qkv.shape[2]
    block = cols // owners
    side, depth = grid_of(lax.axis_size("dp"), lax.axis_size("fsdp"))

    asked = lax.all_to_all(request[:, 0], ALL, split_axis=1, concat_axis=1, tiled=True)
    def swap(values):
        values = values.reshape(owners, capacity, width)
        swapped = lax.all_to_all(values, ALL, split_axis=0, concat_axis=0, tiled=True)
        return swapped.reshape(slots, width)

    offsets = jnp.maximum(request[:, 0].reshape(2, slots), 0)
    picked = (jnp.arange(slots, dtype=jnp.int32) // capacity)[None] * shard_rows + offsets
    ids = jnp.stack([picked // SUB, picked % SUB], axis=1).reshape(4, slots)
    x_rows = jnp.concatenate([x_prompt[0], x_cont[0]], axis=0).astype(F32)
    dy_low = jnp.concatenate([cot_prompt[0], cot_cont[0]], axis=0)
    normed, inverse = normalize(x_rows, gain_attn)
    normed = normed.astype(BF)
    picks = jnp.stack([slot_prompt[0], slot_cont[0]]).transpose(3, 0, 2, 1)
    picks = picks.reshape(picks.shape[0], -1)
    results, (key_full, value_full, ask_full), full = attention_forward(
        side,
        depth,
        picks,
        normed,
        (w_qkv[1], w_qkv[2], w_qkv[0]),
        (w_attn_out, w_mem_query, sub_keys, w_gate, w_mem_out),
        slots,
        0,
    )
    counts, queries, keys, vals, att, lse, all_keys, all_vals = results
    attn_out_full, query_full, keys_full, gate_full, mem_out_full = full
    att, asked = lax.optimization_barrier((att, asked))
    serve_pick = one_hot(asked.reshape(-1), shard_rows)
    served = mm(serve_pick, value_rows).astype(BF).reshape(2, owners, capacity, width)
    tables = lax.all_to_all(served, ALL, split_axis=1, concat_axis=1, tiled=True)
    tables = tables.reshape(2, slots, width)
    hidden = x_rows + mm(att, attn_out_full)
    normed2, inverse2 = normalize(hidden, gain_mem)
    normed2 = normed2.astype(BF)

    mquery = mm(normed2, query_full).astype(BF)
    gate_pre = mm(normed2, gate_full)
    weights, mixing = slot_weights(ids, counts, mquery, keys_full)
    memory_out = lax.dot_general(
        mixing, tables, (((1,), (1,)), ((0,), (0,))), preferred_element_type=F32
    ).reshape(2 * rows, width)
    sigmoid_gate = jax.nn.sigmoid(gate_pre)
    blended = (memory_out * (gate_pre * sigmoid_gate)).astype(BF)
    out = (hidden + mm(blended, mem_out_full)).astype(BF)

    grad_blend = mm_t(dy_low, mem_out_full)
    grad_mem_out = mm_l(blended, dy_low)
    grad_memory = (grad_blend * gate_pre * sigmoid_gate).astype(BF)
    grad_gate = (
        grad_blend * memory_out * sigmoid_gate * (1.0 + gate_pre * (1.0 - sigmoid_gate))
    ).astype(BF)
    slot_grads = lax.dot_general(
        mixing,
        grad_memory.reshape(2, rows, width),
        (((2,), (1,)), ((0,), (0,))),
        preferred_element_type=F32,
    ).astype(BF)
    arrived = [None, swap(slot_grads[1])]
    grad_query, grad_keys = slot_weights_back(
        ids, weights, tables, grad_memory, mquery, keys_full, block
    )
    grad_query, arrived[1], late = lax.optimization_barrier((grad_query, arrived[1], slot_grads[0]))
    arrived[0] = swap(late)
    grad_normed2 = mm_t(grad_query, query_full) + mm_t(grad_gate, gate_full)
    grad_query_w = mm_l(normed2, grad_query).astype(BF)
    grad_gate_w = mm_l(normed2, grad_gate).astype(BF)
    back, gain_mem_part = norm_backward(hidden, inverse2, gain_mem, grad_normed2)
    grad_hidden = dy_low.astype(F32) + back
    hidden_low = grad_hidden.astype(BF)
    grad_attn_out = mm_l(att, hidden_low).astype(BF)
    grad_att = mm_t(hidden_low, attn_out_full).astype(BF)
    grad_att, arrived = lax.optimization_barrier((grad_att, arrived))
    (grad_q, grad_k, grad_v), early, qkv_shard = attention_backward(
        side,
        depth,
        queries,
        keys,
        vals,
        all_keys,
        all_vals,
        lse,
        att,
        grad_att,
        normed,
        (grad_query_w, grad_keys, grad_gate_w, grad_mem_out.astype(BF), grad_attn_out),
        jax.ShapeDtypeStruct((3, cols, cols), BF),
        1,
    )
    grad_rows = mm_l(serve_pick, jnp.concatenate(arrived, axis=0))
    grad_normed = (
        mm_t(grad_q, ask_full) + mm_t(grad_k, key_full) + mm_t(grad_v, value_full)
    )
    grad_x, gain_attn_part = norm_backward(x_rows, inverse, gain_attn, grad_normed)
    grad_x = grad_hidden + grad_x
    gains = jnp.stack([gain_attn_part, gain_mem_part]).reshape(2, owners, block)
    gains = lax.all_to_all(gains.transpose(1, 0, 2), ALL, split_axis=0, concat_axis=0, tiled=True)
    gain_shards = jnp.sum(gains, axis=0)
    sub_shard = early[1].reshape(block, 2, HALF).transpose(1, 0, 2).reshape(2 * block, HALF)
    return (
        out[None, :rows],
        out[None, rows:],
        grad_x[None, :rows],
        grad_x[None, rows:],
        gain_shards[0],
        gain_shards[1],
        qkv_shard,
        early[4],
        early[0],
        sub_shard,
        early[2],
        early[3],
        grad_rows,
    )


def solution(mesh):
    in_specs = (
        P("dp", "fsdp", None),
        P("dp", "fsdp", None),
        P("dp", "fsdp", None),
        P("dp", "fsdp", None),
        P(),
        P(),
        P(None, "fsdp", None),
        P("fsdp", None),
        P("fsdp", None),
        P("fsdp", None),
        P("fsdp", None),
        P("fsdp", None),
        P(("dp", "fsdp"), None),
        P(None, ("dp", "fsdp"), None, None),
        P("dp", "fsdp", None, None),
        P("dp", "fsdp", None, None),
    )
    out_specs = (
        P("dp", "fsdp", None),
        P("dp", "fsdp", None),
        P("dp", "fsdp", None),
        P("dp", "fsdp", None),
        P(("dp", "fsdp")),
        P(("dp", "fsdp")),
        P(None, ("dp", "fsdp"), None),
        P(("dp", "fsdp"), None),
        P(("dp", "fsdp"), None),
        P(("dp", "fsdp"), None),
        P(("dp", "fsdp"), None),
        P(("dp", "fsdp"), None),
        P(("dp", "fsdp"), None),
    )
    return jax.shard_map(
        per_device, mesh=mesh, in_specs=in_specs, out_specs=out_specs, check_vma=False
    )
```

```python
import functools
import jax
import jax.numpy as jnp
from jax import lax
from jax.experimental import pallas as pl
from jax.experimental.pallas import tpu as pltpu
from jax.sharding import PartitionSpec as P
BF = jnp.bfloat16
F32 = jnp.float32
ALL = ("dp", "fsdp")
MESH = pl.DeviceIdType.MESH
LAG = 4
GATHER_LAG = 3
REST_START = 1
REST_DELAY = 6
DEEP_AT = 8
LATE_LAG = 4
LAST_LAG = 14
COLLECT_LAG = 2
AHEAD = 3
HOP_LAG = 1
PAIR = 128
HDIM = 64
MH = 4
HALF = 512
SUB = 256
NEVER = -1e30
PROJECTION_ORDER = ((0, 0), (0, 1), (1, 0), (2, 0), (1, 1), (2, 1))


def mm(left, right):
    return jnp.dot(left, right, preferred_element_type=F32)


def mm_t(left, right):
    return lax.dot_general(left, right, (((1,), (1,)), ((), ())), preferred_element_type=F32)


def mm_l(left, right):
    return lax.dot_general(left, right, (((0,), (0,)), ((), ())), preferred_element_type=F32)


def normalize(matrix, gain_vec):
    inverse = lax.rsqrt(jnp.mean(matrix * matrix, axis=-1, keepdims=True) + 1e-05)
    return (matrix * inverse * gain_vec, inverse)


def norm_backward(matrix, inverse, gain_vec, grad_normed):
    scaled = gain_vec * grad_normed
    cubed = inverse * inverse * inverse
    grad_matrix = inverse * scaled - matrix * cubed * jnp.mean(
        matrix * scaled, axis=-1, keepdims=True
    )
    return (grad_matrix, jnp.sum(grad_normed * matrix * inverse, axis=0))


def grid_of(plane, depth):
    side = 1
    while 2 * side * side < plane:
        side += 1
    return side, depth


def place(side):
    dp = lax.axis_index("dp")
    return (dp // (2 * side), (dp // 2) % side, dp % 2, lax.axis_index("fsdp"))


def device_at(side, y, x, core, z):
    return ((y * side + x) * 2 + core, z)


def greet(side, depth):
    y, x, core, z = place(side)
    barrier = pltpu.get_barrier_semaphore()
    peers = [device_at(side, y, x, 1 - core, z)]
    for hop in range(1, side):
        peers.append(device_at(side, y, (x + hop) % side, core, z))
        peers.append(device_at(side, (y + hop) % side, x, core, z))
    for hop in range(1, depth):
        peers.append(device_at(side, y, x, core, (z + hop) % depth))
    for peer in peers:
        pl.semaphore_signal(barrier, inc=1, device_id=peer, device_id_type=MESH)
    pl.semaphore_wait(barrier, len(peers))


def remote(source, target, send_sem, recv_sem, peer):
    return pltpu.make_async_remote_copy(
        src_ref=source,
        dst_ref=target,
        send_sem=send_sem,
        recv_sem=recv_sem,
        device_id=peer,
        device_id_type=MESH,
    )


class Gather:
    def __init__(self, side, depth, shards, piece=1024):
        self.side, self.depth = side, depth
        self.views, self.outs, self.shapes, self.held, self.layout = [], [], [], [], []
        plane = 2 * side * side
        for shard in shards:
            rows, cols = shard.shape[-2:]
            block, width = rows // plane, min(cols, piece)
            lead = shard.shape[:-2]
            self.views.append(shard.reshape(lead + (side, side, 2, block, cols)))
            leads = range(lead[0]) if lead else (None,)
            self.layout.append(
                [(number, start) for number in leads for start in range(0, cols, width)]
            )
            self.outs.append(
                jax.ShapeDtypeStruct(lead + (depth, side, side, 2, block, cols), BF)
            )
            self.shapes.append(lead + (depth * rows, cols))
            self.held.append(
                pltpu.VMEM((len(self.layout[-1]), side, side, 2, block, width), BF)
            )
        self.count = count = sum(len(columns) for columns in self.layout)
        self.steps = count + depth - 2 + 3 * GATHER_LAG
        dma = pltpu.SemaphoreType.DMA
        self.scratch = self.held + [
            dma((count,)),
            dma((count,)),
            dma((count, depth)),
            dma((count, depth)),
            dma((count, depth)),
            dma((count, depth, side - 1)),
            dma((count, depth, side - 1)),
            dma((count, depth, side - 1)),
            dma((count, depth, side - 1)),
            dma((count, depth)),
            dma((count, depth)),
        ]

    def restore(self, full):
        return [one.reshape(shape) for one, shape in zip(full, self.shapes)]

    def bind(self, sources, outs, scratch):
        self.sources, self.results = sources, outs
        n_in = len(self.layout)
        self.holders = scratch[:n_in]
        (self.in_sem, self.out_sem, self.right_send, self.left_send, self.deep_recv,
         self.one_send, self.one_recv, self.two_send, self.two_recv, self.core_send,
         self.core_recv) = scratch[n_in:]
        self.pieces = []
        for number, columns in enumerate(self.layout):
            width = self.holders[number].shape[-1]
            width = width if sources[number].shape[-1] > width else None
            for inner, (lead, start) in enumerate(columns):
                self.pieces.append((number, lead, start, width, inner))

    def cut(self, refs, k, *spot):
        number, lead, start, width = self.pieces[k][:4]
        ref = refs[number] if lead is None else refs[number].at[lead]
        ref = ref.at[spot] if spot else ref
        if width is None:
            return ref
        return ref.at[(slice(None),) * (len(ref.shape) - 1) + (pl.ds(start, width),)]

    def along_z(self, k, zp, move, source=None):
        y, x, core, z = place(self.side)
        target = self.cut(self.results, k, zp, y, x, core)
        send = self.right_send if move > 0 else self.left_send
        return remote(target if source is None else source, target, send.at[k, zp],
                      self.deep_recv.at[k, zp], device_at(self.side, y, x, core, z + move))

    def one_copy(self, k, zp, hop):
        side = self.side
        y, x, core, z = place(side)
        peer = device_at(side, y, (x + hop) % side, core, z) if k % 2 == 0 else device_at(
            side, (y + hop) % side, x, core, z)
        ref = self.cut(self.results, k, zp, y, x, core)
        return remote(ref, ref, self.one_send.at[k, zp, hop - 1],
                      self.one_recv.at[k, zp, hop - 1], peer)

    def two_copy(self, k, zp, hop):
        side = self.side
        y, x, core, z = place(side)
        x_first = k % 2 == 0
        peer = device_at(side, (y + hop) % side, x, core, z) if x_first else device_at(
            side, y, (x + hop) % side, core, z)
        ref = (self.cut(self.results, k, zp, y, slice(None), core) if x_first
               else self.cut(self.results, k, zp, slice(None), x, core))
        return remote(ref, ref, self.two_send.at[k, zp, hop - 1],
                      self.two_recv.at[k, zp, hop - 1], peer)

    def core_copy(self, k, zp):
        y, x, core, z = place(self.side)
        ref = self.cut(self.results, k, zp, slice(None), slice(None), core)
        return remote(ref, ref, self.core_send.at[k, zp], self.core_recv.at[k, zp],
                      device_at(self.side, y, x, 1 - core, z))

    def take(self, k):
        number, inner = self.pieces[k][0], self.pieces[k][4]
        return pltpu.make_async_copy(self.cut(self.sources, k), self.holders[number].at[inner],
                                     self.in_sem.at[k])

    def put(self, k):
        z = place(self.side)[3]
        number, inner = self.pieces[k][0], self.pieces[k][4]
        return pltpu.make_async_copy(self.holders[number].at[inner],
                                     self.cut(self.results, k, z), self.out_sem.at[k])

    def start(self, k):
        y, x, core, z = place(self.side)
        self.take(k).start()
        own = self.cut(self.sources, k, y, x, core)

        @pl.when(z < self.depth - 1)
        def _():
            self.along_z(k, z, 1, own).start()

        @pl.when(z > 0)
        def _():
            self.along_z(k, z, -1, own).start()

    def step(self, i):
        side, depth = self.side, self.depth
        z = place(side)[3]
        if i < self.count:
            self.take(i).wait()
            self.put(i).start()
        for stage in range(4):
            for distance in range(1, depth):
                k = i - stage * GATHER_LAG - (distance - 1)
                if not 0 <= k < self.count:
                    continue
                for sign in (1, -1):
                    zp = z + sign * distance

                    @pl.when(jnp.logical_and(zp >= 0, zp < depth))
                    def _(k=k, zp=zp, sign=sign, stage=stage):
                        self.arrival(stage, k, zp, sign)

    def arrival(self, stage, k, zp, sign):
        side, depth = self.side, self.depth
        z = place(side)[3]
        if stage == 0:
            self.along_z(k, zp, 1).wait_recv()

            @pl.when(z < depth - 1 if sign < 0 else z > 0)
            def _():
                self.along_z(k, zp, -sign).start()

            for hop in range(1, side):
                self.one_copy(k, zp, hop).start()
        elif stage == 1:
            for hop in range(1, side):
                self.one_copy(k, zp, hop).wait_recv()
            for hop in range(1, side):
                self.two_copy(k, zp, hop).start()
        elif stage == 2:
            for hop in range(1, side):
                self.two_copy(k, zp, hop).wait_recv()
            self.core_copy(k, zp).start()
        else:
            self.core_copy(k, zp).wait_recv()

    def settle(self):
        for k in range(self.count):
            self.put(k).wait()

    def finish(self):
        side, depth = self.side, self.depth
        z = place(side)[3]
        for k in range(self.count):
            for zp in range(depth):
                @pl.when(jnp.logical_and(zp <= z, z < depth - 1))
                def _(k=k, zp=zp):
                    self.along_z(k, zp, 1).wait_send()

                @pl.when(jnp.logical_and(zp >= z, z > 0))
                def _(k=k, zp=zp):
                    self.along_z(k, zp, -1).wait_send()

                @pl.when(zp != z)
                def _(k=k, zp=zp):
                    for hop in range(1, side):
                        self.one_copy(k, zp, hop).wait_send()
                        self.two_copy(k, zp, hop).wait_send()
                    self.core_copy(k, zp).wait_send()


class Reduce:
    def __init__(self, side, depth, grads, piece, lag, deep_at, last_at):
        self.side, self.depth, self.lag = side, depth, lag
        self.deep_at, self.last_at = deep_at, last_at
        self.layout, self.views, self.outs = [], [], []
        self.width = width = piece
        devices = 2 * side * side * depth
        for grad in grads:
            rows, cols = grad.shape[-2:]
            self.block = block = rows // devices
            lead = grad.shape[:-2]
            self.views.append(lead + (side, side, 2, depth, block, cols))
            leads = range(lead[0]) if lead else (None,)
            self.layout += [
                (len(self.outs), number, start) for number in leads for start in range(0, cols, width)
            ]
            self.outs.append(jax.ShapeDtypeStruct(lead + (block, cols), F32))
        self.count = count = len(self.layout)
        self.steps = count + last_at
        dma = pltpu.SemaphoreType.DMA
        self.scratch = [
            pltpu.VMEM((count, side, side, depth, block, width), BF),
            pltpu.VMEM((count, side, side, depth, block, width), BF),
            pltpu.VMEM((count, side - 1, side, depth, block, width), BF),
            pltpu.VMEM((count, side - 1, depth, block, width), BF),
            pltpu.VMEM((count, depth - 1, block, width), BF),
            pltpu.VMEM((count, block, width), F32),
            dma((count,)),
            dma((count,)),
            dma((count,)),
            dma((count, side - 1)),
            dma((count, side - 1)),
            dma((count, side - 1)),
            dma((count, side - 1)),
            dma((count, depth - 1)),
            dma((count, depth - 1)),
        ]

    def bind(self, sources, outs, scratch):
        (self.mine, self.got_core, self.got_one, self.got_two, self.got_deep, self.total,
         self.local_sem, self.core_send, self.core_recv, self.one_send, self.one_recv,
         self.two_send, self.two_recv, self.deep_send, self.deep_recv) = scratch
        self.results, self.sources = outs, sources

    def core_copy(self, k, source):
        y, x, core, z = place(self.side)
        return remote(source, self.got_core.at[k], self.core_send.at[k],
                      self.core_recv.at[k], device_at(self.side, y, x, 1 - core, z))

    def start(self, k):
        core = place(self.side)[2]
        self.core_copy(k, self.sources(k, 1 - core)).start()
        pltpu.make_async_copy(self.sources(k, core), self.mine.at[k], self.local_sem.at[k]).start()

    def one_copy(self, k, hop, x_first):
        side = self.side
        y, x, core, z = place(side)
        peer = device_at(side, y, (x + hop) % side, core, z) if x_first else device_at(
            side, (y + hop) % side, x, core, z)
        source = (self.mine.at[k, :, (x + hop) % side] if x_first
                  else self.mine.at[k, (y + hop) % side])
        return remote(source, self.got_one.at[k, hop - 1], self.one_send.at[k, hop - 1],
                      self.one_recv.at[k, hop - 1], peer)

    def two_copy(self, k, hop, x_first):
        side = self.side
        y, x, core, z = place(side)
        peer = device_at(side, (y + hop) % side, x, core, z) if x_first else device_at(
            side, y, (x + hop) % side, core, z)
        source = (self.mine.at[k, (y + hop) % side, x] if x_first
                  else self.mine.at[k, y, (x + hop) % side])
        return remote(source, self.got_two.at[k, hop - 1], self.two_send.at[k, hop - 1],
                      self.two_recv.at[k, hop - 1], peer)

    def deep_copy(self, k, hop):
        y, x, core, z = place(self.side)
        there = (z + hop) % self.depth
        return remote(self.mine.at[k, y, x, there], self.got_deep.at[k, hop - 1],
                      self.deep_send.at[k, hop - 1], self.deep_recv.at[k, hop - 1],
                      device_at(self.side, y, x, core, there))

    def both_orders(self, k, action):
        @pl.when(k % 2 == 0)
        def _():
            action(True)

        @pl.when(k % 2 == 1)
        def _():
            action(False)

    def added(self, base, others):
        if len(others) == 1:
            return base + others[0]
        value = base.astype(F32)
        for other in others:
            value = value + other.astype(F32)
        return value.astype(base.dtype)

    def after_core(self, k):
        side, depth, mine, got = self.side, self.depth, self.mine, self.got_core
        self.core_copy(k, got.at[k]).wait_recv()
        pltpu.make_async_copy(got.at[k], mine.at[k], self.local_sem.at[k]).wait()

        def add(index, carry):
            spot = (k, index // (side * depth), (index // depth) % side, index % depth)
            mine[spot] = mine[spot] + got[spot]
            return carry

        lax.fori_loop(0, side * side * depth, add, 0)

        def send(x_first):
            for hop in range(1, side):
                self.one_copy(k, hop, x_first).start()

        self.both_orders(k, send)

    def after_one(self, k):
        side, depth, mine = self.side, self.depth, self.mine
        y, x, core, z = place(side)

        def finish(x_first):
            for hop in range(1, side):
                self.one_copy(k, hop, x_first).wait_recv()

            def add(index, carry):
                a, c = index // depth, index % depth
                spot = (k, a, x, c) if x_first else (k, y, a, c)
                mine[spot] = self.added(
                    mine[spot], [self.got_one[k, hop, a, c] for hop in range(side - 1)]
                )
                return carry

            lax.fori_loop(0, side * depth, add, 0)
            for hop in range(1, side):
                self.two_copy(k, hop, x_first).start()

        self.both_orders(k, finish)

    def after_two(self, k):
        side, depth, mine = self.side, self.depth, self.mine
        y, x, core, z = place(side)

        def finish(x_first):
            for hop in range(1, side):
                self.two_copy(k, hop, x_first).wait_recv()

        self.both_orders(k, finish)

        def add(c, carry):
            mine[k, y, x, c] = self.added(
                mine[k, y, x, c], [self.got_two[k, hop, c] for hop in range(side - 1)]
            )
            return carry

        lax.fori_loop(0, depth, add, 0)

    def send_deep(self, k):
        for hop in range(1, self.depth):
            self.deep_copy(k, hop).start()

    def after_deep(self, k):
        y, x, core, z = place(self.side)
        for hop in range(1, self.depth):
            self.deep_copy(k, hop).wait_recv()
        value = self.mine[k, y, x, z].astype(F32)
        for hop in range(self.depth - 1):
            value = value + self.got_deep[k, hop].astype(F32)
        self.total[k] = value

    def step(self, i):
        stages = (
            (0, self.after_core),
            (self.lag, self.after_one),
            (2 * self.lag, self.after_two),
            (self.deep_at, self.send_deep),
            (self.last_at, self.after_deep),
        )
        for lag, action in stages:
            @pl.when(jnp.logical_and(i >= lag, i < self.count + lag))
            def _(lag=lag, action=action):
                action(i - lag)

    def finish(self):
        for k, (number, lead, start) in enumerate(self.layout):
            spot = (slice(None), pl.ds(start, self.width))
            if lead is None:
                self.results[number][spot] = self.total[k]
            else:
                self.results[number][(lead,) + spot] = self.total[k]

        def drain(k, carry):
            self.core_copy(k, self.got_core.at[k]).wait_send()

            def sent(x_first):
                for hop in range(1, self.side):
                    self.one_copy(k, hop, x_first).wait_send()
                    self.two_copy(k, hop, x_first).wait_send()

            self.both_orders(k, sent)
            for hop in range(1, self.depth):
                self.deep_copy(k, hop).wait_send()
            return carry

        lax.fori_loop(0, self.count, drain, 0)


def split_refs(refs, *counts):
    groups, at = [], 0
    for count in counts:
        groups.append(refs[at : at + count])
        at += count
    return groups + [refs[at:]]


def params(call_id, mib):
    return pltpu.CompilerParams(
        collective_id=call_id, has_side_effects=True, vmem_limit_bytes=mib * 1024 * 1024
    )


def half_masks(width):
    lane = lax.broadcasted_iota(jnp.int32, (1, width), 1)
    return (lane < width // 2, lane >= width // 2)


def dot_rows(left, right):
    return lax.dot_general(left, right, (((1,), (1,)), ((), ())), preferred_element_type=F32)


def dot_first(left, right):
    return lax.dot_general(left, right, (((0,), (0,)), ((), ())), preferred_element_type=F32)


def dot_plain(left, right):
    return lax.dot_general(left, right, (((1,), (0,)), ((), ())), preferred_element_type=F32)


def prompt_mask(scores, chunk, z, rows):
    key = lax.broadcasted_iota(jnp.int32, scores.shape, 0) + chunk * rows
    query = lax.broadcasted_iota(jnp.int32, scores.shape, 1)
    seen = jnp.logical_or(query >= rows, key <= query + z * rows)
    return jnp.where(seen, scores, NEVER)


def own_mask(scores):
    key = lax.broadcasted_iota(jnp.int32, scores.shape, 0)
    query = lax.broadcasted_iota(jnp.int32, scores.shape, 1)
    return jnp.where(key <= query, scores, NEVER)


def forward_pair(p, z, rows, depth, q_ref, k_ref, v_ref, keys, vals, att_ref, lse_ref):
    cols = pl.ds(pl.multiple_of(p * PAIR, PAIR), PAIR)
    q_pair = q_ref[:, cols] * jnp.asarray(0.125, BF)
    k_own, v_own = k_ref[pl.ds(rows, rows), cols], v_ref[pl.ds(rows, rows), cols]
    outs = []
    for head, mask in enumerate(half_masks(PAIR)):
        q_head = jnp.where(mask, q_pair, jnp.zeros_like(q_pair))
        scores = [
            prompt_mask(dot_rows(keys[p, chunk], q_head), chunk, z, rows) for chunk in range(depth)
        ]
        own = own_mask(dot_rows(k_own, q_head[rows:]))
        top = jnp.max(scores[0], axis=0, keepdims=True)
        for piece in scores[1:]:
            top = jnp.maximum(top, jnp.max(piece, axis=0, keepdims=True))
        top_c = jnp.maximum(top[:, rows:], jnp.max(own, axis=0, keepdims=True))
        top = jnp.concatenate([top[:, :rows], top_c], axis=1)
        total = jnp.zeros_like(top)
        out = jnp.zeros((PAIR, 2 * rows), F32)
        for chunk in range(depth):
            expo = jnp.exp(scores[chunk] - top)
            total = total + jnp.sum(expo, axis=0, keepdims=True)
            out = out + dot_first(vals[p, chunk], expo.astype(BF))
        expo = jnp.exp(own - top_c)
        total_c = total[:, rows:] + jnp.sum(expo, axis=0, keepdims=True)
        out_c = out[:, rows:] + dot_first(v_own, expo.astype(BF))
        total = jnp.concatenate([total[:, :rows], total_c], axis=1)
        out = jnp.concatenate([out[:, :rows], out_c], axis=1) / total
        lse_ref[pl.ds(2 * p + head, 1), :] = top + jnp.log(total)
        outs.append(out[head * HDIM : (head + 1) * HDIM])
    att_ref[:, cols] = jnp.concatenate(outs, axis=0).T.astype(BF)


def backward_pair(p, z, rows, depth, q_ref, k_ref, v_ref, keys, vals, lse_ref, att_ref, g_ref,
                  dq_ref, dk_ref, dv_ref, part):
    cols = pl.ds(pl.multiple_of(p * PAIR, PAIR), PAIR)
    own_rows = pl.ds(rows, rows)
    q_pair = q_ref[:, cols] * jnp.asarray(0.125, BF)
    g_pair = g_ref[:, cols]
    k_own, v_own = k_ref[own_rows, cols], v_ref[own_rows, cols]
    pulled = (g_pair.astype(F32) * att_ref[:, cols].astype(F32)).T
    masks = half_masks(PAIR)
    q_heads = [jnp.where(mask, q_pair, jnp.zeros_like(q_pair)) for mask in masks]
    g_heads = [jnp.where(mask, g_pair, jnp.zeros_like(g_pair)) for mask in masks]
    lses = [lse_ref[pl.ds(2 * p + head, 1), :] for head in range(2)]
    deltas = [
        jnp.sum(pulled[head * HDIM : (head + 1) * HDIM], axis=0, keepdims=True)
        for head in range(2)
    ]
    dq = [jnp.zeros((PAIR, 2 * rows), F32) for _ in range(2)]
    for chunk in range(depth):
        dk = jnp.zeros((rows, PAIR), F32)
        dv = jnp.zeros((rows, PAIR), F32)
        k_chunk, v_chunk = keys[p, chunk], vals[p, chunk]
        for head in range(2):
            scores = prompt_mask(dot_rows(k_chunk, q_heads[head]), chunk, z, rows)
            prob = jnp.exp(scores - lses[head])
            d_prob = dot_rows(v_chunk, g_heads[head])
            d_score = (prob * (d_prob - deltas[head])).astype(BF)
            dv = dv + dot_plain(prob.astype(BF), g_heads[head])
            dk = dk + dot_plain(d_score, q_heads[head])
            dq[head] = dq[head] + dot_first(k_chunk, d_score)
        part[p, chunk, 0] = dk.astype(BF)
        part[p, chunk, 1] = dv.astype(BF)
    dk = jnp.zeros((rows, PAIR), F32)
    dv = jnp.zeros((rows, PAIR), F32)
    for head in range(2):
        q_head, g_head = q_heads[head][rows:], g_heads[head][rows:]
        scores = own_mask(dot_rows(k_own, q_head))
        prob = jnp.exp(scores - lses[head][:, rows:])
        d_prob = dot_rows(v_own, g_head)
        d_score = (prob * (d_prob - deltas[head][:, rows:])).astype(BF)
        dv = dv + dot_plain(prob.astype(BF), g_head)
        dk = dk + dot_plain(d_score, q_head)
        more = dot_first(k_own, d_score)
        dq[head] = jnp.concatenate([dq[head][:, :rows], dq[head][:, rows:] + more], axis=1)
    dk_ref[own_rows, cols] = dk.astype(BF)
    dv_ref[own_rows, cols] = dv.astype(BF)
    both = jnp.concatenate([dq[0][:HDIM], dq[1][HDIM:]], axis=0) * 0.125
    dq_ref[:, cols] = both.T.astype(BF)


class Exchange:
    def __init__(self, depth, rows, pairs):
        self.depth, self.rows, self.pairs = depth, rows, pairs
        dma = pltpu.SemaphoreType.DMA
        self.scratch = [dma((2, 2, pairs, depth)), dma((2, pairs, depth))]

    def bind(self, owned, gathered, scratch):
        self.owned, self.gathered = owned, gathered
        self.send_sem, self.recv_sem = scratch

    def hop(self, kind, p, zp, move, own=False):
        target = self.gathered[kind].at[p, zp]
        cols = pl.ds(pl.multiple_of(p * PAIR, PAIR), PAIR)
        source = self.owned[kind].at[pl.ds(0, self.rows), cols] if own else target
        z = lax.axis_index("fsdp")
        return remote(source, target, self.send_sem.at[kind, (move + 1) // 2, p, zp],
                      self.recv_sem.at[kind, p, zp], (lax.axis_index("dp"), z + move))

    def offer(self, p):
        z = lax.axis_index("fsdp")
        for move in (1, -1):
            @pl.when(z < self.depth - 1 if move > 0 else z > 0)
            def _(move=move):
                for kind in range(2):
                    self.hop(kind, p, z, move, own=True).start()
        cols = pl.ds(pl.multiple_of(p * PAIR, PAIR), PAIR)
        for kind in range(2):
            self.gathered[kind][p, z] = self.owned[kind][pl.ds(0, self.rows), cols]

    def step(self, i):
        z = lax.axis_index("fsdp")
        for distance in range(1, self.depth):
            p = i - (distance - 1) * HOP_LAG
            for sign in (1, -1):
                zp = z + sign * distance
                seen = jnp.logical_and(zp >= 0, zp < self.depth)

                @pl.when(jnp.logical_and(seen, jnp.logical_and(p >= 0, p < self.pairs)))
                def _(p=p, zp=zp, sign=sign):
                    for kind in range(2):
                        self.hop(kind, p, zp, 1).wait_recv()

                    @pl.when(z < self.depth - 1 if sign < 0 else z > 0)
                    def _():
                        for kind in range(2):
                            self.hop(kind, p, zp, -sign).start()

    def finish(self):
        z = lax.axis_index("fsdp")

        def drain(p, carry):
            for zp in range(self.depth):
                for move in (1, -1):
                    far = zp <= z if move > 0 else zp >= z
                    inner = z < self.depth - 1 if move > 0 else z > 0

                    @pl.when(jnp.logical_and(far, inner))
                    def _(zp=zp, move=move):
                        for kind in range(2):
                            self.hop(kind, p, zp, move).wait_send()
            return carry

        lax.fori_loop(0, self.pairs, drain, 0)


def project(normed_ref, weight, out_ref):
    width = 2 * PAIR

    def run(part, carry):
        cols = pl.ds(pl.multiple_of(part * width, width), width)
        piece = weight[..., cols].reshape(normed_ref.shape[1], width)
        out_ref[:, cols] = dot_plain(normed_ref[...], piece).astype(BF)
        return carry

    lax.fori_loop(0, out_ref.shape[1] // width, run, 0)


def forward_kernel(first, rest, exchange, slots, *refs):
    depth, rows, pairs = exchange.depth, exchange.rows, exchange.pairs
    n = len(rest.views)
    ((picks_ref, normed_ref), shard, shards, outs, weights, full, swap, held,
     others) = split_refs(refs, 2, 3, n, 8, 3, n, len(exchange.scratch), len(first.scratch))
    counts_ref, q_ref, k_ref, v_ref, att_ref, lse_ref, keys, vals = outs
    first.bind(shard, weights, held)
    rest.bind(shards, full, others)
    exchange.bind((k_ref, v_ref), (keys, vals), swap)
    z = lax.axis_index("fsdp")
    blocks = picks_ref.shape[1] // 128
    head = depth - 2 + 3 * GATHER_LAG
    per_turn = -(-blocks // head)
    greet(first.side, depth)
    for k in range(first.count):
        first.start(k)

    def both(turn):
        first.step(turn)
        if 0 <= turn - REST_START < rest.count:
            rest.start(turn - REST_START)
        if turn >= REST_DELAY:
            rest.step(turn - REST_DELAY)

    def gather(i, carry):
        for turn in range(head):
            @pl.when(i == turn)
            def _(turn=turn):
                both(turn)

        for inner in range(per_turn):
            block = i * per_turn + inner

            @pl.when(block < blocks)
            def _(block=block):
                count_block(block, rows, slots, picks_ref, counts_ref)

        return carry

    lax.fori_loop(0, head, gather, 0)
    ahead = min(AHEAD, pairs)
    for k, out_ref in enumerate((k_ref, v_ref, q_ref)):
        both(head + k)
        first.put(k).wait()
        project(normed_ref, weights[k], out_ref)
        if k == 1:
            for p in range(ahead):
                exchange.offer(p)
    for k in range(max(0, first.steps - REST_START), rest.count):
        rest.start(k)
    done = max(0, first.steps - REST_DELAY)
    delay = (depth - 2) * HOP_LAG + 1
    turns = pairs + delay

    def run(i, carry):
        @pl.when(i + ahead < pairs)
        def _():
            exchange.offer(i + ahead)

        exchange.step(i)
        for turn in range(turns):
            number = done + turn
            if number < rest.steps:
                @pl.when(i == turn)
                def _(number=number):
                    rest.step(number)

        @pl.when(i >= delay)
        def _():
            forward_pair(i - delay, z, rows, depth, q_ref, k_ref, v_ref, keys, vals, att_ref,
                         lse_ref)

        return carry

    lax.fori_loop(0, turns, run, 0)
    for number in range(done + turns, rest.steps):
        rest.step(number)
    exchange.finish()
    rest.settle()
    first.finish()
    rest.finish()


def attention_forward(side, depth, picks, normed, projections, shards, slots, call_id):
    rows, width = normed.shape[0] // 2, normed.shape[1]
    pairs = width // PAIR
    first, rest = Gather(side, depth, projections), Gather(side, depth, shards)
    exchange = Exchange(depth, rows, pairs)
    any_space, vmem = pl.BlockSpec(memory_space=pl.ANY), pl.BlockSpec(memory_space=pltpu.VMEM)
    spread = jax.ShapeDtypeStruct((pairs, depth, rows, PAIR), BF)
    flat = jax.ShapeDtypeStruct(normed.shape, BF)
    results = pl.pallas_call(
        functools.partial(forward_kernel, first, rest, exchange, slots),
        out_shape=(
            jax.ShapeDtypeStruct((2, MH, slots, rows), BF),
            flat,
            flat,
            flat,
            flat,
            jax.ShapeDtypeStruct((2 * pairs, 2 * rows), F32),
            spread,
            spread,
        )
        + tuple(first.outs)
        + tuple(rest.outs),
        in_specs=[vmem] * 2 + [any_space] * (3 + len(rest.views)),
        out_specs=(vmem,) * 11 + (any_space,) * len(rest.views),
        scratch_shapes=exchange.scratch + first.scratch + rest.scratch,
        compiler_params=params(call_id, 56),
    )(picks, normed, *first.views, *rest.views)
    return results[:8], first.restore(results[8:11]), rest.restore(results[11:])


class Collect:
    def __init__(self, depth, rows, pairs):
        self.depth, self.rows, self.pairs = depth, rows, pairs
        dma = pltpu.SemaphoreType.DMA
        shape = (pairs, depth, 2, rows, PAIR)
        self.scratch = [
            pltpu.VMEM(shape, BF),
            pltpu.VMEM(shape, BF),
            pltpu.VMEM((pairs, 2, rows, PAIR), BF),
            pltpu.VMEM((2, rows, PAIR), F32),
            dma((2, pairs, depth)),
            dma((2, pairs, depth)),
        ]
        self.steps = pairs + (depth - 1) * COLLECT_LAG + 1

    def bind(self, scratch):
        (self.part, self.arrived, self.second, self.whole, self.send_sem,
         self.recv_sem) = scratch

    def hop(self, p, zd, move, final):
        z = lax.axis_index("fsdp")
        way = (move + 1) // 2
        target = self.second.at[p] if final and move < 0 else self.arrived.at[p, zd]
        return remote(self.part.at[p, zd], target, self.send_sem.at[way, p, zd],
                      self.recv_sem.at[way, p, zd], (lax.axis_index("dp"), z + move))

    def flow(self, p, move):
        depth = self.depth
        z = lax.axis_index("fsdp")
        first = z == 0 if move > 0 else z == depth - 1
        for zd in range(depth - 1, -1, -1) if move > 0 else range(depth):
            beyond = zd > z if move > 0 else zd < z

            @pl.when(jnp.logical_and(jnp.logical_not(first), beyond))
            def _(zd=zd):
                self.hop(p, zd, move, False).wait_recv()

                def add(part, carry):
                    self.part[p, zd, part] = self.part[p, zd, part] + self.arrived[p, zd, part]
                    return carry

                lax.fori_loop(0, 2, add, 0)

            @pl.when(jnp.logical_and(jnp.logical_not(first), zd == z))
            def _(zd=zd):
                self.hop(p, zd, move, True).wait_recv()

            @pl.when(zd == z + move)
            def _(zd=zd):
                self.hop(p, zd, move, True).start()

            @pl.when(jnp.logical_and(beyond, zd != z + move))
            def _(zd=zd):
                self.hop(p, zd, move, False).start()

    def step(self, i):
        depth = self.depth
        z = lax.axis_index("fsdp")
        for move in (1, -1):
            stage = z if move > 0 else depth - 1 - z
            p = i - stage * COLLECT_LAG

            @pl.when(jnp.logical_and(p >= 0, p < self.pairs))
            def _(p=p, move=move):
                self.flow(p, move)

    def result(self, p):
        z = lax.axis_index("fsdp")
        depth = self.depth
        whole = self.whole
        whole[...] = self.part[p, z].astype(F32)

        @pl.when(z > 0)
        def _():
            whole[...] = whole[...] + self.arrived[p, z].astype(F32)

        @pl.when(z < depth - 1)
        def _():
            whole[...] = whole[...] + self.second[p].astype(F32)

        return whole[...]

    def finish(self):
        depth = self.depth
        z = lax.axis_index("fsdp")

        def drain(p, carry):
            for zd in range(depth):
                for move in (1, -1):
                    @pl.when(zd > z if move > 0 else zd < z)
                    def _(zd=zd, move=move):
                        self.hop(p, zd, move, False).wait_send()
            return carry

        lax.fori_loop(0, self.pairs, drain, 0)


def produce(late, stage, k, half, normed_ref, grad_ref):
    side, depth, block, width = late.side, late.depth, late.block, late.width
    run = depth * block
    for start in range(0, normed_ref.shape[1], 2 * PAIR):
        value = dot_first(
            normed_ref[:, start : start + 2 * PAIR], grad_ref[:, half * width : (half + 1) * width]
        ).astype(BF)
        for row in range(0, 2 * PAIR, run):
            number = (start + row) // run
            y, x, core = number // (2 * side), (number // 2) % side, number % 2
            stage[k, y, x, :, :, core * width : (core + 1) * width] = value[row : row + run].reshape(
                depth, block, width)


def backward_kernel(early, late, collect, *refs):
    side, depth, rows, pairs = early.side, collect.depth, collect.rows, collect.pairs
    n = len(early.views)
    ins, grads, (dq_ref, dk_ref, dv_ref), sums, (qkv_sum,), swap, first, second = split_refs(
        refs, 9, n, 3, n, 1, len(collect.scratch), len(early.scratch))
    q_ref, k_ref, v_ref, keys, vals, lse_ref, att_ref, g_ref, normed_ref = ins

    def part_of(k, half):
        number, lead, start = early.layout[k]
        ref = grads[number] if lead is None else grads[number].at[lead]
        return ref.at[:, :, half, :, :, pl.ds(start, early.width)]

    early.bind(part_of, sums, first)
    stage = early.got_core

    def late_part(k, half):
        lanes = pl.ds(pl.multiple_of(half * late.width, late.width), late.width)
        return stage.at[k, :, :, :, :, lanes]

    late.bind(late_part, (qkv_sum,), second)
    collect.bind(swap)
    z = lax.axis_index("fsdp")
    greet(side, depth)
    for k in range(early.count):
        early.start(k)
    last = (depth - 1) * COLLECT_LAG
    ready = max(pairs, early.count)
    halfway = max(ready + 2, last + pairs // 2 - 1)
    settled = max(halfway + 2, last + pairs - 1)
    due = [ready, ready + 1, halfway, halfway + 1, settled, settled + 1]
    late_at = 1 + max(when - number for number, when in enumerate(due))

    def run(i, carry):
        @pl.when(i < pairs)
        def _():
            backward_pair(i, z, rows, depth, q_ref, k_ref, v_ref, keys, vals, lse_ref, att_ref,
                          g_ref, dq_ref, dk_ref, dv_ref, collect.part)

        collect.step(i)
        early.step(i)

        @pl.when(jnp.logical_and(i >= last, i < last + pairs))
        def _():
            p = i - last
            cols = pl.ds(pl.multiple_of(p * PAIR, PAIR), PAIR)
            value = collect.result(p)
            dk_ref[pl.ds(0, rows), cols] = value[0].astype(BF)
            dv_ref[pl.ds(0, rows), cols] = value[1].astype(BF)

        late.step(i - late_at)
        for number, when in enumerate(due):
            @pl.when(i == when)
            def _(number=number):
                kind, half = PROJECTION_ORDER[number]
                produce(late, stage, number, half, normed_ref, (dq_ref, dk_ref, dv_ref)[kind])
                late.start(number)

        return carry

    lax.fori_loop(0, max(early.steps, late_at + late.steps), run, 0)
    collect.finish()
    early.finish()
    late.finish()


def attention_backward(side, depth, q, k, v, keys, vals, lse, att, grad_att, normed, grads, w_qkv,
                       call_id):
    rows, width = q.shape[0] // 2, q.shape[1]
    early = Reduce(side, depth, grads, width, LAG, DEEP_AT, DEEP_AT + LAST_LAG)
    late = Reduce(side, depth, (w_qkv,), width // 2, LATE_LAG, 2 * LATE_LAG, 3 * LATE_LAG)
    late.layout = [(0, kind, half * (width // 2)) for kind, half in PROJECTION_ORDER]
    collect = Collect(depth, rows, width // PAIR)
    any_space, vmem = pl.BlockSpec(memory_space=pl.ANY), pl.BlockSpec(memory_space=pltpu.VMEM)
    results = pl.pallas_call(
        functools.partial(backward_kernel, early, late, collect),
        out_shape=(jax.ShapeDtypeStruct(q.shape, BF),) * 3 + tuple(early.outs) + tuple(late.outs),
        in_specs=[vmem] * 9 + [any_space] * len(grads),
        out_specs=(vmem,) * (4 + len(grads)),
        scratch_shapes=collect.scratch + early.scratch + late.scratch,
        compiler_params=params(call_id, 63),
    )(
        q,
        k,
        v,
        keys,
        vals,
        lse,
        att,
        grad_att,
        normed,
        *[grad.reshape(view) for grad, view in zip(grads, early.views)],
    )
    return results[:3], results[3:-1], results[-1]


def count_block(b, rows, slots, picks_ref, counts_ref):
    low, per_word, bits = 16, 5, 6
    groups = -(-(slots // low) // per_word)
    per_head = rows // 128
    cols = pl.ds(pl.multiple_of(b * 128, 128), 128)
    picks = picks_ref[:, cols]
    high = jnp.right_shift(picks, 4)
    group = jnp.right_shift(high * 13, 6)
    word = group * low + jnp.bitwise_and(picks, low - 1)
    unit = jnp.left_shift(jnp.ones_like(picks), bits * (high - per_word * group))
    spot = lax.broadcasted_iota(jnp.int32, (groups * low, 128), 0)
    words = jnp.zeros((groups * low, 128), jnp.int32)
    for pick in range(picks.shape[0]):
        words = words + jnp.where(spot == word[pick : pick + 1], unit[pick : pick + 1], 0)
    part, head = b // (per_head * MH), (b // per_head) % MH
    lanes = pl.ds(pl.multiple_of((b % per_head) * 128, 128), 128)
    for tile in range(slots // low):
        piece = words[(tile // per_word) * low : (tile // per_word + 1) * low]
        count = jnp.bitwise_and(jnp.right_shift(piece, bits * (tile % per_word)), 2**bits - 1)
        counts_ref[part, head, pl.ds(tile * low, low), lanes] = count.astype(F32).astype(BF)


def selector(ids_ref, index, count):
    ids = ids_ref[pl.ds(index, 1), :]
    spot = lax.broadcasted_iota(jnp.int32, (count, ids.shape[1]), 0)
    return jnp.where(spot == ids, 1.0, 0.0).astype(BF)


def picks_kernel(ids_ref, counts_ref, query_ref, keys_ref, weight_ref, mixing_ref, total):
    head = pl.program_id(0)
    rows = counts_ref.shape[3]
    for part in range(2):
        scores = None
        for half in range(2):
            pick = selector(ids_ref, 2 * part + half, SUB)
            slot_keys = dot_first(pick, keys_ref[half * SUB : (half + 1) * SUB]).astype(BF)
            query = query_ref[part * rows : (part + 1) * rows, half * HALF : (half + 1) * HALF]
            piece = dot_rows(slot_keys, query)
            scores = piece if scores is None else scores + piece
        count = counts_ref[part, 0].astype(F32)
        named = count > 0.0
        top = jnp.max(jnp.where(named, scores, -jnp.inf), axis=0, keepdims=True)
        raised = jnp.where(named, count * jnp.exp(scores - top), 0.0)
        weight = raised / jnp.sum(raised, axis=0, keepdims=True)
        weight_ref[part, 0] = weight

        @pl.when(head == 0)
        def _(part=part, weight=weight):
            total[part] = weight

        @pl.when(head > 0)
        def _(part=part, weight=weight):
            total[part] = total[part] + weight

    @pl.when(head == MH - 1)
    def _():
        mixing_ref[...] = total[...].astype(BF)


def slot_weights(ids, counts, mquery, keys_full):
    slots, rows = counts.shape[2:]
    return pl.pallas_call(
        picks_kernel,
        grid=(MH,),
        out_shape=(
            jax.ShapeDtypeStruct(counts.shape, F32),
            jax.ShapeDtypeStruct((2, slots, rows), BF),
        ),
        in_specs=[
            pl.BlockSpec(ids.shape, lambda m: (0, 0)),
            pl.BlockSpec((2, 1, slots, rows), lambda m: (0, m, 0, 0)),
            pl.BlockSpec((2 * rows, 2 * HALF), lambda m: (0, m)),
            pl.BlockSpec((2 * SUB, HALF), lambda m: (m, 0)),
        ],
        out_specs=(
            pl.BlockSpec((2, 1, slots, rows), lambda m: (0, m, 0, 0)),
            pl.BlockSpec((2, slots, rows), lambda m: (0, 0, 0)),
        ),
        scratch_shapes=[pltpu.VMEM((2, slots, rows), F32)],
        cost_estimate=pl.CostEstimate(
            flops=2 * 2 * MH * slots * 2 * HALF * (SUB + rows),
            bytes_accessed=24 * 2**20,
            transcendentals=2 * MH * slots * rows,
        ),
    )(ids, counts, mquery, keys_full)


def picks_back_kernel(block, ids_ref, weight_ref, table_ref, memory_ref, query_ref, keys_ref,
                      grad_query_ref, grad_keys_ref, grad_mixing):
    head = pl.program_id(0)
    rows = weight_ref.shape[3]

    @pl.when(head == 0)
    def _():
        for part in range(2):
            grad_mixing[part] = dot_rows(
                table_ref[part], memory_ref[part * rows : (part + 1) * rows]
            )

    splits = []
    for part in range(2):
        weight = weight_ref[part, 0]
        pulled = weight * grad_mixing[part]
        grad = pulled - weight * jnp.sum(pulled, axis=0, keepdims=True)
        high = grad.astype(BF)
        splits.append((high, (grad - high.astype(F32)).astype(BF)))
    for half in range(2):
        span = slice(half * HALF, (half + 1) * HALF)
        keys = keys_ref[half * SUB : (half + 1) * SUB]
        subs = []
        for part, (high, low) in enumerate(splits):
            pick = selector(ids_ref, 2 * part + half, SUB)
            subs.append((dot_plain(pick, high) + dot_plain(pick, low)).astype(BF))
        sub = jnp.concatenate(subs, axis=1)
        grad_query_ref[:, span] = dot_first(sub, keys).astype(BF)
        total = dot_plain(sub, query_ref[:, span]).astype(BF)
        for shard in range(SUB // (2 * block)):
            for side in range(2):
                start = (2 * shard + side) * block
                row = half * (SUB // 2) + shard * block
                grad_keys_ref[row : row + block, side * HALF : (side + 1) * HALF] = total[
                    start : start + block
                ]


def slot_weights_back(ids, weights, tables, grad_memory, mquery, keys_full, block):
    slots, rows = weights.shape[2:]
    width = tables.shape[2]
    return pl.pallas_call(
        functools.partial(picks_back_kernel, block),
        grid=(MH,),
        out_shape=(
            jax.ShapeDtypeStruct(mquery.shape, BF),
            jax.ShapeDtypeStruct((MH * SUB, 2 * HALF), BF),
        ),
        in_specs=[
            pl.BlockSpec(ids.shape, lambda m: (0, 0)),
            pl.BlockSpec((2, 1, slots, rows), lambda m: (0, m, 0, 0)),
            pl.BlockSpec((2, slots, width), lambda m: (0, 0, 0)),
            pl.BlockSpec((2 * rows, width), lambda m: (0, 0)),
            pl.BlockSpec((2 * rows, 2 * HALF), lambda m: (0, m)),
            pl.BlockSpec((2 * SUB, HALF), lambda m: (m, 0)),
        ],
        out_specs=(
            pl.BlockSpec((2 * rows, 2 * HALF), lambda m: (0, m)),
            pl.BlockSpec((SUB, 2 * HALF), lambda m: (m, 0)),
        ),
        scratch_shapes=[pltpu.VMEM((2, slots, rows), F32)],
        cost_estimate=pl.CostEstimate(
            flops=2 * 2 * MH * slots * rows * (4 * SUB + 4 * HALF),
            bytes_accessed=24 * 2**20,
            transcendentals=0,
        ),
    )(ids, weights, tables, grad_memory, mquery, keys_full)


def one_hot(ids, count):
    return (ids[:, None] == jnp.arange(count, dtype=jnp.int32)[None, :]).astype(BF)


def per_device(
    x_prompt,
    x_cont,
    cot_prompt,
    cot_cont,
    gain_attn,
    gain_mem,
    w_qkv,
    w_attn_out,
    w_mem_query,
    sub_keys,
    w_gate,
    w_mem_out,
    value_rows,
    request,
    slot_prompt,
    slot_cont,
):
    shard_rows, width = value_rows.shape
    owners, capacity = request.shape[2:]
    slots = owners * capacity
    rows = x_prompt.shape[1]
    cols = w_qkv.shape[2]
    block = cols // owners
    side, depth = grid_of(lax.axis_size("dp"), lax.axis_size("fsdp"))

    asked = lax.all_to_all(request[:, 0], ALL, split_axis=1, concat_axis=1, tiled=True)
    def swap(values):
        values = values.reshape(owners, capacity, width)
        swapped = lax.all_to_all(values, ALL, split_axis=0, concat_axis=0, tiled=True)
        return swapped.reshape(slots, width)

    offsets = jnp.maximum(request[:, 0].reshape(2, slots), 0)
    picked = (jnp.arange(slots, dtype=jnp.int32) // capacity)[None] * shard_rows + offsets
    ids = jnp.stack([picked // SUB, picked % SUB], axis=1).reshape(4, slots)
    x_rows = jnp.concatenate([x_prompt[0], x_cont[0]], axis=0).astype(F32)
    dy_low = jnp.concatenate([cot_prompt[0], cot_cont[0]], axis=0)
    normed, inverse = normalize(x_rows, gain_attn)
    normed = normed.astype(BF)
    picks = jnp.stack([slot_prompt[0], slot_cont[0]]).transpose(3, 0, 2, 1)
    picks = picks.reshape(picks.shape[0], -1)
    results, (key_full, value_full, ask_full), full = attention_forward(
        side,
        depth,
        picks,
        normed,
        (w_qkv[1], w_qkv[2], w_qkv[0]),
        (w_attn_out, w_mem_query, sub_keys, w_gate, w_mem_out),
        slots,
        0,
    )
    counts, queries, keys, vals, att, lse, all_keys, all_vals = results
    attn_out_full, query_full, keys_full, gate_full, mem_out_full = full
    att, asked = lax.optimization_barrier((att, asked))
    serve_pick = one_hot(asked.reshape(-1), shard_rows)
    served = mm(serve_pick, value_rows).astype(BF).reshape(2, owners, capacity, width)
    tables = lax.all_to_all(served, ALL, split_axis=1, concat_axis=1, tiled=True)
    tables = tables.reshape(2, slots, width)
    hidden = x_rows + mm(att, attn_out_full)
    normed2, inverse2 = normalize(hidden, gain_mem)
    normed2 = normed2.astype(BF)

    mquery = mm(normed2, query_full).astype(BF)
    gate_pre = mm(normed2, gate_full)
    weights, mixing = slot_weights(ids, counts, mquery, keys_full)
    memory_out = lax.dot_general(
        mixing, tables, (((1,), (1,)), ((0,), (0,))), preferred_element_type=F32
    ).reshape(2 * rows, width)
    sigmoid_gate = jax.nn.sigmoid(gate_pre)
    blended = (memory_out * (gate_pre * sigmoid_gate)).astype(BF)
    out = (hidden + mm(blended, mem_out_full)).astype(BF)

    grad_blend = mm_t(dy_low, mem_out_full)
    grad_mem_out = mm_l(blended, dy_low)
    grad_memory = (grad_blend * gate_pre * sigmoid_gate).astype(BF)
    grad_gate = (
        grad_blend * memory_out * sigmoid_gate * (1.0 + gate_pre * (1.0 - sigmoid_gate))
    ).astype(BF)
    slot_grads = lax.dot_general(
        mixing,
        grad_memory.reshape(2, rows, width),
        (((2,), (1,)), ((0,), (0,))),
        preferred_element_type=F32,
    ).astype(BF)
    arrived = [None, swap(slot_grads[1])]
    grad_query, grad_keys = slot_weights_back(
        ids, weights, tables, grad_memory, mquery, keys_full, block
    )
    grad_query, arrived[1], late = lax.optimization_barrier((grad_query, arrived[1], slot_grads[0]))
    arrived[0] = swap(late)
    grad_normed2 = mm_t(grad_query, query_full) + mm_t(grad_gate, gate_full)
    grad_query_w = mm_l(normed2, grad_query).astype(BF)
    grad_gate_w = mm_l(normed2, grad_gate).astype(BF)
    back, gain_mem_part = norm_backward(hidden, inverse2, gain_mem, grad_normed2)
    grad_hidden = dy_low.astype(F32) + back
    hidden_low = grad_hidden.astype(BF)
    grad_attn_out = mm_l(att, hidden_low).astype(BF)
    grad_att = mm_t(hidden_low, attn_out_full).astype(BF)
    grad_att, arrived = lax.optimization_barrier((grad_att, arrived))
    (grad_q, grad_k, grad_v), early, qkv_shard = attention_backward(
        side,
        depth,
        queries,
        keys,
        vals,
        all_keys,
        all_vals,
        lse,
        att,
        grad_att,
        normed,
        (grad_query_w, grad_keys, grad_gate_w, grad_mem_out.astype(BF), grad_attn_out),
        jax.ShapeDtypeStruct((3, cols, cols), BF),
        1,
    )
    grad_rows = mm_l(serve_pick, jnp.concatenate(arrived, axis=0))
    grad_normed = (
        mm_t(grad_q, ask_full) + mm_t(grad_k, key_full) + mm_t(grad_v, value_full)
    )
    grad_x, gain_attn_part = norm_backward(x_rows, inverse, gain_attn, grad_normed)
    grad_x = grad_hidden + grad_x
    gains = jnp.stack([gain_attn_part, gain_mem_part]).reshape(2, owners, block)
    gains = lax.all_to_all(gains.transpose(1, 0, 2), ALL, split_axis=0, concat_axis=0, tiled=True)
    gain_shards = jnp.sum(gains, axis=0)
    sub_shard = early[1].reshape(block, 2, HALF).transpose(1, 0, 2).reshape(2 * block, HALF)
    return (
        out[None, :rows],
        out[None, rows:],
        grad_x[None, :rows],
        grad_x[None, rows:],
        gain_shards[0],
        gain_shards[1],
        qkv_shard,
        early[4],
        early[0],
        sub_shard,
        early[2],
        early[3],
        grad_rows,
    )


def solution(mesh):
    in_specs = (
        P("dp", "fsdp", None),
        P("dp", "fsdp", None),
        P("dp", "fsdp", None),
        P("dp", "fsdp", None),
        P(),
        P(),
        P(None, "fsdp", None),
        P("fsdp", None),
        P("fsdp", None),
        P("fsdp", None),
        P("fsdp", None),
        P("fsdp", None),
        P(("dp", "fsdp"), None),
        P(None, ("dp", "fsdp"), None, None),
        P("dp", "fsdp", None, None),
        P("dp", "fsdp", None, None),
    )
    out_specs = (
        P("dp", "fsdp", None),
        P("dp", "fsdp", None),
        P("dp", "fsdp", None),
        P("dp", "fsdp", None),
        P(("dp", "fsdp")),
        P(("dp", "fsdp")),
        P(None, ("dp", "fsdp"), None),
        P(("dp", "fsdp"), None),
        P(("dp", "fsdp"), None),
        P(("dp", "fsdp"), None),
        P(("dp", "fsdp"), None),
        P(("dp", "fsdp"), None),
        P(("dp", "fsdp"), None),
    )
    return jax.shard_map(
        per_device, mesh=mesh, in_specs=in_specs, out_specs=out_specs, check_vma=False
    )
```

```python
import functools
import jax
import jax.numpy as jnp
from jax import lax
from jax.experimental import pallas as pl
from jax.experimental.pallas import tpu as pltpu
from jax.sharding import PartitionSpec as P
BF = jnp.bfloat16
F32 = jnp.float32
ALL = ("dp", "fsdp")
MESH = pl.DeviceIdType.MESH
LAG = 4
GATHER_LAG = 3
REST_START = 1
REST_DELAY = 6
DEEP_AT = 8
LATE_LAG = 4
LAST_LAG = 14
COLLECT_LAG = 2
AHEAD = 3
HOP_LAG = 1
PAIR = 128
HDIM = 64
MH = 4
HALF = 512
SUB = 256
NEVER = -1e30
PROJECTION_ORDER = ((0, 0), (0, 1), (1, 0), (2, 0), (1, 1), (2, 1))


def mm(left, right):
    return jnp.dot(left, right, preferred_element_type=F32)


def mm_t(left, right):
    return lax.dot_general(left, right, (((1,), (1,)), ((), ())), preferred_element_type=F32)


def mm_l(left, right):
    return lax.dot_general(left, right, (((0,), (0,)), ((), ())), preferred_element_type=F32)


def normalize(matrix, gain_vec):
    inverse = lax.rsqrt(jnp.mean(matrix * matrix, axis=-1, keepdims=True) + 1e-05)
    return (matrix * inverse * gain_vec, inverse)


def norm_backward(matrix, inverse, gain_vec, grad_normed):
    scaled = gain_vec * grad_normed
    cubed = inverse * inverse * inverse
    grad_matrix = inverse * scaled - matrix * cubed * jnp.mean(
        matrix * scaled, axis=-1, keepdims=True
    )
    return (grad_matrix, jnp.sum(grad_normed * matrix * inverse, axis=0))


def grid_of(plane, depth):
    side = 1
    while 2 * side * side < plane:
        side += 1
    return side, depth


def place(side):
    dp = lax.axis_index("dp")
    return (dp // (2 * side), (dp // 2) % side, dp % 2, lax.axis_index("fsdp"))


def device_at(side, y, x, core, z):
    return ((y * side + x) * 2 + core, z)


def greet(side, depth):
    y, x, core, z = place(side)
    barrier = pltpu.get_barrier_semaphore()
    peers = [device_at(side, y, x, 1 - core, z)]
    for hop in range(1, side):
        peers.append(device_at(side, y, (x + hop) % side, core, z))
        peers.append(device_at(side, (y + hop) % side, x, core, z))
    for hop in range(1, depth):
        peers.append(device_at(side, y, x, core, (z + hop) % depth))
    for peer in peers:
        pl.semaphore_signal(barrier, inc=1, device_id=peer, device_id_type=MESH)
    pl.semaphore_wait(barrier, len(peers))


def remote(source, target, send_sem, recv_sem, peer):
    return pltpu.make_async_remote_copy(
        src_ref=source,
        dst_ref=target,
        send_sem=send_sem,
        recv_sem=recv_sem,
        device_id=peer,
        device_id_type=MESH,
    )


class Gather:
    def __init__(self, side, depth, shards, piece=1024):
        self.side, self.depth = side, depth
        self.views, self.outs, self.shapes, self.held, self.layout = [], [], [], [], []
        plane = 2 * side * side
        for shard in shards:
            rows, cols = shard.shape[-2:]
            block, width = rows // plane, min(cols, piece)
            lead = shard.shape[:-2]
            self.views.append(shard.reshape(lead + (side, side, 2, block, cols)))
            leads = range(lead[0]) if lead else (None,)
            self.layout.append(
                [(number, start) for number in leads for start in range(0, cols, width)]
            )
            self.outs.append(
                jax.ShapeDtypeStruct(lead + (depth, side, side, 2, block, cols), BF)
            )
            self.shapes.append(lead + (depth * rows, cols))
            self.held.append(
                pltpu.VMEM((len(self.layout[-1]), side, side, 2, block, width), BF)
            )
        self.count = count = sum(len(columns) for columns in self.layout)
        self.steps = count + depth - 2 + 3 * GATHER_LAG
        dma = pltpu.SemaphoreType.DMA
        self.scratch = self.held + [
            dma((count,)),
            dma((count,)),
            dma((count, depth)),
            dma((count, depth)),
            dma((count, depth)),
            dma((count, depth, side - 1)),
            dma((count, depth, side - 1)),
            dma((count, depth, side - 1)),
            dma((count, depth, side - 1)),
            dma((count, depth)),
            dma((count, depth)),
        ]

    def restore(self, full):
        return [one.reshape(shape) for one, shape in zip(full, self.shapes)]

    def bind(self, sources, outs, scratch):
        self.sources, self.results = sources, outs
        n_in = len(self.layout)
        self.holders = scratch[:n_in]
        (self.in_sem, self.out_sem, self.right_send, self.left_send, self.deep_recv,
         self.one_send, self.one_recv, self.two_send, self.two_recv, self.core_send,
         self.core_recv) = scratch[n_in:]
        self.pieces = []
        for number, columns in enumerate(self.layout):
            width = self.holders[number].shape[-1]
            width = width if sources[number].shape[-1] > width else None
            for inner, (lead, start) in enumerate(columns):
                self.pieces.append((number, lead, start, width, inner))

    def cut(self, refs, k, *spot):
        number, lead, start, width = self.pieces[k][:4]
        ref = refs[number] if lead is None else refs[number].at[lead]
        ref = ref.at[spot] if spot else ref
        if width is None:
            return ref
        return ref.at[(slice(None),) * (len(ref.shape) - 1) + (pl.ds(start, width),)]

    def along_z(self, k, zp, move, source=None):
        y, x, core, z = place(self.side)
        target = self.cut(self.results, k, zp, y, x, core)
        send = self.right_send if move > 0 else self.left_send
        return remote(target if source is None else source, target, send.at[k, zp],
                      self.deep_recv.at[k, zp], device_at(self.side, y, x, core, z + move))

    def one_copy(self, k, zp, hop):
        side = self.side
        y, x, core, z = place(side)
        peer = device_at(side, y, (x + hop) % side, core, z) if k % 2 == 0 else device_at(
            side, (y + hop) % side, x, core, z)
        ref = self.cut(self.results, k, zp, y, x, core)
        return remote(ref, ref, self.one_send.at[k, zp, hop - 1],
                      self.one_recv.at[k, zp, hop - 1], peer)

    def two_copy(self, k, zp, hop):
        side = self.side
        y, x, core, z = place(side)
        x_first = k % 2 == 0
        peer = device_at(side, (y + hop) % side, x, core, z) if x_first else device_at(
            side, y, (x + hop) % side, core, z)
        ref = (self.cut(self.results, k, zp, y, slice(None), core) if x_first
               else self.cut(self.results, k, zp, slice(None), x, core))
        return remote(ref, ref, self.two_send.at[k, zp, hop - 1],
                      self.two_recv.at[k, zp, hop - 1], peer)

    def core_copy(self, k, zp):
        y, x, core, z = place(self.side)
        ref = self.cut(self.results, k, zp, slice(None), slice(None), core)
        return remote(ref, ref, self.core_send.at[k, zp], self.core_recv.at[k, zp],
                      device_at(self.side, y, x, 1 - core, z))

    def take(self, k):
        number, inner = self.pieces[k][0], self.pieces[k][4]
        return pltpu.make_async_copy(self.cut(self.sources, k), self.holders[number].at[inner],
                                     self.in_sem.at[k])

    def put(self, k):
        z = place(self.side)[3]
        number, inner = self.pieces[k][0], self.pieces[k][4]
        return pltpu.make_async_copy(self.holders[number].at[inner],
                                     self.cut(self.results, k, z), self.out_sem.at[k])

    def start(self, k):
        y, x, core, z = place(self.side)
        self.take(k).start()
        own = self.cut(self.sources, k, y, x, core)

        @pl.when(z < self.depth - 1)
        def _():
            self.along_z(k, z, 1, own).start()

        @pl.when(z > 0)
        def _():
            self.along_z(k, z, -1, own).start()

    def step(self, i):
        side, depth = self.side, self.depth
        z = place(side)[3]
        if i < self.count:
            self.take(i).wait()
            self.put(i).start()
        for stage in range(4):
            for distance in range(1, depth):
                k = i - stage * GATHER_LAG - (distance - 1)
                if not 0 <= k < self.count:
                    continue
                for sign in (1, -1):
                    zp = z + sign * distance

                    @pl.when(jnp.logical_and(zp >= 0, zp < depth))
                    def _(k=k, zp=zp, sign=sign, stage=stage):
                        self.arrival(stage, k, zp, sign)

    def arrival(self, stage, k, zp, sign):
        side, depth = self.side, self.depth
        z = place(side)[3]
        if stage == 0:
            self.along_z(k, zp, 1).wait_recv()

            @pl.when(z < depth - 1 if sign < 0 else z > 0)
            def _():
                self.along_z(k, zp, -sign).start()

            for hop in range(1, side):
                self.one_copy(k, zp, hop).start()
        elif stage == 1:
            for hop in range(1, side):
                self.one_copy(k, zp, hop).wait_recv()
            for hop in range(1, side):
                self.two_copy(k, zp, hop).start()
        elif stage == 2:
            for hop in range(1, side):
                self.two_copy(k, zp, hop).wait_recv()
            self.core_copy(k, zp).start()
        else:
            self.core_copy(k, zp).wait_recv()

    def settle(self):
        for k in range(self.count):
            self.put(k).wait()

    def finish(self):
        side, depth = self.side, self.depth
        z = place(side)[3]
        for k in range(self.count):
            for zp in range(depth):
                @pl.when(jnp.logical_and(zp <= z, z < depth - 1))
                def _(k=k, zp=zp):
                    self.along_z(k, zp, 1).wait_send()

                @pl.when(jnp.logical_and(zp >= z, z > 0))
                def _(k=k, zp=zp):
                    self.along_z(k, zp, -1).wait_send()

                @pl.when(zp != z)
                def _(k=k, zp=zp):
                    for hop in range(1, side):
                        self.one_copy(k, zp, hop).wait_send()
                        self.two_copy(k, zp, hop).wait_send()
                    self.core_copy(k, zp).wait_send()


class Reduce:
    def __init__(self, side, depth, grads, piece, lag, deep_at, last_at):
        self.side, self.depth, self.lag = side, depth, lag
        self.deep_at, self.last_at = deep_at, last_at
        self.layout, self.views, self.outs = [], [], []
        self.width = width = piece
        devices = 2 * side * side * depth
        for grad in grads:
            rows, cols = grad.shape[-2:]
            self.block = block = rows // devices
            lead = grad.shape[:-2]
            self.views.append(lead + (side, side, 2, depth, block, cols))
            leads = range(lead[0]) if lead else (None,)
            self.layout += [
                (len(self.outs), number, start) for number in leads for start in range(0, cols, width)
            ]
            self.outs.append(jax.ShapeDtypeStruct(lead + (block, cols), F32))
        self.count = count = len(self.layout)
        self.steps = count + last_at
        dma = pltpu.SemaphoreType.DMA
        self.scratch = [
            pltpu.VMEM((count, side, side, depth, block, width), BF),
            pltpu.VMEM((count, side, side, depth, block, width), BF),
            pltpu.VMEM((count, side - 1, side, depth, block, width), BF),
            pltpu.VMEM((count, side - 1, depth, block, width), BF),
            pltpu.VMEM((count, depth - 1, block, width), BF),
            pltpu.VMEM((count, block, width), F32),
            dma((count,)),
            dma((count,)),
            dma((count,)),
            dma((count, side - 1)),
            dma((count, side - 1)),
            dma((count, side - 1)),
            dma((count, side - 1)),
            dma((count, depth - 1)),
            dma((count, depth - 1)),
        ]

    def bind(self, sources, outs, scratch):
        (self.mine, self.got_core, self.got_one, self.got_two, self.got_deep, self.total,
         self.local_sem, self.core_send, self.core_recv, self.one_send, self.one_recv,
         self.two_send, self.two_recv, self.deep_send, self.deep_recv) = scratch
        self.results, self.sources = outs, sources

    def core_copy(self, k, source):
        y, x, core, z = place(self.side)
        return remote(source, self.got_core.at[k], self.core_send.at[k],
                      self.core_recv.at[k], device_at(self.side, y, x, 1 - core, z))

    def start(self, k):
        core = place(self.side)[2]
        self.core_copy(k, self.sources(k, 1 - core)).start()
        pltpu.make_async_copy(self.sources(k, core), self.mine.at[k], self.local_sem.at[k]).start()

    def one_copy(self, k, hop, x_first):
        side = self.side
        y, x, core, z = place(side)
        peer = device_at(side, y, (x + hop) % side, core, z) if x_first else device_at(
            side, (y + hop) % side, x, core, z)
        source = (self.mine.at[k, :, (x + hop) % side] if x_first
                  else self.mine.at[k, (y + hop) % side])
        return remote(source, self.got_one.at[k, hop - 1], self.one_send.at[k, hop - 1],
                      self.one_recv.at[k, hop - 1], peer)

    def two_copy(self, k, hop, x_first):
        side = self.side
        y, x, core, z = place(side)
        peer = device_at(side, (y + hop) % side, x, core, z) if x_first else device_at(
            side, y, (x + hop) % side, core, z)
        source = (self.mine.at[k, (y + hop) % side, x] if x_first
                  else self.mine.at[k, y, (x + hop) % side])
        return remote(source, self.got_two.at[k, hop - 1], self.two_send.at[k, hop - 1],
                      self.two_recv.at[k, hop - 1], peer)

    def deep_copy(self, k, hop):
        y, x, core, z = place(self.side)
        there = (z + hop) % self.depth
        return remote(self.mine.at[k, y, x, there], self.got_deep.at[k, hop - 1],
                      self.deep_send.at[k, hop - 1], self.deep_recv.at[k, hop - 1],
                      device_at(self.side, y, x, core, there))

    def both_orders(self, k, action):
        @pl.when(k % 2 == 0)
        def _():
            action(True)

        @pl.when(k % 2 == 1)
        def _():
            action(False)

    def added(self, base, others):
        if len(others) == 1:
            return base + others[0]
        value = base.astype(F32)
        for other in others:
            value = value + other.astype(F32)
        return value.astype(base.dtype)

    def after_core(self, k):
        side, depth, mine, got = self.side, self.depth, self.mine, self.got_core
        self.core_copy(k, got.at[k]).wait_recv()
        pltpu.make_async_copy(got.at[k], mine.at[k], self.local_sem.at[k]).wait()

        def add(index, carry):
            spot = (k, index // (side * depth), (index // depth) % side, index % depth)
            mine[spot] = mine[spot] + got[spot]
            return carry

        lax.fori_loop(0, side * side * depth, add, 0)

        def send(x_first):
            for hop in range(1, side):
                self.one_copy(k, hop, x_first).start()

        self.both_orders(k, send)

    def after_one(self, k):
        side, depth, mine = self.side, self.depth, self.mine
        y, x, core, z = place(side)

        def finish(x_first):
            for hop in range(1, side):
                self.one_copy(k, hop, x_first).wait_recv()

            def add(index, carry):
                a, c = index // depth, index % depth
                spot = (k, a, x, c) if x_first else (k, y, a, c)
                mine[spot] = self.added(
                    mine[spot], [self.got_one[k, hop, a, c] for hop in range(side - 1)]
                )
                return carry

            lax.fori_loop(0, side * depth, add, 0)
            for hop in range(1, side):
                self.two_copy(k, hop, x_first).start()

        self.both_orders(k, finish)

    def after_two(self, k):
        side, depth, mine = self.side, self.depth, self.mine
        y, x, core, z = place(side)

        def finish(x_first):
            for hop in range(1, side):
                self.two_copy(k, hop, x_first).wait_recv()

        self.both_orders(k, finish)

        def add(c, carry):
            mine[k, y, x, c] = self.added(
                mine[k, y, x, c], [self.got_two[k, hop, c] for hop in range(side - 1)]
            )
            return carry

        lax.fori_loop(0, depth, add, 0)

    def send_deep(self, k):
        for hop in range(1, self.depth):
            self.deep_copy(k, hop).start()

    def after_deep(self, k):
        y, x, core, z = place(self.side)
        for hop in range(1, self.depth):
            self.deep_copy(k, hop).wait_recv()
        value = self.mine[k, y, x, z].astype(F32)
        for hop in range(self.depth - 1):
            value = value + self.got_deep[k, hop].astype(F32)
        self.total[k] = value

    def step(self, i):
        stages = (
            (0, self.after_core),
            (self.lag, self.after_one),
            (2 * self.lag, self.after_two),
            (self.deep_at, self.send_deep),
            (self.last_at, self.after_deep),
        )
        for lag, action in stages:
            @pl.when(jnp.logical_and(i >= lag, i < self.count + lag))
            def _(lag=lag, action=action):
                action(i - lag)

    def finish(self):
        for k, (number, lead, start) in enumerate(self.layout):
            spot = (slice(None), pl.ds(start, self.width))
            if lead is None:
                self.results[number][spot] = self.total[k]
            else:
                self.results[number][(lead,) + spot] = self.total[k]

        def drain(k, carry):
            self.core_copy(k, self.got_core.at[k]).wait_send()

            def sent(x_first):
                for hop in range(1, self.side):
                    self.one_copy(k, hop, x_first).wait_send()
                    self.two_copy(k, hop, x_first).wait_send()

            self.both_orders(k, sent)
            for hop in range(1, self.depth):
                self.deep_copy(k, hop).wait_send()
            return carry

        lax.fori_loop(0, self.count, drain, 0)


def split_refs(refs, *counts):
    groups, at = [], 0
    for count in counts:
        groups.append(refs[at : at + count])
        at += count
    return groups + [refs[at:]]


def params(call_id, mib):
    return pltpu.CompilerParams(
        collective_id=call_id, has_side_effects=True, vmem_limit_bytes=mib * 1024 * 1024
    )


def half_masks(width):
    lane = lax.broadcasted_iota(jnp.int32, (1, width), 1)
    return (lane < width // 2, lane >= width // 2)


def dot_rows(left, right):
    return lax.dot_general(left, right, (((1,), (1,)), ((), ())), preferred_element_type=F32)


def dot_first(left, right):
    return lax.dot_general(left, right, (((0,), (0,)), ((), ())), preferred_element_type=F32)


def dot_plain(left, right):
    return lax.dot_general(left, right, (((1,), (0,)), ((), ())), preferred_element_type=F32)


def prompt_mask(scores, chunk, z, rows):
    key = lax.broadcasted_iota(jnp.int32, scores.shape, 0) + chunk * rows
    query = lax.broadcasted_iota(jnp.int32, scores.shape, 1)
    seen = jnp.logical_or(query >= rows, key <= query + z * rows)
    return jnp.where(seen, scores, NEVER)


def own_mask(scores):
    key = lax.broadcasted_iota(jnp.int32, scores.shape, 0)
    query = lax.broadcasted_iota(jnp.int32, scores.shape, 1)
    return jnp.where(key <= query, scores, NEVER)


def forward_pair(p, z, rows, depth, q_ref, k_ref, v_ref, keys, vals, att_ref, lse_ref):
    cols = pl.ds(pl.multiple_of(p * PAIR, PAIR), PAIR)
    q_pair = q_ref[:, cols] * jnp.asarray(0.125, BF)
    k_own, v_own = k_ref[pl.ds(rows, rows), cols], v_ref[pl.ds(rows, rows), cols]
    outs = []
    for head, mask in enumerate(half_masks(PAIR)):
        q_head = jnp.where(mask, q_pair, jnp.zeros_like(q_pair))
        scores = [
            prompt_mask(dot_rows(keys[p, chunk], q_head), chunk, z, rows) for chunk in range(depth)
        ]
        own = own_mask(dot_rows(k_own, q_head[rows:]))
        top = jnp.max(scores[0], axis=0, keepdims=True)
        for piece in scores[1:]:
            top = jnp.maximum(top, jnp.max(piece, axis=0, keepdims=True))
        top_c = jnp.maximum(top[:, rows:], jnp.max(own, axis=0, keepdims=True))
        top = jnp.concatenate([top[:, :rows], top_c], axis=1)
        total = jnp.zeros_like(top)
        out = jnp.zeros((PAIR, 2 * rows), F32)
        for chunk in range(depth):
            expo = jnp.exp(scores[chunk] - top)
            total = total + jnp.sum(expo, axis=0, keepdims=True)
            out = out + dot_first(vals[p, chunk], expo.astype(BF))
        expo = jnp.exp(own - top_c)
        total_c = total[:, rows:] + jnp.sum(expo, axis=0, keepdims=True)
        out_c = out[:, rows:] + dot_first(v_own, expo.astype(BF))
        total = jnp.concatenate([total[:, :rows], total_c], axis=1)
        out = jnp.concatenate([out[:, :rows], out_c], axis=1) / total
        lse_ref[pl.ds(2 * p + head, 1), :] = top + jnp.log(total)
        outs.append(out[head * HDIM : (head + 1) * HDIM])
    att_ref[:, cols] = jnp.concatenate(outs, axis=0).T.astype(BF)


def backward_pair(p, z, rows, depth, q_ref, k_ref, v_ref, keys, vals, lse_ref, att_ref, g_ref,
                  dq_ref, dk_ref, dv_ref, part):
    cols = pl.ds(pl.multiple_of(p * PAIR, PAIR), PAIR)
    own_rows = pl.ds(rows, rows)
    q_pair = q_ref[:, cols] * jnp.asarray(0.125, BF)
    g_pair = g_ref[:, cols]
    k_own, v_own = k_ref[own_rows, cols], v_ref[own_rows, cols]
    pulled = (g_pair.astype(F32) * att_ref[:, cols].astype(F32)).T
    masks = half_masks(PAIR)
    q_heads = [jnp.where(mask, q_pair, jnp.zeros_like(q_pair)) for mask in masks]
    g_heads = [jnp.where(mask, g_pair, jnp.zeros_like(g_pair)) for mask in masks]
    lses = [lse_ref[pl.ds(2 * p + head, 1), :] for head in range(2)]
    deltas = [
        jnp.sum(pulled[head * HDIM : (head + 1) * HDIM], axis=0, keepdims=True)
        for head in range(2)
    ]
    dq = [jnp.zeros((PAIR, 2 * rows), F32) for _ in range(2)]
    for chunk in range(depth):
        dk = jnp.zeros((rows, PAIR), F32)
        dv = jnp.zeros((rows, PAIR), F32)
        k_chunk, v_chunk = keys[p, chunk], vals[p, chunk]
        for head in range(2):
            scores = prompt_mask(dot_rows(k_chunk, q_heads[head]), chunk, z, rows)
            prob = jnp.exp(scores - lses[head])
            d_prob = dot_rows(v_chunk, g_heads[head])
            d_score = (prob * (d_prob - deltas[head])).astype(BF)
            dv = dv + dot_plain(prob.astype(BF), g_heads[head])
            dk = dk + dot_plain(d_score, q_heads[head])
            dq[head] = dq[head] + dot_first(k_chunk, d_score)
        part[p, chunk, 0] = dk.astype(BF)
        part[p, chunk, 1] = dv.astype(BF)
    dk = jnp.zeros((rows, PAIR), F32)
    dv = jnp.zeros((rows, PAIR), F32)
    for head in range(2):
        q_head, g_head = q_heads[head][rows:], g_heads[head][rows:]
        scores = own_mask(dot_rows(k_own, q_head))
        prob = jnp.exp(scores - lses[head][:, rows:])
        d_prob = dot_rows(v_own, g_head)
        d_score = (prob * (d_prob - deltas[head][:, rows:])).astype(BF)
        dv = dv + dot_plain(prob.astype(BF), g_head)
        dk = dk + dot_plain(d_score, q_head)
        more = dot_first(k_own, d_score)
        dq[head] = jnp.concatenate([dq[head][:, :rows], dq[head][:, rows:] + more], axis=1)
    dk_ref[own_rows, cols] = dk.astype(BF)
    dv_ref[own_rows, cols] = dv.astype(BF)
    both = jnp.concatenate([dq[0][:HDIM], dq[1][HDIM:]], axis=0) * 0.125
    dq_ref[:, cols] = both.T.astype(BF)


class Exchange:
    def __init__(self, depth, rows, pairs):
        self.depth, self.rows, self.pairs = depth, rows, pairs
        dma = pltpu.SemaphoreType.DMA
        self.scratch = [dma((2, 2, pairs, depth)), dma((2, pairs, depth))]

    def bind(self, owned, gathered, scratch):
        self.owned, self.gathered = owned, gathered
        self.send_sem, self.recv_sem = scratch

    def hop(self, kind, p, zp, move, own=False):
        target = self.gathered[kind].at[p, zp]
        cols = pl.ds(pl.multiple_of(p * PAIR, PAIR), PAIR)
        source = self.owned[kind].at[pl.ds(0, self.rows), cols] if own else target
        z = lax.axis_index("fsdp")
        return remote(source, target, self.send_sem.at[kind, (move + 1) // 2, p, zp],
                      self.recv_sem.at[kind, p, zp], (lax.axis_index("dp"), z + move))

    def offer(self, p):
        z = lax.axis_index("fsdp")
        for move in (1, -1):
            @pl.when(z < self.depth - 1 if move > 0 else z > 0)
            def _(move=move):
                for kind in range(2):
                    self.hop(kind, p, z, move, own=True).start()
        cols = pl.ds(pl.multiple_of(p * PAIR, PAIR), PAIR)
        for kind in range(2):
            self.gathered[kind][p, z] = self.owned[kind][pl.ds(0, self.rows), cols]

    def step(self, i):
        z = lax.axis_index("fsdp")
        for distance in range(1, self.depth):
            p = i - (distance - 1) * HOP_LAG
            for sign in (1, -1):
                zp = z + sign * distance
                seen = jnp.logical_and(zp >= 0, zp < self.depth)

                @pl.when(jnp.logical_and(seen, jnp.logical_and(p >= 0, p < self.pairs)))
                def _(p=p, zp=zp, sign=sign):
                    for kind in range(2):
                        self.hop(kind, p, zp, 1).wait_recv()

                    @pl.when(z < self.depth - 1 if sign < 0 else z > 0)
                    def _():
                        for kind in range(2):
                            self.hop(kind, p, zp, -sign).start()

    def finish(self):
        z = lax.axis_index("fsdp")

        def drain(p, carry):
            for zp in range(self.depth):
                for move in (1, -1):
                    far = zp <= z if move > 0 else zp >= z
                    inner = z < self.depth - 1 if move > 0 else z > 0

                    @pl.when(jnp.logical_and(far, inner))
                    def _(zp=zp, move=move):
                        for kind in range(2):
                            self.hop(kind, p, zp, move).wait_send()
            return carry

        lax.fori_loop(0, self.pairs, drain, 0)


def project(normed_ref, weight, out_ref):
    width = 2 * PAIR

    def run(part, carry):
        cols = pl.ds(pl.multiple_of(part * width, width), width)
        piece = weight[..., cols].reshape(normed_ref.shape[1], width)
        out_ref[:, cols] = dot_plain(normed_ref[...], piece).astype(BF)
        return carry

    lax.fori_loop(0, out_ref.shape[1] // width, run, 0)


def forward_kernel(first, rest, exchange, slots, *refs):
    depth, rows, pairs = exchange.depth, exchange.rows, exchange.pairs
    n = len(rest.views)
    ((picks_ref, normed_ref), shard, shards, outs, weights, full, swap, held,
     others) = split_refs(refs, 2, 1, n, 8, 3, n, len(exchange.scratch), len(first.scratch))
    counts_ref, q_ref, k_ref, v_ref, att_ref, lse_ref, keys, vals = outs
    first.bind([shard[0].at[kind] for kind in (1, 2, 0)], weights, held)
    rest.bind(shards, full, others)
    exchange.bind((k_ref, v_ref), (keys, vals), swap)
    z = lax.axis_index("fsdp")
    blocks = picks_ref.shape[1] // 128
    head = depth - 2 + 3 * GATHER_LAG
    per_turn = -(-blocks // head)
    greet(first.side, depth)
    for k in range(first.count):
        first.start(k)

    def both(turn):
        first.step(turn)
        if 0 <= turn - REST_START < rest.count:
            rest.start(turn - REST_START)
        if turn >= REST_DELAY:
            rest.step(turn - REST_DELAY)

    def gather(i, carry):
        for turn in range(head):
            @pl.when(i == turn)
            def _(turn=turn):
                both(turn)

        for inner in range(per_turn):
            block = i * per_turn + inner

            @pl.when(block < blocks)
            def _(block=block):
                count_block(block, rows, slots, picks_ref, counts_ref)

        return carry

    lax.fori_loop(0, head, gather, 0)
    ahead = min(AHEAD, pairs)
    for k, out_ref in enumerate((k_ref, v_ref, q_ref)):
        both(head + k)
        first.put(k).wait()
        project(normed_ref, weights[k], out_ref)
        if k == 1:
            for p in range(ahead):
                exchange.offer(p)
    for k in range(max(0, first.steps - REST_START), rest.count):
        rest.start(k)
    done = max(0, first.steps - REST_DELAY)
    delay = (depth - 2) * HOP_LAG + 1
    turns = pairs + delay

    def run(i, carry):
        @pl.when(i + ahead < pairs)
        def _():
            exchange.offer(i + ahead)

        exchange.step(i)
        for turn in range(turns):
            number = done + turn
            if number < rest.steps:
                @pl.when(i == turn)
                def _(number=number):
                    rest.step(number)

        @pl.when(i >= delay)
        def _():
            forward_pair(i - delay, z, rows, depth, q_ref, k_ref, v_ref, keys, vals, att_ref,
                         lse_ref)

        return carry

    lax.fori_loop(0, turns, run, 0)
    for number in range(done + turns, rest.steps):
        rest.step(number)
    exchange.finish()
    rest.settle()
    first.finish()
    rest.finish()


def attention_forward(side, depth, picks, normed, w_qkv, shards, slots, call_id):
    rows, width = normed.shape[0] // 2, normed.shape[1]
    pairs = width // PAIR
    first, rest = Gather(side, depth, list(w_qkv)), Gather(side, depth, shards)
    packed = w_qkv.reshape(w_qkv.shape[:1] + first.views[0].shape)
    exchange = Exchange(depth, rows, pairs)
    any_space, vmem = pl.BlockSpec(memory_space=pl.ANY), pl.BlockSpec(memory_space=pltpu.VMEM)
    spread = jax.ShapeDtypeStruct((pairs, depth, rows, PAIR), BF)
    flat = jax.ShapeDtypeStruct(normed.shape, BF)
    results = pl.pallas_call(
        functools.partial(forward_kernel, first, rest, exchange, slots),
        out_shape=(
            jax.ShapeDtypeStruct((2, MH, slots, rows), BF),
            flat,
            flat,
            flat,
            flat,
            jax.ShapeDtypeStruct((2 * pairs, 2 * rows), F32),
            spread,
            spread,
        )
        + tuple(first.outs)
        + tuple(rest.outs),
        in_specs=[vmem] * 2 + [any_space] * (1 + len(rest.views)),
        out_specs=(vmem,) * 11 + (any_space,) * len(rest.views),
        scratch_shapes=exchange.scratch + first.scratch + rest.scratch,
        compiler_params=params(call_id, 56),
    )(picks, normed, packed, *rest.views)
    return results[:8], first.restore(results[8:11]), rest.restore(results[11:])


class Collect:
    def __init__(self, depth, rows, pairs):
        self.depth, self.rows, self.pairs = depth, rows, pairs
        dma = pltpu.SemaphoreType.DMA
        shape = (pairs, depth, 2, rows, PAIR)
        self.scratch = [
            pltpu.VMEM(shape, BF),
            pltpu.VMEM(shape, BF),
            pltpu.VMEM((pairs, 2, rows, PAIR), BF),
            pltpu.VMEM((2, rows, PAIR), F32),
            dma((2, pairs, depth)),
            dma((2, pairs, depth)),
        ]
        self.steps = pairs + (depth - 1) * COLLECT_LAG + 1

    def bind(self, scratch):
        (self.part, self.arrived, self.second, self.whole, self.send_sem,
         self.recv_sem) = scratch

    def hop(self, p, zd, move, final):
        z = lax.axis_index("fsdp")
        way = (move + 1) // 2
        target = self.second.at[p] if final and move < 0 else self.arrived.at[p, zd]
        return remote(self.part.at[p, zd], target, self.send_sem.at[way, p, zd],
                      self.recv_sem.at[way, p, zd], (lax.axis_index("dp"), z + move))

    def flow(self, p, move):
        depth = self.depth
        z = lax.axis_index("fsdp")
        first = z == 0 if move > 0 else z == depth - 1
        for zd in range(depth - 1, -1, -1) if move > 0 else range(depth):
            beyond = zd > z if move > 0 else zd < z

            @pl.when(jnp.logical_and(jnp.logical_not(first), beyond))
            def _(zd=zd):
                self.hop(p, zd, move, False).wait_recv()

                def add(part, carry):
                    self.part[p, zd, part] = self.part[p, zd, part] + self.arrived[p, zd, part]
                    return carry

                lax.fori_loop(0, 2, add, 0)

            @pl.when(jnp.logical_and(jnp.logical_not(first), zd == z))
            def _(zd=zd):
                self.hop(p, zd, move, True).wait_recv()

            @pl.when(zd == z + move)
            def _(zd=zd):
                self.hop(p, zd, move, True).start()

            @pl.when(jnp.logical_and(beyond, zd != z + move))
            def _(zd=zd):
                self.hop(p, zd, move, False).start()

    def step(self, i):
        depth = self.depth
        z = lax.axis_index("fsdp")
        for move in (1, -1):
            stage = z if move > 0 else depth - 1 - z
            p = i - stage * COLLECT_LAG

            @pl.when(jnp.logical_and(p >= 0, p < self.pairs))
            def _(p=p, move=move):
                self.flow(p, move)

    def result(self, p):
        z = lax.axis_index("fsdp")
        depth = self.depth
        whole = self.whole
        whole[...] = self.part[p, z].astype(F32)

        @pl.when(z > 0)
        def _():
            whole[...] = whole[...] + self.arrived[p, z].astype(F32)

        @pl.when(z < depth - 1)
        def _():
            whole[...] = whole[...] + self.second[p].astype(F32)

        return whole[...]

    def finish(self):
        depth = self.depth
        z = lax.axis_index("fsdp")

        def drain(p, carry):
            for zd in range(depth):
                for move in (1, -1):
                    @pl.when(zd > z if move > 0 else zd < z)
                    def _(zd=zd, move=move):
                        self.hop(p, zd, move, False).wait_send()
            return carry

        lax.fori_loop(0, self.pairs, drain, 0)


def produce(late, stage, k, half, normed_ref, grad_ref):
    side, depth, block, width = late.side, late.depth, late.block, late.width
    run = depth * block
    for start in range(0, normed_ref.shape[1], 2 * PAIR):
        value = dot_first(
            normed_ref[:, start : start + 2 * PAIR], grad_ref[:, half * width : (half + 1) * width]
        ).astype(BF)
        for row in range(0, 2 * PAIR, run):
            number = (start + row) // run
            y, x, core = number // (2 * side), (number // 2) % side, number % 2
            stage[k, y, x, :, :, core * width : (core + 1) * width] = value[row : row + run].reshape(
                depth, block, width)


def backward_kernel(early, late, collect, *refs):
    side, depth, rows, pairs = early.side, collect.depth, collect.rows, collect.pairs
    n = len(early.views)
    ins, grads, (dq_ref, dk_ref, dv_ref), sums, (qkv_sum,), swap, first, second = split_refs(
        refs, 9, n, 3, n, 1, len(collect.scratch), len(early.scratch))
    q_ref, k_ref, v_ref, keys, vals, lse_ref, att_ref, g_ref, normed_ref = ins

    def part_of(k, half):
        number, lead, start = early.layout[k]
        ref = grads[number] if lead is None else grads[number].at[lead]
        return ref.at[:, :, half, :, :, pl.ds(start, early.width)]

    early.bind(part_of, sums, first)
    stage = early.got_core

    def late_part(k, half):
        lanes = pl.ds(pl.multiple_of(half * late.width, late.width), late.width)
        return stage.at[k, :, :, :, :, lanes]

    late.bind(late_part, (qkv_sum,), second)
    collect.bind(swap)
    z = lax.axis_index("fsdp")
    greet(side, depth)
    for k in range(early.count):
        early.start(k)
    last = (depth - 1) * COLLECT_LAG
    ready = max(pairs, early.count)
    halfway = max(ready + 2, last + pairs // 2 - 1)
    settled = max(halfway + 2, last + pairs - 1)
    due = [ready, ready + 1, halfway, halfway + 1, settled, settled + 1]
    late_at = 1 + max(when - number for number, when in enumerate(due))

    def run(i, carry):
        @pl.when(i < pairs)
        def _():
            backward_pair(i, z, rows, depth, q_ref, k_ref, v_ref, keys, vals, lse_ref, att_ref,
                          g_ref, dq_ref, dk_ref, dv_ref, collect.part)

        collect.step(i)
        early.step(i)

        @pl.when(jnp.logical_and(i >= last, i < last + pairs))
        def _():
            p = i - last
            cols = pl.ds(pl.multiple_of(p * PAIR, PAIR), PAIR)
            value = collect.result(p)
            dk_ref[pl.ds(0, rows), cols] = value[0].astype(BF)
            dv_ref[pl.ds(0, rows), cols] = value[1].astype(BF)

        late.step(i - late_at)
        for number, when in enumerate(due):
            @pl.when(i == when)
            def _(number=number):
                kind, half = PROJECTION_ORDER[number]
                produce(late, stage, number, half, normed_ref, (dq_ref, dk_ref, dv_ref)[kind])
                late.start(number)

        return carry

    lax.fori_loop(0, max(early.steps, late_at + late.steps), run, 0)
    collect.finish()
    early.finish()
    late.finish()


def attention_backward(side, depth, q, k, v, keys, vals, lse, att, grad_att, normed, grads, w_qkv,
                       call_id):
    rows, width = q.shape[0] // 2, q.shape[1]
    early = Reduce(side, depth, grads, width, LAG, DEEP_AT, DEEP_AT + LAST_LAG)
    late = Reduce(side, depth, (w_qkv,), width // 2, LATE_LAG, 2 * LATE_LAG, 3 * LATE_LAG)
    late.layout = [(0, kind, half * (width // 2)) for kind, half in PROJECTION_ORDER]
    collect = Collect(depth, rows, width // PAIR)
    any_space, vmem = pl.BlockSpec(memory_space=pl.ANY), pl.BlockSpec(memory_space=pltpu.VMEM)
    results = pl.pallas_call(
        functools.partial(backward_kernel, early, late, collect),
        out_shape=(jax.ShapeDtypeStruct(q.shape, BF),) * 3 + tuple(early.outs) + tuple(late.outs),
        in_specs=[vmem] * 9 + [any_space] * len(grads),
        out_specs=(vmem,) * (4 + len(grads)),
        scratch_shapes=collect.scratch + early.scratch + late.scratch,
        compiler_params=params(call_id, 63),
    )(
        q,
        k,
        v,
        keys,
        vals,
        lse,
        att,
        grad_att,
        normed,
        *[grad.reshape(view) for grad, view in zip(grads, early.views)],
    )
    return results[:3], results[3:-1], results[-1]


def count_block(b, rows, slots, picks_ref, counts_ref):
    low, per_word, bits = 16, 5, 6
    groups = -(-(slots // low) // per_word)
    per_head = rows // 128
    cols = pl.ds(pl.multiple_of(b * 128, 128), 128)
    picks = picks_ref[:, cols]
    high = jnp.right_shift(picks, 4)
    group = jnp.right_shift(high * 13, 6)
    word = group * low + jnp.bitwise_and(picks, low - 1)
    unit = jnp.left_shift(jnp.ones_like(picks), bits * (high - per_word * group))
    spot = lax.broadcasted_iota(jnp.int32, (groups * low, 128), 0)
    words = jnp.zeros((groups * low, 128), jnp.int32)
    for pick in range(picks.shape[0]):
        words = words + jnp.where(spot == word[pick : pick + 1], unit[pick : pick + 1], 0)
    part, head = b // (per_head * MH), (b // per_head) % MH
    lanes = pl.ds(pl.multiple_of((b % per_head) * 128, 128), 128)
    for tile in range(slots // low):
        piece = words[(tile // per_word) * low : (tile // per_word + 1) * low]
        count = jnp.bitwise_and(jnp.right_shift(piece, bits * (tile % per_word)), 2**bits - 1)
        counts_ref[part, head, pl.ds(tile * low, low), lanes] = count.astype(F32).astype(BF)


def selector(ids_ref, index, count):
    ids = ids_ref[pl.ds(index, 1), :]
    spot = lax.broadcasted_iota(jnp.int32, (count, ids.shape[1]), 0)
    return jnp.where(spot == ids, 1.0, 0.0).astype(BF)


def picks_kernel(ids_ref, counts_ref, query_ref, keys_ref, weight_ref, mixing_ref, total):
    head = pl.program_id(0)
    rows = counts_ref.shape[3]
    for part in range(2):
        scores = None
        for half in range(2):
            pick = selector(ids_ref, 2 * part + half, SUB)
            slot_keys = dot_first(pick, keys_ref[half * SUB : (half + 1) * SUB]).astype(BF)
            query = query_ref[part * rows : (part + 1) * rows, half * HALF : (half + 1) * HALF]
            piece = dot_rows(slot_keys, query)
            scores = piece if scores is None else scores + piece
        count = counts_ref[part, 0].astype(F32)
        named = count > 0.0
        top = jnp.max(jnp.where(named, scores, -jnp.inf), axis=0, keepdims=True)
        raised = jnp.where(named, count * jnp.exp(scores - top), 0.0)
        weight = raised / jnp.sum(raised, axis=0, keepdims=True)
        weight_ref[part, 0] = weight

        @pl.when(head == 0)
        def _(part=part, weight=weight):
            total[part] = weight

        @pl.when(head > 0)
        def _(part=part, weight=weight):
            total[part] = total[part] + weight

    @pl.when(head == MH - 1)
    def _():
        mixing_ref[...] = total[...].astype(BF)


def slot_weights(ids, counts, mquery, keys_full):
    slots, rows = counts.shape[2:]
    return pl.pallas_call(
        picks_kernel,
        grid=(MH,),
        out_shape=(
            jax.ShapeDtypeStruct(counts.shape, F32),
            jax.ShapeDtypeStruct((2, slots, rows), BF),
        ),
        in_specs=[
            pl.BlockSpec(ids.shape, lambda m: (0, 0)),
            pl.BlockSpec((2, 1, slots, rows), lambda m: (0, m, 0, 0)),
            pl.BlockSpec((2 * rows, 2 * HALF), lambda m: (0, m)),
            pl.BlockSpec((2 * SUB, HALF), lambda m: (m, 0)),
        ],
        out_specs=(
            pl.BlockSpec((2, 1, slots, rows), lambda m: (0, m, 0, 0)),
            pl.BlockSpec((2, slots, rows), lambda m: (0, 0, 0)),
        ),
        scratch_shapes=[pltpu.VMEM((2, slots, rows), F32)],
        cost_estimate=pl.CostEstimate(
            flops=2 * 2 * MH * slots * 2 * HALF * (SUB + rows),
            bytes_accessed=24 * 2**20,
            transcendentals=2 * MH * slots * rows,
        ),
    )(ids, counts, mquery, keys_full)


def picks_back_kernel(block, ids_ref, weight_ref, table_ref, memory_ref, query_ref, keys_ref,
                      grad_query_ref, grad_keys_ref, grad_mixing):
    head = pl.program_id(0)
    rows = weight_ref.shape[3]

    @pl.when(head == 0)
    def _():
        for part in range(2):
            grad_mixing[part] = dot_rows(
                table_ref[part], memory_ref[part * rows : (part + 1) * rows]
            )

    splits = []
    for part in range(2):
        weight = weight_ref[part, 0]
        pulled = weight * grad_mixing[part]
        grad = pulled - weight * jnp.sum(pulled, axis=0, keepdims=True)
        high = grad.astype(BF)
        splits.append((high, (grad - high.astype(F32)).astype(BF)))
    for half in range(2):
        span = slice(half * HALF, (half + 1) * HALF)
        keys = keys_ref[half * SUB : (half + 1) * SUB]
        subs = []
        for part, (high, low) in enumerate(splits):
            pick = selector(ids_ref, 2 * part + half, SUB)
            subs.append((dot_plain(pick, high) + dot_plain(pick, low)).astype(BF))
        sub = jnp.concatenate(subs, axis=1)
        grad_query_ref[:, span] = dot_first(sub, keys).astype(BF)
        total = dot_plain(sub, query_ref[:, span]).astype(BF)
        for shard in range(SUB // (2 * block)):
            for side in range(2):
                start = (2 * shard + side) * block
                row = half * (SUB // 2) + shard * block
                grad_keys_ref[row : row + block, side * HALF : (side + 1) * HALF] = total[
                    start : start + block
                ]


def slot_weights_back(ids, weights, tables, grad_memory, mquery, keys_full, block):
    slots, rows = weights.shape[2:]
    width = tables.shape[2]
    return pl.pallas_call(
        functools.partial(picks_back_kernel, block),
        grid=(MH,),
        out_shape=(
            jax.ShapeDtypeStruct(mquery.shape, BF),
            jax.ShapeDtypeStruct((MH * SUB, 2 * HALF), BF),
        ),
        in_specs=[
            pl.BlockSpec(ids.shape, lambda m: (0, 0)),
            pl.BlockSpec((2, 1, slots, rows), lambda m: (0, m, 0, 0)),
            pl.BlockSpec((2, slots, width), lambda m: (0, 0, 0)),
            pl.BlockSpec((2 * rows, width), lambda m: (0, 0)),
            pl.BlockSpec((2 * rows, 2 * HALF), lambda m: (0, m)),
            pl.BlockSpec((2 * SUB, HALF), lambda m: (m, 0)),
        ],
        out_specs=(
            pl.BlockSpec((2 * rows, 2 * HALF), lambda m: (0, m)),
            pl.BlockSpec((SUB, 2 * HALF), lambda m: (m, 0)),
        ),
        scratch_shapes=[pltpu.VMEM((2, slots, rows), F32)],
        cost_estimate=pl.CostEstimate(
            flops=2 * 2 * MH * slots * rows * (4 * SUB + 4 * HALF),
            bytes_accessed=24 * 2**20,
            transcendentals=0,
        ),
    )(ids, weights, tables, grad_memory, mquery, keys_full)


def one_hot(ids, count):
    return (ids[:, None] == jnp.arange(count, dtype=jnp.int32)[None, :]).astype(BF)


def per_device(
    x_prompt,
    x_cont,
    cot_prompt,
    cot_cont,
    gain_attn,
    gain_mem,
    w_qkv,
    w_attn_out,
    w_mem_query,
    sub_keys,
    w_gate,
    w_mem_out,
    value_rows,
    request,
    slot_prompt,
    slot_cont,
):
    shard_rows, width = value_rows.shape
    owners, capacity = request.shape[2:]
    slots = owners * capacity
    rows = x_prompt.shape[1]
    cols = w_qkv.shape[2]
    block = cols // owners
    side, depth = grid_of(lax.axis_size("dp"), lax.axis_size("fsdp"))

    asked = lax.all_to_all(request[:, 0], ALL, split_axis=1, concat_axis=1, tiled=True)
    def swap(values):
        values = values.reshape(owners, capacity, width)
        swapped = lax.all_to_all(values, ALL, split_axis=0, concat_axis=0, tiled=True)
        return swapped.reshape(slots, width)

    offsets = jnp.maximum(request[:, 0].reshape(2, slots), 0)
    picked = (jnp.arange(slots, dtype=jnp.int32) // capacity)[None] * shard_rows + offsets
    ids = jnp.stack([picked // SUB, picked % SUB], axis=1).reshape(4, slots)
    x_rows = jnp.concatenate([x_prompt[0], x_cont[0]], axis=0).astype(F32)
    dy_low = jnp.concatenate([cot_prompt[0], cot_cont[0]], axis=0)
    normed, inverse = normalize(x_rows, gain_attn)
    normed = normed.astype(BF)
    picks = jnp.stack([slot_prompt[0], slot_cont[0]]).transpose(3, 0, 2, 1)
    picks = picks.reshape(picks.shape[0], -1)
    results, (key_full, value_full, ask_full), full = attention_forward(
        side,
        depth,
        picks,
        normed,
        w_qkv,
        (w_attn_out, w_mem_query, sub_keys, w_gate, w_mem_out),
        slots,
        0,
    )
    counts, queries, keys, vals, att, lse, all_keys, all_vals = results
    attn_out_full, query_full, keys_full, gate_full, mem_out_full = full
    att, asked = lax.optimization_barrier((att, asked))
    serve_pick = one_hot(asked.reshape(-1), shard_rows)
    served = mm(serve_pick, value_rows).astype(BF).reshape(2, owners, capacity, width)
    tables = lax.all_to_all(served, ALL, split_axis=1, concat_axis=1, tiled=True)
    tables = tables.reshape(2, slots, width)
    hidden = x_rows + mm(att, attn_out_full)
    normed2, inverse2 = normalize(hidden, gain_mem)
    normed2 = normed2.astype(BF)

    mquery = mm(normed2, query_full).astype(BF)
    gate_pre = mm(normed2, gate_full)
    weights, mixing = slot_weights(ids, counts, mquery, keys_full)
    memory_out = lax.dot_general(
        mixing, tables, (((1,), (1,)), ((0,), (0,))), preferred_element_type=F32
    ).reshape(2 * rows, width)
    sigmoid_gate = jax.nn.sigmoid(gate_pre)
    blended = (memory_out * (gate_pre * sigmoid_gate)).astype(BF)
    out = (hidden + mm(blended, mem_out_full)).astype(BF)

    grad_blend = mm_t(dy_low, mem_out_full)
    grad_mem_out = mm_l(blended, dy_low)
    grad_memory = (grad_blend * gate_pre * sigmoid_gate).astype(BF)
    grad_gate = (
        grad_blend * memory_out * sigmoid_gate * (1.0 + gate_pre * (1.0 - sigmoid_gate))
    ).astype(BF)
    slot_grads = lax.dot_general(
        mixing,
        grad_memory.reshape(2, rows, width),
        (((2,), (1,)), ((0,), (0,))),
        preferred_element_type=F32,
    ).astype(BF)
    arrived = [None, swap(slot_grads[1])]
    grad_query, grad_keys = slot_weights_back(
        ids, weights, tables, grad_memory, mquery, keys_full, block
    )
    grad_query, arrived[1], late = lax.optimization_barrier((grad_query, arrived[1], slot_grads[0]))
    arrived[0] = swap(late)
    grad_normed2 = mm_t(grad_query, query_full) + mm_t(grad_gate, gate_full)
    grad_query_w = mm_l(normed2, grad_query).astype(BF)
    grad_gate_w = mm_l(normed2, grad_gate).astype(BF)
    back, gain_mem_part = norm_backward(hidden, inverse2, gain_mem, grad_normed2)
    grad_hidden = dy_low.astype(F32) + back
    hidden_low = grad_hidden.astype(BF)
    grad_attn_out = mm_l(att, hidden_low).astype(BF)
    grad_att = mm_t(hidden_low, attn_out_full).astype(BF)
    grad_att, arrived = lax.optimization_barrier((grad_att, arrived))
    (grad_q, grad_k, grad_v), early, qkv_shard = attention_backward(
        side,
        depth,
        queries,
        keys,
        vals,
        all_keys,
        all_vals,
        lse,
        att,
        grad_att,
        normed,
        (grad_query_w, grad_keys, grad_gate_w, grad_mem_out.astype(BF), grad_attn_out),
        jax.ShapeDtypeStruct((3, cols, cols), BF),
        1,
    )
    grad_rows = mm_l(serve_pick, jnp.concatenate(arrived, axis=0))
    grad_normed = (
        mm_t(grad_q, ask_full) + mm_t(grad_k, key_full) + mm_t(grad_v, value_full)
    )
    grad_x, gain_attn_part = norm_backward(x_rows, inverse, gain_attn, grad_normed)
    grad_x = grad_hidden + grad_x
    gains = jnp.stack([gain_attn_part, gain_mem_part]).reshape(2, owners, block)
    gains = lax.all_to_all(gains.transpose(1, 0, 2), ALL, split_axis=0, concat_axis=0, tiled=True)
    gain_shards = jnp.sum(gains, axis=0)
    sub_shard = early[1].reshape(block, 2, HALF).transpose(1, 0, 2).reshape(2 * block, HALF)
    return (
        out[None, :rows],
        out[None, rows:],
        grad_x[None, :rows],
        grad_x[None, rows:],
        gain_shards[0],
        gain_shards[1],
        qkv_shard,
        early[4],
        early[0],
        sub_shard,
        early[2],
        early[3],
        grad_rows,
    )


def solution(mesh):
    in_specs = (
        P("dp", "fsdp", None),
        P("dp", "fsdp", None),
        P("dp", "fsdp", None),
        P("dp", "fsdp", None),
        P(),
        P(),
        P(None, "fsdp", None),
        P("fsdp", None),
        P("fsdp", None),
        P("fsdp", None),
        P("fsdp", None),
        P("fsdp", None),
        P(("dp", "fsdp"), None),
        P(None, ("dp", "fsdp"), None, None),
        P("dp", "fsdp", None, None),
        P("dp", "fsdp", None, None),
    )
    out_specs = (
        P("dp", "fsdp", None),
        P("dp", "fsdp", None),
        P("dp", "fsdp", None),
        P("dp", "fsdp", None),
        P(("dp", "fsdp")),
        P(("dp", "fsdp")),
        P(None, ("dp", "fsdp"), None),
        P(("dp", "fsdp"), None),
        P(("dp", "fsdp"), None),
        P(("dp", "fsdp"), None),
        P(("dp", "fsdp"), None),
        P(("dp", "fsdp"), None),
        P(("dp", "fsdp"), None),
    )
    return jax.shard_map(
        per_device, mesh=mesh, in_specs=in_specs, out_specs=out_specs, check_vma=False
    )
```
